32 devices in a mesh: wide: 8 (over y, x, core), narrow: 4 (over z).
Axes of the slice: x: 2, y: 2, z: 4, core: 2. Of those that a mesh axis runs over, the one named last changes fastest.
Arguments:
- tokens: bfloat16 [16384, 1024], P(('wide', 'narrow')), may hold values from -32 to 32
- cotangent: bfloat16 [16384, 1024], P(('wide', 'narrow')), may hold values from -6 to 6
- seq_lengths: int32 [8, 3], P('wide'), may hold values from 1 to 1536, 2048 in all within a row
- step_count: int32 [1], replicated, may hold values from 6 to 20
- norm_params: float32 [2, 1024], replicated, may hold values from -1 to 4.5, as said below
- norm_first: float32 [2, 1024], replicated, may hold values from -12 to 12
- norm_second: float32 [2, 1024], replicated, may hold values from 8 to 32
- proj_weight: float32 [1024, 3072], P('narrow', 'wide'), may hold values from -0.1875 to 0.1875
- proj_first: float32 [1024, 3072], P('narrow', 'wide'), may hold values from -6 to 6
- proj_second: float32 [1024, 3072], P('narrow', 'wide'), may hold values from 2.2 to 9
- merge_weight: float32 [1024, 1024], P('narrow', 'wide'), may hold values from -0.75 to 0.75
- merge_first: float32 [1024, 1024], P('narrow', 'wide'), may hold values from -1.2 to 1.2
- merge_second: float32 [1024, 1024], P('narrow', 'wide'), may hold values from 0.09 to 0.36
- up_weight: float32 [1024, 4096], P(None, 'narrow'), may hold values from -0.1875 to 0.1875
- up_first: float32 [1024, 4096], P(None, 'narrow'), may hold values from -1.4 to 1.4
- up_second: float32 [1024, 4096], P(None, 'narrow'), may hold values from 0.12 to 0.5
- down_weight: float32 [4096, 1024], P('narrow'), may hold values from -0.09375 to 0.09375
- down_first: float32 [4096, 1024], P('narrow'), may hold values from -3.4 to 3.4
- down_second: float32 [4096, 1024], P('narrow'), may hold values from 0.7 to 2.9
Outputs:
- layer_out: bfloat16 [16384, 1024], P(('wide', 'narrow'))
- input_grad: float32 [16384, 1024], P(('wide', 'narrow'))
- grad_norm: float32 [1], replicated
- residual_rms: float32 [1], replicated
- norm_grads: float32 [2, 1024], replicated
- new_norm_params: float32 [2, 1024], replicated
- new_norm_first: float32 [2, 1024], replicated
- new_norm_second: float32 [2, 1024], replicated
- new_proj_weight: float32 [1024, 3072], P('narrow', 'wide')
- new_proj_first: float32 [1024, 3072], P('narrow', 'wide')
- new_proj_second: float32 [1024, 3072], P('narrow', 'wide')
- new_merge_weight: float32 [1024, 1024], P('narrow', 'wide')
- new_merge_first: float32 [1024, 1024], P('narrow', 'wide')
- new_merge_second: float32 [1024, 1024], P('narrow', 'wide')
- new_up_weight: float32 [1024, 4096], P(None, 'narrow')
- new_up_first: float32 [1024, 4096], P(None, 'narrow')
- new_up_second: float32 [1024, 4096], P(None, 'narrow')
- new_down_weight: float32 [4096, 1024], P('narrow')
- new_down_first: float32 [4096, 1024], P('narrow')
- new_down_second: float32 [4096, 1024], P('narrow')
- branch_norms: float32 [2], replicated
- new_proj_copy: bfloat16 [1024, 3072], P('narrow', 'wide')
- new_merge_copy: bfloat16 [1024, 1024], P('narrow', 'wide')
- new_up_copy: bfloat16 [1024, 4096], P(None, 'narrow')
- new_down_copy: bfloat16 [4096, 1024], P('narrow')
The draws below stay inside these ranges and needn't reach their ends.
Inputs may be any that keep to these rules, and one draw needn't show every extreme that they name: `seq_lengths`: row g holds the lengths of the 3 sequences of group g, in order; they sum to 2048, and in every row the longest is exactly 1536. `norm_params`: row 0 holds the gains (positive), row 1 the biases.
All inputs are finite; a program needn't handle non-finite values.
Results may differ from the reference program's by a relative error of at most 0.02.
Values may be sent and summed in bfloat16 or wider, within the bound.
A program may use at most 320 MiB of HBM per device.

```python
import math
from functools import partial
import jax
import jax.numpy as jnp
import numpy as np
from jax import lax

HEADS = 16
HEAD = 64
D = 1024
ROT = 16
FF = 4096
TOK_DEV = 512
GROUP_TOK = 2048
TOKENS = 16384
SEQS = 3
MOST = 1536
NPARAMS = 12584960
N_WIDE = 8


def draw_tokens(key, part):
    normal_key, scale_key = jax.random.split(key)
    row_ramp = jnp.arange(TOKENS, dtype=jnp.float32)[:, None] / (TOKENS - 1)
    entries = jnp.clip(jax.random.normal(normal_key, (TOKENS, D), jnp.float32), -4.0, 4.0)
    rough = jnp.exp(jax.random.uniform(scale_key, (TOKENS, 1), jnp.float32, -0.35, 0.35))
    values = entries * rough * (1.0 + 2.0 * row_ramp)
    return values.astype(jnp.bfloat16)


def draw_norm_params(key, part):
    gain_key, bias_key = jax.random.split(key)
    feature = jnp.arange(D, dtype=jnp.float32) / (D - 1)
    rough = jnp.exp(jax.random.uniform(gain_key, (D,), jnp.float32, -0.35, 0.35))
    gains = (0.5 + feature) * rough
    biases = jnp.clip(0.3 * jax.random.normal(bias_key, (D,), jnp.float32), -1.0, 1.0)
    return jnp.stack([gains, biases]).astype(jnp.float32)


def levels(stream_key, extent, shards, smallest, high):
    level = 1.0
    for dim, blocks in shards:
        draws = jax.random.uniform(jax.random.fold_in(jax.random.fold_in(stream_key, 6), dim), (blocks,), jnp.float32, smallest / len(shards), high / len(shards))
        level = level * jnp.repeat(jnp.exp(draws), extent[dim] // blocks).reshape((-1,) + (1,) * (len(extent) - 1 - dim))
    return level


def split_up(amount, total, most, lean):
    weights = [(1 << 20) // math.isqrt(grade ** lean) + 1 for grade in range(2, amount + 1)]
    rest, given = total - most - (amount - 1), [1] * (amount - 1)
    while rest > 0:
        movable = [i for i in range(amount - 1) if given[i] < most]
        mass, left = sum([weights[i] for i in movable]), rest
        for i in movable:
            extra = min(most - given[i], max(1, left * weights[i] // mass), rest)
            given[i] = given[i] + extra
            rest = rest - extra
    return np.array([most] + given)


def uneven_parts(own_key, amount, total, bound, skew):
    if amount == 2:
        one = jax.random.randint(own_key, (), max(1, total - bound), min(bound, total - 1) + 1)
        return jnp.stack([one, total - one])
    tallies = jnp.asarray(split_up(amount, total, bound, skew), jnp.int32)
    pairs = (amount - 1) // 2
    source_of, taker = tallies[1:1 + 2 * pairs:2], tallies[2:2 + 2 * pairs:2]
    room = jnp.minimum(source_of - 1, bound - taker)
    shifted = jax.random.randint(jax.random.fold_in(own_key, 1), (pairs,), 0, 1 << 20) % (room + 1)
    tallies = tallies.at[1:1 + 2 * pairs:2].set(source_of - shifted).at[2:2 + 2 * pairs:2].set(taker + shifted)
    return tallies[jax.random.permutation(jax.random.fold_in(own_key, 2), amount)]


def bell_draw(stream_key, shape, scale, limit, cuts=(), held_as=jnp.bfloat16):
    values = jax.random.normal(stream_key, shape, jnp.float32) * scale
    if len(cuts) > 0:
        values = levels(stream_key, shape, cuts, -0.22, 0.18) * values
    return jnp.clip(values, min=-limit, max=limit).astype(held_as)


def setup_inputs(seed: int = 0) -> dict:
    key_of = jax.random.split(jax.random.key(seed), 20)
    tokens = draw_tokens(jax.random.fold_in(key_of[19], 71), 0)
    cotangent = bell_draw(key_of[1], (TOKENS, D), 1.0, 6.0, ((0, 32),))
    seq_lengths = jax.vmap(lambda own: uneven_parts(own, SEQS, GROUP_TOK, MOST, 2))(jax.random.split(key_of[2], N_WIDE)).reshape((N_WIDE, SEQS)).astype(jnp.int32)
    step_count = jax.random.randint(key_of[3], (1,), 6, 21).astype(jnp.int32)
    norm_params = draw_norm_params(jax.random.fold_in(key_of[19], 71), 0)
    norm_first = bell_draw(key_of[5], (2, D), 3.0, 12.0, (), jnp.float32)
    norm_second = jnp.clip(jnp.exp(jax.random.uniform(key_of[6], (2, D), jnp.float32, math.log(8.0), math.log(32.0))), 8.0, 32.0)
    proj_weight = bell_draw(key_of[7], (D, 3 * D), D ** -0.5, 0.1875, ((0, 4), (1, 8)), jnp.float32)
    proj_first = bell_draw(key_of[8], (D, 3 * D), 1.5, 6.0, ((0, 4), (1, 8)), jnp.float32)
    proj_second = jnp.clip(jnp.exp(math.log(9.0) - 1.4087672 * jax.random.uniform(key_of[9], (D, 3 * D), jnp.float32) ** levels(key_of[9], (D, 3 * D), ((0, 4), (1, 8)), -0.2, 0.2)), 2.2, 9.0)
    merge_weight = bell_draw(key_of[10], (D, D), (D // 16) ** -0.5, 0.75, ((0, 4), (1, 8)), jnp.float32)
    merge_first = bell_draw(key_of[11], (D, D), 0.3, 1.2, ((0, 4), (1, 8)), jnp.float32)
    merge_second = jnp.clip(jnp.exp(math.log(0.36) - 1.3862944 * jax.random.uniform(key_of[12], (D, D), jnp.float32) ** levels(key_of[12], (D, D), ((0, 4), (1, 8)), -0.2, 0.2)), 0.09, 0.36)
    up_weight = bell_draw(key_of[13], (D, FF), D ** -0.5, 0.1875, ((1, 4),), jnp.float32)
    up_first = bell_draw(key_of[14], (D, FF), 0.35, 1.4, ((1, 4),), jnp.float32)
    up_second = jnp.clip(jnp.exp(math.log(0.5) - 1.4271164 * jax.random.uniform(key_of[15], (D, FF), jnp.float32) ** levels(key_of[15], (D, FF), ((1, 4),), -0.2, 0.2)), 0.12, 0.5)
    down_weight = bell_draw(key_of[16], (FF, D), FF ** -0.5, 0.09375, ((0, 4),), jnp.float32)
    down_first = bell_draw(key_of[17], (FF, D), 0.85, 3.4, ((0, 4),), jnp.float32)
    down_second = jnp.clip(jnp.exp(math.log(2.9) - 1.42138573 * jax.random.uniform(key_of[18], (FF, D), jnp.float32) ** levels(key_of[18], (FF, D), ((0, 4),), -0.2, 0.2)), 0.7, 2.9)
    return dict(tokens=tokens, cotangent=cotangent, seq_lengths=seq_lengths, step_count=step_count, norm_params=norm_params, norm_first=norm_first, norm_second=norm_second, proj_weight=proj_weight, proj_first=proj_first, proj_second=proj_second, merge_weight=merge_weight, merge_first=merge_first, merge_second=merge_second, up_weight=up_weight, up_first=up_first, up_second=up_second, down_weight=down_weight, down_first=down_first, down_second=down_second)


norm_eps = 1e-05
adam_eps = 1e-08
beta_first = 0.5
beta_second = 0.5
decay_rate = 0.01
matrix_rate = 0.1
norm_rate = 1.0
warmup_steps = 20.0
masked_score = -1e+30
highest = lax.Precision.HIGHEST

@jax.custom_vjp
def low(v):
    return lax.optimization_barrier(v.astype(jnp.bfloat16)).astype(jnp.float32)

@jax.custom_vjp
def low_back(v):
    return v

def low_keep(v):
    return (low(v), None)

def low_pass(kept, grad):
    return (grad,)

def back_keep(v):
    return (v, None)

def back_low(kept, grad):
    return (low(grad),)
low.defvjp(low_keep, low_pass)
low_back.defvjp(back_keep, back_low)

def locate(lengths, first_index, row_count):
    token_index = first_index + jnp.arange(row_count, dtype=jnp.int32)
    seq_ends = jnp.cumsum(lengths).astype(jnp.int32)
    starts = seq_ends - lengths
    segment = lax.optimization_barrier(jnp.sum((seq_ends[None, :] <= token_index[:, None]).astype(jnp.int32), axis=1, dtype=jnp.int32))
    choose = segment[:, None] == jnp.arange(lengths.shape[0], dtype=jnp.int32)[None, :]
    seq_start = lax.optimization_barrier(jnp.sum(jnp.where(choose, starts[None, :], 0), axis=1, dtype=jnp.int32))
    return (segment, token_index, token_index - seq_start)

def rotary_tables(position):
    half_rot = ROT // 2
    frequency = jnp.power(10000.0, -2.0 * jnp.arange(half_rot, dtype=jnp.float32) / ROT)
    phases = position.astype(jnp.float32)[:, None] * frequency[None, :]
    return (jnp.cos(phases), jnp.sin(phases))

def rotate(field, cosine_rows, sine_rows):
    half_rot = ROT // 2
    first_half = field[:, :, :half_rot]
    second_half = field[:, :, half_rot:ROT]
    cos_rows = cosine_rows[:, None, :]
    sin_rows = sine_rows[:, None, :]
    return jnp.concatenate([first_half * cos_rows - second_half * sin_rows, second_half * cos_rows + first_half * sin_rows, field[:, :, ROT:]], axis=2)

def attend(queries, keys_all, values, segment, token_index):
    score_scale = HEAD ** (-0.5)

    def one_group(group_items):
        group_query, group_key, group_value, group_seg, group_index = group_items

        def one_block(block_items):
            block_query, block_seg, block_index = block_items
            scores = low_back(jnp.einsum('qhd,khd->hqk', block_query, group_key, precision=highest) * score_scale)
            allowed = (block_seg[:, None] == group_seg[None, :]) & (group_index[None, :] <= block_index[:, None])
            scores = jnp.where(allowed[None], scores, masked_score)
            weights = jax.nn.softmax(scores, axis=-1)
            return jnp.einsum('hqk,khd->qhd', low(weights), group_value, precision=highest)
        blocks = (group_query.reshape(GROUP_TOK // TOK_DEV, TOK_DEV, HEADS, HEAD), group_seg.reshape(GROUP_TOK // TOK_DEV, TOK_DEV), group_index.reshape(GROUP_TOK // TOK_DEV, TOK_DEV))
        return lax.map(jax.checkpoint(one_block), blocks).reshape(GROUP_TOK, D)
    group_items = (queries.reshape(N_WIDE, GROUP_TOK, HEADS, HEAD), keys_all.reshape(N_WIDE, GROUP_TOK, HEADS, HEAD), values.reshape(N_WIDE, GROUP_TOK, HEADS, HEAD), segment.reshape(N_WIDE, GROUP_TOK), token_index.reshape(N_WIDE, GROUP_TOK))
    return lax.map(one_group, group_items).reshape(TOKENS, D)

def forward(residual, norm_vec, proj_matrix, merge_matrix, up_matrix, down_matrix, segment, token_index, position):
    center = residual - lax.optimization_barrier(jnp.mean(residual, axis=1, keepdims=True))
    inv_std = lax.rsqrt(lax.optimization_barrier(jnp.mean(center * center, axis=1, keepdims=True)) + norm_eps)
    normed = low(center * inv_std * norm_vec[0] + norm_vec[1])
    projected = low_back(jnp.dot(normed, proj_matrix, precision=highest))
    cosine_rows, sine_rows = rotary_tables(position)
    queries = low(rotate(projected[:, :D].reshape(TOKENS, HEADS, HEAD), cosine_rows, sine_rows))
    keys_all = low(rotate(projected[:, D:2 * D].reshape(TOKENS, HEADS, HEAD), cosine_rows, sine_rows))
    values = low(projected[:, 2 * D:].reshape(TOKENS, HEADS, HEAD))
    attended = low(low_back(attend(queries, keys_all, values, segment, token_index)))
    merged = jnp.dot(attended, merge_matrix, precision=highest)
    hidden = low_back(jnp.dot(normed, up_matrix, precision=highest))
    activated = low(jax.nn.gelu(hidden, approximate=False))
    branch = jnp.dot(activated, down_matrix, precision=highest)
    return (residual + merged + branch, (merged, branch))

def adam_update(weight, first_moment, second_moment, grad_value, step_rate, decay_coef, first_fix, second_fix):
    new_first = beta_first * first_moment + (1.0 - beta_first) * grad_value
    new_second = beta_second * second_moment + (1.0 - beta_second) * grad_value * grad_value
    step_ratio = new_first / first_fix / (jnp.sqrt(new_second / second_fix) + adam_eps)
    return (weight - step_rate * (step_ratio + decay_coef * weight), new_first, new_second)

def reference(tokens, cotangent, seq_lengths, step_count, norm_params, norm_first, norm_second, proj_weight, proj_first, proj_second, merge_weight, merge_first, merge_second, up_weight, up_first, up_second, down_weight, down_first, down_second):
    segment, token_index, position = jax.vmap(partial(locate, first_index=0, row_count=GROUP_TOK))(seq_lengths)
    segment = segment.reshape(TOKENS)
    token_index = token_index.reshape(TOKENS)
    position = position.reshape(TOKENS)

    def run(residual, norm_vec, proj_matrix, merge_matrix, up_matrix, down_matrix):
        return forward(residual, norm_vec, proj_matrix, merge_matrix, up_matrix, down_matrix, segment, token_index, position)
    result, pullback, branches = jax.vjp(run, tokens.astype(jnp.float32), norm_params, low(proj_weight), low(merge_weight), low(up_weight), low(down_weight), has_aux=True)
    merged, branch = branches
    gradients = pullback(cotangent.astype(jnp.float32))
    input_grad = gradients[0]
    norm_grad, proj_grad, merge_grad, up_grad, down_grad = (gradients[1], gradients[2], gradients[3], gradients[4], gradients[5])
    total_squares = jnp.sum(norm_grad * norm_grad) + jnp.sum(proj_grad * proj_grad) + jnp.sum(merge_grad * merge_grad) + jnp.sum(up_grad * up_grad) + jnp.sum(down_grad * down_grad)
    grad_norm = jnp.sqrt(total_squares)
    clip_factor = jnp.minimum(1.0, math.sqrt(NPARAMS) / grad_norm)
    step_value = step_count[0].astype(jnp.float32)
    first_fix = 1.0 - jnp.power(beta_first, step_value)
    second_fix = 1.0 - jnp.power(beta_second, step_value)
    ramp = jnp.minimum(1.0, step_value / warmup_steps)
    norm_clipped = norm_grad * clip_factor
    new_norm = adam_update(norm_params, norm_first, norm_second, norm_clipped, norm_rate * ramp, 0.0, first_fix, second_fix)
    new_proj = adam_update(proj_weight, proj_first, proj_second, proj_grad * clip_factor, matrix_rate * ramp, decay_rate, first_fix, second_fix)
    new_merge = adam_update(merge_weight, merge_first, merge_second, merge_grad * clip_factor, matrix_rate * ramp, decay_rate, first_fix, second_fix)
    new_up = adam_update(up_weight, up_first, up_second, up_grad * clip_factor, matrix_rate * ramp, decay_rate, first_fix, second_fix)
    new_down = adam_update(down_weight, down_first, down_second, down_grad * clip_factor, matrix_rate * ramp, decay_rate, first_fix, second_fix)
    residual_rms = jnp.sqrt(jnp.mean(result * result)).reshape(1)
    branch_norms = jnp.stack([jnp.sqrt(jnp.mean(merged * merged)), jnp.sqrt(jnp.mean(branch * branch))])
    return (result.astype(jnp.bfloat16), input_grad, grad_norm.reshape(1), residual_rms, norm_clipped, new_norm[0], new_norm[1], new_norm[2], new_proj[0], new_proj[1], new_proj[2], new_merge[0], new_merge[1], new_merge[2], new_up[0], new_up[1], new_up[2], new_down[0], new_down[1], new_down[2], branch_norms, new_proj[0].astype(jnp.bfloat16), new_merge[0].astype(jnp.bfloat16), new_up[0].astype(jnp.bfloat16), new_down[0].astype(jnp.bfloat16))
```

```python
from functools import partial
import math

import jax
import jax.numpy as jnp
from jax import lax
from jax.experimental import pallas as pl
from jax.experimental.pallas import tpu as pltpu
from jax.sharding import PartitionSpec as P

HEADS = 16
HEAD = 64
D = 1024
ROT = 16
LANES = 128
ROW_BLOCK = 512
NPARAMS = 12584960


norm_eps = 1e-05
adam_eps = 1e-08
beta_first = 0.5
beta_second = 0.5
decay_rate = 0.01
matrix_rate = 0.1
norm_rate = 1.0
warmup_steps = 20.0
masked_score = -1e30


def dot_last(left_side, right_side):
    return lax.dot_general(
        left_side, right_side, (((1,), (1,)), ((), ())), preferred_element_type=jnp.float32
    )


def dot_plain(left_side, right_side):
    return lax.dot_general(
        left_side, right_side, (((1,), (0,)), ((), ())), preferred_element_type=jnp.float32
    )


def dot_first(left_side, right_side):
    return lax.dot_general(
        left_side, right_side, (((0,), (0,)), ((), ())), preferred_element_type=jnp.float32
    )


def locate(lengths, token_index):
    seq_ends = jnp.cumsum(lengths)
    starts = seq_ends - lengths
    segment = jnp.sum(
        (seq_ends[None, :] <= token_index[:, None]).astype(jnp.int32), axis=1, dtype=jnp.int32
    )
    choose = segment[:, None] == jnp.arange(lengths.shape[0], dtype=jnp.int32)[None, :]
    seq_start = jnp.sum(jnp.where(choose, starts[None, :], 0), axis=1, dtype=jnp.int32)
    seq_end = jnp.sum(jnp.where(choose, seq_ends[None, :], 0), axis=1, dtype=jnp.int32)
    return (seq_start, seq_end)


def rotary_tables(position):
    half_rot = ROT // 2
    frequency = jnp.power(10000.0, -2.0 * jnp.arange(half_rot, dtype=jnp.float32) / ROT)
    row = jnp.concatenate([frequency, frequency, jnp.zeros((HEAD - ROT,), jnp.float32)])
    row = jnp.tile(row, LANES // HEAD)
    sign = jnp.where(jnp.arange(LANES) % HEAD < half_rot, -1.0, 1.0)
    phases = position.astype(jnp.float32)[:, None] * row[None, :]
    return (jnp.cos(phases), jnp.sin(phases) * sign[None, :])


def partner(field):
    half_rot = ROT // 2
    lane = lax.broadcasted_iota(jnp.int32, field.shape, 1) % HEAD
    return jnp.where(
        lane < half_rot,
        pltpu.roll(field, LANES - half_rot, 1),
        pltpu.roll(field, half_rot, 1),
    )


def project_kernel(rows_ref, weight_ref, cos_ref, sin_ref, out_ref):
    width = out_ref.shape[1]
    projected = dot_plain(rows_ref[...], weight_ref[...])
    for first in range(0, width, LANES):
        piece = projected[:, first : first + LANES]
        part = first // LANES % 3
        if part < 2:
            piece = piece * cos_ref[...] + partner(piece) * sin_ref[...]
        if part == 0:
            piece = piece * HEAD ** (-0.5)
        out_ref[:, first : first + LANES] = piece.astype(jnp.bfloat16)


def project(rows, weight, cosine, sine):
    count, depth = rows.shape
    width = weight.shape[1]
    block = min(ROW_BLOCK, count)
    return pl.pallas_call(
        project_kernel,
        out_shape=jax.ShapeDtypeStruct((count, width), jnp.bfloat16),
        grid=(count // block,),
        in_specs=[
            pl.BlockSpec((block, depth), lambda i: (i, 0)),
            pl.BlockSpec((depth, width), lambda i: (0, 0)),
            pl.BlockSpec((block, LANES), lambda i: (i, 0)),
            pl.BlockSpec((block, LANES), lambda i: (i, 0)),
        ],
        out_specs=pl.BlockSpec((block, width), lambda i: (i, 0)),
        cost_estimate=pl.CostEstimate(
            flops=2 * count * depth * width,
            bytes_accessed=2 * (count * depth + depth * width + count * width),
            transcendentals=0,
        ),
        name="project",
    )(rows, weight, cosine, sine)


def normalize(tokens):
    residual = tokens.astype(jnp.float32)
    center = residual - jnp.mean(residual, axis=1, keepdims=True)
    inv_std = lax.rsqrt(jnp.mean(center * center, axis=1, keepdims=True) + norm_eps)
    return (center * inv_std, inv_std)


def feed_kernel(tokens_ref, params_ref, weight_ref, *refs):
    normed_ref, act_ref, slope_ref = refs[-3:]
    unit, unused = normalize(tokens_ref[...])
    normed_ref[...] = (unit * params_ref[0:1, :] + params_ref[1:2, :]).astype(jnp.bfloat16)
    width = act_ref.shape[1]
    step = min(256, width)
    for first in range(0, width, step):
        hidden = dot_plain(normed_ref[...], weight_ref[:, first : first + step])
        share = 0.5 + 0.5 * lax.erf(hidden * math.sqrt(0.5))
        bell = jnp.exp(hidden * hidden * -0.5) * (1.0 / math.sqrt(2.0 * math.pi))
        act_ref[:, first : first + step] = (hidden * share).astype(jnp.bfloat16)
        slope_ref[:, first : first + step] = share + hidden * bell


def feed(slot, slots, tokens, params, weight, held):
    rows, depth = tokens.shape
    width = weight.shape[1]
    whole = pl.BlockSpec(memory_space=pl.ANY)
    return pl.pallas_call(
        feed_kernel,
        out_shape=(
            jax.ShapeDtypeStruct((slots * rows, depth), jnp.bfloat16),
            jax.ShapeDtypeStruct((slots * rows, width), jnp.bfloat16),
            jax.ShapeDtypeStruct((slots * rows, width), jnp.float32),
        ),
        grid=(2,),
        in_specs=[
            pl.BlockSpec((rows // 2, depth), lambda i: (i, 0)),
            pl.BlockSpec((2, depth), lambda i: (0, 0)),
            pl.BlockSpec((depth, width), lambda i: (0, 0)),
        ]
        + [whole] * len(held),
        out_specs=(
            pl.BlockSpec((rows // 2, depth), lambda i: (2 * slot + i, 0)),
            pl.BlockSpec((rows // 2, width), lambda i: (2 * slot + i, 0)),
            pl.BlockSpec((rows // 2, width), lambda i: (2 * slot + i, 0)),
        ),
        input_output_aliases={3 + k: k for k in range(len(held))},
        cost_estimate=pl.CostEstimate(
            flops=2 * rows * depth * width,
            bytes_accessed=4 * rows * depth + 2 * depth * width + 6 * rows * width,
            transcendentals=2 * rows * width,
        ),
        name="feed",
    )(tokens, params, weight, *held)


def pull_kernel(mixed_ref, hidden_ref, proj_ref, up_ref, tokens_ref, out_ref, sums_ref):
    partial_grad = dot_last(mixed_ref[...], proj_ref[...]) + dot_last(hidden_ref[...], up_ref[...])
    out_ref[...] = partial_grad
    unit, unused = normalize(tokens_ref[...])
    gain = jnp.sum(partial_grad * unit, axis=0, keepdims=True)
    bias = jnp.sum(partial_grad, axis=0, keepdims=True)
    both = jnp.concatenate([gain, bias], axis=0)

    @pl.when(pl.program_id(0) == 0)
    def _():
        sums_ref[...] = both

    @pl.when(pl.program_id(0) > 0)
    def _():
        sums_ref[...] += both


def pull(slot, mixed, hidden_grad, proj, up, tokens):
    rows, depth = tokens.shape
    half = rows // 2
    return pl.pallas_call(
        pull_kernel,
        out_shape=(
            jax.ShapeDtypeStruct((rows, depth), jnp.float32),
            jax.ShapeDtypeStruct((2, depth), jnp.float32),
        ),
        grid=(2,),
        in_specs=[
            pl.BlockSpec((half, mixed.shape[1]), lambda i: (2 * slot + i, 0)),
            pl.BlockSpec((half, hidden_grad.shape[1]), lambda i: (2 * slot + i, 0)),
            pl.BlockSpec(proj.shape, lambda i: (0, 0)),
            pl.BlockSpec(up.shape, lambda i: (0, 0)),
            pl.BlockSpec((half, depth), lambda i: (i, 0)),
        ],
        out_specs=(
            pl.BlockSpec((half, depth), lambda i: (i, 0)),
            pl.BlockSpec((2, depth), lambda i: (0, 0)),
        ),
        cost_estimate=pl.CostEstimate(
            flops=2 * rows * depth * (mixed.shape[1] + hidden_grad.shape[1]),
            bytes_accessed=8 * rows * depth + 2 * depth * (proj.shape[1] + up.shape[1]),
            transcendentals=0,
        ),
        name="pull",
    )(mixed, hidden_grad, proj, up, tokens)


def pick_kernel(index_ref, all_ref, out_ref):
    out_ref[...] = all_ref[...].reshape(out_ref.shape)


def pick_proj(weight_all, span_index, own_width):
    narrow_count, shards, rows, cols = weight_all.shape
    units = own_width // LANES
    per_shard = cols // LANES - 1
    per_part = D // LANES

    def source(c, index_ref):
        unit = (c % 3) * per_part + index_ref[0] * units + c // 3
        return (0, unit // per_shard, 0, unit % per_shard)

    return pl.pallas_call(
        pick_kernel,
        out_shape=jax.ShapeDtypeStruct((D, 3 * own_width), jnp.bfloat16),
        grid_spec=pltpu.PrefetchScalarGridSpec(
            num_scalar_prefetch=1,
            grid=(3 * units,),
            in_specs=[pl.BlockSpec((narrow_count, 1, rows, LANES), source)],
            out_specs=pl.BlockSpec((D, LANES), lambda c, index_ref: (0, c)),
        ),
        cost_estimate=pl.CostEstimate(
            flops=0, bytes_accessed=12 * D * own_width, transcendentals=0
        ),
        name="pick_proj",
    )(span_index.reshape(1), weight_all)


def turn_kernel(slots_ref, all_ref, out_ref):
    narrow_count, unused, rows, cols = all_ref.shape
    for t in range(narrow_count):
        out_ref[t * rows : (t + 1) * rows, :] = all_ref[slots_ref[t], 0]


def pick_merge(weight_all, slots, own_width):
    narrow_count, shards, rows, cols = weight_all.shape
    return pl.pallas_call(
        turn_kernel,
        out_shape=jax.ShapeDtypeStruct((D, D), jnp.bfloat16),
        grid_spec=pltpu.PrefetchScalarGridSpec(
            num_scalar_prefetch=1,
            grid=(shards,),
            in_specs=[
                pl.BlockSpec(
                    (narrow_count, 1, rows, LANES),
                    lambda j, slots_ref: (0, j, 0, cols // LANES - 1),
                )
            ],
            out_specs=pl.BlockSpec((D, LANES), lambda j, slots_ref: (0, j)),
        ),
        cost_estimate=pl.CostEstimate(flops=0, bytes_accessed=4 * D * D, transcendentals=0),
        name="pick_merge",
    )(slots, weight_all)


def head_lanes(field, head):
    lane = lax.broadcasted_iota(jnp.int32, field.shape, 1)
    keep = (lane >= head * HEAD) & (lane < (head + 1) * HEAD)
    return jnp.where(keep, field, jnp.zeros_like(field))


def pair_allowed(start_row, key_first, key_count, query_first, query_count):
    key_index = key_first + lax.broadcasted_iota(jnp.int32, (key_count, query_count), 0)
    query_index = query_first + lax.broadcasted_iota(jnp.int32, (key_count, query_count), 1)
    return (key_index >= start_row) & (key_index <= query_index)


def attend_kernel(
    block_q,
    block_k,
    heads_in,
    slots_ref,
    first_ref,
    last_ref,
    start_ref,
    query_ref,
    key_ref,
    value_ref,
    *refs,
):
    out_ref, tall_ref, log_ref, turned, best, total, summed = refs[-7:]
    index = pl.program_id(0)
    key_blocks = key_ref.shape[0] // block_k

    @pl.when(index == 0)
    def _():
        for j in range(key_blocks):
            piece = value_ref[j * block_k : (j + 1) * block_k, :].astype(jnp.float32)
            turned[:, j * block_k : (j + 1) * block_k] = piece.T.astype(jnp.bfloat16)

    query_first = index * block_q
    low = first_ref[index] // block_k
    high = (query_first + block_q - 1) // block_k + 1
    start_row = start_ref[...]
    queries = [head_lanes(query_ref[...], head) for head in range(heads_in)]
    best[...] = jnp.full_like(best, masked_score)
    total[...] = jnp.zeros_like(total)
    summed[...] = jnp.zeros_like(summed)

    def visit(j, masked):
        key_rows = pl.ds(pl.multiple_of(slots_ref[j] * block_k, block_k), block_k)
        keys = key_ref[key_rows, :]
        if masked:
            allowed = pair_allowed(start_row, j * block_k, block_k, query_first, block_q)
        for head in range(heads_in):
            scores = dot_last(keys, queries[head])
            if masked:
                scores = jnp.where(allowed, scores, masked_score)
            old = best[head : head + 1, :]
            new = jnp.maximum(old, jnp.max(scores, axis=0, keepdims=True))
            weights = jnp.exp(scores - new)
            if masked:
                weights = jnp.where(allowed, weights, 0.0)
            factor = jnp.exp(old - new)
            best[head : head + 1, :] = new
            total[head : head + 1, :] = total[head : head + 1, :] * factor + jnp.sum(
                weights, axis=0, keepdims=True
            )
            rows = slice(head * HEAD, (head + 1) * HEAD)
            summed[rows, :] = summed[rows, :] * factor + dot_plain(
                turned[rows, key_rows], weights.astype(jnp.bfloat16)
            )

    def step(j, carry):
        whole = (j * block_k >= last_ref[index]) & ((j + 1) * block_k - 1 <= query_first)

        @pl.when(whole)
        def _():
            visit(j, False)

        @pl.when(jnp.logical_not(whole))
        def _():
            visit(j, True)

        return carry

    lax.fori_loop(low, high, step, 0)
    for head in range(heads_in):
        rows = slice(head * HEAD, (head + 1) * HEAD)
        weight = total[head : head + 1, :]
        tall_ref[rows, :] = summed[rows, :] / weight
        log_ref[0, head : head + 1, :] = best[head : head + 1, :] + jnp.log(weight)
    if heads_in * HEAD < LANES:
        tall_ref[heads_in * HEAD :, :] = jnp.zeros_like(tall_ref[heads_in * HEAD :, :])
    log_ref[0, heads_in:, :] = jnp.zeros_like(log_ref[0, heads_in:, :])
    out_ref[...] = tall_ref[...].T.astype(jnp.bfloat16)


def attend(pair, packed, slots, first, last, starts, heads_in, block_q, block_k, held):
    count, width = packed.shape
    pairs = width // 3 // LANES
    whole = pl.BlockSpec(memory_space=pl.ANY)
    return pl.pallas_call(
        partial(attend_kernel, block_q, block_k, heads_in),
        out_shape=(
            jax.ShapeDtypeStruct((count, pairs * LANES), jnp.bfloat16),
            jax.ShapeDtypeStruct((pairs * LANES, count), jnp.float32),
            jax.ShapeDtypeStruct((pairs, 8, count), jnp.float32),
        ),
        grid_spec=pltpu.PrefetchScalarGridSpec(
            num_scalar_prefetch=3,
            grid=(count // block_q,),
            in_specs=[
                pl.BlockSpec((1, block_q), lambda i, slots_ref, *_: (0, slots_ref[i])),
                pl.BlockSpec((block_q, LANES), lambda i, slots_ref, *_: (slots_ref[i], 3 * pair)),
                pl.BlockSpec((count, LANES), lambda i, *_: (0, 3 * pair + 1)),
                pl.BlockSpec((count, LANES), lambda i, *_: (0, 3 * pair + 2)),
            ]
            + [whole] * len(held),
            out_specs=(
                pl.BlockSpec((block_q, LANES), lambda i, slots_ref, *_: (slots_ref[i], pair)),
                pl.BlockSpec((LANES, block_q), lambda i, slots_ref, *_: (pair, slots_ref[i])),
                pl.BlockSpec((1, 8, block_q), lambda i, slots_ref, *_: (pair, 0, slots_ref[i])),
            ),
            scratch_shapes=[
                pltpu.VMEM((LANES, count), jnp.bfloat16),
                pltpu.VMEM((8, block_q), jnp.float32),
                pltpu.VMEM((8, block_q), jnp.float32),
                pltpu.VMEM((LANES, block_q), jnp.float32),
            ],
        ),
        input_output_aliases={7 + k: k for k in range(len(held))},
        cost_estimate=pl.CostEstimate(
            flops=2 * 2 * count * count * LANES,
            bytes_accessed=12 * count * LANES,
            transcendentals=2 * count * count,
        ),
        name="attend",
    )(slots, first, last, starts.reshape(1, count), packed, packed, packed, *held)


def attend_back_kernel(
    block_q,
    block_k,
    heads_in,
    slots_ref,
    last_ref,
    end_ref,
    start_ref,
    cos_ref,
    sin_ref,
    query_ref,
    key_ref,
    value_ref,
    tall_ref,
    log_ref,
    grad_ref,
    *refs,
):
    out_ref, turned, masked_q, masked_g, delta, tall_q, key_sum, value_sum = refs[-8:]
    index = pl.program_id(0)
    count = query_ref.shape[0]

    def turn_back(field, rows):
        return field * cos_ref[rows, :] - partner(field) * sin_ref[rows, :]

    @pl.when(index == 0)
    def _():
        def prepare(j, carry):
            rows = pl.ds(pl.multiple_of(j * block_k, block_k), block_k)
            turned[:, rows] = key_ref[rows, :].astype(jnp.float32).T.astype(jnp.bfloat16)
            grads = grad_ref[rows, :]
            product = grads.astype(jnp.float32).T * tall_ref[:, rows]
            for head in range(heads_in):
                masked_q[head, rows, :] = head_lanes(query_ref[rows, :], head)
                masked_g[head, rows, :] = head_lanes(grads, head)
                delta[head : head + 1, rows] = jnp.sum(
                    product[head * HEAD : (head + 1) * HEAD, :], axis=0, keepdims=True
                )
            tall_q[:, rows] = jnp.zeros((LANES, block_k), jnp.float32)
            return carry

        lax.fori_loop(0, count // block_k, prepare, 0)

    key_first = index * block_k
    key_rows = pl.ds(pl.multiple_of(slots_ref[index] * block_k, block_k), block_k)
    keys = key_ref[key_rows, :]
    values = value_ref[key_rows, :]
    key_sum[...] = jnp.zeros_like(key_sum)
    value_sum[...] = jnp.zeros_like(value_sum)

    def visit(i, masked):
        query_first = i * block_q
        rows = pl.ds(pl.multiple_of(slots_ref[i] * block_q, block_q), block_q)
        if masked:
            allowed = pair_allowed(
                start_ref[0:1, rows], key_first, block_k, query_first, block_q
            )
        for head in range(heads_in):
            queries = masked_q[head, rows, :]
            grads = masked_g[head, rows, :]
            scores = dot_last(keys, queries)
            probs = jnp.exp(scores - log_ref[0, head : head + 1, rows])
            if masked:
                probs = jnp.where(allowed, probs, 0.0)
            value_sum[...] += dot_plain(probs.astype(jnp.bfloat16), grads)
            prob_grad = dot_last(values, grads)
            score_grad = (probs * (prob_grad - delta[head : head + 1, rows])).astype(jnp.bfloat16)
            key_sum[...] += dot_plain(score_grad, queries)
            lanes = slice(head * HEAD, (head + 1) * HEAD)
            tall_q[lanes, rows] += dot_plain(turned[lanes, key_rows], score_grad)

    def step(i, carry):
        whole = (key_first >= last_ref[i]) & (key_first + block_k - 1 <= i * block_q)

        @pl.when(whole)
        def _():
            visit(i, False)

        @pl.when(jnp.logical_not(whole))
        def _():
            visit(i, True)

        return carry

    lax.fori_loop(key_first // block_q, (end_ref[index] - 1) // block_q + 1, step, 0)
    out_ref[key_rows, LANES : 2 * LANES] = turn_back(key_sum[...], key_rows).astype(jnp.bfloat16)
    out_ref[key_rows, 2 * LANES :] = value_sum[...].astype(jnp.bfloat16)

    @pl.when(index == pl.num_programs(0) - 1)
    def _():
        def finish(j, carry):
            rows = pl.ds(pl.multiple_of(j * block_k, block_k), block_k)
            field = tall_q[:, rows].T * HEAD ** (-0.5)
            out_ref[rows, :LANES] = turn_back(field, rows).astype(jnp.bfloat16)
            return carry

        lax.fori_loop(0, count // block_k, finish, 0)


def attend_back(
    pair, packed, slots, last, end, starts, cosine, sine, tall, logs, grads,
    heads_in, block_q, block_k, held,
):
    count, width = packed.shape
    whole = pl.BlockSpec(memory_space=pl.ANY)
    return pl.pallas_call(
        partial(attend_back_kernel, block_q, block_k, heads_in),
        out_shape=jax.ShapeDtypeStruct((count, width), jnp.bfloat16),
        grid_spec=pltpu.PrefetchScalarGridSpec(
            num_scalar_prefetch=3,
            grid=(count // block_k,),
            in_specs=[
                pl.BlockSpec((1, count), lambda i, *_: (0, 0)),
                pl.BlockSpec((count, LANES), lambda i, *_: (0, 0)),
                pl.BlockSpec((count, LANES), lambda i, *_: (0, 0)),
                pl.BlockSpec((count, LANES), lambda i, *_: (0, 3 * pair)),
                pl.BlockSpec((count, LANES), lambda i, *_: (0, 3 * pair + 1)),
                pl.BlockSpec((count, LANES), lambda i, *_: (0, 3 * pair + 2)),
                pl.BlockSpec((LANES, count), lambda i, *_: (pair, 0)),
                pl.BlockSpec((1, 8, count), lambda i, *_: (pair, 0, 0)),
                pl.BlockSpec((count, LANES), lambda i, *_: (0, pair)),
            ]
            + [whole] * len(held),
            out_specs=pl.BlockSpec((count, 3 * LANES), lambda i, *_: (0, pair)),
            scratch_shapes=[
                pltpu.VMEM((LANES, count), jnp.bfloat16),
                pltpu.VMEM((heads_in, count, LANES), jnp.bfloat16),
                pltpu.VMEM((heads_in, count, LANES), jnp.bfloat16),
                pltpu.VMEM((8, count), jnp.float32),
                pltpu.VMEM((LANES, count), jnp.float32),
                pltpu.VMEM((block_k, LANES), jnp.float32),
                pltpu.VMEM((block_k, LANES), jnp.float32),
            ],
        ),
        input_output_aliases={12 + k: k for k in range(len(held))},
        compiler_params=pltpu.CompilerParams(vmem_limit_bytes=60 << 20),
        cost_estimate=pl.CostEstimate(
            flops=5 * 2 * count * count * LANES,
            bytes_accessed=20 * count * LANES,
            transcendentals=2 * count * count,
        ),
        name="attend_back",
    )(
        slots, last, end, starts.reshape(1, count), cosine, sine,
        packed, packed, packed, tall, logs, grads, *held,
    )


def finish_kernel(narrow_count, wide_count, own_units, per_shard, *refs):
    exchange = own_units > 0
    if exchange:
        (
            parts_ref, piece_ref, total_ref, block_ref, near, far, near_sum,
            send_near, recv_near, send_far, recv_far, send_piece, recv_piece,
        ) = refs
    else:
        (
            parts_ref, total_ref, near, far, near_sum, send_near, recv_near, send_far, recv_far,
        ) = refs
    narrow_me = lax.axis_index("narrow")
    wide_me = lax.axis_index("wide")

    def place(narrow_at, wide_at):
        return {"narrow": narrow_at, "wide": wide_at}

    mesh_ids = pl.DeviceIdType.MESH
    barrier = pltpu.get_barrier_semaphore()
    greeted = 0
    for ahead in range(narrow_count):
        for across in range(wide_count):
            if (ahead > 0) + (across > 0) == 0 or (not exchange and ahead > 0 and across > 0):
                continue
            greeted += 1
            pl.semaphore_signal(
                barrier,
                inc=1,
                device_id=place(
                    lax.rem(narrow_me + ahead, narrow_count), lax.rem(wide_me + across, wide_count)
                ),
                device_id_type=mesh_ids,
            )
    pl.semaphore_wait(barrier, greeted)
    near_copies = []
    for ahead in range(1, narrow_count):
        copy = pltpu.make_async_remote_copy(
            src_ref=parts_ref,
            dst_ref=near.at[narrow_me],
            send_sem=send_near.at[ahead - 1],
            recv_sem=recv_near.at[ahead - 1],
            device_id=place(lax.rem(narrow_me + ahead, narrow_count), wide_me),
            device_id_type=mesh_ids,
        )
        copy.start()
        near_copies.append(copy)
    near[narrow_me] = parts_ref[...]
    if exchange:
        rows = piece_ref.shape[0]
        halves = block_ref.shape[0] // rows
        half_me = lax.rem(wide_me, halves)
        narrow_to = lax.div(wide_me, halves)
        moves = []
        for unit in range(3 * own_units):
            whole_unit = (unit % 3) * (D // LANES) + narrow_me * own_units + unit // 3
            wide_to = lax.div(whole_unit, per_shard)
            column = lax.rem(whole_unit, per_shard)
            source = piece_ref.at[:, unit * LANES : (unit + 1) * LANES]
            target = block_ref.at[
                pl.ds(pl.multiple_of(half_me * rows, rows), rows),
                pl.ds(pl.multiple_of(column * LANES, LANES), LANES),
            ]
            arrived = recv_piece.at[half_me * per_shard + column]
            remote = pltpu.make_async_remote_copy(
                src_ref=source,
                dst_ref=target,
                send_sem=send_piece.at[unit],
                recv_sem=arrived,
                device_id=place(narrow_to, wide_to),
                device_id_type=mesh_ids,
            )
            here = pltpu.make_async_copy(source, target, arrived)
            mine = (narrow_to == narrow_me) & (wide_to == wide_me)
            pl.when(jnp.logical_not(mine))(remote.start)
            pl.when(mine)(here.start)
            moves.append((mine, remote))
    for copy in near_copies:
        copy.wait()
    value = near[0]
    for k in range(1, narrow_count):
        value = value + near[k]
    near_sum[...] = value
    far_copies = []
    for across in range(1, wide_count):
        copy = pltpu.make_async_remote_copy(
            src_ref=near_sum,
            dst_ref=far.at[wide_me],
            send_sem=send_far.at[across - 1],
            recv_sem=recv_far.at[across - 1],
            device_id=place(narrow_me, lax.rem(wide_me + across, wide_count)),
            device_id_type=mesh_ids,
        )
        copy.start()
        far_copies.append(copy)
    far[wide_me] = value
    for copy in far_copies:
        copy.wait()
    value = far[0]
    for k in range(1, wide_count):
        value = value + far[k]
    total_ref[...] = value
    if exchange:
        for mine, remote in moves:
            pl.when(jnp.logical_not(mine))(remote.wait_send)
        for half in range(halves):
            for column in range(per_shard):
                pltpu.make_async_copy(
                    piece_ref.at[:, 0:LANES],
                    block_ref.at[
                        half * rows : (half + 1) * rows, column * LANES : (column + 1) * LANES
                    ],
                    recv_piece.at[half * per_shard + column],
                ).wait()


def finish(parts, piece, narrow_count, wide_count, own_width, proj_cols):
    shape = parts.shape
    exchange = piece is not None
    own_units = own_width // LANES if exchange else 0
    per_shard = proj_cols // LANES
    vmem = pl.BlockSpec(memory_space=pltpu.VMEM)
    shapes = [jax.ShapeDtypeStruct(shape, jnp.float32)]
    scratch = [
        pltpu.VMEM((narrow_count,) + shape, jnp.float32),
        pltpu.VMEM((wide_count,) + shape, jnp.float32),
        pltpu.VMEM(shape, jnp.float32),
        pltpu.SemaphoreType.DMA((narrow_count - 1,)),
        pltpu.SemaphoreType.DMA((narrow_count - 1,)),
        pltpu.SemaphoreType.DMA((wide_count - 1,)),
        pltpu.SemaphoreType.DMA((wide_count - 1,)),
    ]
    if exchange:
        shapes.append(jax.ShapeDtypeStruct((D // narrow_count, proj_cols), jnp.bfloat16))
        scratch += [
            pltpu.SemaphoreType.DMA((3 * own_units,)),
            pltpu.SemaphoreType.DMA((3 * own_units,)),
        ]
    return pl.pallas_call(
        partial(finish_kernel, narrow_count, wide_count, own_units, per_shard),
        out_shape=tuple(shapes),
        in_specs=[vmem] * len(shapes),
        out_specs=(vmem,) * len(shapes),
        scratch_shapes=scratch,
        compiler_params=pltpu.CompilerParams(collective_id=0, has_side_effects=True),
        name="finish",
    )(*([parts, piece] if exchange else [parts]))


def adam_update(
    weight, first_moment, second_moment, grad_value, step_rate, decay_coef, first_fix, second_fix
):
    new_first = beta_first * first_moment + (1.0 - beta_first) * grad_value
    new_second = beta_second * second_moment + (1.0 - beta_second) * grad_value * grad_value
    step_ratio = new_first / first_fix / (jnp.sqrt(new_second / second_fix) + adam_eps)
    return (weight - step_rate * (step_ratio + decay_coef * weight), new_first, new_second)


def shards(
    tokens,
    cotangent,
    seq_lengths,
    step_count,
    norm_params,
    norm_first,
    norm_second,
    proj_weight,
    proj_first,
    proj_second,
    merge_weight,
    merge_first,
    merge_second,
    up_weight,
    up_first,
    up_second,
    down_weight,
    down_first,
    down_second,
):
    tok_rows = tokens.shape[0]
    narrow_count = lax.axis_size("narrow")
    wide_count = lax.axis_size("wide")
    span_index = lax.axis_index("narrow")
    group_rows = tok_rows * narrow_count
    own_width = HEADS // narrow_count * HEAD
    held_width = max(own_width, LANES)
    heads_in = min(own_width, LANES) // HEAD
    shard_rows = D // narrow_count
    proj_cols = proj_weight.shape[1]
    lengths = seq_lengths[0]
    onward = [(i, (i + 1) % narrow_count) for i in range(narrow_count)]
    slots = lax.rem(
        span_index + narrow_count - jnp.arange(narrow_count, dtype=jnp.int32), narrow_count
    )

    def pad_lanes(array, axis):
        extra = [(0, 0)] * array.ndim
        extra[axis] = (0, held_width - own_width)
        return jnp.pad(array, extra) if held_width > own_width else array

    def meet(*values):
        return lax.optimization_barrier(values)

    def send_on(array):
        return lax.ppermute(array, "narrow", onward)

    def rows_of(array, slot):
        return array[slot * tok_rows : (slot + 1) * tok_rows]

    direct = own_width % LANES == 0 and proj_cols % LANES == 0 and merge_weight.shape[1] == LANES
    weight_part = jnp.concatenate(
        [proj_weight.astype(jnp.bfloat16), merge_weight.astype(jnp.bfloat16)], axis=1
    )
    weight_all = lax.all_gather(weight_part, ("narrow", "wide"), axis=0).reshape(
        narrow_count, wide_count, shard_rows, -1
    )
    up_slice = up_weight.astype(jnp.bfloat16)
    down_slice = down_weight.astype(jnp.bfloat16)

    places = (
        slots[:, None] * tok_rows + jnp.arange(tok_rows, dtype=jnp.int32)[None, :]
    ).reshape(group_rows)
    seq_start, unused = locate(lengths, places)
    cosine, sine = rotary_tables(places - seq_start)
    block_first = jnp.arange(narrow_count, dtype=jnp.int32) * tok_rows
    first_start, unused = locate(lengths, block_first)
    last_start, last_end = locate(lengths, block_first + (tok_rows - 1))

    token_blocks = [tokens]
    held = ()
    for slot in range(narrow_count - 1):
        moving = send_on(token_blocks[slot])
        held = feed(slot, narrow_count, token_blocks[slot], norm_params, up_slice, held)
        moving, *held = meet(moving, *held)
        token_blocks.append(moving)
    grad_first, last_block = meet(cotangent, token_blocks[-1])
    token_blocks[-1] = last_block
    grad_blocks = [grad_first]

    moving = send_on(grad_first)
    gathered, activated, slope = feed(
        narrow_count - 1, narrow_count, last_block, norm_params, up_slice, held
    )
    if direct:
        proj_own = pick_proj(weight_all, span_index, own_width)
        merge_turn = pick_merge(weight_all, slots, own_width)
    else:
        turned_all = jnp.transpose(weight_all, (0, 2, 1, 3))
        proj_copy = turned_all[..., :proj_cols].reshape(D, 3, narrow_count, own_width)
        proj_own = pad_lanes(
            lax.dynamic_index_in_dim(proj_copy, span_index, axis=2, keepdims=False), 2
        ).reshape(D, 3 * held_width)
        merge_copy = turned_all[..., proj_cols:].reshape(narrow_count, own_width, D)
        merge_turn = jnp.take(merge_copy, slots, axis=0).reshape(D, D)
    packed = project(gathered, proj_own, cosine, sine)
    moving, packed = meet(moving, packed)
    grad_blocks.append(moving)

    pairs = held_width // LANES
    attended_held = ()
    for hop in range(2, max(narrow_count, pairs + 2)):
        if hop < narrow_count:
            moving = send_on(grad_blocks[-1])
        if hop - 2 < pairs:
            attended_held = attend(
                hop - 2, packed, slots, first_start, last_start, seq_start,
                heads_in, tok_rows, tok_rows, attended_held,
            )
        moving, *attended_held = meet(moving, *attended_held)
        if hop < narrow_count:
            grad_blocks.append(moving)
    attended, tall, logs = attended_held
    grads_all = jnp.concatenate(grad_blocks, axis=0)

    def down_term(slot):
        return dot_plain(rows_of(activated, slot), down_slice)

    def wide_sum(grad):
        return lax.psum_scatter(grad, "wide", scatter_dimension=0, tiled=True)

    pieces = []
    for ahead in range(narrow_count):
        piece = rows_of(attended, (narrow_count - ahead) % narrow_count)[:, :own_width]
        if ahead > 0:
            piece = lax.ppermute(
                piece,
                "narrow",
                [(i, (i + ahead) % narrow_count) for i in range(narrow_count)],
            )
        pieces.append(piece)

    first_term = down_term(1).astype(jnp.bfloat16)
    first_term, grads_all = meet(first_term, grads_all)
    moving = send_on(first_term)
    hidden_grad = (dot_last(grads_all, down_slice) * slope).astype(jnp.bfloat16)
    down_grad = dot_first(activated, grads_all).astype(jnp.bfloat16)
    up_grad = dot_first(gathered, hidden_grad).astype(jnp.bfloat16)
    attended_grad = pad_lanes(
        dot_last(grads_all, merge_turn[:own_width]).astype(jnp.bfloat16), 1
    )
    moving, hidden_grad, attended_grad = meet(moving, hidden_grad, attended_grad)
    mixed_held = ()
    for hop in range(2, max(narrow_count, pairs + 2)):
        if hop < narrow_count:
            moving = send_on((moving.astype(jnp.float32) + down_term(hop)).astype(jnp.bfloat16))
        if hop - 2 < pairs:
            mixed_held = (
                attend_back(
                    hop - 2, packed, slots, last_start, last_end, seq_start, cosine, sine,
                    tall, logs, attended_grad, heads_in, tok_rows, tok_rows, mixed_held,
                ),
            )
        moving, *mixed_held = meet(moving, *mixed_held)
    (mixed_grad,) = mixed_held
    branch = moving.astype(jnp.float32) + down_term(0)
    merged = dot_plain(jnp.concatenate(pieces, axis=1), merge_turn)
    unit_rows, inv_std = normalize(tokens)
    output_rows = tokens.astype(jnp.float32) + merged + branch
    layer_out = output_rows.astype(jnp.bfloat16)

    terms = [None] * narrow_count
    norm_part = None
    for slot in list(range(1, narrow_count)) + [0]:
        terms[slot], sums = pull(
            slot, mixed_grad, hidden_grad, proj_own, up_slice, token_blocks[slot]
        )
        norm_part = sums if norm_part is None else norm_part + sums
    moving = terms[1].astype(jnp.bfloat16)
    for slot in list(range(2, narrow_count)) + [0]:
        normed_grad = send_on(moving).astype(jnp.float32) + terms[slot]
        moving = normed_grad.astype(jnp.bfloat16)
    unit_grad = normed_grad * norm_params[0]
    input_grad = cotangent.astype(jnp.float32) + inv_std * (
        unit_grad
        - jnp.mean(unit_grad, axis=1, keepdims=True)
        - unit_rows * jnp.mean(unit_grad * unit_rows, axis=1, keepdims=True)
    )

    part_rows = D // wide_count
    feed_part = wide_sum(
        jnp.concatenate(
            [
                up_grad.reshape(wide_count, part_rows, -1),
                down_grad.reshape(wide_count, part_rows, -1),
            ],
            axis=1,
        ).reshape(2 * D, -1)
    )
    proj_grad = dot_first(gathered, mixed_grad).astype(jnp.bfloat16)
    merge_grad = dot_first(grads_all, attended).astype(jnp.bfloat16)
    if not direct:
        proj_grad = proj_grad.reshape(D, 3, held_width)[:, :, :own_width].reshape(D, -1)
        merge_grad = merge_grad[:, :own_width]
    heads_part = wide_sum(jnp.concatenate([proj_grad, merge_grad], axis=1))
    merge_block = heads_part[:, 3 * own_width :].T.astype(jnp.float32)

    def squares(array):
        value = array.astype(jnp.float32)
        return jnp.sum(value * value)

    scalars = jnp.stack(
        [
            squares(heads_part) + squares(feed_part),
            squares(output_rows),
            squares(merged),
            squares(branch),
        ]
    )
    parts = jnp.concatenate(
        [norm_part.reshape(2 * D // LANES, LANES), jnp.pad(scalars, (0, LANES - 4))[None, :]]
    )
    parts = jnp.pad(parts, ((0, 7), (0, 0)))
    if direct:
        summed, proj_block = finish(
            parts, heads_part, narrow_count, wide_count, own_width, proj_cols
        )
        proj_block = proj_block.astype(jnp.float32)
    else:
        (summed,) = finish(parts, None, narrow_count, wide_count, own_width, proj_cols)
        cross = lax.all_gather(heads_part[:, : 3 * own_width], "narrow", axis=0).reshape(
            narrow_count, part_rows, 3, own_width
        )
        cross = jnp.transpose(cross, (1, 2, 0, 3)).reshape(part_rows, wide_count, proj_cols)
        cross = lax.all_to_all(jnp.transpose(cross, (1, 0, 2)), "wide", 0, 0)
        proj_block = lax.dynamic_slice_in_dim(
            cross.reshape(D, proj_cols), span_index * shard_rows, shard_rows, axis=0
        ).astype(jnp.float32)
    norm_total = summed[: 2 * D // LANES].reshape(2, D)
    square_total = summed[2 * D // LANES, 0:1]
    output_squares = summed[2 * D // LANES, 1:2]
    branch_squares = summed[2 * D // LANES, 2:4]
    feed_all = lax.all_gather(feed_part, "wide", axis=0).reshape(
        wide_count, 2, part_rows, -1
    ).astype(jnp.float32)
    up_sum = feed_all[:, 0].reshape(up_weight.shape)
    down_sum = feed_all[:, 1].reshape(down_weight.shape)
    grad_norm = jnp.sqrt(square_total + jnp.sum(norm_total * norm_total))
    clip_factor = jnp.minimum(1.0, math.sqrt(NPARAMS) / grad_norm)
    entry_count = wide_count * group_rows * D
    residual_rms = jnp.sqrt(output_squares / entry_count)
    branch_norms = jnp.sqrt(branch_squares / entry_count)
    step_value = step_count[0].astype(jnp.float32)
    first_fix = 1.0 - jnp.power(beta_first, step_value)
    second_fix = 1.0 - jnp.power(beta_second, step_value)
    ramp = jnp.minimum(1.0, step_value / warmup_steps)
    norm_clipped = norm_total * clip_factor
    new_norm = adam_update(
        norm_params,
        norm_first,
        norm_second,
        norm_clipped,
        norm_rate * ramp,
        0.0,
        first_fix,
        second_fix,
    )
    new_proj = adam_update(
        proj_weight,
        proj_first,
        proj_second,
        proj_block * clip_factor,
        matrix_rate * ramp,
        decay_rate,
        first_fix,
        second_fix,
    )
    new_merge = adam_update(
        merge_weight,
        merge_first,
        merge_second,
        merge_block * clip_factor,
        matrix_rate * ramp,
        decay_rate,
        first_fix,
        second_fix,
    )
    new_up = adam_update(
        up_weight,
        up_first,
        up_second,
        up_sum * clip_factor,
        matrix_rate * ramp,
        decay_rate,
        first_fix,
        second_fix,
    )
    new_down = adam_update(
        down_weight,
        down_first,
        down_second,
        down_sum * clip_factor,
        matrix_rate * ramp,
        decay_rate,
        first_fix,
        second_fix,
    )
    return (
        layer_out,
        input_grad,
        grad_norm,
        residual_rms,
        norm_clipped,
        new_norm[0],
        new_norm[1],
        new_norm[2],
        new_proj[0],
        new_proj[1],
        new_proj[2],
        new_merge[0],
        new_merge[1],
        new_merge[2],
        new_up[0],
        new_up[1],
        new_up[2],
        new_down[0],
        new_down[1],
        new_down[2],
        branch_norms,
        new_proj[0].astype(jnp.bfloat16),
        new_merge[0].astype(jnp.bfloat16),
        new_up[0].astype(jnp.bfloat16),
        new_down[0].astype(jnp.bfloat16),
    )


def solution(mesh):
    placed = (
        P(("wide", "narrow"), None),
        P(("wide", "narrow"), None),
        P("wide", None),
        P(),
        P(),
        P(),
        P(),
        P("narrow", "wide"),
        P("narrow", "wide"),
        P("narrow", "wide"),
        P("narrow", "wide"),
        P("narrow", "wide"),
        P("narrow", "wide"),
        P(None, "narrow"),
        P(None, "narrow"),
        P(None, "narrow"),
        P("narrow", None),
        P("narrow", None),
        P("narrow", None),
    )
    return jax.shard_map(
        shards,
        mesh=mesh,
        in_specs=placed,
        out_specs=(
            P(("wide", "narrow"), None),
            P(("wide", "narrow"), None),
            P(),
            P(),
            P(),
            P(),
            P(),
            P(),
            P("narrow", "wide"),
            P("narrow", "wide"),
            P("narrow", "wide"),
            P("narrow", "wide"),
            P("narrow", "wide"),
            P("narrow", "wide"),
            P(None, "narrow"),
            P(None, "narrow"),
            P(None, "narrow"),
            P("narrow", None),
            P("narrow", None),
            P("narrow", None),
            P(),
            P("narrow", "wide"),
            P("narrow", "wide"),
            P(None, "narrow"),
            P("narrow", None),
        ),
        check_vma=False,
    )
```

```python
from functools import partial
import math

import jax
import jax.numpy as jnp
from jax import lax
from jax.experimental import pallas as pl
from jax.experimental.pallas import tpu as pltpu
from jax.sharding import PartitionSpec as P

HEADS = 16
HEAD = 64
D = 1024
ROT = 16
LANES = 128
ROW_BLOCK = 512
NPARAMS = 12584960


norm_eps = 1e-05
adam_eps = 1e-08
beta_first = 0.5
beta_second = 0.5
decay_rate = 0.01
matrix_rate = 0.1
norm_rate = 1.0
warmup_steps = 20.0
masked_score = -1e30
short = pl.CostEstimate(flops=0, bytes_accessed=0, transcendentals=0)


def dot_last(left_side, right_side):
    return lax.dot_general(
        left_side, right_side, (((1,), (1,)), ((), ())), preferred_element_type=jnp.float32
    )


def dot_plain(left_side, right_side):
    return lax.dot_general(
        left_side, right_side, (((1,), (0,)), ((), ())), preferred_element_type=jnp.float32
    )


def dot_first(left_side, right_side):
    return lax.dot_general(
        left_side, right_side, (((0,), (0,)), ((), ())), preferred_element_type=jnp.float32
    )


def locate(lengths, token_index):
    seq_ends = jnp.cumsum(lengths)
    starts = seq_ends - lengths
    segment = jnp.sum(
        (seq_ends[None, :] <= token_index[:, None]).astype(jnp.int32), axis=1, dtype=jnp.int32
    )
    choose = segment[:, None] == jnp.arange(lengths.shape[0], dtype=jnp.int32)[None, :]
    seq_start = jnp.sum(jnp.where(choose, starts[None, :], 0), axis=1, dtype=jnp.int32)
    seq_end = jnp.sum(jnp.where(choose, seq_ends[None, :], 0), axis=1, dtype=jnp.int32)
    return (seq_start, seq_end)


def rotary_tables(position):
    half_rot = ROT // 2
    frequency = jnp.power(10000.0, -2.0 * jnp.arange(half_rot, dtype=jnp.float32) / ROT)
    row = jnp.concatenate([frequency, frequency, jnp.zeros((HEAD - ROT,), jnp.float32)])
    row = jnp.tile(row, LANES // HEAD)
    sign = jnp.where(jnp.arange(LANES) % HEAD < half_rot, -1.0, 1.0)
    phases = position.astype(jnp.float32)[:, None] * row[None, :]
    return (jnp.cos(phases), jnp.sin(phases) * sign[None, :])


def partner(field):
    half_rot = ROT // 2
    lane = lax.broadcasted_iota(jnp.int32, field.shape, 1) % HEAD
    return jnp.where(
        lane < half_rot,
        pltpu.roll(field, LANES - half_rot, 1),
        pltpu.roll(field, half_rot, 1),
    )


def project_kernel(rows_ref, weight_ref, cos_ref, sin_ref, out_ref):
    width = out_ref.shape[1]
    projected = dot_plain(rows_ref[...], weight_ref[...])
    for first in range(0, width, LANES):
        piece = projected[:, first : first + LANES]
        part = first // LANES % 3
        if part < 2:
            piece = piece * cos_ref[...] + partner(piece) * sin_ref[...]
        if part == 0:
            piece = piece * HEAD ** (-0.5)
        out_ref[:, first : first + LANES] = piece.astype(jnp.bfloat16)


def project(rows, weight, cosine, sine):
    count, depth = rows.shape
    width = weight.shape[1]
    block = min(ROW_BLOCK, count)
    return pl.pallas_call(
        project_kernel,
        out_shape=jax.ShapeDtypeStruct((count, width), jnp.bfloat16),
        grid=(count // block,),
        in_specs=[
            pl.BlockSpec((block, depth), lambda i: (i, 0)),
            pl.BlockSpec((depth, width), lambda i: (0, 0)),
            pl.BlockSpec((block, LANES), lambda i: (i, 0)),
            pl.BlockSpec((block, LANES), lambda i: (i, 0)),
        ],
        out_specs=pl.BlockSpec((block, width), lambda i: (i, 0)),
        cost_estimate=short,
        name="project",
    )(rows, weight, cosine, sine)


def normalize(tokens):
    residual = tokens.astype(jnp.float32)
    center = residual - jnp.mean(residual, axis=1, keepdims=True)
    inv_std = lax.rsqrt(jnp.mean(center * center, axis=1, keepdims=True) + norm_eps)
    return (center * inv_std, inv_std)


def feed_kernel(tokens_ref, params_ref, weight_ref, *refs):
    normed_ref, act_ref, slope_ref = refs[-3:]
    unit, unused = normalize(tokens_ref[...])
    normed_ref[...] = (unit * params_ref[0:1, :] + params_ref[1:2, :]).astype(jnp.bfloat16)
    width = act_ref.shape[1]
    step = min(256, width)
    for first in range(0, width, step):
        hidden = dot_plain(normed_ref[...], weight_ref[:, first : first + step])
        share = 0.5 + 0.5 * lax.erf(hidden * math.sqrt(0.5))
        bell = jnp.exp(hidden * hidden * -0.5) * (1.0 / math.sqrt(2.0 * math.pi))
        act_ref[:, first : first + step] = (hidden * share).astype(jnp.bfloat16)
        slope_ref[:, first : first + step] = share + hidden * bell


def feed(slot, slots, tokens, params, weight, held):
    rows, depth = tokens.shape
    width = weight.shape[1]
    whole = pl.BlockSpec(memory_space=pl.ANY)
    return pl.pallas_call(
        feed_kernel,
        out_shape=(
            jax.ShapeDtypeStruct((slots * rows, depth), jnp.bfloat16),
            jax.ShapeDtypeStruct((slots * rows, width), jnp.bfloat16),
            jax.ShapeDtypeStruct((slots * rows, width), jnp.float32),
        ),
        grid=(2,),
        in_specs=[
            pl.BlockSpec((rows // 2, depth), lambda i: (i, 0)),
            pl.BlockSpec((2, depth), lambda i: (0, 0)),
            pl.BlockSpec((depth, width), lambda i: (0, 0)),
        ]
        + [whole] * len(held),
        out_specs=(
            pl.BlockSpec((rows // 2, depth), lambda i: (2 * slot + i, 0)),
            pl.BlockSpec((rows // 2, width), lambda i: (2 * slot + i, 0)),
            pl.BlockSpec((rows // 2, width), lambda i: (2 * slot + i, 0)),
        ),
        input_output_aliases={3 + k: k for k in range(len(held))},
        cost_estimate=short,
        name="feed",
    )(tokens, params, weight, *held)


def push_kernel(grad_ref, slope_ref, down_ref, merge_ref, *refs):
    all_ref, hidden_ref, attended_ref = refs[-3:]
    grads = grad_ref[...]
    all_ref[...] = grads
    hidden_ref[...] = (dot_last(grads, down_ref[...]) * slope_ref[...]).astype(jnp.bfloat16)
    attended_ref[...] = dot_last(grads, merge_ref[...]).astype(jnp.bfloat16)


def push(slot, slots, grads, slope, down, merge, held):
    rows, depth = grads.shape
    width = slope.shape[1]
    own = merge.shape[0]
    half = rows // 2
    whole = pl.BlockSpec(memory_space=pl.ANY)
    return pl.pallas_call(
        push_kernel,
        out_shape=(
            jax.ShapeDtypeStruct((slots * rows, depth), jnp.bfloat16),
            jax.ShapeDtypeStruct((slots * rows, width), jnp.bfloat16),
            jax.ShapeDtypeStruct((slots * rows, own), jnp.bfloat16),
        ),
        grid=(2,),
        in_specs=[
            pl.BlockSpec((half, depth), lambda i: (i, 0)),
            pl.BlockSpec((half, width), lambda i: (2 * slot + i, 0)),
            pl.BlockSpec(down.shape, lambda i: (0, 0)),
            pl.BlockSpec(merge.shape, lambda i: (0, 0)),
        ]
        + [whole] * len(held),
        out_specs=(
            pl.BlockSpec((half, depth), lambda i: (2 * slot + i, 0)),
            pl.BlockSpec((half, width), lambda i: (2 * slot + i, 0)),
            pl.BlockSpec((half, own), lambda i: (2 * slot + i, 0)),
        ),
        input_output_aliases={4 + k: k for k in range(len(held))},
        cost_estimate=short,
        name="push",
    )(grads, slope, down, merge, *held)


def pull_kernel(mixed_ref, hidden_ref, proj_ref, up_ref, tokens_ref, out_ref, sums_ref):
    partial_grad = dot_last(mixed_ref[...], proj_ref[...]) + dot_last(hidden_ref[...], up_ref[...])
    out_ref[...] = partial_grad
    unit, unused = normalize(tokens_ref[...])
    gain = jnp.sum(partial_grad * unit, axis=0, keepdims=True)
    bias = jnp.sum(partial_grad, axis=0, keepdims=True)
    both = jnp.concatenate([gain, bias], axis=0)

    @pl.when(pl.program_id(0) == 0)
    def _():
        sums_ref[...] = both

    @pl.when(pl.program_id(0) > 0)
    def _():
        sums_ref[...] += both


def pull(slot, mixed, hidden_grad, proj, up, tokens):
    rows, depth = tokens.shape
    half = rows // 2
    return pl.pallas_call(
        pull_kernel,
        out_shape=(
            jax.ShapeDtypeStruct((rows, depth), jnp.float32),
            jax.ShapeDtypeStruct((2, depth), jnp.float32),
        ),
        grid=(2,),
        in_specs=[
            pl.BlockSpec((half, mixed.shape[1]), lambda i: (2 * slot + i, 0)),
            pl.BlockSpec((half, hidden_grad.shape[1]), lambda i: (2 * slot + i, 0)),
            pl.BlockSpec(proj.shape, lambda i: (0, 0)),
            pl.BlockSpec(up.shape, lambda i: (0, 0)),
            pl.BlockSpec((half, depth), lambda i: (i, 0)),
        ],
        out_specs=(
            pl.BlockSpec((half, depth), lambda i: (i, 0)),
            pl.BlockSpec((2, depth), lambda i: (0, 0)),
        ),
        cost_estimate=short,
        name="pull",
    )(mixed, hidden_grad, proj, up, tokens)


def pick_kernel(index_ref, all_ref, out_ref):
    out_ref[...] = all_ref[...].reshape(out_ref.shape)


def pick_proj(weight_all, span_index, own_width):
    shards, narrow_count, rows, cols = weight_all.shape
    units = own_width // LANES
    per_shard = cols // LANES
    per_part = D // LANES

    def source(c, index_ref):
        unit = (c % 3) * per_part + index_ref[0] * units + c // 3
        return (unit // per_shard, 0, 0, unit % per_shard)

    return pl.pallas_call(
        pick_kernel,
        out_shape=jax.ShapeDtypeStruct((D, 3 * own_width), jnp.bfloat16),
        grid_spec=pltpu.PrefetchScalarGridSpec(
            num_scalar_prefetch=1,
            grid=(3 * units,),
            in_specs=[pl.BlockSpec((1, narrow_count, rows, LANES), source)],
            out_specs=pl.BlockSpec((D, LANES), lambda c, index_ref: (0, c)),
        ),
        cost_estimate=short,
        name="pick_proj",
    )(span_index.reshape(1), weight_all)


def turn_kernel(slots_ref, all_ref, out_ref):
    unused, narrow_count, rows, cols = all_ref.shape
    for t in range(narrow_count):
        out_ref[t * rows : (t + 1) * rows, :] = all_ref[0, slots_ref[t]]


def pick_merge(weight_all, slots, own_width):
    shards, narrow_count, rows, cols = weight_all.shape
    return pl.pallas_call(
        turn_kernel,
        out_shape=jax.ShapeDtypeStruct((D, D), jnp.bfloat16),
        grid_spec=pltpu.PrefetchScalarGridSpec(
            num_scalar_prefetch=1,
            grid=(shards,),
            in_specs=[
                pl.BlockSpec(
                    (1, narrow_count, rows, LANES),
                    lambda j, slots_ref: (j, 0, 0, 0),
                )
            ],
            out_specs=pl.BlockSpec((D, LANES), lambda j, slots_ref: (0, j)),
        ),
        cost_estimate=short,
        name="pick_merge",
    )(slots, weight_all)


def head_lanes(field, head):
    lane = lax.broadcasted_iota(jnp.int32, field.shape, 1)
    keep = (lane >= head * HEAD) & (lane < (head + 1) * HEAD)
    return jnp.where(keep, field, jnp.zeros_like(field))


def pair_allowed(start_row, key_first, key_count, query_first, query_count):
    key_index = key_first + lax.broadcasted_iota(jnp.int32, (key_count, query_count), 0)
    query_index = query_first + lax.broadcasted_iota(jnp.int32, (key_count, query_count), 1)
    return (key_index >= start_row) & (key_index <= query_index)


def attend_kernel(
    block_q,
    block_k,
    heads_in,
    slots_ref,
    first_ref,
    last_ref,
    start_ref,
    query_ref,
    key_ref,
    value_ref,
    *refs,
):
    out_ref, tall_ref, log_ref, turned, best, total, summed = refs[-7:]
    index = pl.program_id(0)
    key_blocks = key_ref.shape[0] // block_k

    @pl.when(index == 0)
    def _():
        for j in range(key_blocks):
            piece = value_ref[j * block_k : (j + 1) * block_k, :].astype(jnp.float32)
            turned[:, j * block_k : (j + 1) * block_k] = piece.T.astype(jnp.bfloat16)

    query_first = index * block_q
    low = first_ref[index] // block_k
    high = (query_first + block_q - 1) // block_k + 1
    start_row = start_ref[...]
    queries = [head_lanes(query_ref[...], head) for head in range(heads_in)]
    best[...] = jnp.full_like(best, masked_score)
    total[...] = jnp.zeros_like(total)
    summed[...] = jnp.zeros_like(summed)

    def visit(j, masked):
        key_rows = pl.ds(pl.multiple_of(slots_ref[j] * block_k, block_k), block_k)
        keys = key_ref[key_rows, :]
        if masked:
            allowed = pair_allowed(start_row, j * block_k, block_k, query_first, block_q)
        for head in range(heads_in):
            scores = dot_last(keys, queries[head])
            if masked:
                scores = jnp.where(allowed, scores, masked_score)
            old = best[head : head + 1, :]
            new = jnp.maximum(old, jnp.max(scores, axis=0, keepdims=True))
            weights = jnp.exp(scores - new)
            if masked:
                weights = jnp.where(allowed, weights, 0.0)
            factor = jnp.exp(old - new)
            best[head : head + 1, :] = new
            total[head : head + 1, :] = total[head : head + 1, :] * factor + jnp.sum(
                weights, axis=0, keepdims=True
            )
            rows = slice(head * HEAD, (head + 1) * HEAD)
            summed[rows, :] = summed[rows, :] * factor + dot_plain(
                turned[rows, key_rows], weights.astype(jnp.bfloat16)
            )

    def step(j, carry):
        whole = (j * block_k >= last_ref[index]) & ((j + 1) * block_k - 1 <= query_first)

        @pl.when(whole)
        def _():
            visit(j, False)

        @pl.when(jnp.logical_not(whole))
        def _():
            visit(j, True)

        return carry

    lax.fori_loop(low, high, step, 0)
    for head in range(heads_in):
        rows = slice(head * HEAD, (head + 1) * HEAD)
        weight = total[head : head + 1, :]
        tall_ref[rows, :] = summed[rows, :] / weight
        log_ref[0, head : head + 1, :] = best[head : head + 1, :] + jnp.log(weight)
    if heads_in * HEAD < LANES:
        tall_ref[heads_in * HEAD :, :] = jnp.zeros_like(tall_ref[heads_in * HEAD :, :])
    log_ref[0, heads_in:, :] = jnp.zeros_like(log_ref[0, heads_in:, :])
    out_ref[...] = tall_ref[...].T.astype(jnp.bfloat16)


def attend(pair, packed, slots, first, last, starts, heads_in, block_q, block_k, held):
    count, width = packed.shape
    pairs = width // 3 // LANES
    whole = pl.BlockSpec(memory_space=pl.ANY)
    return pl.pallas_call(
        partial(attend_kernel, block_q, block_k, heads_in),
        out_shape=(
            jax.ShapeDtypeStruct((count, pairs * LANES), jnp.bfloat16),
            jax.ShapeDtypeStruct((pairs * LANES, count), jnp.float32),
            jax.ShapeDtypeStruct((pairs, 8, count), jnp.float32),
        ),
        grid_spec=pltpu.PrefetchScalarGridSpec(
            num_scalar_prefetch=3,
            grid=(count // block_q,),
            in_specs=[
                pl.BlockSpec((1, block_q), lambda i, slots_ref, *_: (0, slots_ref[i])),
                pl.BlockSpec((block_q, LANES), lambda i, slots_ref, *_: (slots_ref[i], 3 * pair)),
                pl.BlockSpec((count, LANES), lambda i, *_: (0, 3 * pair + 1)),
                pl.BlockSpec((count, LANES), lambda i, *_: (0, 3 * pair + 2)),
            ]
            + [whole] * len(held),
            out_specs=(
                pl.BlockSpec((block_q, LANES), lambda i, slots_ref, *_: (slots_ref[i], pair)),
                pl.BlockSpec((LANES, block_q), lambda i, slots_ref, *_: (pair, slots_ref[i])),
                pl.BlockSpec((1, 8, block_q), lambda i, slots_ref, *_: (pair, 0, slots_ref[i])),
            ),
            scratch_shapes=[
                pltpu.VMEM((LANES, count), jnp.bfloat16),
                pltpu.VMEM((8, block_q), jnp.float32),
                pltpu.VMEM((8, block_q), jnp.float32),
                pltpu.VMEM((LANES, block_q), jnp.float32),
            ],
        ),
        input_output_aliases={7 + k: k for k in range(len(held))},
        cost_estimate=short,
        name="attend",
    )(slots, first, last, starts.reshape(1, count), packed, packed, packed, *held)


def attend_back_kernel(
    block_q,
    block_k,
    heads_in,
    slots_ref,
    last_ref,
    end_ref,
    start_ref,
    cos_ref,
    sin_ref,
    query_ref,
    key_ref,
    value_ref,
    tall_ref,
    log_ref,
    grad_ref,
    out_ref,
    turned,
    masked_q,
    masked_g,
    delta,
    tall_q,
    key_sum,
    value_sum,
):
    index = pl.program_id(1)
    count = query_ref.shape[0]

    def turn_back(field, rows):
        return field * cos_ref[rows, :] - partner(field) * sin_ref[rows, :]

    @pl.when(index == 0)
    def _():
        def prepare(j, carry):
            rows = pl.ds(pl.multiple_of(j * block_k, block_k), block_k)
            turned[:, rows] = key_ref[rows, :].astype(jnp.float32).T.astype(jnp.bfloat16)
            grads = grad_ref[rows, :]
            product = grads.astype(jnp.float32).T * tall_ref[:, rows]
            for head in range(heads_in):
                masked_q[head, rows, :] = head_lanes(query_ref[rows, :], head)
                masked_g[head, rows, :] = head_lanes(grads, head)
                delta[head : head + 1, rows] = jnp.sum(
                    product[head * HEAD : (head + 1) * HEAD, :], axis=0, keepdims=True
                )
            tall_q[:, rows] = jnp.zeros((LANES, block_k), jnp.float32)
            return carry

        lax.fori_loop(0, count // block_k, prepare, 0)

    key_first = index * block_k
    key_rows = pl.ds(pl.multiple_of(slots_ref[index] * block_k, block_k), block_k)
    keys = key_ref[key_rows, :]
    values = value_ref[key_rows, :]
    key_sum[...] = jnp.zeros_like(key_sum)
    value_sum[...] = jnp.zeros_like(value_sum)

    def visit(i, masked):
        query_first = i * block_q
        rows = pl.ds(pl.multiple_of(slots_ref[i] * block_q, block_q), block_q)
        if masked:
            allowed = pair_allowed(
                start_ref[0:1, rows], key_first, block_k, query_first, block_q
            )
        for head in range(heads_in):
            queries = masked_q[head, rows, :]
            grads = masked_g[head, rows, :]
            scores = dot_last(keys, queries)
            probs = jnp.exp(scores - log_ref[0, head : head + 1, rows])
            if masked:
                probs = jnp.where(allowed, probs, 0.0)
            value_sum[...] += dot_plain(probs.astype(jnp.bfloat16), grads)
            prob_grad = dot_last(values, grads)
            score_grad = (probs * (prob_grad - delta[head : head + 1, rows])).astype(jnp.bfloat16)
            key_sum[...] += dot_plain(score_grad, queries)
            lanes = slice(head * HEAD, (head + 1) * HEAD)
            tall_q[lanes, rows] += dot_plain(turned[lanes, key_rows], score_grad)

    def step(i, carry):
        whole = (key_first >= last_ref[i]) & (key_first + block_k - 1 <= i * block_q)

        @pl.when(whole)
        def _():
            visit(i, False)

        @pl.when(jnp.logical_not(whole))
        def _():
            visit(i, True)

        return carry

    lax.fori_loop(key_first // block_q, (end_ref[index] - 1) // block_q + 1, step, 0)
    out_ref[key_rows, LANES : 2 * LANES] = turn_back(key_sum[...], key_rows).astype(jnp.bfloat16)
    out_ref[key_rows, 2 * LANES :] = value_sum[...].astype(jnp.bfloat16)

    @pl.when(index == pl.num_programs(1) - 1)
    def _():
        def finish(j, carry):
            rows = pl.ds(pl.multiple_of(j * block_k, block_k), block_k)
            field = tall_q[:, rows].T * HEAD ** (-0.5)
            out_ref[rows, :LANES] = turn_back(field, rows).astype(jnp.bfloat16)
            return carry

        lax.fori_loop(0, count // block_k, finish, 0)


def attend_back(
    packed, slots, last, end, starts, cosine, sine, tall, logs, grads, heads_in, block_q, block_k
):
    count, width = packed.shape
    pairs = width // 3 // LANES
    return pl.pallas_call(
        partial(attend_back_kernel, block_q, block_k, heads_in),
        out_shape=jax.ShapeDtypeStruct((count, width), jnp.bfloat16),
        grid_spec=pltpu.PrefetchScalarGridSpec(
            num_scalar_prefetch=3,
            grid=(pairs, count // block_k),
            in_specs=[
                pl.BlockSpec((1, count), lambda p, i, *_: (0, 0)),
                pl.BlockSpec((count, LANES), lambda p, i, *_: (0, 0)),
                pl.BlockSpec((count, LANES), lambda p, i, *_: (0, 0)),
                pl.BlockSpec((count, LANES), lambda p, i, *_: (0, 3 * p)),
                pl.BlockSpec((count, LANES), lambda p, i, *_: (0, 3 * p + 1)),
                pl.BlockSpec((count, LANES), lambda p, i, *_: (0, 3 * p + 2)),
                pl.BlockSpec((LANES, count), lambda p, i, *_: (p, 0)),
                pl.BlockSpec((1, 8, count), lambda p, i, *_: (p, 0, 0)),
                pl.BlockSpec((count, LANES), lambda p, i, *_: (0, p)),
            ],
            out_specs=pl.BlockSpec((count, 3 * LANES), lambda p, i, *_: (0, p)),
            scratch_shapes=[
                pltpu.VMEM((LANES, count), jnp.bfloat16),
                pltpu.VMEM((heads_in, count, LANES), jnp.bfloat16),
                pltpu.VMEM((heads_in, count, LANES), jnp.bfloat16),
                pltpu.VMEM((8, count), jnp.float32),
                pltpu.VMEM((LANES, count), jnp.float32),
                pltpu.VMEM((block_k, LANES), jnp.float32),
                pltpu.VMEM((block_k, LANES), jnp.float32),
            ],
        ),
        compiler_params=pltpu.CompilerParams(vmem_limit_bytes=60 << 20),
        cost_estimate=short,
        name="attend_back",
    )(
        slots, last, end, starts.reshape(1, count), cosine, sine,
        packed, packed, packed, tall, logs, grads,
    )


def finish_kernel(narrow_count, wide_count, own_units, per_shard, *refs):
    exchange = own_units > 0
    if exchange:
        (
            parts_ref, piece_ref, total_ref, block_ref, near, far, near_sum,
            send_near, recv_near, send_far, recv_far, send_piece, recv_piece,
        ) = refs
    else:
        (
            parts_ref, total_ref, near, far, near_sum, send_near, recv_near, send_far, recv_far,
        ) = refs
    narrow_me = lax.axis_index("narrow")
    wide_me = lax.axis_index("wide")

    def place(narrow_at, wide_at):
        return {"narrow": narrow_at, "wide": wide_at}

    mesh_ids = pl.DeviceIdType.MESH
    barrier = pltpu.get_barrier_semaphore()
    greeted = 0
    for ahead in range(narrow_count):
        for across in range(wide_count):
            if (ahead > 0) + (across > 0) == 0 or (not exchange and ahead > 0 and across > 0):
                continue
            greeted += 1
            pl.semaphore_signal(
                barrier,
                inc=1,
                device_id=place(
                    lax.rem(narrow_me + ahead, narrow_count), lax.rem(wide_me + across, wide_count)
                ),
                device_id_type=mesh_ids,
            )
    pl.semaphore_wait(barrier, greeted)
    near_copies = []
    for ahead in range(1, narrow_count):
        copy = pltpu.make_async_remote_copy(
            src_ref=parts_ref,
            dst_ref=near.at[narrow_me],
            send_sem=send_near.at[ahead - 1],
            recv_sem=recv_near.at[ahead - 1],
            device_id=place(lax.rem(narrow_me + ahead, narrow_count), wide_me),
            device_id_type=mesh_ids,
        )
        copy.start()
        near_copies.append(copy)
    near[narrow_me] = parts_ref[...]
    if exchange:
        rows = piece_ref.shape[0]
        halves = block_ref.shape[0] // rows
        half_me = lax.rem(wide_me, halves)
        narrow_to = lax.div(wide_me, halves)
        moves = []
        for unit in range(3 * own_units):
            whole_unit = (unit % 3) * (D // LANES) + narrow_me * own_units + unit // 3
            wide_to = lax.div(whole_unit, per_shard)
            column = lax.rem(whole_unit, per_shard)
            source = piece_ref.at[:, unit * LANES : (unit + 1) * LANES]
            target = block_ref.at[
                pl.ds(pl.multiple_of(half_me * rows, rows), rows),
                pl.ds(pl.multiple_of(column * LANES, LANES), LANES),
            ]
            arrived = recv_piece.at[half_me * per_shard + column]
            remote = pltpu.make_async_remote_copy(
                src_ref=source,
                dst_ref=target,
                send_sem=send_piece.at[unit],
                recv_sem=arrived,
                device_id=place(narrow_to, wide_to),
                device_id_type=mesh_ids,
            )
            here = pltpu.make_async_copy(source, target, arrived)
            mine = (narrow_to == narrow_me) & (wide_to == wide_me)
            pl.when(jnp.logical_not(mine))(remote.start)
            pl.when(mine)(here.start)
            moves.append((mine, remote))
    for copy in near_copies:
        copy.wait()
    value = near[0]
    for k in range(1, narrow_count):
        value = value + near[k]
    near_sum[...] = value
    far_copies = []
    for across in range(1, wide_count):
        copy = pltpu.make_async_remote_copy(
            src_ref=near_sum,
            dst_ref=far.at[wide_me],
            send_sem=send_far.at[across - 1],
            recv_sem=recv_far.at[across - 1],
            device_id=place(narrow_me, lax.rem(wide_me + across, wide_count)),
            device_id_type=mesh_ids,
        )
        copy.start()
        far_copies.append(copy)
    far[wide_me] = value
    for copy in far_copies:
        copy.wait()
    value = far[0]
    for k in range(1, wide_count):
        value = value + far[k]
    total_ref[...] = value
    if exchange:
        for mine, remote in moves:
            pl.when(jnp.logical_not(mine))(remote.wait_send)
        for half in range(halves):
            for column in range(per_shard):
                pltpu.make_async_copy(
                    piece_ref.at[:, 0:LANES],
                    block_ref.at[
                        half * rows : (half + 1) * rows, column * LANES : (column + 1) * LANES
                    ],
                    recv_piece.at[half * per_shard + column],
                ).wait()


def finish(parts, piece, narrow_count, wide_count, own_width, proj_cols):
    shape = parts.shape
    exchange = piece is not None
    own_units = own_width // LANES if exchange else 0
    per_shard = proj_cols // LANES
    vmem = pl.BlockSpec(memory_space=pltpu.VMEM)
    shapes = [jax.ShapeDtypeStruct(shape, jnp.float32)]
    scratch = [
        pltpu.VMEM((narrow_count,) + shape, jnp.float32),
        pltpu.VMEM((wide_count,) + shape, jnp.float32),
        pltpu.VMEM(shape, jnp.float32),
        pltpu.SemaphoreType.DMA((narrow_count - 1,)),
        pltpu.SemaphoreType.DMA((narrow_count - 1,)),
        pltpu.SemaphoreType.DMA((wide_count - 1,)),
        pltpu.SemaphoreType.DMA((wide_count - 1,)),
    ]
    if exchange:
        shapes.append(jax.ShapeDtypeStruct((D // narrow_count, proj_cols), jnp.bfloat16))
        scratch += [
            pltpu.SemaphoreType.DMA((3 * own_units,)),
            pltpu.SemaphoreType.DMA((3 * own_units,)),
        ]
    return pl.pallas_call(
        partial(finish_kernel, narrow_count, wide_count, own_units, per_shard),
        out_shape=tuple(shapes),
        in_specs=[vmem] * len(shapes),
        out_specs=(vmem,) * len(shapes),
        scratch_shapes=scratch,
        compiler_params=pltpu.CompilerParams(collective_id=0, has_side_effects=True),
        name="finish",
    )(*([parts, piece] if exchange else [parts]))


def adam_update(
    weight, first_moment, second_moment, grad_value, step_rate, decay_coef, first_fix, second_fix
):
    new_first = beta_first * first_moment + (1.0 - beta_first) * grad_value
    new_second = beta_second * second_moment + (1.0 - beta_second) * grad_value * grad_value
    step_ratio = new_first / first_fix / (jnp.sqrt(new_second / second_fix) + adam_eps)
    return (weight - step_rate * (step_ratio + decay_coef * weight), new_first, new_second)


def adam_kernel(scale_ref, grads_ref, *refs):
    clip_factor, step_rate, first_scale, second_scale = [scale_ref[0, k] for k in range(4)]
    for matrix in range(2):
        weight = refs[3 * matrix][...]
        gradient = grads_ref[0, matrix].astype(jnp.float32) * clip_factor
        new_first = beta_first * refs[3 * matrix + 1][...] + (1.0 - beta_first) * gradient
        new_second = (
            beta_second * refs[3 * matrix + 2][...] + (1.0 - beta_second) * gradient * gradient
        )
        ratio = new_first * first_scale / (jnp.sqrt(new_second * second_scale) + adam_eps)
        new_weight = weight - step_rate * (ratio + decay_rate * weight)
        outs = refs[6 + 4 * matrix : 10 + 4 * matrix]
        for out_ref, value in zip(outs, (new_weight, new_first, new_second)):
            out_ref[...] = value
        outs[3][...] = new_weight.astype(jnp.bfloat16)


def adam_feed(scales, grads_all, *states):
    count, matrices, rows, cols = grads_all.shape
    block = pl.BlockSpec((rows, cols), lambda i: (i, 0))
    full = jax.ShapeDtypeStruct((count * rows, cols), jnp.float32)
    copy = jax.ShapeDtypeStruct((count * rows, cols), jnp.bfloat16)
    return pl.pallas_call(
        adam_kernel,
        out_shape=(full, full, full, copy) * 2,
        grid=(count,),
        in_specs=[
            pl.BlockSpec(memory_space=pltpu.SMEM),
            pl.BlockSpec((1, matrices, rows, cols), lambda i: (i, 0, 0, 0)),
        ]
        + [block] * 6,
        out_specs=(block,) * 8,
        cost_estimate=short,
        name="adam_feed",
    )(scales, grads_all, *states)


def shards(
    tokens,
    cotangent,
    seq_lengths,
    step_count,
    norm_params,
    norm_first,
    norm_second,
    proj_weight,
    proj_first,
    proj_second,
    merge_weight,
    merge_first,
    merge_second,
    up_weight,
    up_first,
    up_second,
    down_weight,
    down_first,
    down_second,
):
    tok_rows = tokens.shape[0]
    narrow_count = lax.axis_size("narrow")
    wide_count = lax.axis_size("wide")
    span_index = lax.axis_index("narrow")
    group_rows = tok_rows * narrow_count
    own_width = HEADS // narrow_count * HEAD
    held_width = max(own_width, LANES)
    heads_in = min(own_width, LANES) // HEAD
    shard_rows = D // narrow_count
    proj_cols = proj_weight.shape[1]
    lengths = seq_lengths[0]
    onward = [(i, (i + 1) % narrow_count) for i in range(narrow_count)]
    slots = lax.rem(
        span_index + narrow_count - jnp.arange(narrow_count, dtype=jnp.int32), narrow_count
    )

    def pad_lanes(array, axis):
        extra = [(0, 0)] * array.ndim
        extra[axis] = (0, held_width - own_width)
        return jnp.pad(array, extra) if held_width > own_width else array

    def meet(*values):
        return lax.optimization_barrier(values)

    def send_on(array):
        return lax.ppermute(array, "narrow", onward)

    def rows_of(array, slot):
        return array[slot * tok_rows : (slot + 1) * tok_rows]

    direct = own_width % LANES == 0 and proj_cols % LANES == 0 and merge_weight.shape[1] == LANES
    weight_part = jnp.concatenate(
        [proj_weight.astype(jnp.bfloat16), merge_weight.astype(jnp.bfloat16)], axis=1
    )
    weight_rows = lax.all_gather(weight_part, "narrow", axis=0, tiled=True)
    up_slice = up_weight.astype(jnp.bfloat16)
    down_slice = down_weight.astype(jnp.bfloat16)

    def wide_all(array):
        return lax.all_gather(array, "wide", axis=0).reshape(
            wide_count, narrow_count, shard_rows, -1
        )

    order = list(range(1, narrow_count)) + [0]
    pairs = held_width // LANES
    token_blocks = [tokens]
    held = ()
    for slot in range(narrow_count - 1):
        moving = send_on(token_blocks[slot])
        held = feed(slot, narrow_count, token_blocks[slot], norm_params, up_slice, held)
        moving, held = meet(moving, held)
        if slot == 0:
            lengths, slots, moving, weight_rows = meet(lengths, slots, moving, weight_rows)
            proj_all = wide_all(weight_rows[:, :proj_cols])
            merge_all = wide_all(weight_rows[:, proj_cols:])
        if slot == 1 or narrow_count == 2:
            places = (
                slots[:, None] * tok_rows + jnp.arange(tok_rows, dtype=jnp.int32)[None, :]
            ).reshape(group_rows)
            seq_start, unused = locate(lengths, places)
            cosine, sine = rotary_tables(places - seq_start)
            block_first = jnp.arange(narrow_count, dtype=jnp.int32) * tok_rows
            first_start, unused = locate(lengths, block_first)
            last_start, last_end = locate(lengths, block_first + (tok_rows - 1))
            moving, cosine, sine, first_start, last_start, last_end = meet(
                moving, cosine, sine, first_start, last_start, last_end
            )
        elif slot == 2:
            moving, down_slice = meet(moving, down_slice)
        token_blocks.append(moving)
    grad_first, last_block = meet(cotangent, token_blocks[-1])
    token_blocks[-1] = last_block
    grad_blocks = [grad_first]

    moving = send_on(grad_first)
    gathered, activated, slope = feed(
        narrow_count - 1, narrow_count, last_block, norm_params, up_slice, held
    )
    if direct:
        proj_own = pick_proj(proj_all, span_index, own_width)
        merge_turn = pick_merge(merge_all, slots, own_width)
    else:
        proj_copy = jnp.transpose(proj_all, (1, 2, 0, 3)).reshape(
            D, 3, narrow_count, own_width
        )
        proj_own = pad_lanes(
            lax.dynamic_index_in_dim(proj_copy, span_index, axis=2, keepdims=False), 2
        ).reshape(D, 3 * held_width)
        merge_copy = jnp.transpose(merge_all, (1, 2, 0, 3)).reshape(
            narrow_count, own_width, D
        )
        merge_turn = jnp.take(merge_copy, slots, axis=0).reshape(D, D)
    merge_own = pad_lanes(merge_turn[:own_width], 0)
    packed = project(gathered, proj_own, cosine, sine)
    moving, packed, activated, slope = meet(moving, packed, activated, slope)
    grad_blocks.append(moving)

    def down_term(slot):
        return dot_plain(rows_of(activated, slot), down_slice)

    def wide_sum(grad):
        return lax.psum_scatter(grad, "wide", scatter_dimension=0, tiled=True)

    def attend_pair(pair, attended_held):
        return attend(
            pair, packed, slots, first_start, last_start, seq_start,
            heads_in, tok_rows, tok_rows, attended_held,
        )

    def push_slot(slot, push_held):
        return push(
            slot, narrow_count, grad_blocks[slot], slope, down_slice, merge_own, push_held
        )

    attended_held = ()
    push_held = ()
    pushed = 0
    first_term = down_term(1).astype(jnp.bfloat16)
    for hop in range(2, narrow_count):
        moving = send_on(grad_blocks[-1])
        if hop - 2 < pairs:
            attended_held = attend_pair(hop - 2, attended_held)
        for pushed in range(pushed, hop):
            push_held = push_slot(pushed, push_held)
        pushed = hop
        moving, attended_held, push_held, first_term = meet(
            moving, attended_held, push_held, first_term
        )
        grad_blocks.append(moving)
    for pair in range(narrow_count - 2, pairs):
        attended_held = attend_pair(pair, attended_held)
    attended, tall, logs = attended_held

    moving = send_on(first_term)
    for slot in range(pushed, narrow_count):
        push_held = push_slot(slot, push_held)
    grads_all, hidden_grad, attended_grad = push_held
    part_rows = D // wide_count
    down_grad = dot_first(activated, grads_all).astype(jnp.bfloat16)
    up_grad = dot_first(gathered, hidden_grad).astype(jnp.bfloat16)
    next_term = down_term(order[1])
    pieces = [
        rows_of(attended, (narrow_count - ahead) % narrow_count)[:, :own_width]
        for ahead in range(narrow_count)
    ]
    moving, pieces, up_grad, down_grad, attended_grad, next_term = meet(
        moving, pieces, up_grad, down_grad, attended_grad, next_term
    )
    feed_grad = jnp.concatenate(
        [
            up_grad.reshape(wide_count, part_rows, -1),
            down_grad.reshape(wide_count, part_rows, -1),
        ],
        axis=1,
    ).reshape(2 * D, -1)
    feed_part = wide_sum(feed_grad)

    def heads_back():
        mixed = attend_back(
            packed, slots, last_start, last_end, seq_start, cosine, sine,
            tall, logs, attended_grad, heads_in, tok_rows, tok_rows,
        )
        proj_grad = dot_first(gathered, mixed).astype(jnp.bfloat16)
        merge_grad = dot_first(grads_all, attended).astype(jnp.bfloat16)
        if not direct:
            proj_grad = proj_grad.reshape(D, 3, held_width)[:, :, :own_width].reshape(D, -1)
            merge_grad = merge_grad[:, :own_width]
        return (mixed, jnp.concatenate([proj_grad, merge_grad], axis=1))

    for ahead in range(1, narrow_count):
        pieces[ahead] = lax.ppermute(
            pieces[ahead],
            "narrow",
            [(i, (i + ahead) % narrow_count) for i in range(narrow_count)],
        )
    terms = []
    norm_part = jnp.zeros((2, D), jnp.float32)

    def pull_more(count, mixed, norm_part):
        for slot in order[len(terms) : len(terms) + count]:
            term, sums = pull(slot, mixed, hidden_grad, proj_own, up_slice, token_blocks[slot])
            terms.append(term)
            norm_part = norm_part + sums
        return norm_part

    if narrow_count == 2:
        mixed_grad, heads_grad = heads_back()
        pieces, mixed_grad, heads_grad = meet(pieces, mixed_grad, heads_grad)
    for place, slot in enumerate(order[1:-1]):
        moving = send_on((moving.astype(jnp.float32) + next_term).astype(jnp.bfloat16))
        next_term = down_term(order[place + 2])
        if place == 0:
            mixed_grad, heads_grad = heads_back()
            moving, pieces, mixed_grad, heads_grad, next_term = meet(
                moving, pieces, mixed_grad, heads_grad, next_term
            )
            heads_part = wide_sum(heads_grad)
        else:
            norm_part = pull_more(4, mixed_grad, norm_part)
            moving, terms, norm_part, next_term = meet(moving, terms, norm_part, next_term)
        if slot == narrow_count - 1:
            moving, feed_part = meet(moving, feed_part)
    if narrow_count == 2:
        heads_part = wide_sum(heads_grad)
    norm_part = pull_more(narrow_count, mixed_grad, norm_part)
    feed_all = lax.all_gather(feed_part, "wide", axis=0).reshape(
        wide_count, 2, part_rows, -1
    )

    branch_moving = moving
    moving = send_on(terms[0].astype(jnp.bfloat16))
    branch = branch_moving.astype(jnp.float32) + next_term
    merged = dot_plain(jnp.concatenate(pieces, axis=1), merge_turn)
    unit_rows, inv_std = normalize(tokens)
    output_rows = tokens.astype(jnp.float32) + merged + branch
    layer_out = output_rows.astype(jnp.bfloat16)

    def squares(array):
        value = array.astype(jnp.float32)
        return jnp.sum(value * value)

    row_squares = [squares(output_rows), squares(merged), squares(branch)]
    sent = None
    for place in range(1, narrow_count - 1):
        if place == 1:
            moving, row_squares, norm_part = meet(moving, row_squares, norm_part)
        elif place == narrow_count - 2:
            moving, heads_part = meet(moving, heads_part)
        sent = (moving.astype(jnp.float32) + terms[place]).astype(jnp.bfloat16)
        if place < narrow_count - 2:
            moving = send_on(sent)

    scalars = jnp.stack(
        [
            squares(heads_part) + squares(feed_part),
        ]
        + row_squares
    )
    parts = jnp.concatenate(
        [norm_part.reshape(2 * D // LANES, LANES), jnp.pad(scalars, (0, LANES - 4))[None, :]]
    )
    parts = jnp.pad(parts, ((0, 7), (0, 0)))
    if sent is not None:
        sent, parts = meet(sent, parts)
        moving = send_on(sent)
    merge_block = heads_part[:, 3 * own_width :].T.astype(jnp.float32)
    if direct:
        summed, proj_block = finish(
            parts, heads_part, narrow_count, wide_count, own_width, proj_cols
        )
        proj_block = proj_block.astype(jnp.float32)
    else:
        (summed,) = finish(parts, None, narrow_count, wide_count, own_width, proj_cols)
        cross = lax.all_gather(heads_part[:, : 3 * own_width], "narrow", axis=0).reshape(
            narrow_count, part_rows, 3, own_width
        )
        cross = jnp.transpose(cross, (1, 2, 0, 3)).reshape(part_rows, wide_count, proj_cols)
        cross = lax.all_to_all(jnp.transpose(cross, (1, 0, 2)), "wide", 0, 0)
        proj_block = lax.dynamic_slice_in_dim(
            cross.reshape(D, proj_cols), span_index * shard_rows, shard_rows, axis=0
        ).astype(jnp.float32)
    norm_total = summed[: 2 * D // LANES].reshape(2, D)
    square_total = summed[2 * D // LANES, 0:1]
    output_squares = summed[2 * D // LANES, 1:2]
    branch_squares = summed[2 * D // LANES, 2:4]
    grad_norm = jnp.sqrt(square_total + jnp.sum(norm_total * norm_total))
    clip_factor = jnp.minimum(1.0, math.sqrt(NPARAMS) / grad_norm)
    entry_count = wide_count * group_rows * D
    residual_rms = jnp.sqrt(output_squares / entry_count)
    branch_norms = jnp.sqrt(branch_squares / entry_count)
    step_value = step_count[0].astype(jnp.float32)
    first_fix = 1.0 - jnp.power(beta_first, step_value)
    second_fix = 1.0 - jnp.power(beta_second, step_value)
    ramp = jnp.minimum(1.0, step_value / warmup_steps)
    norm_clipped = norm_total * clip_factor
    new_norm = adam_update(
        norm_params,
        norm_first,
        norm_second,
        norm_clipped,
        norm_rate * ramp,
        0.0,
        first_fix,
        second_fix,
    )
    new_proj = adam_update(
        proj_weight,
        proj_first,
        proj_second,
        proj_block * clip_factor,
        matrix_rate * ramp,
        decay_rate,
        first_fix,
        second_fix,
    )
    new_merge = adam_update(
        merge_weight,
        merge_first,
        merge_second,
        merge_block * clip_factor,
        matrix_rate * ramp,
        decay_rate,
        first_fix,
        second_fix,
    )
    if direct:
        scales = jnp.stack(
            [clip_factor[0], matrix_rate * ramp, 1.0 / first_fix, 1.0 / second_fix]
        ).reshape(1, 4)
        updated = adam_feed(
            scales, feed_all, up_weight, up_first, up_second, down_weight, down_first, down_second
        )
        new_up, new_down = (updated[:4], updated[4:])
    else:
        feed_sums = feed_all.astype(jnp.float32)
        new_up, new_down = [
            adam_update(
                *state,
                feed_sums[:, matrix].reshape(state[0].shape) * clip_factor,
                matrix_rate * ramp,
                decay_rate,
                first_fix,
                second_fix,
            )
            for matrix, state in enumerate(
                [(up_weight, up_first, up_second), (down_weight, down_first, down_second)]
            )
        ]
        new_up, new_down = [new + (new[0].astype(jnp.bfloat16),) for new in (new_up, new_down)]
    moving, new_up = meet(moving, new_up)
    normed_grad = moving.astype(jnp.float32) + terms[-1]
    unit_grad = normed_grad * norm_params[0]
    input_grad = cotangent.astype(jnp.float32) + inv_std * (
        unit_grad
        - jnp.mean(unit_grad, axis=1, keepdims=True)
        - unit_rows * jnp.mean(unit_grad * unit_rows, axis=1, keepdims=True)
    )
    return (
        layer_out,
        input_grad,
        grad_norm,
        residual_rms,
        norm_clipped,
        new_norm[0],
        new_norm[1],
        new_norm[2],
        new_proj[0],
        new_proj[1],
        new_proj[2],
        new_merge[0],
        new_merge[1],
        new_merge[2],
        new_up[0],
        new_up[1],
        new_up[2],
        new_down[0],
        new_down[1],
        new_down[2],
        branch_norms,
        new_proj[0].astype(jnp.bfloat16),
        new_merge[0].astype(jnp.bfloat16),
        new_up[3],
        new_down[3],
    )


def solution(mesh):
    placed = (
        P(("wide", "narrow"), None),
        P(("wide", "narrow"), None),
        P("wide", None),
        P(),
        P(),
        P(),
        P(),
        P("narrow", "wide"),
        P("narrow", "wide"),
        P("narrow", "wide"),
        P("narrow", "wide"),
        P("narrow", "wide"),
        P("narrow", "wide"),
        P(None, "narrow"),
        P(None, "narrow"),
        P(None, "narrow"),
        P("narrow", None),
        P("narrow", None),
        P("narrow", None),
    )
    return jax.shard_map(
        shards,
        mesh=mesh,
        in_specs=placed,
        out_specs=(
            P(("wide", "narrow"), None),
            P(("wide", "narrow"), None),
            P(),
            P(),
            P(),
            P(),
            P(),
            P(),
            P("narrow", "wide"),
            P("narrow", "wide"),
            P("narrow", "wide"),
            P("narrow", "wide"),
            P("narrow", "wide"),
            P("narrow", "wide"),
            P(None, "narrow"),
            P(None, "narrow"),
            P(None, "narrow"),
            P("narrow", None),
            P("narrow", None),
            P("narrow", None),
            P(),
            P("narrow", "wide"),
            P("narrow", "wide"),
            P(None, "narrow"),
            P("narrow", None),
        ),
        check_vma=False,
    )
```

```python
from functools import partial
import math

import jax
import jax.numpy as jnp
from jax import lax
from jax.experimental import pallas as pl
from jax.experimental.pallas import tpu as pltpu
from jax.sharding import PartitionSpec as P

HEADS = 16
HEAD = 64
D = 1024
ROT = 16
LANES = 128
ROW_BLOCK = 512
NPARAMS = 12584960


norm_eps = 1e-05
adam_eps = 1e-08
beta_first = 0.5
beta_second = 0.5
decay_rate = 0.01
matrix_rate = 0.1
norm_rate = 1.0
warmup_steps = 20.0
masked_score = -1e30
short = pl.CostEstimate(flops=0, bytes_accessed=0, transcendentals=0)


def dot_last(left_side, right_side):
    return lax.dot_general(
        left_side, right_side, (((1,), (1,)), ((), ())), preferred_element_type=jnp.float32
    )


def dot_plain(left_side, right_side):
    return lax.dot_general(
        left_side, right_side, (((1,), (0,)), ((), ())), preferred_element_type=jnp.float32
    )


def dot_first(left_side, right_side):
    return lax.dot_general(
        left_side, right_side, (((0,), (0,)), ((), ())), preferred_element_type=jnp.float32
    )


def locate(lengths, token_index):
    seq_ends = jnp.cumsum(lengths)
    starts = seq_ends - lengths
    segment = jnp.sum(
        (seq_ends[None, :] <= token_index[:, None]).astype(jnp.int32), axis=1, dtype=jnp.int32
    )
    choose = segment[:, None] == jnp.arange(lengths.shape[0], dtype=jnp.int32)[None, :]
    seq_start = jnp.sum(jnp.where(choose, starts[None, :], 0), axis=1, dtype=jnp.int32)
    seq_end = jnp.sum(jnp.where(choose, seq_ends[None, :], 0), axis=1, dtype=jnp.int32)
    return (seq_start, seq_end)


def rotary_tables(position):
    half_rot = ROT // 2
    frequency = jnp.power(10000.0, -2.0 * jnp.arange(half_rot, dtype=jnp.float32) / ROT)
    row = jnp.concatenate([frequency, frequency, jnp.zeros((HEAD - ROT,), jnp.float32)])
    row = jnp.tile(row, LANES // HEAD)
    sign = jnp.where(jnp.arange(LANES) % HEAD < half_rot, -1.0, 1.0)
    phases = position.astype(jnp.float32)[:, None] * row[None, :]
    return (jnp.cos(phases), jnp.sin(phases) * sign[None, :])


def partner(field):
    half_rot = ROT // 2
    lane = lax.broadcasted_iota(jnp.int32, field.shape, 1) % HEAD
    return jnp.where(
        lane < half_rot,
        pltpu.roll(field, LANES - half_rot, 1),
        pltpu.roll(field, half_rot, 1),
    )


def project_kernel(rows_ref, weight_ref, cos_ref, sin_ref, out_ref):
    width = out_ref.shape[1]
    projected = dot_plain(rows_ref[...], weight_ref[...])
    for first in range(0, width, LANES):
        piece = projected[:, first : first + LANES]
        part = first // LANES % 3
        if part < 2:
            piece = piece * cos_ref[...] + partner(piece) * sin_ref[...]
        if part == 0:
            piece = piece * HEAD ** (-0.5)
        out_ref[:, first : first + LANES] = piece.astype(jnp.bfloat16)


def project(rows, weight, cosine, sine):
    count, depth = rows.shape
    width = weight.shape[1]
    block = min(ROW_BLOCK, count)
    return pl.pallas_call(
        project_kernel,
        out_shape=jax.ShapeDtypeStruct((count, width), jnp.bfloat16),
        grid=(count // block,),
        in_specs=[
            pl.BlockSpec((block, depth), lambda i: (i, 0)),
            pl.BlockSpec((depth, width), lambda i: (0, 0)),
            pl.BlockSpec((block, LANES), lambda i: (i, 0)),
            pl.BlockSpec((block, LANES), lambda i: (i, 0)),
        ],
        out_specs=pl.BlockSpec((block, width), lambda i: (i, 0)),
        cost_estimate=short,
        name="project",
    )(rows, weight, cosine, sine)


def normalize(tokens):
    residual = tokens.astype(jnp.float32)
    center = residual - jnp.mean(residual, axis=1, keepdims=True)
    inv_std = lax.rsqrt(jnp.mean(center * center, axis=1, keepdims=True) + norm_eps)
    return (center * inv_std, inv_std)


def feed_kernel(tokens_ref, params_ref, weight_ref, *refs):
    normed_ref, act_ref, slope_ref = refs[-3:]
    unit, unused = normalize(tokens_ref[...])
    normed_ref[...] = (unit * params_ref[0:1, :] + params_ref[1:2, :]).astype(jnp.bfloat16)
    width = act_ref.shape[1]
    step = min(256, width)
    for first in range(0, width, step):
        hidden = dot_plain(normed_ref[...], weight_ref[:, first : first + step])
        share = 0.5 + 0.5 * lax.erf(hidden * math.sqrt(0.5))
        bell = jnp.exp(hidden * hidden * -0.5) * (1.0 / math.sqrt(2.0 * math.pi))
        act_ref[:, first : first + step] = (hidden * share).astype(jnp.bfloat16)
        slope_ref[:, first : first + step] = share + hidden * bell


def feed(slot, slots, tokens, params, weight, held):
    rows, depth = tokens.shape
    width = weight.shape[1]
    whole = pl.BlockSpec(memory_space=pl.ANY)
    return pl.pallas_call(
        feed_kernel,
        out_shape=(
            jax.ShapeDtypeStruct((slots * rows, depth), jnp.bfloat16),
            jax.ShapeDtypeStruct((slots * rows, width), jnp.bfloat16),
            jax.ShapeDtypeStruct((slots * rows, width), jnp.float32),
        ),
        grid=(2,),
        in_specs=[
            pl.BlockSpec((rows // 2, depth), lambda i: (i, 0)),
            pl.BlockSpec((2, depth), lambda i: (0, 0)),
            pl.BlockSpec((depth, width), lambda i: (0, 0)),
        ]
        + [whole] * len(held),
        out_specs=(
            pl.BlockSpec((rows // 2, depth), lambda i: (2 * slot + i, 0)),
            pl.BlockSpec((rows // 2, width), lambda i: (2 * slot + i, 0)),
            pl.BlockSpec((rows // 2, width), lambda i: (2 * slot + i, 0)),
        ),
        input_output_aliases={3 + k: k for k in range(len(held))},
        cost_estimate=short,
        name="feed",
    )(tokens, params, weight, *held)


def push_kernel(index_ref, grad_ref, slope_ref, down_ref, merge_ref, *refs):
    all_ref, hidden_ref, attended_ref, merge_own = refs[-4:]

    @pl.when(pl.program_id(0) == 0)
    def _():
        if len(merge_ref.shape) == 4:
            for w in range(merge_ref.shape[0]):
                merge_own[:, w * LANES : (w + 1) * LANES] = merge_ref[w, 0]
        else:
            merge_own[...] = merge_ref[...]

    grads = grad_ref[...]
    all_ref[...] = grads
    hidden_ref[...] = (dot_last(grads, down_ref[...]) * slope_ref[...]).astype(jnp.bfloat16)
    attended_ref[...] = dot_last(grads, merge_own[...]).astype(jnp.bfloat16)


def push(slot, slots, grads, slope, down, merge, span_index, held):
    rows, depth = grads.shape
    width = slope.shape[1]
    half = rows // 2
    whole = pl.BlockSpec(memory_space=pl.ANY)
    if merge.ndim == 4:
        own = merge.shape[2]
        merge_spec = pl.BlockSpec(
            (merge.shape[0], 1, own, LANES), lambda i, index_ref: (0, index_ref[0], 0, 0)
        )
    else:
        own = merge.shape[0]
        merge_spec = pl.BlockSpec(merge.shape, lambda i, index_ref: (0, 0))

    def place(i, index_ref):
        return (2 * slot + i, 0)

    return pl.pallas_call(
        push_kernel,
        out_shape=(
            jax.ShapeDtypeStruct((slots * rows, depth), jnp.bfloat16),
            jax.ShapeDtypeStruct((slots * rows, width), jnp.bfloat16),
            jax.ShapeDtypeStruct((slots * rows, own), jnp.bfloat16),
        ),
        grid_spec=pltpu.PrefetchScalarGridSpec(
            num_scalar_prefetch=1,
            grid=(2,),
            in_specs=[
                pl.BlockSpec((half, depth), lambda i, index_ref: (i, 0)),
                pl.BlockSpec((half, width), place),
                pl.BlockSpec(down.shape, lambda i, index_ref: (0, 0)),
                merge_spec,
            ]
            + [whole] * len(held),
            out_specs=(
                pl.BlockSpec((half, depth), place),
                pl.BlockSpec((half, width), place),
                pl.BlockSpec((half, own), place),
            ),
            scratch_shapes=[pltpu.VMEM((own, depth), jnp.bfloat16)],
        ),
        input_output_aliases={5 + k: k for k in range(len(held))},
        cost_estimate=short,
        name="push",
    )(span_index.reshape(1), grads, slope, down, merge, *held)


def pull_kernel(mixed_ref, hidden_ref, proj_ref, up_ref, tokens_ref, out_ref, sums_ref):
    partial_grad = dot_last(mixed_ref[...], proj_ref[...]) + dot_last(hidden_ref[...], up_ref[...])
    out_ref[...] = partial_grad
    unit, unused = normalize(tokens_ref[...])
    gain = jnp.sum(partial_grad * unit, axis=0, keepdims=True)
    bias = jnp.sum(partial_grad, axis=0, keepdims=True)
    both = jnp.concatenate([gain, bias], axis=0)

    @pl.when(pl.program_id(0) == 0)
    def _():
        sums_ref[...] = both

    @pl.when(pl.program_id(0) > 0)
    def _():
        sums_ref[...] += both


def pull(slot, mixed, hidden_grad, proj, up, tokens):
    rows, depth = tokens.shape
    half = rows // 2
    return pl.pallas_call(
        pull_kernel,
        out_shape=(
            jax.ShapeDtypeStruct((rows, depth), jnp.float32),
            jax.ShapeDtypeStruct((2, depth), jnp.float32),
        ),
        grid=(2,),
        in_specs=[
            pl.BlockSpec((half, mixed.shape[1]), lambda i: (2 * slot + i, 0)),
            pl.BlockSpec((half, hidden_grad.shape[1]), lambda i: (2 * slot + i, 0)),
            pl.BlockSpec(proj.shape, lambda i: (0, 0)),
            pl.BlockSpec(up.shape, lambda i: (0, 0)),
            pl.BlockSpec((half, depth), lambda i: (i, 0)),
        ],
        out_specs=(
            pl.BlockSpec((half, depth), lambda i: (i, 0)),
            pl.BlockSpec((2, depth), lambda i: (0, 0)),
        ),
        cost_estimate=short,
        name="pull",
    )(mixed, hidden_grad, proj, up, tokens)


def project_all_kernel(index_ref, rows_ref, cos_ref, sin_ref, *refs):
    unit_refs, (out_ref, weight_ref) = refs[:-2], refs[-2:]

    @pl.when(pl.program_id(0) == 0)
    def _():
        for c, unit_ref in enumerate(unit_refs):
            weight_ref[:, c * LANES : (c + 1) * LANES] = unit_ref[...].reshape(D, LANES)

    project_kernel(rows_ref, weight_ref, cos_ref, sin_ref, out_ref)


def project_all(rows, weight_all, span_index, own_width, cosine, sine):
    count, depth = rows.shape
    shards, narrow_count, shard_rows, cols = weight_all.shape
    units = own_width // LANES
    width = 3 * own_width
    per_shard = cols // LANES
    per_part = D // LANES
    block = min(ROW_BLOCK, count)

    def source(c, i, index_ref):
        unit = (c % 3) * per_part + index_ref[0] * units + c // 3
        return (unit // per_shard, 0, 0, unit % per_shard)

    return pl.pallas_call(
        project_all_kernel,
        out_shape=(
            jax.ShapeDtypeStruct((count, width), jnp.bfloat16),
            jax.ShapeDtypeStruct((D, width), jnp.bfloat16),
        ),
        grid_spec=pltpu.PrefetchScalarGridSpec(
            num_scalar_prefetch=1,
            grid=(count // block,),
            in_specs=[
                pl.BlockSpec((block, depth), lambda i, index_ref: (i, 0)),
                pl.BlockSpec((block, LANES), lambda i, index_ref: (i, 0)),
                pl.BlockSpec((block, LANES), lambda i, index_ref: (i, 0)),
            ]
            + [
                pl.BlockSpec((1, narrow_count, shard_rows, LANES), partial(source, c))
                for c in range(3 * units)
            ],
            out_specs=(
                pl.BlockSpec((block, width), lambda i, index_ref: (i, 0)),
                pl.BlockSpec((D, width), lambda i, index_ref: (0, 0)),
            ),
        ),
        cost_estimate=short,
        name="project_all",
    )(span_index.reshape(1), rows, cosine, sine, *[weight_all] * (3 * units))


def turn_kernel(slots_ref, all_ref, out_ref):
    unused, narrow_count, rows, cols = all_ref.shape
    for t in range(narrow_count):
        out_ref[t * rows : (t + 1) * rows, :] = all_ref[0, slots_ref[t]]


def pick_merge(weight_all, slots, own_width):
    shards, narrow_count, rows, cols = weight_all.shape
    return pl.pallas_call(
        turn_kernel,
        out_shape=jax.ShapeDtypeStruct((D, D), jnp.bfloat16),
        grid_spec=pltpu.PrefetchScalarGridSpec(
            num_scalar_prefetch=1,
            grid=(shards,),
            in_specs=[
                pl.BlockSpec(
                    (1, narrow_count, rows, LANES),
                    lambda j, slots_ref: (j, 0, 0, 0),
                )
            ],
            out_specs=pl.BlockSpec((D, LANES), lambda j, slots_ref: (0, j)),
        ),
        cost_estimate=short,
        name="pick_merge",
    )(slots, weight_all)


def head_lanes(field, head):
    lane = lax.broadcasted_iota(jnp.int32, field.shape, 1)
    keep = (lane >= head * HEAD) & (lane < (head + 1) * HEAD)
    return jnp.where(keep, field, jnp.zeros_like(field))


def pair_allowed(start_row, key_first, key_count, query_first, query_count):
    key_index = key_first + lax.broadcasted_iota(jnp.int32, (key_count, query_count), 0)
    query_index = query_first + lax.broadcasted_iota(jnp.int32, (key_count, query_count), 1)
    return (key_index >= start_row) & (key_index <= query_index)


def attend_kernel(
    block_q,
    block_k,
    heads_in,
    slots_ref,
    first_ref,
    last_ref,
    start_ref,
    query_ref,
    key_ref,
    value_ref,
    *refs,
):
    out_ref, tall_ref, log_ref, turned, best, total, summed = refs[-7:]
    index = pl.program_id(0)
    key_blocks = key_ref.shape[0] // block_k

    @pl.when(index == 0)
    def _():
        for j in range(key_blocks):
            piece = value_ref[j * block_k : (j + 1) * block_k, :].astype(jnp.float32)
            turned[:, j * block_k : (j + 1) * block_k] = piece.T.astype(jnp.bfloat16)

    query_first = index * block_q
    low = first_ref[index] // block_k
    high = (query_first + block_q - 1) // block_k + 1
    start_row = start_ref[...]
    queries = [head_lanes(query_ref[...], head) for head in range(heads_in)]
    best[...] = jnp.full_like(best, masked_score)
    total[...] = jnp.zeros_like(total)
    summed[...] = jnp.zeros_like(summed)

    def visit(j, masked):
        key_rows = pl.ds(pl.multiple_of(slots_ref[j] * block_k, block_k), block_k)
        keys = key_ref[key_rows, :]
        if masked:
            allowed = pair_allowed(start_row, j * block_k, block_k, query_first, block_q)
        for head in range(heads_in):
            scores = dot_last(keys, queries[head])
            if masked:
                scores = jnp.where(allowed, scores, masked_score)
            old = best[head : head + 1, :]
            new = jnp.maximum(old, jnp.max(scores, axis=0, keepdims=True))
            weights = jnp.exp(scores - new)
            if masked:
                weights = jnp.where(allowed, weights, 0.0)
            factor = jnp.exp(old - new)
            best[head : head + 1, :] = new
            total[head : head + 1, :] = total[head : head + 1, :] * factor + jnp.sum(
                weights, axis=0, keepdims=True
            )
            rows = slice(head * HEAD, (head + 1) * HEAD)
            summed[rows, :] = summed[rows, :] * factor + dot_plain(
                turned[rows, key_rows], weights.astype(jnp.bfloat16)
            )

    def step(j, carry):
        whole = (j * block_k >= last_ref[index]) & ((j + 1) * block_k - 1 <= query_first)

        @pl.when(whole)
        def _():
            visit(j, False)

        @pl.when(jnp.logical_not(whole))
        def _():
            visit(j, True)

        return carry

    lax.fori_loop(low, high, step, 0)
    for head in range(heads_in):
        rows = slice(head * HEAD, (head + 1) * HEAD)
        weight = total[head : head + 1, :]
        tall_ref[rows, :] = summed[rows, :] / weight
        log_ref[0, head : head + 1, :] = best[head : head + 1, :] + jnp.log(weight)
    if heads_in * HEAD < LANES:
        tall_ref[heads_in * HEAD :, :] = jnp.zeros_like(tall_ref[heads_in * HEAD :, :])
    log_ref[0, heads_in:, :] = jnp.zeros_like(log_ref[0, heads_in:, :])
    out_ref[...] = tall_ref[...].T.astype(jnp.bfloat16)


def attend(pair, packed, slots, first, last, starts, heads_in, block_q, block_k, held):
    count, width = packed.shape
    pairs = width // 3 // LANES
    whole = pl.BlockSpec(memory_space=pl.ANY)
    return pl.pallas_call(
        partial(attend_kernel, block_q, block_k, heads_in),
        out_shape=(
            jax.ShapeDtypeStruct((count, pairs * LANES), jnp.bfloat16),
            jax.ShapeDtypeStruct((pairs * LANES, count), jnp.float32),
            jax.ShapeDtypeStruct((pairs, 8, count), jnp.float32),
        ),
        grid_spec=pltpu.PrefetchScalarGridSpec(
            num_scalar_prefetch=3,
            grid=(count // block_q,),
            in_specs=[
                pl.BlockSpec((1, block_q), lambda i, slots_ref, *_: (0, slots_ref[i])),
                pl.BlockSpec((block_q, LANES), lambda i, slots_ref, *_: (slots_ref[i], 3 * pair)),
                pl.BlockSpec((count, LANES), lambda i, *_: (0, 3 * pair + 1)),
                pl.BlockSpec((count, LANES), lambda i, *_: (0, 3 * pair + 2)),
            ]
            + [whole] * len(held),
            out_specs=(
                pl.BlockSpec((block_q, LANES), lambda i, slots_ref, *_: (slots_ref[i], pair)),
                pl.BlockSpec((LANES, block_q), lambda i, slots_ref, *_: (pair, slots_ref[i])),
                pl.BlockSpec((1, 8, block_q), lambda i, slots_ref, *_: (pair, 0, slots_ref[i])),
            ),
            scratch_shapes=[
                pltpu.VMEM((LANES, count), jnp.bfloat16),
                pltpu.VMEM((8, block_q), jnp.float32),
                pltpu.VMEM((8, block_q), jnp.float32),
                pltpu.VMEM((LANES, block_q), jnp.float32),
            ],
        ),
        input_output_aliases={7 + k: k for k in range(len(held))},
        cost_estimate=short,
        name="attend",
    )(slots, first, last, starts.reshape(1, count), packed, packed, packed, *held)


def attend_back_kernel(
    block_q,
    block_k,
    heads_in,
    slots_ref,
    last_ref,
    end_ref,
    start_ref,
    cos_ref,
    sin_ref,
    query_ref,
    key_ref,
    value_ref,
    tall_ref,
    log_ref,
    grad_ref,
    out_ref,
    turned,
    masked_q,
    masked_g,
    delta,
    tall_q,
    key_sum,
    value_sum,
):
    index = pl.program_id(1)
    count = query_ref.shape[0]

    def turn_back(field, rows):
        return field * cos_ref[rows, :] - partner(field) * sin_ref[rows, :]

    @pl.when(index == 0)
    def _():
        def prepare(j, carry):
            rows = pl.ds(pl.multiple_of(j * block_k, block_k), block_k)
            turned[:, rows] = key_ref[rows, :].astype(jnp.float32).T.astype(jnp.bfloat16)
            grads = grad_ref[rows, :]
            product = grads.astype(jnp.float32).T * tall_ref[:, rows]
            for head in range(heads_in):
                masked_q[head, rows, :] = head_lanes(query_ref[rows, :], head)
                masked_g[head, rows, :] = head_lanes(grads, head)
                delta[head : head + 1, rows] = jnp.sum(
                    product[head * HEAD : (head + 1) * HEAD, :], axis=0, keepdims=True
                )
            tall_q[:, rows] = jnp.zeros((LANES, block_k), jnp.float32)
            return carry

        lax.fori_loop(0, count // block_k, prepare, 0)

    key_first = index * block_k
    key_rows = pl.ds(pl.multiple_of(slots_ref[index] * block_k, block_k), block_k)
    keys = key_ref[key_rows, :]
    values = value_ref[key_rows, :]
    key_sum[...] = jnp.zeros_like(key_sum)
    value_sum[...] = jnp.zeros_like(value_sum)

    def visit(i, masked):
        query_first = i * block_q
        rows = pl.ds(pl.multiple_of(slots_ref[i] * block_q, block_q), block_q)
        if masked:
            allowed = pair_allowed(
                start_ref[0:1, rows], key_first, block_k, query_first, block_q
            )
        for head in range(heads_in):
            queries = masked_q[head, rows, :]
            grads = masked_g[head, rows, :]
            scores = dot_last(keys, queries)
            probs = jnp.exp(scores - log_ref[0, head : head + 1, rows])
            if masked:
                probs = jnp.where(allowed, probs, 0.0)
            value_sum[...] += dot_plain(probs.astype(jnp.bfloat16), grads)
            prob_grad = dot_last(values, grads)
            score_grad = (probs * (prob_grad - delta[head : head + 1, rows])).astype(jnp.bfloat16)
            key_sum[...] += dot_plain(score_grad, queries)
            lanes = slice(head * HEAD, (head + 1) * HEAD)
            tall_q[lanes, rows] += dot_plain(turned[lanes, key_rows], score_grad)

    def step(i, carry):
        whole = (key_first >= last_ref[i]) & (key_first + block_k - 1 <= i * block_q)

        @pl.when(whole)
        def _():
            visit(i, False)

        @pl.when(jnp.logical_not(whole))
        def _():
            visit(i, True)

        return carry

    lax.fori_loop(key_first // block_q, (end_ref[index] - 1) // block_q + 1, step, 0)
    out_ref[key_rows, LANES : 2 * LANES] = turn_back(key_sum[...], key_rows).astype(jnp.bfloat16)
    out_ref[key_rows, 2 * LANES :] = value_sum[...].astype(jnp.bfloat16)

    @pl.when(index == pl.num_programs(1) - 1)
    def _():
        def finish(j, carry):
            rows = pl.ds(pl.multiple_of(j * block_k, block_k), block_k)
            field = tall_q[:, rows].T * HEAD ** (-0.5)
            out_ref[rows, :LANES] = turn_back(field, rows).astype(jnp.bfloat16)
            return carry

        lax.fori_loop(0, count // block_k, finish, 0)


def attend_back(
    packed, slots, last, end, starts, cosine, sine, tall, logs, grads, heads_in, block_q, block_k
):
    count, width = packed.shape
    pairs = width // 3 // LANES
    return pl.pallas_call(
        partial(attend_back_kernel, block_q, block_k, heads_in),
        out_shape=jax.ShapeDtypeStruct((count, width), jnp.bfloat16),
        grid_spec=pltpu.PrefetchScalarGridSpec(
            num_scalar_prefetch=3,
            grid=(pairs, count // block_k),
            in_specs=[
                pl.BlockSpec((1, count), lambda p, i, *_: (0, 0)),
                pl.BlockSpec((count, LANES), lambda p, i, *_: (0, 0)),
                pl.BlockSpec((count, LANES), lambda p, i, *_: (0, 0)),
                pl.BlockSpec((count, LANES), lambda p, i, *_: (0, 3 * p)),
                pl.BlockSpec((count, LANES), lambda p, i, *_: (0, 3 * p + 1)),
                pl.BlockSpec((count, LANES), lambda p, i, *_: (0, 3 * p + 2)),
                pl.BlockSpec((LANES, count), lambda p, i, *_: (p, 0)),
                pl.BlockSpec((1, 8, count), lambda p, i, *_: (p, 0, 0)),
                pl.BlockSpec((count, LANES), lambda p, i, *_: (0, p)),
            ],
            out_specs=pl.BlockSpec((count, 3 * LANES), lambda p, i, *_: (0, p)),
            scratch_shapes=[
                pltpu.VMEM((LANES, count), jnp.bfloat16),
                pltpu.VMEM((heads_in, count, LANES), jnp.bfloat16),
                pltpu.VMEM((heads_in, count, LANES), jnp.bfloat16),
                pltpu.VMEM((8, count), jnp.float32),
                pltpu.VMEM((LANES, count), jnp.float32),
                pltpu.VMEM((block_k, LANES), jnp.float32),
                pltpu.VMEM((block_k, LANES), jnp.float32),
            ],
        ),
        compiler_params=pltpu.CompilerParams(vmem_limit_bytes=60 << 20),
        cost_estimate=short,
        name="attend_back",
    )(
        slots, last, end, starts.reshape(1, count), cosine, sine,
        packed, packed, packed, tall, logs, grads,
    )


def finish_kernel(narrow_count, wide_count, own_units, per_shard, entries, *refs):
    exchange = own_units > 0
    if exchange:
        (
            parts_ref, piece_ref, feed_ref, total_ref, stats_ref, block_ref, mine, near, far, near_sum,
            send_near, recv_near, send_far, recv_far, send_piece, recv_piece,
        ) = refs
    else:
        (
            parts_ref, piece_ref, feed_ref, total_ref, stats_ref, mine, near, far, near_sum,
            send_near, recv_near, send_far, recv_far,
        ) = refs
    narrow_me = lax.axis_index("narrow")
    wide_me = lax.axis_index("wide")

    def place(narrow_at, wide_at):
        return {"narrow": narrow_at, "wide": wide_at}

    def square_sum(value):
        value = value.astype(jnp.float32)
        return jnp.sum(
            jnp.sum(value * value, axis=0, keepdims=True), axis=1, keepdims=True
        )

    norm_rows = 2 * D // LANES
    row_at = lax.broadcasted_iota(jnp.int32, mine.shape, 0)
    lane_at = lax.broadcasted_iota(jnp.int32, mine.shape, 1)
    mine[...] = parts_ref[...] + jnp.where(
        (row_at == norm_rows) & (lane_at == 0),
        square_sum(piece_ref[...]) + square_sum(feed_ref[...]),
        0.0,
    )
    mesh_ids = pl.DeviceIdType.MESH
    barrier = pltpu.get_barrier_semaphore()
    greeted = 0
    for ahead in range(narrow_count):
        for across in range(wide_count):
            if (ahead > 0) + (across > 0) == 0 or (not exchange and ahead > 0 and across > 0):
                continue
            greeted += 1
            pl.semaphore_signal(
                barrier,
                inc=1,
                device_id=place(
                    lax.rem(narrow_me + ahead, narrow_count), lax.rem(wide_me + across, wide_count)
                ),
                device_id_type=mesh_ids,
            )
    pl.semaphore_wait(barrier, greeted)
    near_copies = []
    for ahead in range(1, narrow_count):
        copy = pltpu.make_async_remote_copy(
            src_ref=mine,
            dst_ref=near.at[narrow_me],
            send_sem=send_near.at[ahead - 1],
            recv_sem=recv_near.at[ahead - 1],
            device_id=place(lax.rem(narrow_me + ahead, narrow_count), wide_me),
            device_id_type=mesh_ids,
        )
        copy.start()
        near_copies.append(copy)
    near[narrow_me] = mine[...]
    if exchange:
        rows = piece_ref.shape[0]
        halves = block_ref.shape[0] // rows
        half_me = lax.rem(wide_me, halves)
        narrow_to = lax.div(wide_me, halves)
        moves = []
        for unit in range(3 * own_units):
            whole_unit = (unit % 3) * (D // LANES) + narrow_me * own_units + unit // 3
            wide_to = lax.div(whole_unit, per_shard)
            column = lax.rem(whole_unit, per_shard)
            source = piece_ref.at[:, unit * LANES : (unit + 1) * LANES]
            target = block_ref.at[
                pl.ds(pl.multiple_of(half_me * rows, rows), rows),
                pl.ds(pl.multiple_of(column * LANES, LANES), LANES),
            ]
            arrived = recv_piece.at[half_me * per_shard + column]
            remote = pltpu.make_async_remote_copy(
                src_ref=source,
                dst_ref=target,
                send_sem=send_piece.at[unit],
                recv_sem=arrived,
                device_id=place(narrow_to, wide_to),
                device_id_type=mesh_ids,
            )
            here = pltpu.make_async_copy(source, target, arrived)
            stays = (narrow_to == narrow_me) & (wide_to == wide_me)
            pl.when(jnp.logical_not(stays))(remote.start)
            pl.when(stays)(here.start)
            moves.append((stays, remote))
    for copy in near_copies:
        copy.wait()
    value = near[0]
    for k in range(1, narrow_count):
        value = value + near[k]
    near_sum[...] = value
    far_copies = []
    for across in range(1, wide_count):
        copy = pltpu.make_async_remote_copy(
            src_ref=near_sum,
            dst_ref=far.at[wide_me],
            send_sem=send_far.at[across - 1],
            recv_sem=recv_far.at[across - 1],
            device_id=place(narrow_me, lax.rem(wide_me + across, wide_count)),
            device_id_type=mesh_ids,
        )
        copy.start()
        far_copies.append(copy)
    far[wide_me] = value
    for copy in far_copies:
        copy.wait()
    value = far[0]
    for k in range(1, wide_count):
        value = value + far[k]
    total_ref[...] = value
    grad_norm = jnp.sqrt(square_sum(value[:norm_rows]) + value[norm_rows : norm_rows + 1, 0:1])
    stats = [jnp.minimum(1.0, math.sqrt(NPARAMS) / grad_norm), grad_norm] + [
        jnp.sqrt(value[norm_rows : norm_rows + 1, k : k + 1] / entries) for k in (1, 2, 3)
    ]
    stats_ref[...] = jnp.zeros_like(stats_ref)
    for row, stat in enumerate(stats):
        stats_ref[row : row + 1, :] = jnp.broadcast_to(stat, (1, LANES))
    if exchange:
        for stays, remote in moves:
            pl.when(jnp.logical_not(stays))(remote.wait_send)
        for half in range(halves):
            for column in range(per_shard):
                pltpu.make_async_copy(
                    piece_ref.at[:, 0:LANES],
                    block_ref.at[
                        half * rows : (half + 1) * rows, column * LANES : (column + 1) * LANES
                    ],
                    recv_piece.at[half * per_shard + column],
                ).wait()


def finish(
    parts, piece, feed_piece, exchange, narrow_count, wide_count, own_width, proj_cols, entries
):
    shape = parts.shape
    own_units = own_width // LANES if exchange else 0
    per_shard = proj_cols // LANES
    vmem = pl.BlockSpec(memory_space=pltpu.VMEM)
    shapes = [
        jax.ShapeDtypeStruct(shape, jnp.float32),
        jax.ShapeDtypeStruct((8, LANES), jnp.float32),
    ]
    scratch = [
        pltpu.VMEM(shape, jnp.float32),
        pltpu.VMEM((narrow_count,) + shape, jnp.float32),
        pltpu.VMEM((wide_count,) + shape, jnp.float32),
        pltpu.VMEM(shape, jnp.float32),
        pltpu.SemaphoreType.DMA((narrow_count - 1,)),
        pltpu.SemaphoreType.DMA((narrow_count - 1,)),
        pltpu.SemaphoreType.DMA((wide_count - 1,)),
        pltpu.SemaphoreType.DMA((wide_count - 1,)),
    ]
    if exchange:
        shapes.append(jax.ShapeDtypeStruct((D // narrow_count, proj_cols), jnp.bfloat16))
        scratch += [
            pltpu.SemaphoreType.DMA((3 * own_units,)),
            pltpu.SemaphoreType.DMA((3 * own_units,)),
        ]
    return pl.pallas_call(
        partial(finish_kernel, narrow_count, wide_count, own_units, per_shard, entries),
        out_shape=tuple(shapes),
        in_specs=[vmem] * 3,
        out_specs=(vmem,) * len(shapes),
        scratch_shapes=scratch,
        compiler_params=pltpu.CompilerParams(collective_id=0, has_side_effects=True),
        name="finish",
    )(parts, piece, feed_piece)


def adam_update(
    weight, first_moment, second_moment, grad_value, step_rate, decay_coef, first_fix, second_fix
):
    new_first = beta_first * first_moment + (1.0 - beta_first) * grad_value
    new_second = beta_second * second_moment + (1.0 - beta_second) * grad_value * grad_value
    step_ratio = new_first / first_fix / (jnp.sqrt(new_second / second_fix) + adam_eps)
    return (weight - step_rate * (step_ratio + decay_coef * weight), new_first, new_second)


def adam_step(weight, first_moment, second_moment, gradient, step_rate, decay_coef, scales):
    new_first = beta_first * first_moment + (1.0 - beta_first) * gradient
    new_second = beta_second * second_moment + (1.0 - beta_second) * gradient * gradient
    ratio = new_first * scales[0] / (jnp.sqrt(new_second * scales[1]) + adam_eps)
    return (weight - step_rate * (ratio + decay_coef * weight), new_first, new_second)


def adam_kernel(scale_ref, stats_ref, grads_ref, total_ref, proj_ref, merge_ref, *refs):
    states, outs = refs[:15], refs[15:-1]
    norm_grads = refs[-1]
    matrix_step, norm_step = scale_ref[0, 0], scale_ref[0, 1]
    scales = (scale_ref[0, 2], scale_ref[0, 3])
    clip_factor = stats_ref[0:1, 0:1]

    def update(matrix, gradient, step_rate, decay_coef):
        state = [ref[...] for ref in states[3 * matrix : 3 * matrix + 3]]
        new = adam_step(*state, gradient * clip_factor, step_rate, decay_coef, scales)
        for out_ref, value in zip(outs[4 * matrix : 4 * matrix + 3], new):
            out_ref[...] = value
        return new[0]

    for matrix in range(2):
        gradient = grads_ref[0, matrix].astype(jnp.float32)
        weight = update(matrix, gradient, matrix_step, decay_rate)
        outs[4 * matrix + 3][...] = weight.astype(jnp.bfloat16)

    @pl.when(pl.program_id(0) == 0)
    def _():
        for matrix, gradient in (
            (2, proj_ref[...].astype(jnp.float32)),
            (3, merge_ref[...].astype(jnp.float32).T),
        ):
            weight = update(matrix, gradient, matrix_step, decay_rate)
            outs[4 * matrix + 3][...] = weight.astype(jnp.bfloat16)
        per_row = D // LANES
        for k in range(2 * per_row):
            at = k % per_row
            norm_grads[k // per_row : k // per_row + 1, at * LANES : (at + 1) * LANES] = total_ref[
                k : k + 1, :
            ]
        update(4, norm_grads[...], norm_step, 0.0)
        outs[19][...] = norm_grads[...] * clip_factor


def adam_all(scales, stats, grads_all, total, proj_block, heads_part, own_width, states):
    count, matrices, rows, cols = grads_all.shape
    block = pl.BlockSpec((rows, cols), lambda i: (i, 0))

    def same(array):
        return pl.BlockSpec(array.shape, lambda i: (0, 0))

    feed_out = jax.ShapeDtypeStruct((count * rows, cols), jnp.float32)
    feed_copy = jax.ShapeDtypeStruct((count * rows, cols), jnp.bfloat16)
    shapes = [feed_out, feed_out, feed_out, feed_copy] * 2
    specs = [block] * 8
    for state in states[6::3]:
        full = jax.ShapeDtypeStruct(state.shape, jnp.float32)
        copy = jax.ShapeDtypeStruct(
            state.shape, jnp.float32 if state is states[12] else jnp.bfloat16
        )
        shapes += [full, full, full, copy]
        specs += [same(state)] * 4
    return pl.pallas_call(
        adam_kernel,
        out_shape=tuple(shapes),
        grid=(count,),
        in_specs=[
            pl.BlockSpec(memory_space=pltpu.SMEM),
            same(stats),
            pl.BlockSpec((1, matrices, rows, cols), lambda i: (i, 0, 0, 0)),
            same(total),
            same(proj_block),
            pl.BlockSpec((heads_part.shape[0], own_width), lambda i: (0, 3)),
        ]
        + [block] * 6
        + [same(state) for state in states[6:]],
        out_specs=tuple(specs),
        scratch_shapes=[pltpu.VMEM((2, D), jnp.float32)],
        cost_estimate=short,
        name="adam_all",
    )(scales, stats, grads_all, total, proj_block, heads_part, *states)


def shards(
    tokens,
    cotangent,
    seq_lengths,
    step_count,
    norm_params,
    norm_first,
    norm_second,
    proj_weight,
    proj_first,
    proj_second,
    merge_weight,
    merge_first,
    merge_second,
    up_weight,
    up_first,
    up_second,
    down_weight,
    down_first,
    down_second,
):
    tok_rows = tokens.shape[0]
    narrow_count = lax.axis_size("narrow")
    wide_count = lax.axis_size("wide")
    span_index = lax.axis_index("narrow")
    group_rows = tok_rows * narrow_count
    own_width = HEADS // narrow_count * HEAD
    held_width = max(own_width, LANES)
    heads_in = min(own_width, LANES) // HEAD
    shard_rows = D // narrow_count
    proj_cols = proj_weight.shape[1]
    lengths = seq_lengths[0]
    onward = [(i, (i + 1) % narrow_count) for i in range(narrow_count)]
    slots = lax.rem(
        span_index + narrow_count - jnp.arange(narrow_count, dtype=jnp.int32), narrow_count
    )

    def pad_lanes(array, axis):
        extra = [(0, 0)] * array.ndim
        extra[axis] = (0, held_width - own_width)
        return jnp.pad(array, extra) if held_width > own_width else array

    def meet(*values):
        return lax.optimization_barrier(values)

    def send_on(array):
        return lax.ppermute(array, "narrow", onward)

    def rows_of(array, slot):
        return array[slot * tok_rows : (slot + 1) * tok_rows]

    direct = own_width % LANES == 0 and proj_cols % LANES == 0 and merge_weight.shape[1] == LANES
    weight_part = jnp.concatenate(
        [proj_weight.astype(jnp.bfloat16), merge_weight.astype(jnp.bfloat16)], axis=1
    )
    weight_rows = lax.all_gather(weight_part, "narrow", axis=0, tiled=True)
    up_slice = up_weight.astype(jnp.bfloat16)
    down_slice = down_weight.astype(jnp.bfloat16)

    def wide_all(array):
        return lax.all_gather(array, "wide", axis=0).reshape(
            wide_count, narrow_count, shard_rows, -1
        )

    def down_term(rows, slot):
        return dot_plain(rows_of(rows, slot), down_slice)

    order = list(range(1, narrow_count)) + [0]
    pairs = held_width // LANES
    token_blocks = [tokens]
    held = ()
    for slot in range(narrow_count - 1):
        moving = send_on(token_blocks[slot])
        held = feed(slot, narrow_count, token_blocks[slot], norm_params, up_slice, held)
        moving, held = meet(moving, held)
        if slot == 0:
            lengths, slots, moving, weight_rows = meet(lengths, slots, moving, weight_rows)
            proj_all = wide_all(weight_rows[:, :proj_cols])
            merge_all = wide_all(weight_rows[:, proj_cols:])
        if slot == 1:
            places = (
                slots[:, None] * tok_rows + jnp.arange(tok_rows, dtype=jnp.int32)[None, :]
            ).reshape(group_rows)
            seq_start, unused = locate(lengths, places)
            cosine, sine = rotary_tables(places - seq_start)
            block_first = jnp.arange(narrow_count, dtype=jnp.int32) * tok_rows
            first_start, unused = locate(lengths, block_first)
            last_start, last_end = locate(lengths, block_first + (tok_rows - 1))
            moving, cosine, sine, first_start, last_start, last_end = meet(
                moving, cosine, sine, first_start, last_start, last_end
            )
        elif slot == 2:
            first_term = down_term(held[1], 1).astype(jnp.bfloat16)
            next_term = down_term(held[1], order[1])
            moving, held, down_slice, first_term, next_term = meet(
                moving, held, down_slice, first_term, next_term
            )
        token_blocks.append(moving)
    grad_first, last_block = meet(cotangent, token_blocks[-1])
    token_blocks[-1] = last_block
    grad_blocks = [grad_first]

    moving = send_on(grad_first)
    gathered, activated, slope = feed(
        narrow_count - 1, narrow_count, last_block, norm_params, up_slice, held
    )
    if direct:
        packed, proj_own = project_all(
            gathered, proj_all, span_index, own_width, cosine, sine
        )
        merge_own = merge_all
    else:
        proj_copy = jnp.transpose(proj_all, (1, 2, 0, 3)).reshape(
            D, 3, narrow_count, own_width
        )
        proj_own = pad_lanes(
            lax.dynamic_index_in_dim(proj_copy, span_index, axis=2, keepdims=False), 2
        ).reshape(D, 3 * held_width)
        merge_copy = jnp.transpose(merge_all, (1, 2, 0, 3)).reshape(
            narrow_count, own_width, D
        )
        merge_own = pad_lanes(
            lax.dynamic_index_in_dim(merge_copy, span_index, axis=0, keepdims=False), 0
        )
        packed = project(gathered, proj_own, cosine, sine)

    def push_slot(slot, push_held):
        return push(
            slot, narrow_count, grad_blocks[slot], slope, down_slice, merge_own, span_index,
            push_held,
        )

    push_held = push_slot(0, ())
    moving, packed, activated, slope, push_held = meet(
        moving, packed, activated, slope, push_held
    )
    grad_blocks.append(moving)

    def wide_sum(grad):
        return lax.psum_scatter(grad, "wide", scatter_dimension=0, tiled=True)

    def attend_pair(pair, attended_held):
        return attend(
            pair, packed, slots, first_start, last_start, seq_start,
            heads_in, tok_rows, tok_rows, attended_held,
        )

    attended_held = ()
    for hop in range(2, narrow_count):
        moving = send_on(grad_blocks[-1])
        if hop - 2 < pairs:
            attended_held = attend_pair(hop - 2, attended_held)
        push_held = push_slot(hop - 1, push_held)
        moving, attended_held, push_held = meet(moving, attended_held, push_held)
        grad_blocks.append(moving)
    for pair in range(narrow_count - 2, pairs):
        attended_held = attend_pair(pair, attended_held)
    attended, tall, logs = attended_held

    moving = send_on(first_term)
    push_held = push_slot(narrow_count - 1, push_held)
    grads_all, hidden_grad, attended_grad = push_held
    part_rows = D // wide_count
    down_grad = dot_first(activated, grads_all).astype(jnp.bfloat16)
    up_grad = dot_first(gathered, hidden_grad).astype(jnp.bfloat16)
    pieces = [
        rows_of(attended, (narrow_count - ahead) % narrow_count)[:, :own_width]
        for ahead in range(narrow_count)
    ]
    moving, pieces, up_grad, down_grad, attended_grad = meet(
        moving, pieces, up_grad, down_grad, attended_grad
    )
    feed_grad = jnp.concatenate(
        [
            up_grad.reshape(wide_count, part_rows, -1),
            down_grad.reshape(wide_count, part_rows, -1),
        ],
        axis=1,
    ).reshape(2 * D, -1)
    feed_part = wide_sum(feed_grad)

    def heads_back():
        mixed = attend_back(
            packed, slots, last_start, last_end, seq_start, cosine, sine,
            tall, logs, attended_grad, heads_in, tok_rows, tok_rows,
        )
        proj_grad = dot_first(gathered, mixed).astype(jnp.bfloat16)
        merge_grad = dot_first(grads_all, attended).astype(jnp.bfloat16)
        if not direct:
            proj_grad = proj_grad.reshape(D, 3, held_width)[:, :, :own_width].reshape(D, -1)
            merge_grad = merge_grad[:, :own_width]
        return (mixed, jnp.concatenate([proj_grad, merge_grad], axis=1))

    for ahead in range(1, narrow_count):
        pieces[ahead] = lax.ppermute(
            pieces[ahead],
            "narrow",
            [(i, (i + ahead) % narrow_count) for i in range(narrow_count)],
        )
    terms = []
    norm_part = jnp.zeros((2, D), jnp.float32)

    def pull_more(count, mixed, norm_part):
        for slot in order[len(terms) : len(terms) + count]:
            term, sums = pull(slot, mixed, hidden_grad, proj_own, up_slice, token_blocks[slot])
            terms.append(term)
            norm_part = norm_part + sums
        return norm_part

    for place, slot in enumerate(order[1:-1]):
        moving = send_on((moving.astype(jnp.float32) + next_term).astype(jnp.bfloat16))
        next_term = down_term(activated, order[place + 2])
        if place == 0:
            mixed_grad, heads_grad = heads_back()
            moving, pieces, mixed_grad, heads_grad, next_term = meet(
                moving, pieces, mixed_grad, heads_grad, next_term
            )
            heads_part = wide_sum(heads_grad)
        else:
            norm_part = pull_more(3, mixed_grad, norm_part)
            moving, terms, norm_part, next_term = meet(moving, terms, norm_part, next_term)
        if slot == narrow_count - 1:
            moving, feed_part, merge_all, slots = meet(moving, feed_part, merge_all, slots)
    norm_part = pull_more(narrow_count, mixed_grad, norm_part)
    feed_all = lax.all_gather(feed_part, "wide", axis=0).reshape(
        wide_count, 2, part_rows, -1
    )

    branch_moving = moving
    moving = send_on(terms[0].astype(jnp.bfloat16))
    branch = branch_moving.astype(jnp.float32) + next_term
    if direct:
        merge_turn = pick_merge(merge_all, slots, own_width)
    else:
        merge_turn = jnp.take(
            jnp.transpose(merge_all, (1, 2, 0, 3)).reshape(narrow_count, own_width, D),
            slots,
            axis=0,
        ).reshape(D, D)
    merged = dot_plain(jnp.concatenate(pieces, axis=1), merge_turn)
    unit_rows, inv_std = normalize(tokens)
    output_rows = tokens.astype(jnp.float32) + merged + branch
    layer_out = output_rows.astype(jnp.bfloat16)

    def squares(array):
        value = array.astype(jnp.float32)
        return jnp.sum(value * value)

    row_squares = [squares(output_rows), squares(merged), squares(branch)]
    scalars = jnp.stack([jnp.zeros((), jnp.float32)] + row_squares)
    parts = jnp.concatenate(
        [norm_part.reshape(2 * D // LANES, LANES), jnp.pad(scalars, (0, LANES - 4))[None, :]]
    )
    parts = jnp.pad(parts, ((0, 7), (0, 0)))
    step_value = step_count[0].astype(jnp.float32)
    first_fix = 1.0 - jnp.power(beta_first, step_value)
    second_fix = 1.0 - jnp.power(beta_second, step_value)
    ramp = jnp.minimum(1.0, step_value / warmup_steps)
    scales = jnp.stack(
        [matrix_rate * ramp, norm_rate * ramp, 1.0 / first_fix, 1.0 / second_fix]
    ).reshape(1, 4)
    entries = wide_count * group_rows * D
    for place in range(1, narrow_count - 1):
        last_but_one = place == narrow_count - 3
        if last_but_one:
            moving, parts, heads_part, scales = meet(moving, parts, heads_part, scales)
        sent = (moving.astype(jnp.float32) + terms[place]).astype(jnp.bfloat16)
        if last_but_one:
            sent, parts = meet(sent, parts)
        elif place == narrow_count - 2:
            sent, summed = meet(sent, summed)
        moving = send_on(sent)
        if last_but_one:
            summed = finish(
                parts, heads_part, feed_part, direct, narrow_count, wide_count, own_width,
                proj_cols, entries,
            )
            moving, summed = meet(moving, summed)

    stats = summed[1]
    if direct:
        total, stats, proj_block = summed
        updated = adam_all(
            scales, stats, feed_all, total, proj_block, heads_part, own_width,
            [
                up_weight, up_first, up_second, down_weight, down_first, down_second,
                proj_weight, proj_first, proj_second, merge_weight, merge_first, merge_second,
                norm_params, norm_first, norm_second,
            ],
        )
    else:
        total, stats = summed
        clip_factor = stats[0, 0:1]
        cross = lax.all_gather(heads_part[:, : 3 * own_width], "narrow", axis=0).reshape(
            narrow_count, part_rows, 3, own_width
        )
        cross = jnp.transpose(cross, (1, 2, 0, 3)).reshape(part_rows, wide_count, proj_cols)
        cross = lax.all_to_all(jnp.transpose(cross, (1, 0, 2)), "wide", 0, 0)
        proj_block = lax.dynamic_slice_in_dim(
            cross.reshape(D, proj_cols), span_index * shard_rows, shard_rows, axis=0
        )
        merge_block = heads_part[:, 3 * own_width :].T
        norm_total = total[: 2 * D // LANES].reshape(2, D)
        feed_sums = feed_all.astype(jnp.float32)
        updated = []
        for state, gradient, step_rate, decay_coef in (
            ((up_weight, up_first, up_second), feed_sums[:, 0], matrix_rate, decay_rate),
            ((down_weight, down_first, down_second), feed_sums[:, 1], matrix_rate, decay_rate),
            ((proj_weight, proj_first, proj_second), proj_block, matrix_rate, decay_rate),
            ((merge_weight, merge_first, merge_second), merge_block, matrix_rate, decay_rate),
            ((norm_params, norm_first, norm_second), norm_total, norm_rate, 0.0),
        ):
            clipped = gradient.reshape(state[0].shape).astype(jnp.float32) * clip_factor
            new = adam_update(
                *state, clipped, step_rate * ramp, decay_coef, first_fix, second_fix
            )
            updated += [*new, clipped if state[0] is norm_params else new[0].astype(jnp.bfloat16)]
    new_up, new_down, new_proj, new_merge, new_norm = [
        updated[4 * k : 4 * k + 4] for k in range(5)
    ]
    moving, new_up = meet(moving, new_up)
    normed_grad = moving.astype(jnp.float32) + terms[-1]
    unit_grad = normed_grad * norm_params[0]
    input_grad = cotangent.astype(jnp.float32) + inv_std * (
        unit_grad
        - jnp.mean(unit_grad, axis=1, keepdims=True)
        - unit_rows * jnp.mean(unit_grad * unit_rows, axis=1, keepdims=True)
    )
    return (
        layer_out,
        input_grad,
        stats[1, 0:1],
        stats[2, 0:1],
        new_norm[3],
        new_norm[0],
        new_norm[1],
        new_norm[2],
        new_proj[0],
        new_proj[1],
        new_proj[2],
        new_merge[0],
        new_merge[1],
        new_merge[2],
        new_up[0],
        new_up[1],
        new_up[2],
        new_down[0],
        new_down[1],
        new_down[2],
        stats[3:5, 0],
        new_proj[3],
        new_merge[3],
        new_up[3],
        new_down[3],
    )


def solution(mesh):
    placed = (
        P(("wide", "narrow"), None),
        P(("wide", "narrow"), None),
        P("wide", None),
        P(),
        P(),
        P(),
        P(),
        P("narrow", "wide"),
        P("narrow", "wide"),
        P("narrow", "wide"),
        P("narrow", "wide"),
        P("narrow", "wide"),
        P("narrow", "wide"),
        P(None, "narrow"),
        P(None, "narrow"),
        P(None, "narrow"),
        P("narrow", None),
        P("narrow", None),
        P("narrow", None),
    )
    return jax.shard_map(
        shards,
        mesh=mesh,
        in_specs=placed,
        out_specs=(
            P(("wide", "narrow"), None),
            P(("wide", "narrow"), None),
            P(),
            P(),
            P(),
            P(),
            P(),
            P(),
            P("narrow", "wide"),
            P("narrow", "wide"),
            P("narrow", "wide"),
            P("narrow", "wide"),
            P("narrow", "wide"),
            P("narrow", "wide"),
            P(None, "narrow"),
            P(None, "narrow"),
            P(None, "narrow"),
            P("narrow", None),
            P("narrow", None),
            P("narrow", None),
            P(),
            P("narrow", "wide"),
            P("narrow", "wide"),
            P(None, "narrow"),
            P("narrow", None),
        ),
        check_vma=False,
    )
```

```python
from functools import partial
import math

import jax
import jax.numpy as jnp
from jax import lax
from jax.experimental import pallas as pl
from jax.experimental.pallas import tpu as pltpu
from jax.sharding import PartitionSpec as P

HEADS = 16
HEAD = 64
D = 1024
ROT = 16
LANES = 128
ROW_BLOCK = 512
NPARAMS = 12584960


norm_eps = 1e-05
adam_eps = 1e-08
beta_first = 0.5
beta_second = 0.5
decay_rate = 0.01
matrix_rate = 0.1
norm_rate = 1.0
warmup_steps = 20.0
masked_score = -1e30
short = pl.CostEstimate(flops=0, bytes_accessed=0, transcendentals=0)


def dot_last(left_side, right_side):
    return lax.dot_general(
        left_side, right_side, (((1,), (1,)), ((), ())), preferred_element_type=jnp.float32
    )


def dot_plain(left_side, right_side):
    return lax.dot_general(
        left_side, right_side, (((1,), (0,)), ((), ())), preferred_element_type=jnp.float32
    )


def dot_first(left_side, right_side):
    return lax.dot_general(
        left_side, right_side, (((0,), (0,)), ((), ())), preferred_element_type=jnp.float32
    )


def locate(lengths, token_index):
    seq_ends = jnp.cumsum(lengths)
    starts = seq_ends - lengths
    segment = jnp.sum(
        (seq_ends[None, :] <= token_index[:, None]).astype(jnp.int32), axis=1, dtype=jnp.int32
    )
    choose = segment[:, None] == jnp.arange(lengths.shape[0], dtype=jnp.int32)[None, :]
    seq_start = jnp.sum(jnp.where(choose, starts[None, :], 0), axis=1, dtype=jnp.int32)
    seq_end = jnp.sum(jnp.where(choose, seq_ends[None, :], 0), axis=1, dtype=jnp.int32)
    return (seq_start, seq_end)


def rotary_tables(position):
    half_rot = ROT // 2
    frequency = jnp.power(10000.0, -2.0 * jnp.arange(half_rot, dtype=jnp.float32) / ROT)
    row = jnp.concatenate([frequency, frequency, jnp.zeros((HEAD - ROT,), jnp.float32)])
    row = jnp.tile(row, LANES // HEAD)
    sign = jnp.where(jnp.arange(LANES) % HEAD < half_rot, -1.0, 1.0)
    phases = position.astype(jnp.float32)[:, None] * row[None, :]
    return (jnp.cos(phases), jnp.sin(phases) * sign[None, :])


def partner(field):
    half_rot = ROT // 2
    lane = lax.broadcasted_iota(jnp.int32, field.shape, 1) % HEAD
    return jnp.where(
        lane < half_rot,
        pltpu.roll(field, LANES - half_rot, 1),
        pltpu.roll(field, half_rot, 1),
    )


def project_kernel(rows_ref, weight_ref, cos_ref, sin_ref, out_ref):
    width = out_ref.shape[1]
    projected = dot_plain(rows_ref[...], weight_ref[...])
    for first in range(0, width, LANES):
        piece = projected[:, first : first + LANES]
        part = first // LANES % 3
        if part < 2:
            piece = piece * cos_ref[...] + partner(piece) * sin_ref[...]
        if part == 0:
            piece = piece * HEAD ** (-0.5)
        out_ref[:, first : first + LANES] = piece.astype(jnp.bfloat16)


def project(rows, weight, cosine, sine):
    count, depth = rows.shape
    width = weight.shape[1]
    block = min(ROW_BLOCK, count)
    return pl.pallas_call(
        project_kernel,
        out_shape=jax.ShapeDtypeStruct((count, width), jnp.bfloat16),
        grid=(count // block,),
        in_specs=[
            pl.BlockSpec((block, depth), lambda i: (i, 0)),
            pl.BlockSpec((depth, width), lambda i: (0, 0)),
            pl.BlockSpec((block, LANES), lambda i: (i, 0)),
            pl.BlockSpec((block, LANES), lambda i: (i, 0)),
        ],
        out_specs=pl.BlockSpec((block, width), lambda i: (i, 0)),
        cost_estimate=short,
        name="project",
    )(rows, weight, cosine, sine)


def normalize(tokens):
    residual = tokens.astype(jnp.float32)
    center = residual - jnp.mean(residual, axis=1, keepdims=True)
    inv_std = lax.rsqrt(jnp.mean(center * center, axis=1, keepdims=True) + norm_eps)
    return (center * inv_std, inv_std)


def feed_kernel(tokens_ref, params_ref, weight_ref, *refs):
    normed_ref, act_ref, slope_ref = refs[-3:]
    unit, unused = normalize(tokens_ref[...])
    normed_ref[...] = (unit * params_ref[0:1, :] + params_ref[1:2, :]).astype(jnp.bfloat16)
    width = act_ref.shape[1]
    step = min(256, width)
    for first in range(0, width, step):
        hidden = dot_plain(normed_ref[...], weight_ref[:, first : first + step])
        share = 0.5 + 0.5 * lax.erf(hidden * math.sqrt(0.5))
        bell = jnp.exp(hidden * hidden * -0.5) * (1.0 / math.sqrt(2.0 * math.pi))
        act_ref[:, first : first + step] = (hidden * share).astype(jnp.bfloat16)
        slope_ref[:, first : first + step] = share + hidden * bell


def feed(slot, slots, tokens, params, weight, held):
    rows, depth = tokens.shape
    width = weight.shape[1]
    whole = pl.BlockSpec(memory_space=pl.ANY)
    return pl.pallas_call(
        feed_kernel,
        out_shape=(
            jax.ShapeDtypeStruct((slots * rows, depth), jnp.bfloat16),
            jax.ShapeDtypeStruct((slots * rows, width), jnp.bfloat16),
            jax.ShapeDtypeStruct((slots * rows, width), jnp.float32),
        ),
        grid=(2,),
        in_specs=[
            pl.BlockSpec((rows // 2, depth), lambda i: (i, 0)),
            pl.BlockSpec((2, depth), lambda i: (0, 0)),
            pl.BlockSpec((depth, width), lambda i: (0, 0)),
        ]
        + [whole] * len(held),
        out_specs=(
            pl.BlockSpec((rows // 2, depth), lambda i: (2 * slot + i, 0)),
            pl.BlockSpec((rows // 2, width), lambda i: (2 * slot + i, 0)),
            pl.BlockSpec((rows // 2, width), lambda i: (2 * slot + i, 0)),
        ),
        input_output_aliases={3 + k: k for k in range(len(held))},
        cost_estimate=short,
        name="feed",
    )(tokens, params, weight, *held)


def push_kernel(index_ref, grad_ref, slope_ref, down_ref, merge_ref, *refs):
    all_ref, hidden_ref, attended_ref, merge_own = refs[-4:]

    @pl.when(pl.program_id(0) == 0)
    def _():
        if len(merge_ref.shape) == 4:
            for w in range(merge_ref.shape[0]):
                merge_own[:, w * LANES : (w + 1) * LANES] = merge_ref[w, 0]
        else:
            merge_own[...] = merge_ref[...]

    grads = grad_ref[...]
    all_ref[...] = grads
    hidden_ref[...] = (dot_last(grads, down_ref[...]) * slope_ref[...]).astype(jnp.bfloat16)
    attended_ref[...] = dot_last(grads, merge_own[...]).astype(jnp.bfloat16)


def push(slot, slots, grads, slope, down, merge, span_index, held):
    rows, depth = grads.shape
    width = slope.shape[1]
    half = rows // 2
    whole = pl.BlockSpec(memory_space=pl.ANY)
    if merge.ndim == 4:
        own = merge.shape[2]
        merge_spec = pl.BlockSpec(
            (merge.shape[0], 1, own, LANES), lambda i, index_ref: (0, index_ref[0], 0, 0)
        )
    else:
        own = merge.shape[0]
        merge_spec = pl.BlockSpec(merge.shape, lambda i, index_ref: (0, 0))

    def place(i, index_ref):
        return (2 * slot + i, 0)

    return pl.pallas_call(
        push_kernel,
        out_shape=(
            jax.ShapeDtypeStruct((slots * rows, depth), jnp.bfloat16),
            jax.ShapeDtypeStruct((slots * rows, width), jnp.bfloat16),
            jax.ShapeDtypeStruct((slots * rows, own), jnp.bfloat16),
        ),
        grid_spec=pltpu.PrefetchScalarGridSpec(
            num_scalar_prefetch=1,
            grid=(2,),
            in_specs=[
                pl.BlockSpec((half, depth), lambda i, index_ref: (i, 0)),
                pl.BlockSpec((half, width), place),
                pl.BlockSpec(down.shape, lambda i, index_ref: (0, 0)),
                merge_spec,
            ]
            + [whole] * len(held),
            out_specs=(
                pl.BlockSpec((half, depth), place),
                pl.BlockSpec((half, width), place),
                pl.BlockSpec((half, own), place),
            ),
            scratch_shapes=[pltpu.VMEM((own, depth), jnp.bfloat16)],
        ),
        input_output_aliases={5 + k: k for k in range(len(held))},
        cost_estimate=short,
        name="push",
    )(span_index.reshape(1), grads, slope, down, merge, *held)


def pull_kernel(mixed_ref, hidden_ref, proj_ref, up_ref, tokens_ref, out_ref, sums_ref):
    partial_grad = dot_last(mixed_ref[...], proj_ref[...]) + dot_last(hidden_ref[...], up_ref[...])
    out_ref[...] = partial_grad
    unit, unused = normalize(tokens_ref[...])
    gain = jnp.sum(partial_grad * unit, axis=0, keepdims=True)
    bias = jnp.sum(partial_grad, axis=0, keepdims=True)
    both = jnp.concatenate([gain, bias], axis=0)

    @pl.when(pl.program_id(0) == 0)
    def _():
        sums_ref[...] = both

    @pl.when(pl.program_id(0) > 0)
    def _():
        sums_ref[...] += both


def pull(slot, mixed, hidden_grad, proj, up, tokens):
    rows, depth = tokens.shape
    half = rows // 2
    return pl.pallas_call(
        pull_kernel,
        out_shape=(
            jax.ShapeDtypeStruct((rows, depth), jnp.float32),
            jax.ShapeDtypeStruct((2, depth), jnp.float32),
        ),
        grid=(2,),
        in_specs=[
            pl.BlockSpec((half, mixed.shape[1]), lambda i: (2 * slot + i, 0)),
            pl.BlockSpec((half, hidden_grad.shape[1]), lambda i: (2 * slot + i, 0)),
            pl.BlockSpec(proj.shape, lambda i: (0, 0)),
            pl.BlockSpec(up.shape, lambda i: (0, 0)),
            pl.BlockSpec((half, depth), lambda i: (i, 0)),
        ],
        out_specs=(
            pl.BlockSpec((half, depth), lambda i: (i, 0)),
            pl.BlockSpec((2, depth), lambda i: (0, 0)),
        ),
        cost_estimate=short,
        name="pull",
    )(mixed, hidden_grad, proj, up, tokens)


def project_all_kernel(index_ref, rows_ref, cos_ref, sin_ref, *refs):
    unit_refs, (out_ref, weight_ref) = refs[:-2], refs[-2:]

    @pl.when(pl.program_id(0) == 0)
    def _():
        for c, unit_ref in enumerate(unit_refs):
            weight_ref[:, c * LANES : (c + 1) * LANES] = unit_ref[...].reshape(D, LANES)

    project_kernel(rows_ref, weight_ref, cos_ref, sin_ref, out_ref)


def project_all(rows, weight_all, span_index, own_width, cosine, sine):
    count, depth = rows.shape
    shards, narrow_count, shard_rows, cols = weight_all.shape
    units = own_width // LANES
    width = 3 * own_width
    per_shard = cols // LANES
    per_part = D // LANES
    block = min(ROW_BLOCK, count)

    def source(c, i, index_ref):
        unit = (c % 3) * per_part + index_ref[0] * units + c // 3
        return (unit // per_shard, 0, 0, unit % per_shard)

    return pl.pallas_call(
        project_all_kernel,
        out_shape=(
            jax.ShapeDtypeStruct((count, width), jnp.bfloat16),
            jax.ShapeDtypeStruct((D, width), jnp.bfloat16),
        ),
        grid_spec=pltpu.PrefetchScalarGridSpec(
            num_scalar_prefetch=1,
            grid=(count // block,),
            in_specs=[
                pl.BlockSpec((block, depth), lambda i, index_ref: (i, 0)),
                pl.BlockSpec((block, LANES), lambda i, index_ref: (i, 0)),
                pl.BlockSpec((block, LANES), lambda i, index_ref: (i, 0)),
            ]
            + [
                pl.BlockSpec((1, narrow_count, shard_rows, LANES), partial(source, c))
                for c in range(3 * units)
            ],
            out_specs=(
                pl.BlockSpec((block, width), lambda i, index_ref: (i, 0)),
                pl.BlockSpec((D, width), lambda i, index_ref: (0, 0)),
            ),
        ),
        cost_estimate=short,
        name="project_all",
    )(span_index.reshape(1), rows, cosine, sine, *[weight_all] * (3 * units))


def turn_kernel(slots_ref, all_ref, out_ref):
    unused, narrow_count, rows, cols = all_ref.shape
    for t in range(narrow_count):
        out_ref[t * rows : (t + 1) * rows, :] = all_ref[0, slots_ref[t]]


def pick_merge(weight_all, slots, own_width):
    shards, narrow_count, rows, cols = weight_all.shape
    return pl.pallas_call(
        turn_kernel,
        out_shape=jax.ShapeDtypeStruct((D, D), jnp.bfloat16),
        grid_spec=pltpu.PrefetchScalarGridSpec(
            num_scalar_prefetch=1,
            grid=(shards,),
            in_specs=[
                pl.BlockSpec(
                    (1, narrow_count, rows, LANES),
                    lambda j, slots_ref: (j, 0, 0, 0),
                )
            ],
            out_specs=pl.BlockSpec((D, LANES), lambda j, slots_ref: (0, j)),
        ),
        cost_estimate=short,
        name="pick_merge",
    )(slots, weight_all)


def head_lanes(field, head):
    lane = lax.broadcasted_iota(jnp.int32, field.shape, 1)
    keep = (lane >= head * HEAD) & (lane < (head + 1) * HEAD)
    return jnp.where(keep, field, jnp.zeros_like(field))


def pair_allowed(start_row, key_first, key_count, query_first, query_count):
    key_index = key_first + lax.broadcasted_iota(jnp.int32, (key_count, query_count), 0)
    query_index = query_first + lax.broadcasted_iota(jnp.int32, (key_count, query_count), 1)
    return (key_index >= start_row) & (key_index <= query_index)


def attend_kernel(
    block_q,
    block_k,
    heads_in,
    slots_ref,
    first_ref,
    last_ref,
    start_ref,
    query_ref,
    key_ref,
    value_ref,
    *refs,
):
    out_ref, tall_ref, log_ref, turned, best, total, summed = refs[-7:]
    index = pl.program_id(0)
    key_blocks = key_ref.shape[0] // block_k

    @pl.when(index == 0)
    def _():
        for j in range(key_blocks):
            piece = value_ref[j * block_k : (j + 1) * block_k, :].astype(jnp.float32)
            turned[:, j * block_k : (j + 1) * block_k] = piece.T.astype(jnp.bfloat16)

    query_first = index * block_q
    low = first_ref[index] // block_k
    high = (query_first + block_q - 1) // block_k + 1
    start_row = start_ref[...]
    queries = [head_lanes(query_ref[...], head) for head in range(heads_in)]
    best[...] = jnp.full_like(best, masked_score)
    total[...] = jnp.zeros_like(total)
    summed[...] = jnp.zeros_like(summed)

    def visit(j, masked):
        key_rows = pl.ds(pl.multiple_of(slots_ref[j] * block_k, block_k), block_k)
        keys = key_ref[key_rows, :]
        if masked:
            allowed = pair_allowed(start_row, j * block_k, block_k, query_first, block_q)
        for head in range(heads_in):
            scores = dot_last(keys, queries[head])
            if masked:
                scores = jnp.where(allowed, scores, masked_score)
            old = best[head : head + 1, :]
            new = jnp.maximum(old, jnp.max(scores, axis=0, keepdims=True))
            weights = jnp.exp(scores - new)
            if masked:
                weights = jnp.where(allowed, weights, 0.0)
            factor = jnp.exp(old - new)
            best[head : head + 1, :] = new
            total[head : head + 1, :] = total[head : head + 1, :] * factor + jnp.sum(
                weights, axis=0, keepdims=True
            )
            rows = slice(head * HEAD, (head + 1) * HEAD)
            summed[rows, :] = summed[rows, :] * factor + dot_plain(
                turned[rows, key_rows], weights.astype(jnp.bfloat16)
            )

    def step(j, carry):
        whole = (j * block_k >= last_ref[index]) & ((j + 1) * block_k - 1 <= query_first)

        @pl.when(whole)
        def _():
            visit(j, False)

        @pl.when(jnp.logical_not(whole))
        def _():
            visit(j, True)

        return carry

    lax.fori_loop(low, high, step, 0)
    for head in range(heads_in):
        rows = slice(head * HEAD, (head + 1) * HEAD)
        weight = total[head : head + 1, :]
        tall_ref[rows, :] = summed[rows, :] / weight
        log_ref[0, head : head + 1, :] = best[head : head + 1, :] + jnp.log(weight)
    if heads_in * HEAD < LANES:
        tall_ref[heads_in * HEAD :, :] = jnp.zeros_like(tall_ref[heads_in * HEAD :, :])
    log_ref[0, heads_in:, :] = jnp.zeros_like(log_ref[0, heads_in:, :])
    out_ref[...] = tall_ref[...].T.astype(jnp.bfloat16)


def attend(pair, packed, slots, first, last, starts, heads_in, block_q, block_k, held):
    count, width = packed.shape
    pairs = width // 3 // LANES
    whole = pl.BlockSpec(memory_space=pl.ANY)
    return pl.pallas_call(
        partial(attend_kernel, block_q, block_k, heads_in),
        out_shape=(
            jax.ShapeDtypeStruct((count, pairs * LANES), jnp.bfloat16),
            jax.ShapeDtypeStruct((pairs * LANES, count), jnp.float32),
            jax.ShapeDtypeStruct((pairs, 8, count), jnp.float32),
        ),
        grid_spec=pltpu.PrefetchScalarGridSpec(
            num_scalar_prefetch=3,
            grid=(count // block_q,),
            in_specs=[
                pl.BlockSpec((1, block_q), lambda i, slots_ref, *_: (0, slots_ref[i])),
                pl.BlockSpec((block_q, LANES), lambda i, slots_ref, *_: (slots_ref[i], 3 * pair)),
                pl.BlockSpec((count, LANES), lambda i, *_: (0, 3 * pair + 1)),
                pl.BlockSpec((count, LANES), lambda i, *_: (0, 3 * pair + 2)),
            ]
            + [whole] * len(held),
            out_specs=(
                pl.BlockSpec((block_q, LANES), lambda i, slots_ref, *_: (slots_ref[i], pair)),
                pl.BlockSpec((LANES, block_q), lambda i, slots_ref, *_: (pair, slots_ref[i])),
                pl.BlockSpec((1, 8, block_q), lambda i, slots_ref, *_: (pair, 0, slots_ref[i])),
            ),
            scratch_shapes=[
                pltpu.VMEM((LANES, count), jnp.bfloat16),
                pltpu.VMEM((8, block_q), jnp.float32),
                pltpu.VMEM((8, block_q), jnp.float32),
                pltpu.VMEM((LANES, block_q), jnp.float32),
            ],
        ),
        input_output_aliases={7 + k: k for k in range(len(held))},
        cost_estimate=short,
        name="attend",
    )(slots, first, last, starts.reshape(1, count), packed, packed, packed, *held)


def attend_back_kernel(
    block_q,
    block_k,
    heads_in,
    slots_ref,
    last_ref,
    end_ref,
    start_ref,
    cos_ref,
    sin_ref,
    query_ref,
    key_ref,
    value_ref,
    tall_ref,
    log_ref,
    grad_ref,
    out_ref,
    turned,
    masked_q,
    masked_g,
    delta,
    tall_q,
    key_sum,
    value_sum,
):
    index = pl.program_id(1)
    count = query_ref.shape[0]

    def turn_back(field, rows):
        return field * cos_ref[rows, :] - partner(field) * sin_ref[rows, :]

    @pl.when(index == 0)
    def _():
        def prepare(j, carry):
            rows = pl.ds(pl.multiple_of(j * block_k, block_k), block_k)
            turned[:, rows] = key_ref[rows, :].astype(jnp.float32).T.astype(jnp.bfloat16)
            grads = grad_ref[rows, :]
            product = grads.astype(jnp.float32).T * tall_ref[:, rows]
            for head in range(heads_in):
                masked_q[head, rows, :] = head_lanes(query_ref[rows, :], head)
                masked_g[head, rows, :] = head_lanes(grads, head)
                delta[head : head + 1, rows] = jnp.sum(
                    product[head * HEAD : (head + 1) * HEAD, :], axis=0, keepdims=True
                )
            tall_q[:, rows] = jnp.zeros((LANES, block_k), jnp.float32)
            return carry

        lax.fori_loop(0, count // block_k, prepare, 0)

    key_first = index * block_k
    key_rows = pl.ds(pl.multiple_of(slots_ref[index] * block_k, block_k), block_k)
    keys = key_ref[key_rows, :]
    values = value_ref[key_rows, :]
    key_sum[...] = jnp.zeros_like(key_sum)
    value_sum[...] = jnp.zeros_like(value_sum)

    def visit(i, masked):
        query_first = i * block_q
        rows = pl.ds(pl.multiple_of(slots_ref[i] * block_q, block_q), block_q)
        if masked:
            allowed = pair_allowed(
                start_ref[0:1, rows], key_first, block_k, query_first, block_q
            )
        for head in range(heads_in):
            queries = masked_q[head, rows, :]
            grads = masked_g[head, rows, :]
            scores = dot_last(keys, queries)
            probs = jnp.exp(scores - log_ref[0, head : head + 1, rows])
            if masked:
                probs = jnp.where(allowed, probs, 0.0)
            value_sum[...] += dot_plain(probs.astype(jnp.bfloat16), grads)
            prob_grad = dot_last(values, grads)
            score_grad = (probs * (prob_grad - delta[head : head + 1, rows])).astype(jnp.bfloat16)
            key_sum[...] += dot_plain(score_grad, queries)
            lanes = slice(head * HEAD, (head + 1) * HEAD)
            tall_q[lanes, rows] += dot_plain(turned[lanes, key_rows], score_grad)

    def step(i, carry):
        whole = (key_first >= last_ref[i]) & (key_first + block_k - 1 <= i * block_q)

        @pl.when(whole)
        def _():
            visit(i, False)

        @pl.when(jnp.logical_not(whole))
        def _():
            visit(i, True)

        return carry

    lax.fori_loop(key_first // block_q, (end_ref[index] - 1) // block_q + 1, step, 0)
    out_ref[key_rows, LANES : 2 * LANES] = turn_back(key_sum[...], key_rows).astype(jnp.bfloat16)
    out_ref[key_rows, 2 * LANES :] = value_sum[...].astype(jnp.bfloat16)

    @pl.when(index == pl.num_programs(1) - 1)
    def _():
        def finish(j, carry):
            rows = pl.ds(pl.multiple_of(j * block_k, block_k), block_k)
            field = tall_q[:, rows].T * HEAD ** (-0.5)
            out_ref[rows, :LANES] = turn_back(field, rows).astype(jnp.bfloat16)
            return carry

        lax.fori_loop(0, count // block_k, finish, 0)


def attend_back(
    packed, slots, last, end, starts, cosine, sine, tall, logs, grads, heads_in, block_q, block_k
):
    count, width = packed.shape
    pairs = width // 3 // LANES
    return pl.pallas_call(
        partial(attend_back_kernel, block_q, block_k, heads_in),
        out_shape=jax.ShapeDtypeStruct((count, width), jnp.bfloat16),
        grid_spec=pltpu.PrefetchScalarGridSpec(
            num_scalar_prefetch=3,
            grid=(pairs, count // block_k),
            in_specs=[
                pl.BlockSpec((1, count), lambda p, i, *_: (0, 0)),
                pl.BlockSpec((count, LANES), lambda p, i, *_: (0, 0)),
                pl.BlockSpec((count, LANES), lambda p, i, *_: (0, 0)),
                pl.BlockSpec((count, LANES), lambda p, i, *_: (0, 3 * p)),
                pl.BlockSpec((count, LANES), lambda p, i, *_: (0, 3 * p + 1)),
                pl.BlockSpec((count, LANES), lambda p, i, *_: (0, 3 * p + 2)),
                pl.BlockSpec((LANES, count), lambda p, i, *_: (p, 0)),
                pl.BlockSpec((1, 8, count), lambda p, i, *_: (p, 0, 0)),
                pl.BlockSpec((count, LANES), lambda p, i, *_: (0, p)),
            ],
            out_specs=pl.BlockSpec((count, 3 * LANES), lambda p, i, *_: (0, p)),
            scratch_shapes=[
                pltpu.VMEM((LANES, count), jnp.bfloat16),
                pltpu.VMEM((heads_in, count, LANES), jnp.bfloat16),
                pltpu.VMEM((heads_in, count, LANES), jnp.bfloat16),
                pltpu.VMEM((8, count), jnp.float32),
                pltpu.VMEM((LANES, count), jnp.float32),
                pltpu.VMEM((block_k, LANES), jnp.float32),
                pltpu.VMEM((block_k, LANES), jnp.float32),
            ],
        ),
        compiler_params=pltpu.CompilerParams(vmem_limit_bytes=60 << 20),
        cost_estimate=short,
        name="attend_back",
    )(
        slots, last, end, starts.reshape(1, count), cosine, sine,
        packed, packed, packed, tall, logs, grads,
    )


def finish_kernel(narrow_count, wide_count, own_units, per_shard, entries, *refs):
    exchange = own_units > 0
    if exchange:
        (
            parts_ref, piece_ref, feed_ref, total_ref, stats_ref, block_ref, mine, near, far, near_sum,
            send_near, recv_near, send_far, recv_far, send_piece, recv_piece,
        ) = refs
    else:
        (
            parts_ref, piece_ref, feed_ref, total_ref, stats_ref, mine, near, far, near_sum,
            send_near, recv_near, send_far, recv_far,
        ) = refs
    narrow_me = lax.axis_index("narrow")
    wide_me = lax.axis_index("wide")

    def place(narrow_at, wide_at):
        return {"narrow": narrow_at, "wide": wide_at}

    def square_sum(value):
        value = value.astype(jnp.float32)
        return jnp.sum(
            jnp.sum(value * value, axis=0, keepdims=True), axis=1, keepdims=True
        )

    norm_rows = 2 * D // LANES
    row_at = lax.broadcasted_iota(jnp.int32, mine.shape, 0)
    lane_at = lax.broadcasted_iota(jnp.int32, mine.shape, 1)
    mine[...] = parts_ref[...] + jnp.where(
        (row_at == norm_rows) & (lane_at == 0),
        square_sum(piece_ref[...]) + square_sum(feed_ref[...]),
        0.0,
    )
    mesh_ids = pl.DeviceIdType.MESH
    barrier = pltpu.get_barrier_semaphore()
    greeted = 0
    for ahead in range(narrow_count):
        for across in range(wide_count):
            if (ahead > 0) + (across > 0) == 0 or (not exchange and ahead > 0 and across > 0):
                continue
            greeted += 1
            pl.semaphore_signal(
                barrier,
                inc=1,
                device_id=place(
                    lax.rem(narrow_me + ahead, narrow_count), lax.rem(wide_me + across, wide_count)
                ),
                device_id_type=mesh_ids,
            )
    pl.semaphore_wait(barrier, greeted)
    near_copies = []
    for ahead in range(1, narrow_count):
        copy = pltpu.make_async_remote_copy(
            src_ref=mine,
            dst_ref=near.at[narrow_me],
            send_sem=send_near.at[ahead - 1],
            recv_sem=recv_near.at[ahead - 1],
            device_id=place(lax.rem(narrow_me + ahead, narrow_count), wide_me),
            device_id_type=mesh_ids,
        )
        copy.start()
        near_copies.append(copy)
    near[narrow_me] = mine[...]
    if exchange:
        rows = piece_ref.shape[0]
        halves = block_ref.shape[0] // rows
        half_me = lax.rem(wide_me, halves)
        narrow_to = lax.div(wide_me, halves)
        moves = []
        for unit in range(3 * own_units):
            whole_unit = (unit % 3) * (D // LANES) + narrow_me * own_units + unit // 3
            wide_to = lax.div(whole_unit, per_shard)
            column = lax.rem(whole_unit, per_shard)
            source = piece_ref.at[:, unit * LANES : (unit + 1) * LANES]
            target = block_ref.at[
                pl.ds(pl.multiple_of(half_me * rows, rows), rows),
                pl.ds(pl.multiple_of(column * LANES, LANES), LANES),
            ]
            arrived = recv_piece.at[half_me * per_shard + column]
            remote = pltpu.make_async_remote_copy(
                src_ref=source,
                dst_ref=target,
                send_sem=send_piece.at[unit],
                recv_sem=arrived,
                device_id=place(narrow_to, wide_to),
                device_id_type=mesh_ids,
            )
            here = pltpu.make_async_copy(source, target, arrived)
            stays = (narrow_to == narrow_me) & (wide_to == wide_me)
            pl.when(jnp.logical_not(stays))(remote.start)
            pl.when(stays)(here.start)
            moves.append((stays, remote))
    for copy in near_copies:
        copy.wait()
    value = near[0]
    for k in range(1, narrow_count):
        value = value + near[k]
    near_sum[...] = value
    far_copies = []
    for across in range(1, wide_count):
        copy = pltpu.make_async_remote_copy(
            src_ref=near_sum,
            dst_ref=far.at[wide_me],
            send_sem=send_far.at[across - 1],
            recv_sem=recv_far.at[across - 1],
            device_id=place(narrow_me, lax.rem(wide_me + across, wide_count)),
            device_id_type=mesh_ids,
        )
        copy.start()
        far_copies.append(copy)
    far[wide_me] = value
    for copy in far_copies:
        copy.wait()
    value = far[0]
    for k in range(1, wide_count):
        value = value + far[k]
    total_ref[...] = value
    grad_norm = jnp.sqrt(square_sum(value[:norm_rows]) + value[norm_rows : norm_rows + 1, 0:1])
    stats = [jnp.minimum(1.0, math.sqrt(NPARAMS) / grad_norm), grad_norm] + [
        jnp.sqrt(value[norm_rows : norm_rows + 1, k : k + 1] / entries) for k in (1, 2, 3)
    ]
    stats_ref[...] = jnp.zeros_like(stats_ref)
    for row, stat in enumerate(stats):
        stats_ref[row : row + 1, :] = jnp.broadcast_to(stat, (1, LANES))
    if exchange:
        for stays, remote in moves:
            pl.when(jnp.logical_not(stays))(remote.wait_send)
        for half in range(halves):
            for column in range(per_shard):
                pltpu.make_async_copy(
                    piece_ref.at[:, 0:LANES],
                    block_ref.at[
                        half * rows : (half + 1) * rows, column * LANES : (column + 1) * LANES
                    ],
                    recv_piece.at[half * per_shard + column],
                ).wait()


def finish(
    parts, piece, feed_piece, exchange, narrow_count, wide_count, own_width, proj_cols, entries
):
    shape = parts.shape
    own_units = own_width // LANES if exchange else 0
    per_shard = proj_cols // LANES
    vmem = pl.BlockSpec(memory_space=pltpu.VMEM)
    shapes = [
        jax.ShapeDtypeStruct(shape, jnp.float32),
        jax.ShapeDtypeStruct((8, LANES), jnp.float32),
    ]
    scratch = [
        pltpu.VMEM(shape, jnp.float32),
        pltpu.VMEM((narrow_count,) + shape, jnp.float32),
        pltpu.VMEM((wide_count,) + shape, jnp.float32),
        pltpu.VMEM(shape, jnp.float32),
        pltpu.SemaphoreType.DMA((narrow_count - 1,)),
        pltpu.SemaphoreType.DMA((narrow_count - 1,)),
        pltpu.SemaphoreType.DMA((wide_count - 1,)),
        pltpu.SemaphoreType.DMA((wide_count - 1,)),
    ]
    if exchange:
        shapes.append(jax.ShapeDtypeStruct((D // narrow_count, proj_cols), jnp.bfloat16))
        scratch += [
            pltpu.SemaphoreType.DMA((3 * own_units,)),
            pltpu.SemaphoreType.DMA((3 * own_units,)),
        ]
    return pl.pallas_call(
        partial(finish_kernel, narrow_count, wide_count, own_units, per_shard, entries),
        out_shape=tuple(shapes),
        in_specs=[vmem] * 3,
        out_specs=(vmem,) * len(shapes),
        scratch_shapes=scratch,
        compiler_params=pltpu.CompilerParams(collective_id=0, has_side_effects=True),
        name="finish",
    )(parts, piece, feed_piece)


def adam_update(
    weight, first_moment, second_moment, grad_value, step_rate, decay_coef, first_fix, second_fix
):
    new_first = beta_first * first_moment + (1.0 - beta_first) * grad_value
    new_second = beta_second * second_moment + (1.0 - beta_second) * grad_value * grad_value
    step_ratio = new_first / first_fix / (jnp.sqrt(new_second / second_fix) + adam_eps)
    return (weight - step_rate * (step_ratio + decay_coef * weight), new_first, new_second)


def adam_step(weight, first_moment, second_moment, gradient, step_rate, decay_coef, scales):
    new_first = beta_first * first_moment + (1.0 - beta_first) * gradient
    new_second = beta_second * second_moment + (1.0 - beta_second) * gradient * gradient
    ratio = new_first * scales[0] / (jnp.sqrt(new_second * scales[1]) + adam_eps)
    return (weight - step_rate * (ratio + decay_coef * weight), new_first, new_second)


def adam_kernel(scale_ref, stats_ref, grads_ref, total_ref, proj_ref, merge_ref, *refs):
    states, outs = refs[:15], refs[15:-1]
    norm_grads = refs[-1]
    matrix_step, norm_step = scale_ref[0, 0], scale_ref[0, 1]
    scales = (scale_ref[0, 2], scale_ref[0, 3])
    clip_factor = stats_ref[0:1, 0:1]

    def update(matrix, gradient, step_rate, decay_coef):
        state = [ref[...] for ref in states[3 * matrix : 3 * matrix + 3]]
        new = adam_step(*state, gradient * clip_factor, step_rate, decay_coef, scales)
        for out_ref, value in zip(outs[4 * matrix : 4 * matrix + 3], new):
            out_ref[...] = value
        return new[0]

    for matrix in range(2):
        gradient = grads_ref[0, matrix].astype(jnp.float32)
        weight = update(matrix, gradient, matrix_step, decay_rate)
        outs[4 * matrix + 3][...] = weight.astype(jnp.bfloat16)

    @pl.when(pl.program_id(0) == 0)
    def _():
        for matrix, gradient in (
            (2, proj_ref[...].astype(jnp.float32)),
            (3, merge_ref[...].astype(jnp.float32).T),
        ):
            weight = update(matrix, gradient, matrix_step, decay_rate)
            outs[4 * matrix + 3][...] = weight.astype(jnp.bfloat16)
        per_row = D // LANES
        for k in range(2 * per_row):
            at = k % per_row
            norm_grads[k // per_row : k // per_row + 1, at * LANES : (at + 1) * LANES] = total_ref[
                k : k + 1, :
            ]
        update(4, norm_grads[...], norm_step, 0.0)
        outs[19][...] = norm_grads[...] * clip_factor


def adam_all(scales, stats, grads_all, total, proj_block, heads_part, own_width, states):
    count, matrices, rows, cols = grads_all.shape
    block = pl.BlockSpec((rows, cols), lambda i: (i, 0))

    def same(array):
        return pl.BlockSpec(array.shape, lambda i: (0, 0))

    feed_out = jax.ShapeDtypeStruct((count * rows, cols), jnp.float32)
    feed_copy = jax.ShapeDtypeStruct((count * rows, cols), jnp.bfloat16)
    shapes = [feed_out, feed_out, feed_out, feed_copy] * 2
    specs = [block] * 8
    for state in states[6::3]:
        full = jax.ShapeDtypeStruct(state.shape, jnp.float32)
        copy = jax.ShapeDtypeStruct(
            state.shape, jnp.float32 if state is states[12] else jnp.bfloat16
        )
        shapes += [full, full, full, copy]
        specs += [same(state)] * 4
    return pl.pallas_call(
        adam_kernel,
        out_shape=tuple(shapes),
        grid=(count,),
        in_specs=[
            pl.BlockSpec(memory_space=pltpu.SMEM),
            same(stats),
            pl.BlockSpec((1, matrices, rows, cols), lambda i: (i, 0, 0, 0)),
            same(total),
            same(proj_block),
            pl.BlockSpec((heads_part.shape[0], own_width), lambda i: (0, 3)),
        ]
        + [block] * 6
        + [same(state) for state in states[6:]],
        out_specs=tuple(specs),
        scratch_shapes=[pltpu.VMEM((2, D), jnp.float32)],
        cost_estimate=short,
        name="adam_all",
    )(scales, stats, grads_all, total, proj_block, heads_part, *states)


def shards(
    tokens,
    cotangent,
    seq_lengths,
    step_count,
    norm_params,
    norm_first,
    norm_second,
    proj_weight,
    proj_first,
    proj_second,
    merge_weight,
    merge_first,
    merge_second,
    up_weight,
    up_first,
    up_second,
    down_weight,
    down_first,
    down_second,
):
    tok_rows = tokens.shape[0]
    narrow_count = lax.axis_size("narrow")
    wide_count = lax.axis_size("wide")
    span_index = lax.axis_index("narrow")
    group_rows = tok_rows * narrow_count
    own_width = HEADS // narrow_count * HEAD
    held_width = max(own_width, LANES)
    heads_in = min(own_width, LANES) // HEAD
    shard_rows = D // narrow_count
    proj_cols = proj_weight.shape[1]
    lengths = seq_lengths[0]
    onward = [(i, (i + 1) % narrow_count) for i in range(narrow_count)]
    slots = lax.rem(
        span_index + narrow_count - jnp.arange(narrow_count, dtype=jnp.int32), narrow_count
    )

    def pad_lanes(array, axis):
        extra = [(0, 0)] * array.ndim
        extra[axis] = (0, held_width - own_width)
        return jnp.pad(array, extra) if held_width > own_width else array

    def meet(*values):
        return lax.optimization_barrier(values)

    def send_on(array):
        return lax.ppermute(array, "narrow", onward)

    def rows_of(array, slot):
        return array[slot * tok_rows : (slot + 1) * tok_rows]

    direct = own_width % LANES == 0 and proj_cols % LANES == 0 and merge_weight.shape[1] == LANES
    weight_part = jnp.concatenate(
        [proj_weight.astype(jnp.bfloat16), merge_weight.astype(jnp.bfloat16)], axis=1
    )
    weight_rows = lax.all_gather(weight_part, "narrow", axis=0, tiled=True)
    up_slice = up_weight.astype(jnp.bfloat16)
    down_slice = down_weight.astype(jnp.bfloat16)

    def wide_all(array):
        return lax.all_gather(array, "wide", axis=0).reshape(
            wide_count, narrow_count, shard_rows, -1
        )

    def down_term(rows, slot):
        return dot_plain(rows_of(rows, slot), down_slice)

    order = list(range(1, narrow_count)) + [0]
    pairs = held_width // LANES
    token_blocks = [tokens]
    held = ()
    for slot in range(narrow_count - 1):
        moving = send_on(token_blocks[slot])
        held = feed(slot, narrow_count, token_blocks[slot], norm_params, up_slice, held)
        if slot != 2:
            moving, held = meet(moving, held)
        if slot == 0:
            lengths, slots, moving, weight_rows = meet(lengths, slots, moving, weight_rows)
            proj_all = wide_all(weight_rows[:, :proj_cols])
            merge_all = wide_all(weight_rows[:, proj_cols:])
        if slot == 1:
            places = (
                slots[:, None] * tok_rows + jnp.arange(tok_rows, dtype=jnp.int32)[None, :]
            ).reshape(group_rows)
            seq_start, unused = locate(lengths, places)
            cosine, sine = rotary_tables(places - seq_start)
            block_first = jnp.arange(narrow_count, dtype=jnp.int32) * tok_rows
            first_start, unused = locate(lengths, block_first)
            last_start, last_end = locate(lengths, block_first + (tok_rows - 1))
            moving, cosine, sine, first_start, last_start, last_end = meet(
                moving, cosine, sine, first_start, last_start, last_end
            )
        elif slot == 2:
            first_term = down_term(held[1], 1).astype(jnp.bfloat16)
            next_term = down_term(held[1], order[1])
            moving, held, down_slice, first_term, next_term = meet(
                moving, held, down_slice, first_term, next_term
            )
        token_blocks.append(moving)
    grad_first, last_block = meet(cotangent, token_blocks[-1])
    token_blocks[-1] = last_block
    grad_blocks = [grad_first]

    moving = send_on(grad_first)
    gathered, activated, slope = feed(
        narrow_count - 1, narrow_count, last_block, norm_params, up_slice, held
    )
    if direct:
        packed, proj_own = project_all(
            gathered, proj_all, span_index, own_width, cosine, sine
        )
        merge_own = merge_all
    else:
        proj_copy = jnp.transpose(proj_all, (1, 2, 0, 3)).reshape(
            D, 3, narrow_count, own_width
        )
        proj_own = pad_lanes(
            lax.dynamic_index_in_dim(proj_copy, span_index, axis=2, keepdims=False), 2
        ).reshape(D, 3 * held_width)
        merge_copy = jnp.transpose(merge_all, (1, 2, 0, 3)).reshape(
            narrow_count, own_width, D
        )
        merge_own = pad_lanes(
            lax.dynamic_index_in_dim(merge_copy, span_index, axis=0, keepdims=False), 0
        )
        packed = project(gathered, proj_own, cosine, sine)

    def push_slot(slot, push_held):
        return push(
            slot, narrow_count, grad_blocks[slot], slope, down_slice, merge_own, span_index,
            push_held,
        )

    push_held = push_slot(0, ())
    moving, packed, activated, slope, push_held = meet(
        moving, packed, activated, slope, push_held
    )
    grad_blocks.append(moving)

    def wide_sum(grad):
        return lax.psum_scatter(grad, "wide", scatter_dimension=0, tiled=True)

    def attend_pair(pair, attended_held):
        return attend(
            pair, packed, slots, first_start, last_start, seq_start,
            heads_in, tok_rows, tok_rows, attended_held,
        )

    attended_held = ()
    for hop in range(2, narrow_count):
        moving = send_on(grad_blocks[-1])
        if hop - 2 < pairs:
            attended_held = attend_pair(hop - 2, attended_held)
        push_held = push_slot(hop - 1, push_held)
        moving, attended_held, push_held = meet(moving, attended_held, push_held)
        grad_blocks.append(moving)
    for pair in range(narrow_count - 2, pairs):
        attended_held = attend_pair(pair, attended_held)
    attended, tall, logs = attended_held

    moving = send_on(first_term)
    push_held = push_slot(narrow_count - 1, push_held)
    grads_all, hidden_grad, attended_grad = push_held
    part_rows = D // wide_count
    down_grad = dot_first(activated, grads_all).astype(jnp.bfloat16)
    up_grad = dot_first(gathered, hidden_grad).astype(jnp.bfloat16)
    pieces = [
        rows_of(attended, (narrow_count - ahead) % narrow_count)[:, :own_width]
        for ahead in range(narrow_count)
    ]
    moving, pieces, up_grad, down_grad, attended_grad = meet(
        moving, pieces, up_grad, down_grad, attended_grad
    )
    feed_grad = jnp.concatenate(
        [
            up_grad.reshape(wide_count, part_rows, -1),
            down_grad.reshape(wide_count, part_rows, -1),
        ],
        axis=1,
    ).reshape(2 * D, -1)
    feed_part = wide_sum(feed_grad)

    def heads_back():
        mixed = attend_back(
            packed, slots, last_start, last_end, seq_start, cosine, sine,
            tall, logs, attended_grad, heads_in, tok_rows, tok_rows,
        )
        proj_grad = dot_first(gathered, mixed).astype(jnp.bfloat16)
        merge_grad = dot_first(grads_all, attended).astype(jnp.bfloat16)
        if not direct:
            proj_grad = proj_grad.reshape(D, 3, held_width)[:, :, :own_width].reshape(D, -1)
            merge_grad = merge_grad[:, :own_width]
        return (mixed, proj_grad, merge_grad)

    for ahead in range(1, narrow_count):
        pieces[ahead] = lax.ppermute(
            pieces[ahead],
            "narrow",
            [(i, (i + ahead) % narrow_count) for i in range(narrow_count)],
        )
    terms = []
    norm_part = jnp.zeros((2, D), jnp.float32)

    def pull_more(count, mixed, norm_part):
        for slot in order[len(terms) : len(terms) + count]:
            term, sums = pull(slot, mixed, hidden_grad, proj_own, up_slice, token_blocks[slot])
            terms.append(term)
            norm_part = norm_part + sums
        return norm_part

    for place, slot in enumerate(order[1:-1]):
        moving = send_on((moving.astype(jnp.float32) + next_term).astype(jnp.bfloat16))
        next_term = down_term(activated, order[place + 2])
        if place == 0:
            mixed_grad, *heads_grads = heads_back()
            moving, pieces, mixed_grad, heads_grads, next_term, feed_part = meet(
                moving, pieces, mixed_grad, heads_grads, next_term, feed_part
            )
            feed_all = lax.all_gather(feed_part, "wide", axis=0).reshape(
                wide_count, 2, part_rows, -1
            )
            heads_part = wide_sum(jnp.concatenate(heads_grads, axis=1))
        else:
            norm_part = pull_more(3, mixed_grad, norm_part)
            moving, terms, norm_part, next_term = meet(moving, terms, norm_part, next_term)
        if slot == narrow_count - 1:
            moving, merge_all, slots = meet(moving, merge_all, slots)
    norm_part = pull_more(narrow_count, mixed_grad, norm_part)
    branch_moving = moving
    moving = send_on(terms[0].astype(jnp.bfloat16))
    branch = branch_moving.astype(jnp.float32) + next_term
    if direct:
        merge_turn = pick_merge(merge_all, slots, own_width)
    else:
        merge_turn = jnp.take(
            jnp.transpose(merge_all, (1, 2, 0, 3)).reshape(narrow_count, own_width, D),
            slots,
            axis=0,
        ).reshape(D, D)
    merged = dot_plain(jnp.concatenate(pieces, axis=1), merge_turn)
    unit_rows, inv_std = normalize(tokens)
    output_rows = tokens.astype(jnp.float32) + merged + branch
    layer_out = output_rows.astype(jnp.bfloat16)

    def squares(array):
        value = array.astype(jnp.float32)
        return jnp.sum(value * value)

    row_squares = [squares(output_rows), squares(merged), squares(branch)]
    scalars = jnp.stack([jnp.zeros((), jnp.float32)] + row_squares)
    parts = jnp.concatenate(
        [norm_part.reshape(2 * D // LANES, LANES), jnp.pad(scalars, (0, LANES - 4))[None, :]]
    )
    parts = jnp.pad(parts, ((0, 7), (0, 0)))
    step_value = step_count[0].astype(jnp.float32)
    first_fix = 1.0 - jnp.power(beta_first, step_value)
    second_fix = 1.0 - jnp.power(beta_second, step_value)
    ramp = jnp.minimum(1.0, step_value / warmup_steps)
    scales = jnp.stack(
        [matrix_rate * ramp, norm_rate * ramp, 1.0 / first_fix, 1.0 / second_fix]
    ).reshape(1, 4)
    entries = wide_count * group_rows * D
    for place in range(1, narrow_count - 1):
        last = place == narrow_count - 2
        if last:
            moving, parts, heads_part, scales = meet(moving, parts, heads_part, scales)
        sent = (moving.astype(jnp.float32) + terms[place]).astype(jnp.bfloat16)
        if last:
            sent, parts = meet(sent, parts)
            summed = finish(
                parts, heads_part, feed_part, direct, narrow_count, wide_count, own_width,
                proj_cols, entries,
            )
            sent, summed = meet(sent, summed)
        moving = send_on(sent)

    stats = summed[1]
    if direct:
        total, stats, proj_block = summed
        updated = adam_all(
            scales, stats, feed_all, total, proj_block, heads_part, own_width,
            [
                up_weight, up_first, up_second, down_weight, down_first, down_second,
                proj_weight, proj_first, proj_second, merge_weight, merge_first, merge_second,
                norm_params, norm_first, norm_second,
            ],
        )
    else:
        total, stats = summed
        clip_factor = stats[0, 0:1]
        cross = lax.all_gather(heads_part[:, : 3 * own_width], "narrow", axis=0).reshape(
            narrow_count, part_rows, 3, own_width
        )
        cross = jnp.transpose(cross, (1, 2, 0, 3)).reshape(part_rows, wide_count, proj_cols)
        cross = lax.all_to_all(jnp.transpose(cross, (1, 0, 2)), "wide", 0, 0)
        proj_block = lax.dynamic_slice_in_dim(
            cross.reshape(D, proj_cols), span_index * shard_rows, shard_rows, axis=0
        )
        merge_block = heads_part[:, 3 * own_width :].T
        norm_total = total[: 2 * D // LANES].reshape(2, D)
        feed_sums = feed_all.astype(jnp.float32)
        updated = []
        for state, gradient, step_rate, decay_coef in (
            ((up_weight, up_first, up_second), feed_sums[:, 0], matrix_rate, decay_rate),
            ((down_weight, down_first, down_second), feed_sums[:, 1], matrix_rate, decay_rate),
            ((proj_weight, proj_first, proj_second), proj_block, matrix_rate, decay_rate),
            ((merge_weight, merge_first, merge_second), merge_block, matrix_rate, decay_rate),
            ((norm_params, norm_first, norm_second), norm_total, norm_rate, 0.0),
        ):
            clipped = gradient.reshape(state[0].shape).astype(jnp.float32) * clip_factor
            new = adam_update(
                *state, clipped, step_rate * ramp, decay_coef, first_fix, second_fix
            )
            updated += [*new, clipped if state[0] is norm_params else new[0].astype(jnp.bfloat16)]
    new_up, new_down, new_proj, new_merge, new_norm = [
        updated[4 * k : 4 * k + 4] for k in range(5)
    ]
    moving, new_up = meet(moving, new_up)
    normed_grad = moving.astype(jnp.float32) + terms[-1]
    unit_grad = normed_grad * norm_params[0]
    input_grad = cotangent.astype(jnp.float32) + inv_std * (
        unit_grad
        - jnp.mean(unit_grad, axis=1, keepdims=True)
        - unit_rows * jnp.mean(unit_grad * unit_rows, axis=1, keepdims=True)
    )
    return (
        layer_out,
        input_grad,
        stats[1, 0:1],
        stats[2, 0:1],
        new_norm[3],
        new_norm[0],
        new_norm[1],
        new_norm[2],
        new_proj[0],
        new_proj[1],
        new_proj[2],
        new_merge[0],
        new_merge[1],
        new_merge[2],
        new_up[0],
        new_up[1],
        new_up[2],
        new_down[0],
        new_down[1],
        new_down[2],
        stats[3:5, 0],
        new_proj[3],
        new_merge[3],
        new_up[3],
        new_down[3],
    )


def solution(mesh):
    placed = (
        P(("wide", "narrow"), None),
        P(("wide", "narrow"), None),
        P("wide", None),
        P(),
        P(),
        P(),
        P(),
        P("narrow", "wide"),
        P("narrow", "wide"),
        P("narrow", "wide"),
        P("narrow", "wide"),
        P("narrow", "wide"),
        P("narrow", "wide"),
        P(None, "narrow"),
        P(None, "narrow"),
        P(None, "narrow"),
        P("narrow", None),
        P("narrow", None),
        P("narrow", None),
    )
    return jax.shard_map(
        shards,
        mesh=mesh,
        in_specs=placed,
        out_specs=(
            P(("wide", "narrow"), None),
            P(("wide", "narrow"), None),
            P(),
            P(),
            P(),
            P(),
            P(),
            P(),
            P("narrow", "wide"),
            P("narrow", "wide"),
            P("narrow", "wide"),
            P("narrow", "wide"),
            P("narrow", "wide"),
            P("narrow", "wide"),
            P(None, "narrow"),
            P(None, "narrow"),
            P(None, "narrow"),
            P("narrow", None),
            P("narrow", None),
            P("narrow", None),
            P(),
            P("narrow", "wide"),
            P("narrow", "wide"),
            P(None, "narrow"),
            P("narrow", None),
        ),
        check_vma=False,
    )
```

```python
from functools import partial
import math

import jax
import jax.numpy as jnp
from jax import lax
from jax.experimental import pallas as pl
from jax.experimental.pallas import tpu as pltpu
from jax.sharding import PartitionSpec as P

HEADS = 16
HEAD = 64
D = 1024
ROT = 16
LANES = 128
ROW_BLOCK = 512
NPARAMS = 12584960


norm_eps = 1e-05
adam_eps = 1e-08
beta_first = 0.5
beta_second = 0.5
decay_rate = 0.01
matrix_rate = 0.1
norm_rate = 1.0
warmup_steps = 20.0
masked_score = -1e30
short = pl.CostEstimate(flops=0, bytes_accessed=0, transcendentals=0)


def dot_last(left_side, right_side):
    return lax.dot_general(
        left_side, right_side, (((1,), (1,)), ((), ())), preferred_element_type=jnp.float32
    )


def dot_plain(left_side, right_side):
    return lax.dot_general(
        left_side, right_side, (((1,), (0,)), ((), ())), preferred_element_type=jnp.float32
    )


def dot_first(left_side, right_side):
    return lax.dot_general(
        left_side, right_side, (((0,), (0,)), ((), ())), preferred_element_type=jnp.float32
    )


def locate(lengths, token_index):
    seq_ends = jnp.cumsum(lengths)
    starts = seq_ends - lengths
    segment = jnp.sum(
        (seq_ends[None, :] <= token_index[:, None]).astype(jnp.int32), axis=1, dtype=jnp.int32
    )
    choose = segment[:, None] == jnp.arange(lengths.shape[0], dtype=jnp.int32)[None, :]
    seq_start = jnp.sum(jnp.where(choose, starts[None, :], 0), axis=1, dtype=jnp.int32)
    seq_end = jnp.sum(jnp.where(choose, seq_ends[None, :], 0), axis=1, dtype=jnp.int32)
    return (seq_start, seq_end)


def rotary_tables(position):
    half_rot = ROT // 2
    frequency = jnp.power(10000.0, -2.0 * jnp.arange(half_rot, dtype=jnp.float32) / ROT)
    row = jnp.concatenate([frequency, frequency, jnp.zeros((HEAD - ROT,), jnp.float32)])
    row = jnp.tile(row, LANES // HEAD)
    sign = jnp.where(jnp.arange(LANES) % HEAD < half_rot, -1.0, 1.0)
    phases = position.astype(jnp.float32)[:, None] * row[None, :]
    return (jnp.cos(phases), jnp.sin(phases) * sign[None, :])


def partner(field):
    half_rot = ROT // 2
    lane = lax.broadcasted_iota(jnp.int32, field.shape, 1) % HEAD
    return jnp.where(
        lane < half_rot,
        pltpu.roll(field, LANES - half_rot, 1),
        pltpu.roll(field, half_rot, 1),
    )


def project_kernel(rows_ref, weight_ref, cos_ref, sin_ref, out_ref):
    width = out_ref.shape[1]
    projected = dot_plain(rows_ref[...], weight_ref[...])
    for first in range(0, width, LANES):
        piece = projected[:, first : first + LANES]
        part = first // LANES % 3
        if part < 2:
            piece = piece * cos_ref[...] + partner(piece) * sin_ref[...]
        if part == 0:
            piece = piece * HEAD ** (-0.5)
        out_ref[:, first : first + LANES] = piece.astype(jnp.bfloat16)


def project(rows, weight, cosine, sine):
    count, depth = rows.shape
    width = weight.shape[1]
    block = min(ROW_BLOCK, count)
    return pl.pallas_call(
        project_kernel,
        out_shape=jax.ShapeDtypeStruct((count, width), jnp.bfloat16),
        grid=(count // block,),
        in_specs=[
            pl.BlockSpec((block, depth), lambda i: (i, 0)),
            pl.BlockSpec((depth, width), lambda i: (0, 0)),
            pl.BlockSpec((block, LANES), lambda i: (i, 0)),
            pl.BlockSpec((block, LANES), lambda i: (i, 0)),
        ],
        out_specs=pl.BlockSpec((block, width), lambda i: (i, 0)),
        cost_estimate=short,
        name="project",
    )(rows, weight, cosine, sine)


def normalize(tokens):
    residual = tokens.astype(jnp.float32)
    center = residual - jnp.mean(residual, axis=1, keepdims=True)
    inv_std = lax.rsqrt(jnp.mean(center * center, axis=1, keepdims=True) + norm_eps)
    return (center * inv_std, inv_std)


def feed_kernel(tokens_ref, params_ref, weight_ref, *refs):
    normed_ref, act_ref, slope_ref = refs[-3:]
    unit, unused = normalize(tokens_ref[...])
    normed_ref[...] = (unit * params_ref[0:1, :] + params_ref[1:2, :]).astype(jnp.bfloat16)
    width = act_ref.shape[1]
    step = min(256, width)
    for first in range(0, width, step):
        hidden = dot_plain(normed_ref[...], weight_ref[:, first : first + step])
        share = 0.5 + 0.5 * lax.erf(hidden * math.sqrt(0.5))
        bell = jnp.exp(hidden * hidden * -0.5) * (1.0 / math.sqrt(2.0 * math.pi))
        act_ref[:, first : first + step] = (hidden * share).astype(jnp.bfloat16)
        slope_ref[:, first : first + step] = share + hidden * bell


def feed(slot, slots, tokens, params, weight, held):
    rows, depth = tokens.shape
    width = weight.shape[1]
    whole = pl.BlockSpec(memory_space=pl.ANY)
    return pl.pallas_call(
        feed_kernel,
        out_shape=(
            jax.ShapeDtypeStruct((slots * rows, depth), jnp.bfloat16),
            jax.ShapeDtypeStruct((slots * rows, width), jnp.bfloat16),
            jax.ShapeDtypeStruct((slots * rows, width), jnp.float32),
        ),
        grid=(2,),
        in_specs=[
            pl.BlockSpec((rows // 2, depth), lambda i: (i, 0)),
            pl.BlockSpec((2, depth), lambda i: (0, 0)),
            pl.BlockSpec((depth, width), lambda i: (0, 0)),
        ]
        + [whole] * len(held),
        out_specs=(
            pl.BlockSpec((rows // 2, depth), lambda i: (2 * slot + i, 0)),
            pl.BlockSpec((rows // 2, width), lambda i: (2 * slot + i, 0)),
            pl.BlockSpec((rows // 2, width), lambda i: (2 * slot + i, 0)),
        ),
        input_output_aliases={3 + k: k for k in range(len(held))},
        cost_estimate=short,
        name="feed",
    )(tokens, params, weight, *held)


def outer_kernel(split, first_left, first_right, second_left, second_right, out_ref, first, second):
    step = pl.program_id(0)
    for left_ref, right_ref, total in (
        (first_left, first_right, first),
        (second_left, second_right, second),
    ):
        term = dot_first(left_ref[...], right_ref[...])

        @pl.when(step == 0)
        def _():
            total[...] = term

        @pl.when(step > 0)
        def _():
            total[...] += term

    @pl.when(step == pl.num_programs(0) - 1)
    def _():
        if split:
            blocks, unused, rows, cols = out_ref.shape
            for matrix, total in enumerate((first, second)):
                for block in range(blocks):
                    out_ref[block, matrix] = total[block * rows : (block + 1) * rows, :].astype(
                        jnp.bfloat16
                    )
        else:
            width = first.shape[1]
            out_ref[:, :width] = first[...].astype(jnp.bfloat16)
            out_ref[:, width:] = second[...].astype(jnp.bfloat16)


def outer(blocks, first_left, first_right, second_left, second_right):
    count, depth = first_left.shape
    rows = min(ROW_BLOCK, count)
    widths = [first_right.shape[1], second_right.shape[1]]
    shape = (blocks, 2, depth // blocks, widths[0]) if blocks else (depth, sum(widths))
    operands = (first_left, first_right, second_left, second_right)
    return pl.pallas_call(
        partial(outer_kernel, bool(blocks)),
        out_shape=jax.ShapeDtypeStruct(shape, jnp.bfloat16),
        grid=(count // rows,),
        in_specs=[pl.BlockSpec((rows, array.shape[1]), lambda k: (k, 0)) for array in operands],
        out_specs=pl.BlockSpec(shape, lambda k: (0,) * len(shape)),
        scratch_shapes=[pltpu.VMEM((depth, width), jnp.float32) for width in widths],
        cost_estimate=short,
        name="outer",
    )(*operands)


def push_kernel(index_ref, grad_ref, slope_ref, down_ref, merge_ref, *refs):
    all_ref, hidden_ref, attended_ref, merge_own = refs[-4:]

    @pl.when(pl.program_id(0) == 0)
    def _():
        if len(merge_ref.shape) == 4:
            for w in range(merge_ref.shape[0]):
                merge_own[:, w * LANES : (w + 1) * LANES] = merge_ref[w, 0]
        else:
            merge_own[...] = merge_ref[...]

    grads = grad_ref[...]
    all_ref[...] = grads
    hidden_ref[...] = (dot_last(grads, down_ref[...]) * slope_ref[...]).astype(jnp.bfloat16)
    attended_ref[...] = dot_last(grads, merge_own[...]).astype(jnp.bfloat16)


def push(slot, slots, grads, slope, down, merge, span_index, held):
    rows, depth = grads.shape
    width = slope.shape[1]
    half = rows // 2
    whole = pl.BlockSpec(memory_space=pl.ANY)
    if merge.ndim == 4:
        own = merge.shape[2]
        merge_spec = pl.BlockSpec(
            (merge.shape[0], 1, own, LANES), lambda i, index_ref: (0, index_ref[0], 0, 0)
        )
    else:
        own = merge.shape[0]
        merge_spec = pl.BlockSpec(merge.shape, lambda i, index_ref: (0, 0))

    def place(i, index_ref):
        return (2 * slot + i, 0)

    return pl.pallas_call(
        push_kernel,
        out_shape=(
            jax.ShapeDtypeStruct((slots * rows, depth), jnp.bfloat16),
            jax.ShapeDtypeStruct((slots * rows, width), jnp.bfloat16),
            jax.ShapeDtypeStruct((slots * rows, own), jnp.bfloat16),
        ),
        grid_spec=pltpu.PrefetchScalarGridSpec(
            num_scalar_prefetch=1,
            grid=(2,),
            in_specs=[
                pl.BlockSpec((half, depth), lambda i, index_ref: (i, 0)),
                pl.BlockSpec((half, width), place),
                pl.BlockSpec(down.shape, lambda i, index_ref: (0, 0)),
                merge_spec,
            ]
            + [whole] * len(held),
            out_specs=(
                pl.BlockSpec((half, depth), place),
                pl.BlockSpec((half, width), place),
                pl.BlockSpec((half, own), place),
            ),
            scratch_shapes=[pltpu.VMEM((own, depth), jnp.bfloat16)],
        ),
        input_output_aliases={5 + k: k for k in range(len(held))},
        cost_estimate=short,
        name="push",
    )(span_index.reshape(1), grads, slope, down, merge, *held)


def pull_kernel(mixed_ref, hidden_ref, proj_ref, up_ref, tokens_ref, out_ref, sums_ref):
    partial_grad = dot_last(mixed_ref[...], proj_ref[...]) + dot_last(hidden_ref[...], up_ref[...])
    out_ref[...] = partial_grad
    unit, unused = normalize(tokens_ref[...])
    gain = jnp.sum(partial_grad * unit, axis=0, keepdims=True)
    bias = jnp.sum(partial_grad, axis=0, keepdims=True)
    both = jnp.concatenate([gain, bias], axis=0)

    @pl.when(pl.program_id(0) == 0)
    def _():
        sums_ref[...] = both

    @pl.when(pl.program_id(0) > 0)
    def _():
        sums_ref[...] += both


def pull(slot, mixed, hidden_grad, proj, up, tokens):
    rows, depth = tokens.shape
    half = rows // 2
    return pl.pallas_call(
        pull_kernel,
        out_shape=(
            jax.ShapeDtypeStruct((rows, depth), jnp.float32),
            jax.ShapeDtypeStruct((2, depth), jnp.float32),
        ),
        grid=(2,),
        in_specs=[
            pl.BlockSpec((half, mixed.shape[1]), lambda i: (2 * slot + i, 0)),
            pl.BlockSpec((half, hidden_grad.shape[1]), lambda i: (2 * slot + i, 0)),
            pl.BlockSpec(proj.shape, lambda i: (0, 0)),
            pl.BlockSpec(up.shape, lambda i: (0, 0)),
            pl.BlockSpec((half, depth), lambda i: (i, 0)),
        ],
        out_specs=(
            pl.BlockSpec((half, depth), lambda i: (i, 0)),
            pl.BlockSpec((2, depth), lambda i: (0, 0)),
        ),
        cost_estimate=short,
        name="pull",
    )(mixed, hidden_grad, proj, up, tokens)


def project_all_kernel(index_ref, rows_ref, cos_ref, sin_ref, *refs):
    unit_refs, (out_ref, weight_ref) = refs[:-2], refs[-2:]

    @pl.when(pl.program_id(0) == 0)
    def _():
        for c, unit_ref in enumerate(unit_refs):
            weight_ref[:, c * LANES : (c + 1) * LANES] = unit_ref[...].reshape(D, LANES)

    project_kernel(rows_ref, weight_ref, cos_ref, sin_ref, out_ref)


def project_all(rows, weight_all, span_index, own_width, cosine, sine):
    count, depth = rows.shape
    shards, narrow_count, shard_rows, cols = weight_all.shape
    units = own_width // LANES
    width = 3 * own_width
    per_shard = cols // LANES
    per_part = D // LANES
    block = min(ROW_BLOCK, count)

    def source(c, i, index_ref):
        unit = (c % 3) * per_part + index_ref[0] * units + c // 3
        return (unit // per_shard, 0, 0, unit % per_shard)

    return pl.pallas_call(
        project_all_kernel,
        out_shape=(
            jax.ShapeDtypeStruct((count, width), jnp.bfloat16),
            jax.ShapeDtypeStruct((D, width), jnp.bfloat16),
        ),
        grid_spec=pltpu.PrefetchScalarGridSpec(
            num_scalar_prefetch=1,
            grid=(count // block,),
            in_specs=[
                pl.BlockSpec((block, depth), lambda i, index_ref: (i, 0)),
                pl.BlockSpec((block, LANES), lambda i, index_ref: (i, 0)),
                pl.BlockSpec((block, LANES), lambda i, index_ref: (i, 0)),
            ]
            + [
                pl.BlockSpec((1, narrow_count, shard_rows, LANES), partial(source, c))
                for c in range(3 * units)
            ],
            out_specs=(
                pl.BlockSpec((block, width), lambda i, index_ref: (i, 0)),
                pl.BlockSpec((D, width), lambda i, index_ref: (0, 0)),
            ),
        ),
        cost_estimate=short,
        name="project_all",
    )(span_index.reshape(1), rows, cosine, sine, *[weight_all] * (3 * units))


def turn_kernel(slots_ref, all_ref, out_ref):
    unused, narrow_count, rows, cols = all_ref.shape
    for t in range(narrow_count):
        out_ref[t * rows : (t + 1) * rows, :] = all_ref[0, slots_ref[t]]


def pick_merge(weight_all, slots, own_width):
    shards, narrow_count, rows, cols = weight_all.shape
    return pl.pallas_call(
        turn_kernel,
        out_shape=jax.ShapeDtypeStruct((D, D), jnp.bfloat16),
        grid_spec=pltpu.PrefetchScalarGridSpec(
            num_scalar_prefetch=1,
            grid=(shards,),
            in_specs=[
                pl.BlockSpec(
                    (1, narrow_count, rows, LANES),
                    lambda j, slots_ref: (j, 0, 0, 0),
                )
            ],
            out_specs=pl.BlockSpec((D, LANES), lambda j, slots_ref: (0, j)),
        ),
        cost_estimate=short,
        name="pick_merge",
    )(slots, weight_all)


def head_lanes(field, head):
    lane = lax.broadcasted_iota(jnp.int32, field.shape, 1)
    keep = (lane >= head * HEAD) & (lane < (head + 1) * HEAD)
    return jnp.where(keep, field, jnp.zeros_like(field))


def pair_allowed(start_row, key_first, key_count, query_first, query_count):
    key_index = key_first + lax.broadcasted_iota(jnp.int32, (key_count, query_count), 0)
    query_index = query_first + lax.broadcasted_iota(jnp.int32, (key_count, query_count), 1)
    return (key_index >= start_row) & (key_index <= query_index)


def attend_kernel(
    block_q,
    block_k,
    heads_in,
    slots_ref,
    first_ref,
    last_ref,
    start_ref,
    query_ref,
    key_ref,
    value_ref,
    *refs,
):
    out_ref, tall_ref, log_ref, turned, best, total, summed = refs[-7:]
    index = pl.program_id(0)
    key_blocks = key_ref.shape[0] // block_k

    @pl.when(index == 0)
    def _():
        for j in range(key_blocks):
            piece = value_ref[j * block_k : (j + 1) * block_k, :].astype(jnp.float32)
            turned[:, j * block_k : (j + 1) * block_k] = piece.T.astype(jnp.bfloat16)

    query_first = index * block_q
    low = first_ref[index] // block_k
    high = (query_first + block_q - 1) // block_k + 1
    start_row = start_ref[...]
    queries = [head_lanes(query_ref[...], head) for head in range(heads_in)]
    best[...] = jnp.full_like(best, masked_score)
    total[...] = jnp.zeros_like(total)
    summed[...] = jnp.zeros_like(summed)

    def visit(j, masked):
        key_rows = pl.ds(pl.multiple_of(slots_ref[j] * block_k, block_k), block_k)
        keys = key_ref[key_rows, :]
        if masked:
            allowed = pair_allowed(start_row, j * block_k, block_k, query_first, block_q)
        for head in range(heads_in):
            scores = dot_last(keys, queries[head])
            if masked:
                scores = jnp.where(allowed, scores, masked_score)
            old = best[head : head + 1, :]
            new = jnp.maximum(old, jnp.max(scores, axis=0, keepdims=True))
            weights = jnp.exp(scores - new)
            if masked:
                weights = jnp.where(allowed, weights, 0.0)
            factor = jnp.exp(old - new)
            best[head : head + 1, :] = new
            total[head : head + 1, :] = total[head : head + 1, :] * factor + jnp.sum(
                weights, axis=0, keepdims=True
            )
            rows = slice(head * HEAD, (head + 1) * HEAD)
            summed[rows, :] = summed[rows, :] * factor + dot_plain(
                turned[rows, key_rows], weights.astype(jnp.bfloat16)
            )

    def step(j, carry):
        whole = (j * block_k >= last_ref[index]) & ((j + 1) * block_k - 1 <= query_first)

        @pl.when(whole)
        def _():
            visit(j, False)

        @pl.when(jnp.logical_not(whole))
        def _():
            visit(j, True)

        return carry

    lax.fori_loop(low, high, step, 0)
    for head in range(heads_in):
        rows = slice(head * HEAD, (head + 1) * HEAD)
        weight = total[head : head + 1, :]
        tall_ref[rows, :] = summed[rows, :] / weight
        log_ref[0, head : head + 1, :] = best[head : head + 1, :] + jnp.log(weight)
    if heads_in * HEAD < LANES:
        tall_ref[heads_in * HEAD :, :] = jnp.zeros_like(tall_ref[heads_in * HEAD :, :])
    log_ref[0, heads_in:, :] = jnp.zeros_like(log_ref[0, heads_in:, :])
    out_ref[...] = tall_ref[...].T.astype(jnp.bfloat16)


def attend(pair, packed, slots, first, last, starts, heads_in, block_q, block_k, held):
    count, width = packed.shape
    pairs = width // 3 // LANES
    whole = pl.BlockSpec(memory_space=pl.ANY)
    return pl.pallas_call(
        partial(attend_kernel, block_q, block_k, heads_in),
        out_shape=(
            jax.ShapeDtypeStruct((count, pairs * LANES), jnp.bfloat16),
            jax.ShapeDtypeStruct((pairs * LANES, count), jnp.float32),
            jax.ShapeDtypeStruct((pairs, 8, count), jnp.float32),
        ),
        grid_spec=pltpu.PrefetchScalarGridSpec(
            num_scalar_prefetch=3,
            grid=(count // block_q,),
            in_specs=[
                pl.BlockSpec((1, block_q), lambda i, slots_ref, *_: (0, slots_ref[i])),
                pl.BlockSpec((block_q, LANES), lambda i, slots_ref, *_: (slots_ref[i], 3 * pair)),
                pl.BlockSpec((count, LANES), lambda i, *_: (0, 3 * pair + 1)),
                pl.BlockSpec((count, LANES), lambda i, *_: (0, 3 * pair + 2)),
            ]
            + [whole] * len(held),
            out_specs=(
                pl.BlockSpec((block_q, LANES), lambda i, slots_ref, *_: (slots_ref[i], pair)),
                pl.BlockSpec((LANES, block_q), lambda i, slots_ref, *_: (pair, slots_ref[i])),
                pl.BlockSpec((1, 8, block_q), lambda i, slots_ref, *_: (pair, 0, slots_ref[i])),
            ),
            scratch_shapes=[
                pltpu.VMEM((LANES, count), jnp.bfloat16),
                pltpu.VMEM((8, block_q), jnp.float32),
                pltpu.VMEM((8, block_q), jnp.float32),
                pltpu.VMEM((LANES, block_q), jnp.float32),
            ],
        ),
        input_output_aliases={7 + k: k for k in range(len(held))},
        cost_estimate=short,
        name="attend",
    )(slots, first, last, starts.reshape(1, count), packed, packed, packed, *held)


def attend_back_kernel(
    block_q,
    block_k,
    heads_in,
    slots_ref,
    last_ref,
    end_ref,
    start_ref,
    cos_ref,
    sin_ref,
    query_ref,
    key_ref,
    value_ref,
    tall_ref,
    log_ref,
    grad_ref,
    out_ref,
    turned,
    masked_q,
    masked_g,
    delta,
    tall_q,
    key_sum,
    value_sum,
):
    index = pl.program_id(1)
    count = query_ref.shape[0]

    def turn_back(field, rows):
        return field * cos_ref[rows, :] - partner(field) * sin_ref[rows, :]

    @pl.when(index == 0)
    def _():
        def prepare(j, carry):
            rows = pl.ds(pl.multiple_of(j * block_k, block_k), block_k)
            turned[:, rows] = key_ref[rows, :].astype(jnp.float32).T.astype(jnp.bfloat16)
            grads = grad_ref[rows, :]
            product = grads.astype(jnp.float32).T * tall_ref[:, rows]
            for head in range(heads_in):
                masked_q[head, rows, :] = head_lanes(query_ref[rows, :], head)
                masked_g[head, rows, :] = head_lanes(grads, head)
                delta[head : head + 1, rows] = jnp.sum(
                    product[head * HEAD : (head + 1) * HEAD, :], axis=0, keepdims=True
                )
            tall_q[:, rows] = jnp.zeros((LANES, block_k), jnp.float32)
            return carry

        lax.fori_loop(0, count // block_k, prepare, 0)

    key_first = index * block_k
    key_rows = pl.ds(pl.multiple_of(slots_ref[index] * block_k, block_k), block_k)
    keys = key_ref[key_rows, :]
    values = value_ref[key_rows, :]
    key_sum[...] = jnp.zeros_like(key_sum)
    value_sum[...] = jnp.zeros_like(value_sum)

    def visit(i, masked):
        query_first = i * block_q
        rows = pl.ds(pl.multiple_of(slots_ref[i] * block_q, block_q), block_q)
        if masked:
            allowed = pair_allowed(
                start_ref[0:1, rows], key_first, block_k, query_first, block_q
            )
        for head in range(heads_in):
            queries = masked_q[head, rows, :]
            grads = masked_g[head, rows, :]
            scores = dot_last(keys, queries)
            probs = jnp.exp(scores - log_ref[0, head : head + 1, rows])
            if masked:
                probs = jnp.where(allowed, probs, 0.0)
            value_sum[...] += dot_plain(probs.astype(jnp.bfloat16), grads)
            prob_grad = dot_last(values, grads)
            score_grad = (probs * (prob_grad - delta[head : head + 1, rows])).astype(jnp.bfloat16)
            key_sum[...] += dot_plain(score_grad, queries)
            lanes = slice(head * HEAD, (head + 1) * HEAD)
            tall_q[lanes, rows] += dot_plain(turned[lanes, key_rows], score_grad)

    def step(i, carry):
        whole = (key_first >= last_ref[i]) & (key_first + block_k - 1 <= i * block_q)

        @pl.when(whole)
        def _():
            visit(i, False)

        @pl.when(jnp.logical_not(whole))
        def _():
            visit(i, True)

        return carry

    lax.fori_loop(key_first // block_q, (end_ref[index] - 1) // block_q + 1, step, 0)
    out_ref[key_rows, LANES : 2 * LANES] = turn_back(key_sum[...], key_rows).astype(jnp.bfloat16)
    out_ref[key_rows, 2 * LANES :] = value_sum[...].astype(jnp.bfloat16)

    @pl.when(index == pl.num_programs(1) - 1)
    def _():
        def finish(j, carry):
            rows = pl.ds(pl.multiple_of(j * block_k, block_k), block_k)
            field = tall_q[:, rows].T * HEAD ** (-0.5)
            out_ref[rows, :LANES] = turn_back(field, rows).astype(jnp.bfloat16)
            return carry

        lax.fori_loop(0, count // block_k, finish, 0)


def attend_back(
    packed, slots, last, end, starts, cosine, sine, tall, logs, grads, heads_in, block_q, block_k
):
    count, width = packed.shape
    pairs = width // 3 // LANES
    return pl.pallas_call(
        partial(attend_back_kernel, block_q, block_k, heads_in),
        out_shape=jax.ShapeDtypeStruct((count, width), jnp.bfloat16),
        grid_spec=pltpu.PrefetchScalarGridSpec(
            num_scalar_prefetch=3,
            grid=(pairs, count // block_k),
            in_specs=[
                pl.BlockSpec((1, count), lambda p, i, *_: (0, 0)),
                pl.BlockSpec((count, LANES), lambda p, i, *_: (0, 0)),
                pl.BlockSpec((count, LANES), lambda p, i, *_: (0, 0)),
                pl.BlockSpec((count, LANES), lambda p, i, *_: (0, 3 * p)),
                pl.BlockSpec((count, LANES), lambda p, i, *_: (0, 3 * p + 1)),
                pl.BlockSpec((count, LANES), lambda p, i, *_: (0, 3 * p + 2)),
                pl.BlockSpec((LANES, count), lambda p, i, *_: (p, 0)),
                pl.BlockSpec((1, 8, count), lambda p, i, *_: (p, 0, 0)),
                pl.BlockSpec((count, LANES), lambda p, i, *_: (0, p)),
            ],
            out_specs=pl.BlockSpec((count, 3 * LANES), lambda p, i, *_: (0, p)),
            scratch_shapes=[
                pltpu.VMEM((LANES, count), jnp.bfloat16),
                pltpu.VMEM((heads_in, count, LANES), jnp.bfloat16),
                pltpu.VMEM((heads_in, count, LANES), jnp.bfloat16),
                pltpu.VMEM((8, count), jnp.float32),
                pltpu.VMEM((LANES, count), jnp.float32),
                pltpu.VMEM((block_k, LANES), jnp.float32),
                pltpu.VMEM((block_k, LANES), jnp.float32),
            ],
        ),
        compiler_params=pltpu.CompilerParams(vmem_limit_bytes=60 << 20),
        cost_estimate=short,
        name="attend_back",
    )(
        slots, last, end, starts.reshape(1, count), cosine, sine,
        packed, packed, packed, tall, logs, grads,
    )


def finish_kernel(narrow_count, wide_count, own_units, per_shard, entries, *refs):
    exchange = own_units > 0
    if exchange:
        (
            parts_ref, piece_ref, feed_ref, sent_ref, total_ref, stats_ref, arrived_ref, block_ref,
            mine, near, far, near_sum, send_near, recv_near, send_far, recv_far, send_ring, recv_ring,
            send_piece, recv_piece,
        ) = refs
    else:
        (
            parts_ref, piece_ref, feed_ref, sent_ref, total_ref, stats_ref, arrived_ref,
            mine, near, far, near_sum, send_near, recv_near, send_far, recv_far, send_ring, recv_ring,
        ) = refs
    narrow_me = lax.axis_index("narrow")
    wide_me = lax.axis_index("wide")

    def place(narrow_at, wide_at):
        return {"narrow": narrow_at, "wide": wide_at}

    def square_sum(value):
        value = value.astype(jnp.float32)
        return jnp.sum(
            jnp.sum(value * value, axis=0, keepdims=True), axis=1, keepdims=True
        )

    norm_rows = 2 * D // LANES
    row_at = lax.broadcasted_iota(jnp.int32, mine.shape, 0)
    lane_at = lax.broadcasted_iota(jnp.int32, mine.shape, 1)
    mine[...] = parts_ref[...] + jnp.where(
        (row_at == norm_rows) & (lane_at == 0),
        square_sum(piece_ref[...]) + square_sum(feed_ref[...]),
        0.0,
    )
    mesh_ids = pl.DeviceIdType.MESH
    barrier = pltpu.get_barrier_semaphore()
    greeted = 0
    for ahead in range(narrow_count):
        for across in range(wide_count):
            if (ahead > 0) + (across > 0) == 0 or (not exchange and ahead > 0 and across > 0):
                continue
            greeted += 1
            pl.semaphore_signal(
                barrier,
                inc=1,
                device_id=place(
                    lax.rem(narrow_me + ahead, narrow_count), lax.rem(wide_me + across, wide_count)
                ),
                device_id_type=mesh_ids,
            )
    pl.semaphore_wait(barrier, greeted)
    near_copies = []
    for ahead in range(1, narrow_count):
        copy = pltpu.make_async_remote_copy(
            src_ref=mine,
            dst_ref=near.at[narrow_me],
            send_sem=send_near.at[ahead - 1],
            recv_sem=recv_near.at[ahead - 1],
            device_id=place(lax.rem(narrow_me + ahead, narrow_count), wide_me),
            device_id_type=mesh_ids,
        )
        copy.start()
        near_copies.append(copy)
    near[narrow_me] = mine[...]
    if exchange:
        rows = piece_ref.shape[0]
        halves = block_ref.shape[0] // rows
        half_me = lax.rem(wide_me, halves)
        narrow_to = lax.div(wide_me, halves)
        moves = []
        for unit in range(3 * own_units):
            whole_unit = (unit % 3) * (D // LANES) + narrow_me * own_units + unit // 3
            wide_to = lax.div(whole_unit, per_shard)
            column = lax.rem(whole_unit, per_shard)
            source = piece_ref.at[:, unit * LANES : (unit + 1) * LANES]
            target = block_ref.at[
                pl.ds(pl.multiple_of(half_me * rows, rows), rows),
                pl.ds(pl.multiple_of(column * LANES, LANES), LANES),
            ]
            arrived = recv_piece.at[half_me * per_shard + column]
            remote = pltpu.make_async_remote_copy(
                src_ref=source,
                dst_ref=target,
                send_sem=send_piece.at[unit],
                recv_sem=arrived,
                device_id=place(narrow_to, wide_to),
                device_id_type=mesh_ids,
            )
            here = pltpu.make_async_copy(source, target, arrived)
            stays = (narrow_to == narrow_me) & (wide_to == wide_me)
            pl.when(jnp.logical_not(stays))(remote.start)
            pl.when(stays)(here.start)
            moves.append((stays, remote))
    for copy in near_copies:
        copy.wait()
    ring = pltpu.make_async_remote_copy(
        src_ref=sent_ref,
        dst_ref=arrived_ref,
        send_sem=send_ring,
        recv_sem=recv_ring,
        device_id=place(lax.rem(narrow_me + 1, narrow_count), wide_me),
        device_id_type=mesh_ids,
    )
    ring.start()
    value = near[0]
    for k in range(1, narrow_count):
        value = value + near[k]
    near_sum[...] = value
    far_copies = []
    for across in range(1, wide_count):
        copy = pltpu.make_async_remote_copy(
            src_ref=near_sum,
            dst_ref=far.at[wide_me],
            send_sem=send_far.at[across - 1],
            recv_sem=recv_far.at[across - 1],
            device_id=place(narrow_me, lax.rem(wide_me + across, wide_count)),
            device_id_type=mesh_ids,
        )
        copy.start()
        far_copies.append(copy)
    far[wide_me] = value
    for copy in far_copies:
        copy.wait()
    value = far[0]
    for k in range(1, wide_count):
        value = value + far[k]
    total_ref[...] = value
    grad_norm = jnp.sqrt(square_sum(value[:norm_rows]) + value[norm_rows : norm_rows + 1, 0:1])
    stats = [jnp.minimum(1.0, math.sqrt(NPARAMS) / grad_norm), grad_norm] + [
        jnp.sqrt(value[norm_rows : norm_rows + 1, k : k + 1] / entries) for k in (1, 2, 3)
    ]
    stats_ref[...] = jnp.zeros_like(stats_ref)
    for row, stat in enumerate(stats):
        stats_ref[row : row + 1, :] = jnp.broadcast_to(stat, (1, LANES))
    if exchange:
        for stays, remote in moves:
            pl.when(jnp.logical_not(stays))(remote.wait_send)
        for half in range(halves):
            for column in range(per_shard):
                pltpu.make_async_copy(
                    piece_ref.at[:, 0:LANES],
                    block_ref.at[
                        half * rows : (half + 1) * rows, column * LANES : (column + 1) * LANES
                    ],
                    recv_piece.at[half * per_shard + column],
                ).wait()
    ring.wait()


def finish(
    parts, piece, feed_piece, sent, exchange, narrow_count, wide_count, own_width, proj_cols, entries
):
    shape = parts.shape
    own_units = own_width // LANES if exchange else 0
    per_shard = proj_cols // LANES
    vmem = pl.BlockSpec(memory_space=pltpu.VMEM)
    shapes = [
        jax.ShapeDtypeStruct(shape, jnp.float32),
        jax.ShapeDtypeStruct((8, LANES), jnp.float32),
        jax.ShapeDtypeStruct(sent.shape, sent.dtype),
    ]
    whole = pl.BlockSpec(memory_space=pl.ANY)
    scratch = [
        pltpu.VMEM(shape, jnp.float32),
        pltpu.VMEM((narrow_count,) + shape, jnp.float32),
        pltpu.VMEM((wide_count,) + shape, jnp.float32),
        pltpu.VMEM(shape, jnp.float32),
        pltpu.SemaphoreType.DMA((narrow_count - 1,)),
        pltpu.SemaphoreType.DMA((narrow_count - 1,)),
        pltpu.SemaphoreType.DMA((wide_count - 1,)),
        pltpu.SemaphoreType.DMA((wide_count - 1,)),
        pltpu.SemaphoreType.DMA,
        pltpu.SemaphoreType.DMA,
    ]
    if exchange:
        shapes.append(jax.ShapeDtypeStruct((D // narrow_count, proj_cols), jnp.bfloat16))
        scratch += [
            pltpu.SemaphoreType.DMA((3 * own_units,)),
            pltpu.SemaphoreType.DMA((3 * own_units,)),
        ]
    return pl.pallas_call(
        partial(finish_kernel, narrow_count, wide_count, own_units, per_shard, entries),
        out_shape=tuple(shapes),
        in_specs=[vmem] * 3 + [whole],
        out_specs=(vmem, vmem, whole) + (vmem,) * (len(shapes) - 3),
        scratch_shapes=scratch,
        compiler_params=pltpu.CompilerParams(collective_id=0, has_side_effects=True),
        name="finish",
    )(parts, piece, feed_piece, sent)


def adam_update(
    weight, first_moment, second_moment, grad_value, step_rate, decay_coef, first_fix, second_fix
):
    new_first = beta_first * first_moment + (1.0 - beta_first) * grad_value
    new_second = beta_second * second_moment + (1.0 - beta_second) * grad_value * grad_value
    step_ratio = new_first / first_fix / (jnp.sqrt(new_second / second_fix) + adam_eps)
    return (weight - step_rate * (step_ratio + decay_coef * weight), new_first, new_second)


def adam_step(weight, first_moment, second_moment, gradient, step_rate, decay_coef, scales):
    new_first = beta_first * first_moment + (1.0 - beta_first) * gradient
    new_second = beta_second * second_moment + (1.0 - beta_second) * gradient * gradient
    ratio = new_first * scales[0] / (jnp.sqrt(new_second * scales[1]) + adam_eps)
    return (weight - step_rate * (ratio + decay_coef * weight), new_first, new_second)


def adam_kernel(scale_ref, stats_ref, grads_ref, total_ref, proj_ref, merge_ref, *refs):
    states, outs = refs[:15], refs[15:-1]
    norm_grads = refs[-1]
    matrix_step, norm_step = scale_ref[0, 0], scale_ref[0, 1]
    scales = (scale_ref[0, 2], scale_ref[0, 3])
    clip_factor = stats_ref[0:1, 0:1]

    def update(matrix, gradient, step_rate, decay_coef):
        state = [ref[...] for ref in states[3 * matrix : 3 * matrix + 3]]
        new = adam_step(*state, gradient * clip_factor, step_rate, decay_coef, scales)
        for out_ref, value in zip(outs[4 * matrix : 4 * matrix + 3], new):
            out_ref[...] = value
        return new[0]

    for matrix in range(2):
        gradient = grads_ref[0, matrix].astype(jnp.float32)
        weight = update(matrix, gradient, matrix_step, decay_rate)
        outs[4 * matrix + 3][...] = weight.astype(jnp.bfloat16)

    @pl.when(pl.program_id(0) == 0)
    def _():
        for matrix, gradient in (
            (2, proj_ref[...].astype(jnp.float32)),
            (3, merge_ref[...].astype(jnp.float32).T),
        ):
            weight = update(matrix, gradient, matrix_step, decay_rate)
            outs[4 * matrix + 3][...] = weight.astype(jnp.bfloat16)
        per_row = D // LANES
        for k in range(2 * per_row):
            at = k % per_row
            norm_grads[k // per_row : k // per_row + 1, at * LANES : (at + 1) * LANES] = total_ref[
                k : k + 1, :
            ]
        update(4, norm_grads[...], norm_step, 0.0)
        outs[19][...] = norm_grads[...] * clip_factor


def adam_all(scales, stats, grads_all, total, proj_block, heads_part, own_width, states):
    count, matrices, rows, cols = grads_all.shape
    block = pl.BlockSpec((rows, cols), lambda i: (i, 0))

    def same(array):
        return pl.BlockSpec(array.shape, lambda i: (0, 0))

    feed_out = jax.ShapeDtypeStruct((count * rows, cols), jnp.float32)
    feed_copy = jax.ShapeDtypeStruct((count * rows, cols), jnp.bfloat16)
    shapes = [feed_out, feed_out, feed_out, feed_copy] * 2
    specs = [block] * 8
    for state in states[6::3]:
        full = jax.ShapeDtypeStruct(state.shape, jnp.float32)
        copy = jax.ShapeDtypeStruct(
            state.shape, jnp.float32 if state is states[12] else jnp.bfloat16
        )
        shapes += [full, full, full, copy]
        specs += [same(state)] * 4
    return pl.pallas_call(
        adam_kernel,
        out_shape=tuple(shapes),
        grid=(count,),
        in_specs=[
            pl.BlockSpec(memory_space=pltpu.SMEM),
            same(stats),
            pl.BlockSpec((1, matrices, rows, cols), lambda i: (i, 0, 0, 0)),
            same(total),
            same(proj_block),
            pl.BlockSpec((heads_part.shape[0], own_width), lambda i: (0, 3)),
        ]
        + [block] * 6
        + [same(state) for state in states[6:]],
        out_specs=tuple(specs),
        scratch_shapes=[pltpu.VMEM((2, D), jnp.float32)],
        cost_estimate=short,
        name="adam_all",
    )(scales, stats, grads_all, total, proj_block, heads_part, *states)


def shards(
    tokens,
    cotangent,
    seq_lengths,
    step_count,
    norm_params,
    norm_first,
    norm_second,
    proj_weight,
    proj_first,
    proj_second,
    merge_weight,
    merge_first,
    merge_second,
    up_weight,
    up_first,
    up_second,
    down_weight,
    down_first,
    down_second,
):
    tok_rows = tokens.shape[0]
    narrow_count = lax.axis_size("narrow")
    wide_count = lax.axis_size("wide")
    span_index = lax.axis_index("narrow")
    group_rows = tok_rows * narrow_count
    own_width = HEADS // narrow_count * HEAD
    held_width = max(own_width, LANES)
    heads_in = min(own_width, LANES) // HEAD
    shard_rows = D // narrow_count
    proj_cols = proj_weight.shape[1]
    lengths = seq_lengths[0]
    onward = [(i, (i + 1) % narrow_count) for i in range(narrow_count)]
    slots = lax.rem(
        span_index + narrow_count - jnp.arange(narrow_count, dtype=jnp.int32), narrow_count
    )

    def pad_lanes(array, axis):
        extra = [(0, 0)] * array.ndim
        extra[axis] = (0, held_width - own_width)
        return jnp.pad(array, extra) if held_width > own_width else array

    def meet(*values):
        return lax.optimization_barrier(values)

    def send_on(array):
        return lax.ppermute(array, "narrow", onward)

    def rows_of(array, slot):
        return array[slot * tok_rows : (slot + 1) * tok_rows]

    direct = own_width % LANES == 0 and proj_cols % LANES == 0 and merge_weight.shape[1] == LANES
    weight_part = jnp.concatenate(
        [proj_weight.astype(jnp.bfloat16), merge_weight.astype(jnp.bfloat16)], axis=1
    )
    weight_rows = lax.all_gather(weight_part, "narrow", axis=0, tiled=True)
    up_slice = up_weight.astype(jnp.bfloat16)
    down_slice = down_weight.astype(jnp.bfloat16)

    def wide_all(array):
        return lax.all_gather(array, "wide", axis=0).reshape(
            wide_count, narrow_count, shard_rows, -1
        )

    def down_term(rows, slot):
        return dot_plain(rows_of(rows, slot), down_slice)

    order = list(range(1, narrow_count)) + [0]
    pairs = held_width // LANES
    token_blocks = [tokens]
    held = ()
    for slot in range(narrow_count - 1):
        moving = send_on(token_blocks[slot])
        held = feed(slot, narrow_count, token_blocks[slot], norm_params, up_slice, held)
        if slot > 0:
            ready = [slot - 1, slot] if slot == narrow_count - 2 else [slot - 1]
            for block in ready:
                term = down_term(held[1], block)
                branch_terms.append(term.astype(jnp.bfloat16) if block == 1 else term)
            moving, held, branch_terms, down_slice = meet(moving, held, branch_terms, down_slice)
        else:
            moving, held = meet(moving, held)
        if slot == 0:
            lengths, slots, moving, weight_rows = meet(lengths, slots, moving, weight_rows)
            proj_all = wide_all(weight_rows[:, :proj_cols])
            merge_all = wide_all(weight_rows[:, proj_cols:])
            branch_terms = []
        if slot == 1:
            places = (
                slots[:, None] * tok_rows + jnp.arange(tok_rows, dtype=jnp.int32)[None, :]
            ).reshape(group_rows)
            seq_start, unused = locate(lengths, places)
            cosine, sine = rotary_tables(places - seq_start)
            block_first = jnp.arange(narrow_count, dtype=jnp.int32) * tok_rows
            first_start, unused = locate(lengths, block_first)
            last_start, last_end = locate(lengths, block_first + (tok_rows - 1))
            moving, cosine, sine, first_start, last_start, last_end = meet(
                moving, cosine, sine, first_start, last_start, last_end
            )
        token_blocks.append(moving)
    grad_first, last_block = meet(cotangent, token_blocks[-1])
    token_blocks[-1] = last_block
    grad_blocks = [grad_first]

    moving = send_on(grad_first)
    gathered, activated, slope = feed(
        narrow_count - 1, narrow_count, last_block, norm_params, up_slice, held
    )
    if direct:
        packed, proj_own = project_all(
            gathered, proj_all, span_index, own_width, cosine, sine
        )
        merge_own = merge_all
    else:
        proj_copy = jnp.transpose(proj_all, (1, 2, 0, 3)).reshape(
            D, 3, narrow_count, own_width
        )
        proj_own = pad_lanes(
            lax.dynamic_index_in_dim(proj_copy, span_index, axis=2, keepdims=False), 2
        ).reshape(D, 3 * held_width)
        merge_copy = jnp.transpose(merge_all, (1, 2, 0, 3)).reshape(
            narrow_count, own_width, D
        )
        merge_own = pad_lanes(
            lax.dynamic_index_in_dim(merge_copy, span_index, axis=0, keepdims=False), 0
        )
        packed = project(gathered, proj_own, cosine, sine)

    def push_slot(slot, push_held):
        return push(
            slot, narrow_count, grad_blocks[slot], slope, down_slice, merge_own, span_index,
            push_held,
        )

    push_held = push_slot(0, ())
    branch_terms.append(down_term(activated, narrow_count - 1))
    moving, packed, activated, slope, push_held, branch_terms = meet(
        moving, packed, activated, slope, push_held, branch_terms
    )
    grad_blocks.append(moving)

    def wide_sum(grad):
        return lax.psum_scatter(grad, "wide", scatter_dimension=0, tiled=True)

    def attend_pair(pair, attended_held):
        return attend(
            pair, packed, slots, first_start, last_start, seq_start,
            heads_in, tok_rows, tok_rows, attended_held,
        )

    attended_held = ()
    for hop in range(2, narrow_count):
        moving = send_on(grad_blocks[-1])
        if hop - 2 < pairs:
            attended_held = attend_pair(hop - 2, attended_held)
        push_held = push_slot(hop - 1, push_held)
        moving, attended_held, push_held = meet(moving, attended_held, push_held)
        grad_blocks.append(moving)
    for pair in range(narrow_count - 2, pairs):
        attended_held = attend_pair(pair, attended_held)
    attended, tall, logs = attended_held

    moving = send_on(branch_terms[1])
    push_held = push_slot(narrow_count - 1, push_held)
    grads_all, hidden_grad, attended_grad = push_held
    part_rows = D // wide_count
    if direct:
        feed_grad = outer(wide_count, gathered, hidden_grad, activated, grads_all)
    else:
        down_grad = dot_first(activated, grads_all).astype(jnp.bfloat16)
        up_grad = dot_first(gathered, hidden_grad).astype(jnp.bfloat16)
        feed_grad = jnp.stack(
            [
                up_grad.reshape(wide_count, part_rows, -1),
                down_grad.reshape(wide_count, part_rows, -1),
            ],
            axis=1,
        )
    feed_grad = feed_grad.reshape(2 * D, -1)
    pieces = [
        rows_of(attended, (narrow_count - ahead) % narrow_count)[:, :own_width]
        for ahead in range(narrow_count)
    ]
    moving, pieces, feed_grad, attended_grad = meet(moving, pieces, feed_grad, attended_grad)
    feed_part = wide_sum(feed_grad)

    for ahead in range(1, narrow_count):
        pieces[ahead] = lax.ppermute(
            pieces[ahead],
            "narrow",
            [(i, (i + ahead) % narrow_count) for i in range(narrow_count)],
        )
    terms = []
    norm_part = jnp.zeros((2, D), jnp.float32)

    def pull_more(count, mixed, norm_part):
        for slot in order[len(terms) : len(terms) + count]:
            term, sums = pull(slot, mixed, hidden_grad, proj_own, up_slice, token_blocks[slot])
            terms.append(term)
            norm_part = norm_part + sums
        return norm_part

    for place, slot in enumerate(order[1:-1]):
        moving = send_on((moving.astype(jnp.float32) + branch_terms[slot]).astype(jnp.bfloat16))
        if place == 0:
            mixed_grad = attend_back(
                packed, slots, last_start, last_end, seq_start, cosine, sine,
                tall, logs, attended_grad, heads_in, tok_rows, tok_rows,
            )
            if direct:
                heads_grad = outer(0, gathered, mixed_grad, grads_all, attended)
            else:
                proj_grad = dot_first(gathered, mixed_grad).astype(jnp.bfloat16)
                merge_grad = dot_first(grads_all, attended).astype(jnp.bfloat16)
                proj_grad = proj_grad.reshape(D, 3, held_width)[:, :, :own_width]
                heads_grad = jnp.concatenate(
                    [proj_grad.reshape(D, 3 * own_width), merge_grad[:, :own_width]], axis=1
                )
            moving, pieces, mixed_grad, heads_grad, feed_part = meet(
                moving, pieces, mixed_grad, heads_grad, feed_part
            )
            heads_part = wide_sum(heads_grad)
        else:
            norm_part = pull_more(3, mixed_grad, norm_part)
            moving, terms, norm_part, merge_all, slots, feed_part = meet(
                moving, terms, norm_part, merge_all, slots, feed_part
            )
        if place == narrow_count - 3:
            feed_all = lax.all_gather(feed_part, "wide", axis=0).reshape(
                wide_count, 2, part_rows, -1
            )
    branch_moving = moving
    moving = send_on(terms[0].astype(jnp.bfloat16))
    norm_part = pull_more(narrow_count, mixed_grad, norm_part)
    branch = branch_moving.astype(jnp.float32) + branch_terms[0]
    if direct:
        merge_turn = pick_merge(merge_all, slots, own_width)
    else:
        merge_turn = jnp.take(
            jnp.transpose(merge_all, (1, 2, 0, 3)).reshape(narrow_count, own_width, D),
            slots,
            axis=0,
        ).reshape(D, D)
    merged = dot_plain(jnp.concatenate(pieces, axis=1), merge_turn)
    unit_rows, inv_std = normalize(tokens)
    output_rows = tokens.astype(jnp.float32) + merged + branch
    layer_out = output_rows.astype(jnp.bfloat16)

    def squares(array):
        value = array.astype(jnp.float32)
        return jnp.sum(value * value)

    row_squares = [squares(output_rows), squares(merged), squares(branch)]
    scalars = jnp.stack([jnp.zeros((), jnp.float32)] + row_squares)
    parts = jnp.concatenate(
        [norm_part.reshape(2 * D // LANES, LANES), jnp.pad(scalars, (0, LANES - 4))[None, :]]
    )
    parts = jnp.pad(parts, ((0, 7), (0, 0)))
    step_value = step_count[0].astype(jnp.float32)
    first_fix = 1.0 - jnp.power(beta_first, step_value)
    second_fix = 1.0 - jnp.power(beta_second, step_value)
    ramp = jnp.minimum(1.0, step_value / warmup_steps)
    scales = jnp.stack(
        [matrix_rate * ramp, norm_rate * ramp, 1.0 / first_fix, 1.0 / second_fix]
    ).reshape(1, 4)
    entries = wide_count * group_rows * D
    for place in range(1, narrow_count - 1):
        if place == narrow_count - 3:
            moving, parts, heads_part, scales = meet(moving, parts, heads_part, scales)
        sent = (moving.astype(jnp.float32) + terms[place]).astype(jnp.bfloat16)
        if place == narrow_count - 3:
            total, stats, moving, *proj_block = finish(
                parts, heads_part, feed_part, sent, direct, narrow_count, wide_count, own_width,
                proj_cols, entries,
            )
            continue
        if place == narrow_count - 2:
            sent, total, stats, proj_block = meet(sent, total, stats, proj_block)
        moving = send_on(sent)

    if direct:
        updated = adam_all(
            scales, stats, feed_all, total, proj_block[0], heads_part, own_width,
            [
                up_weight, up_first, up_second, down_weight, down_first, down_second,
                proj_weight, proj_first, proj_second, merge_weight, merge_first, merge_second,
                norm_params, norm_first, norm_second,
            ],
        )
    else:
        clip_factor = stats[0, 0:1]
        cross = lax.all_gather(heads_part[:, : 3 * own_width], "narrow", axis=0).reshape(
            narrow_count, part_rows, 3, own_width
        )
        cross = jnp.transpose(cross, (1, 2, 0, 3)).reshape(part_rows, wide_count, proj_cols)
        cross = lax.all_to_all(jnp.transpose(cross, (1, 0, 2)), "wide", 0, 0)
        proj_block = lax.dynamic_slice_in_dim(
            cross.reshape(D, proj_cols), span_index * shard_rows, shard_rows, axis=0
        )
        merge_block = heads_part[:, 3 * own_width :].T
        norm_total = total[: 2 * D // LANES].reshape(2, D)
        feed_sums = feed_all.astype(jnp.float32)
        updated = []
        for state, gradient, step_rate, decay_coef in (
            ((up_weight, up_first, up_second), feed_sums[:, 0], matrix_rate, decay_rate),
            ((down_weight, down_first, down_second), feed_sums[:, 1], matrix_rate, decay_rate),
            ((proj_weight, proj_first, proj_second), proj_block, matrix_rate, decay_rate),
            ((merge_weight, merge_first, merge_second), merge_block, matrix_rate, decay_rate),
            ((norm_params, norm_first, norm_second), norm_total, norm_rate, 0.0),
        ):
            clipped = gradient.reshape(state[0].shape).astype(jnp.float32) * clip_factor
            new = adam_update(
                *state, clipped, step_rate * ramp, decay_coef, first_fix, second_fix
            )
            updated += [*new, clipped if state[0] is norm_params else new[0].astype(jnp.bfloat16)]
    new_up, new_down, new_proj, new_merge, new_norm = [
        updated[4 * k : 4 * k + 4] for k in range(5)
    ]
    moving, new_up = meet(moving, new_up)
    normed_grad = moving.astype(jnp.float32) + terms[-1]
    unit_grad = normed_grad * norm_params[0]
    input_grad = cotangent.astype(jnp.float32) + inv_std * (
        unit_grad
        - jnp.mean(unit_grad, axis=1, keepdims=True)
        - unit_rows * jnp.mean(unit_grad * unit_rows, axis=1, keepdims=True)
    )
    return (
        layer_out,
        input_grad,
        stats[1, 0:1],
        stats[2, 0:1],
        new_norm[3],
        new_norm[0],
        new_norm[1],
        new_norm[2],
        new_proj[0],
        new_proj[1],
        new_proj[2],
        new_merge[0],
        new_merge[1],
        new_merge[2],
        new_up[0],
        new_up[1],
        new_up[2],
        new_down[0],
        new_down[1],
        new_down[2],
        stats[3:5, 0],
        new_proj[3],
        new_merge[3],
        new_up[3],
        new_down[3],
    )


def solution(mesh):
    placed = (
        P(("wide", "narrow"), None),
        P(("wide", "narrow"), None),
        P("wide", None),
        P(),
        P(),
        P(),
        P(),
        P("narrow", "wide"),
        P("narrow", "wide"),
        P("narrow", "wide"),
        P("narrow", "wide"),
        P("narrow", "wide"),
        P("narrow", "wide"),
        P(None, "narrow"),
        P(None, "narrow"),
        P(None, "narrow"),
        P("narrow", None),
        P("narrow", None),
        P("narrow", None),
    )
    return jax.shard_map(
        shards,
        mesh=mesh,
        in_specs=placed,
        out_specs=(
            P(("wide", "narrow"), None),
            P(("wide", "narrow"), None),
            P(),
            P(),
            P(),
            P(),
            P(),
            P(),
            P("narrow", "wide"),
            P("narrow", "wide"),
            P("narrow", "wide"),
            P("narrow", "wide"),
            P("narrow", "wide"),
            P("narrow", "wide"),
            P(None, "narrow"),
            P(None, "narrow"),
            P(None, "narrow"),
            P("narrow", None),
            P("narrow", None),
            P("narrow", None),
            P(),
            P("narrow", "wide"),
            P("narrow", "wide"),
            P(None, "narrow"),
            P("narrow", None),
        ),
        check_vma=False,
    )
```

```python
from functools import partial
import math

import jax
import jax.numpy as jnp
from jax import lax
from jax.experimental import pallas as pl
from jax.experimental.pallas import tpu as pltpu
from jax.sharding import PartitionSpec as P

HEADS = 16
HEAD = 64
D = 1024
ROT = 16
LANES = 128
ROW_BLOCK = 512
NPARAMS = 12584960


norm_eps = 1e-05
adam_eps = 1e-08
beta_first = 0.5
beta_second = 0.5
decay_rate = 0.01
matrix_rate = 0.1
norm_rate = 1.0
warmup_steps = 20.0
masked_score = -1e30
short = pl.CostEstimate(flops=0, bytes_accessed=0, transcendentals=0)


def dot_last(left_side, right_side):
    return lax.dot_general(
        left_side, right_side, (((1,), (1,)), ((), ())), preferred_element_type=jnp.float32
    )


def dot_plain(left_side, right_side):
    return lax.dot_general(
        left_side, right_side, (((1,), (0,)), ((), ())), preferred_element_type=jnp.float32
    )


def dot_first(left_side, right_side):
    return lax.dot_general(
        left_side, right_side, (((0,), (0,)), ((), ())), preferred_element_type=jnp.float32
    )


def in_chunks(total, chunk, body):
    def step(index, carry):
        body(pl.ds(pl.multiple_of(index * chunk, chunk), chunk))
        return carry

    lax.fori_loop(0, total // chunk, step, 0)


def locate(lengths, token_index):
    seq_ends = jnp.cumsum(lengths)
    starts = seq_ends - lengths
    segment = jnp.sum(
        (seq_ends[None, :] <= token_index[:, None]).astype(jnp.int32), axis=1, dtype=jnp.int32
    )
    choose = segment[:, None] == jnp.arange(lengths.shape[0], dtype=jnp.int32)[None, :]
    seq_start = jnp.sum(jnp.where(choose, starts[None, :], 0), axis=1, dtype=jnp.int32)
    seq_end = jnp.sum(jnp.where(choose, seq_ends[None, :], 0), axis=1, dtype=jnp.int32)
    return (seq_start, seq_end)


def rotary_tables(position):
    half_rot = ROT // 2
    frequency = jnp.power(10000.0, -2.0 * jnp.arange(half_rot, dtype=jnp.float32) / ROT)
    row = jnp.concatenate([frequency, frequency, jnp.zeros((HEAD - ROT,), jnp.float32)])
    row = jnp.tile(row, LANES // HEAD)
    sign = jnp.where(jnp.arange(LANES) % HEAD < half_rot, -1.0, 1.0)
    phases = position.astype(jnp.float32)[:, None] * row[None, :]
    return (jnp.cos(phases), jnp.sin(phases) * sign[None, :])


def partner(field):
    half_rot = ROT // 2
    lane = lax.broadcasted_iota(jnp.int32, field.shape, 1) % HEAD
    return jnp.where(
        lane < half_rot,
        pltpu.roll(field, LANES - half_rot, 1),
        pltpu.roll(field, half_rot, 1),
    )


def project_kernel(rows_ref, weight_ref, cos_ref, sin_ref, out_ref):
    width = out_ref.shape[1]
    projected = dot_plain(rows_ref[...], weight_ref[...])
    for first in range(0, width, LANES):
        piece = projected[:, first : first + LANES]
        part = first // LANES % 3
        if part < 2:
            piece = piece * cos_ref[...] + partner(piece) * sin_ref[...]
        if part == 0:
            piece = piece * HEAD ** (-0.5)
        out_ref[:, first : first + LANES] = piece.astype(jnp.bfloat16)


def project(rows, weight, cosine, sine):
    count, depth = rows.shape
    width = weight.shape[1]
    block = min(ROW_BLOCK, count)
    return pl.pallas_call(
        project_kernel,
        out_shape=jax.ShapeDtypeStruct((count, width), jnp.bfloat16),
        grid=(count // block,),
        in_specs=[
            pl.BlockSpec((block, depth), lambda i: (i, 0)),
            pl.BlockSpec((depth, width), lambda i: (0, 0)),
            pl.BlockSpec((block, LANES), lambda i: (i, 0)),
            pl.BlockSpec((block, LANES), lambda i: (i, 0)),
        ],
        out_specs=pl.BlockSpec((block, width), lambda i: (i, 0)),
        cost_estimate=short,
        name="project",
    )(rows, weight, cosine, sine)


def normalize(tokens):
    residual = tokens.astype(jnp.float32)
    center = residual - jnp.mean(residual, axis=1, keepdims=True)
    inv_std = lax.rsqrt(jnp.mean(center * center, axis=1, keepdims=True) + norm_eps)
    return (center * inv_std, inv_std)


def feed_kernel(tokens_ref, params_ref, weight_ref, *refs):
    normed_ref, act_ref, slope_ref = refs[-3:]
    unit, unused = normalize(tokens_ref[...])
    normed_ref[...] = (unit * params_ref[0:1, :] + params_ref[1:2, :]).astype(jnp.bfloat16)
    width = act_ref.shape[1]

    def column(cols):
        hidden = dot_plain(normed_ref[...], weight_ref[:, cols])
        share = 0.5 + 0.5 * lax.erf(hidden * math.sqrt(0.5))
        bell = jnp.exp(hidden * hidden * -0.5) * (1.0 / math.sqrt(2.0 * math.pi))
        act_ref[:, cols] = (hidden * share).astype(jnp.bfloat16)
        slope_ref[:, cols] = share + hidden * bell

    in_chunks(width, min(256, width), column)


def feed(slot, slots, tokens, params, weight, held):
    rows, depth = tokens.shape
    width = weight.shape[1]
    whole = pl.BlockSpec(memory_space=pl.ANY)
    return pl.pallas_call(
        feed_kernel,
        out_shape=(
            jax.ShapeDtypeStruct((slots * rows, depth), jnp.bfloat16),
            jax.ShapeDtypeStruct((slots * rows, width), jnp.bfloat16),
            jax.ShapeDtypeStruct((slots * rows, width), jnp.float32),
        ),
        grid=(2,),
        in_specs=[
            pl.BlockSpec((rows // 2, depth), lambda i: (i, 0)),
            pl.BlockSpec((2, depth), lambda i: (0, 0)),
            pl.BlockSpec((depth, width), lambda i: (0, 0)),
        ]
        + [whole] * len(held),
        out_specs=(
            pl.BlockSpec((rows // 2, depth), lambda i: (2 * slot + i, 0)),
            pl.BlockSpec((rows // 2, width), lambda i: (2 * slot + i, 0)),
            pl.BlockSpec((rows // 2, width), lambda i: (2 * slot + i, 0)),
        ),
        input_output_aliases={3 + k: k for k in range(len(held))},
        cost_estimate=short,
        name="feed",
    )(tokens, params, weight, *held)


def down_kernel(active_ref, down_ref, out_ref):
    def column(cols):
        out_ref[:, cols] = dot_plain(active_ref[...], down_ref[:, cols]).astype(out_ref.dtype)

    in_chunks(out_ref.shape[1], 256, column)


def down_term(slot, slots, activated, down, kept):
    rows = activated.shape[0] // slots
    width, depth = down.shape
    half = rows // 2
    return pl.pallas_call(
        down_kernel,
        out_shape=jax.ShapeDtypeStruct((rows, depth), kept),
        grid=(2,),
        in_specs=[
            pl.BlockSpec((half, width), lambda i: (2 * slot + i, 0)),
            pl.BlockSpec((width, depth), lambda i: (0, 0)),
        ],
        out_specs=pl.BlockSpec((half, depth), lambda i: (i, 0)),
        cost_estimate=short,
        name="down_term",
    )(activated, down)


def outer_kernel(split, first_left, first_right, second_left, second_right, out_ref, first, second):
    begun = pl.program_id(0) > 0
    for left_ref, right_ref, total in (
        (first_left, first_right, first),
        (second_left, second_right, second),
    ):

        def chunk(rows):
            term = dot_first(left_ref[:, rows], right_ref[...])
            total[rows, :] = jnp.where(begun, total[rows, :], 0.0) + term

        in_chunks(total.shape[0], 512, chunk)

    @pl.when(pl.program_id(0) == pl.num_programs(0) - 1)
    def _():
        if split:
            blocks, unused, rows, cols = out_ref.shape

            def write(block, carry):
                at = pl.ds(pl.multiple_of(block * rows, rows), rows)
                out_ref[block, 0] = first[at, :].astype(jnp.bfloat16)
                out_ref[block, 1] = second[at, :].astype(jnp.bfloat16)
                return carry

            lax.fori_loop(0, blocks, write, 0)
        else:
            width = first.shape[1]

            def write_rows(rows):
                out_ref[rows, :width] = first[rows, :].astype(jnp.bfloat16)
                out_ref[rows, width:] = second[rows, :].astype(jnp.bfloat16)

            in_chunks(first.shape[0], 128, write_rows)


def outer(blocks, first_left, first_right, second_left, second_right):
    count, depth = first_left.shape
    rows = min(ROW_BLOCK, count)
    widths = [first_right.shape[1], second_right.shape[1]]
    shape = (blocks, 2, depth // blocks, widths[0]) if blocks else (depth, sum(widths))
    operands = (first_left, first_right, second_left, second_right)
    return pl.pallas_call(
        partial(outer_kernel, bool(blocks)),
        out_shape=jax.ShapeDtypeStruct(shape, jnp.bfloat16),
        grid=(count // rows,),
        in_specs=[pl.BlockSpec((rows, array.shape[1]), lambda k: (k, 0)) for array in operands],
        out_specs=pl.BlockSpec(shape, lambda k: (0,) * len(shape)),
        scratch_shapes=[pltpu.VMEM((depth, width), jnp.float32) for width in widths],
        cost_estimate=short,
        name="outer",
    )(*operands)


def push_kernel(index_ref, grad_ref, slope_ref, down_ref, merge_ref, *refs):
    all_ref, hidden_ref, attended_ref, merge_own = refs[-4:]

    @pl.when(pl.program_id(0) == 0)
    def _():
        if len(merge_ref.shape) == 4:
            for w in range(merge_ref.shape[0]):
                merge_own[:, w * LANES : (w + 1) * LANES] = merge_ref[w, 0]
        else:
            merge_own[...] = merge_ref[...]

    grads = grad_ref[...]
    all_ref[...] = grads

    def column(cols):
        hidden = dot_last(grad_ref[...], down_ref[cols, :]) * slope_ref[:, cols]
        hidden_ref[:, cols] = hidden.astype(jnp.bfloat16)

    in_chunks(down_ref.shape[0], min(512, down_ref.shape[0]), column)
    attended_ref[...] = dot_last(grads, merge_own[...]).astype(jnp.bfloat16)


def push(slot, slots, grads, slope, down, merge, span_index, held):
    rows, depth = grads.shape
    width = slope.shape[1]
    half = rows // 2
    whole = pl.BlockSpec(memory_space=pl.ANY)
    if merge.ndim == 4:
        own = merge.shape[2]
        merge_spec = pl.BlockSpec(
            (merge.shape[0], 1, own, LANES), lambda i, index_ref: (0, index_ref[0], 0, 0)
        )
    else:
        own = merge.shape[0]
        merge_spec = pl.BlockSpec(merge.shape, lambda i, index_ref: (0, 0))

    def place(i, index_ref):
        return (2 * slot + i, 0)

    return pl.pallas_call(
        push_kernel,
        out_shape=(
            jax.ShapeDtypeStruct((slots * rows, depth), jnp.bfloat16),
            jax.ShapeDtypeStruct((slots * rows, width), jnp.bfloat16),
            jax.ShapeDtypeStruct((slots * rows, own), jnp.bfloat16),
        ),
        grid_spec=pltpu.PrefetchScalarGridSpec(
            num_scalar_prefetch=1,
            grid=(2,),
            in_specs=[
                pl.BlockSpec((half, depth), lambda i, index_ref: (i, 0)),
                pl.BlockSpec((half, width), place),
                pl.BlockSpec(down.shape, lambda i, index_ref: (0, 0)),
                merge_spec,
            ]
            + [whole] * len(held),
            out_specs=(
                pl.BlockSpec((half, depth), place),
                pl.BlockSpec((half, width), place),
                pl.BlockSpec((half, own), place),
            ),
            scratch_shapes=[pltpu.VMEM((own, depth), jnp.bfloat16)],
        ),
        input_output_aliases={5 + k: k for k in range(len(held))},
        cost_estimate=short,
        name="push",
    )(span_index.reshape(1), grads, slope, down, merge, *held)


def pull_kernel(mixed_ref, hidden_ref, proj_ref, up_ref, tokens_ref, out_ref, sums_ref, unit_ref):
    unit_ref[...] = normalize(tokens_ref[...])[0]
    begun = pl.program_id(0) > 0

    def column(cols):
        partial_grad = dot_last(mixed_ref[...], proj_ref[cols, :]) + dot_last(
            hidden_ref[...], up_ref[cols, :]
        )
        out_ref[:, cols] = partial_grad.astype(out_ref.dtype)
        gain = jnp.sum(partial_grad * unit_ref[:, cols], axis=0, keepdims=True)
        bias = jnp.sum(partial_grad, axis=0, keepdims=True)
        both = jnp.concatenate([gain, bias], axis=0)
        sums_ref[:, cols] = jnp.where(begun, sums_ref[:, cols], 0.0) + both

    in_chunks(proj_ref.shape[0], 256, column)


def pull(slot, mixed, hidden_grad, proj, up, tokens, kept):
    rows, depth = tokens.shape
    half = rows // 2
    return pl.pallas_call(
        pull_kernel,
        out_shape=(
            jax.ShapeDtypeStruct((rows, depth), kept),
            jax.ShapeDtypeStruct((2, depth), jnp.float32),
        ),
        grid=(2,),
        in_specs=[
            pl.BlockSpec((half, mixed.shape[1]), lambda i: (2 * slot + i, 0)),
            pl.BlockSpec((half, hidden_grad.shape[1]), lambda i: (2 * slot + i, 0)),
            pl.BlockSpec(proj.shape, lambda i: (0, 0)),
            pl.BlockSpec(up.shape, lambda i: (0, 0)),
            pl.BlockSpec((half, depth), lambda i: (i, 0)),
        ],
        out_specs=(
            pl.BlockSpec((half, depth), lambda i: (i, 0)),
            pl.BlockSpec((2, depth), lambda i: (0, 0)),
        ),
        scratch_shapes=[pltpu.VMEM((half, depth), jnp.float32)],
        cost_estimate=short,
        name="pull",
    )(mixed, hidden_grad, proj, up, tokens)


def project_all_kernel(index_ref, rows_ref, cos_ref, sin_ref, *refs):
    unit_refs, (out_ref, weight_ref) = refs[:-2], refs[-2:]

    @pl.when(pl.program_id(0) == 0)
    def _():
        for c, unit_ref in enumerate(unit_refs):
            weight_ref[:, c * LANES : (c + 1) * LANES] = unit_ref[...].reshape(D, LANES)

    project_kernel(rows_ref, weight_ref, cos_ref, sin_ref, out_ref)


def project_all(rows, weight_all, span_index, own_width, cosine, sine):
    count, depth = rows.shape
    shards, narrow_count, shard_rows, cols = weight_all.shape
    units = own_width // LANES
    width = 3 * own_width
    per_shard = cols // LANES
    per_part = D // LANES
    block = min(ROW_BLOCK, count)

    def source(c, i, index_ref):
        unit = (c % 3) * per_part + index_ref[0] * units + c // 3
        return (unit // per_shard, 0, 0, unit % per_shard)

    return pl.pallas_call(
        project_all_kernel,
        out_shape=(
            jax.ShapeDtypeStruct((count, width), jnp.bfloat16),
            jax.ShapeDtypeStruct((D, width), jnp.bfloat16),
        ),
        grid_spec=pltpu.PrefetchScalarGridSpec(
            num_scalar_prefetch=1,
            grid=(count // block,),
            in_specs=[
                pl.BlockSpec((block, depth), lambda i, index_ref: (i, 0)),
                pl.BlockSpec((block, LANES), lambda i, index_ref: (i, 0)),
                pl.BlockSpec((block, LANES), lambda i, index_ref: (i, 0)),
            ]
            + [
                pl.BlockSpec((1, narrow_count, shard_rows, LANES), partial(source, c))
                for c in range(3 * units)
            ],
            out_specs=(
                pl.BlockSpec((block, width), lambda i, index_ref: (i, 0)),
                pl.BlockSpec((D, width), lambda i, index_ref: (0, 0)),
            ),
        ),
        cost_estimate=short,
        name="project_all",
    )(span_index.reshape(1), rows, cosine, sine, *[weight_all] * (3 * units))


def turn_kernel(slots_ref, all_ref, out_ref):
    unused, narrow_count, rows, cols = all_ref.shape
    for t in range(narrow_count):
        out_ref[t * rows : (t + 1) * rows, :] = all_ref[0, slots_ref[t]]


def pick_merge(weight_all, slots, own_width):
    shards, narrow_count, rows, cols = weight_all.shape
    return pl.pallas_call(
        turn_kernel,
        out_shape=jax.ShapeDtypeStruct((D, D), jnp.bfloat16),
        grid_spec=pltpu.PrefetchScalarGridSpec(
            num_scalar_prefetch=1,
            grid=(shards,),
            in_specs=[
                pl.BlockSpec(
                    (1, narrow_count, rows, LANES),
                    lambda j, slots_ref: (j, 0, 0, 0),
                )
            ],
            out_specs=pl.BlockSpec((D, LANES), lambda j, slots_ref: (0, j)),
        ),
        cost_estimate=short,
        name="pick_merge",
    )(slots, weight_all)


def head_lanes(field, head):
    lane = lax.broadcasted_iota(jnp.int32, field.shape, 1)
    keep = (lane >= head * HEAD) & (lane < (head + 1) * HEAD)
    return jnp.where(keep, field, jnp.zeros_like(field))


def pair_allowed(start_row, key_first, key_count, query_first, query_count):
    key_index = key_first + lax.broadcasted_iota(jnp.int32, (key_count, query_count), 0)
    query_index = query_first + lax.broadcasted_iota(jnp.int32, (key_count, query_count), 1)
    return (key_index >= start_row) & (key_index <= query_index)


def attend_kernel(
    block_q,
    block_k,
    heads_in,
    slots_ref,
    first_ref,
    last_ref,
    start_ref,
    query_ref,
    key_ref,
    value_ref,
    *refs,
):
    out_ref, tall_ref, log_ref, turned, best, total, summed = refs[-7:]
    index = pl.program_id(0)
    key_blocks = key_ref.shape[0] // block_k

    @pl.when(index == 0)
    def _():
        for j in range(key_blocks):
            piece = value_ref[j * block_k : (j + 1) * block_k, :].astype(jnp.float32)
            turned[:, j * block_k : (j + 1) * block_k] = piece.T.astype(jnp.bfloat16)

    query_first = index * block_q
    low = first_ref[index] // block_k
    high = (query_first + block_q - 1) // block_k + 1
    start_row = start_ref[...]
    queries = [head_lanes(query_ref[...], head) for head in range(heads_in)]
    best[...] = jnp.full_like(best, masked_score)
    total[...] = jnp.zeros_like(total)
    summed[...] = jnp.zeros_like(summed)

    def visit(j, masked):
        key_rows = pl.ds(pl.multiple_of(slots_ref[j] * block_k, block_k), block_k)
        keys = key_ref[key_rows, :]
        if masked:
            allowed = pair_allowed(start_row, j * block_k, block_k, query_first, block_q)
        for head in range(heads_in):
            scores = dot_last(keys, queries[head])
            if masked:
                scores = jnp.where(allowed, scores, masked_score)
            old = best[head : head + 1, :]
            new = jnp.maximum(old, jnp.max(scores, axis=0, keepdims=True))
            weights = jnp.exp(scores - new)
            if masked:
                weights = jnp.where(allowed, weights, 0.0)
            factor = jnp.exp(old - new)
            best[head : head + 1, :] = new
            total[head : head + 1, :] = total[head : head + 1, :] * factor + jnp.sum(
                weights, axis=0, keepdims=True
            )
            rows = slice(head * HEAD, (head + 1) * HEAD)
            summed[rows, :] = summed[rows, :] * factor + dot_plain(
                turned[rows, key_rows], weights.astype(jnp.bfloat16)
            )

    def step(j, carry):
        whole = (j * block_k >= last_ref[index]) & ((j + 1) * block_k - 1 <= query_first)

        @pl.when(whole)
        def _():
            visit(j, False)

        @pl.when(jnp.logical_not(whole))
        def _():
            visit(j, True)

        return carry

    lax.fori_loop(low, high, step, 0)
    for head in range(heads_in):
        rows = slice(head * HEAD, (head + 1) * HEAD)
        weight = total[head : head + 1, :]
        tall_ref[rows, :] = summed[rows, :] / weight
        log_ref[0, head : head + 1, :] = best[head : head + 1, :] + jnp.log(weight)
    if heads_in * HEAD < LANES:
        tall_ref[heads_in * HEAD :, :] = jnp.zeros_like(tall_ref[heads_in * HEAD :, :])
    log_ref[0, heads_in:, :] = jnp.zeros_like(log_ref[0, heads_in:, :])
    out_ref[...] = tall_ref[...].T.astype(jnp.bfloat16)


def attend(pair, packed, slots, first, last, starts, heads_in, block_q, block_k, held):
    count, width = packed.shape
    pairs = width // 3 // LANES
    whole = pl.BlockSpec(memory_space=pl.ANY)
    return pl.pallas_call(
        partial(attend_kernel, block_q, block_k, heads_in),
        out_shape=(
            jax.ShapeDtypeStruct((count, pairs * LANES), jnp.bfloat16),
            jax.ShapeDtypeStruct((pairs * LANES, count), jnp.float32),
            jax.ShapeDtypeStruct((pairs, 8, count), jnp.float32),
        ),
        grid_spec=pltpu.PrefetchScalarGridSpec(
            num_scalar_prefetch=3,
            grid=(count // block_q,),
            in_specs=[
                pl.BlockSpec((1, block_q), lambda i, slots_ref, *_: (0, slots_ref[i])),
                pl.BlockSpec((block_q, LANES), lambda i, slots_ref, *_: (slots_ref[i], 3 * pair)),
                pl.BlockSpec((count, LANES), lambda i, *_: (0, 3 * pair + 1)),
                pl.BlockSpec((count, LANES), lambda i, *_: (0, 3 * pair + 2)),
            ]
            + [whole] * len(held),
            out_specs=(
                pl.BlockSpec((block_q, LANES), lambda i, slots_ref, *_: (slots_ref[i], pair)),
                pl.BlockSpec((LANES, block_q), lambda i, slots_ref, *_: (pair, slots_ref[i])),
                pl.BlockSpec((1, 8, block_q), lambda i, slots_ref, *_: (pair, 0, slots_ref[i])),
            ),
            scratch_shapes=[
                pltpu.VMEM((LANES, count), jnp.bfloat16),
                pltpu.VMEM((8, block_q), jnp.float32),
                pltpu.VMEM((8, block_q), jnp.float32),
                pltpu.VMEM((LANES, block_q), jnp.float32),
            ],
        ),
        input_output_aliases={7 + k: k for k in range(len(held))},
        cost_estimate=short,
        name="attend",
    )(slots, first, last, starts.reshape(1, count), packed, packed, packed, *held)


def attend_back_kernel(
    block_q,
    block_k,
    heads_in,
    slots_ref,
    last_ref,
    end_ref,
    start_ref,
    cos_ref,
    sin_ref,
    query_ref,
    key_ref,
    value_ref,
    tall_ref,
    log_ref,
    grad_ref,
    out_ref,
    turned,
    masked_q,
    masked_g,
    delta,
    tall_q,
    key_sum,
    value_sum,
):
    index = pl.program_id(1)
    count = query_ref.shape[0]

    def turn_back(field, rows):
        return field * cos_ref[rows, :] - partner(field) * sin_ref[rows, :]

    @pl.when(index == 0)
    def _():
        def prepare(j, carry):
            rows = pl.ds(pl.multiple_of(j * block_k, block_k), block_k)
            turned[:, rows] = key_ref[rows, :].astype(jnp.float32).T.astype(jnp.bfloat16)
            grads = grad_ref[rows, :]
            product = grads.astype(jnp.float32).T * tall_ref[:, rows]
            for head in range(heads_in):
                masked_q[head, rows, :] = head_lanes(query_ref[rows, :], head)
                masked_g[head, rows, :] = head_lanes(grads, head)
                delta[head : head + 1, rows] = jnp.sum(
                    product[head * HEAD : (head + 1) * HEAD, :], axis=0, keepdims=True
                )
            tall_q[:, rows] = jnp.zeros((LANES, block_k), jnp.float32)
            return carry

        lax.fori_loop(0, count // block_k, prepare, 0)

    key_first = index * block_k
    key_rows = pl.ds(pl.multiple_of(slots_ref[index] * block_k, block_k), block_k)
    keys = key_ref[key_rows, :]
    values = value_ref[key_rows, :]
    key_sum[...] = jnp.zeros_like(key_sum)
    value_sum[...] = jnp.zeros_like(value_sum)

    def visit(i, masked):
        query_first = i * block_q
        rows = pl.ds(pl.multiple_of(slots_ref[i] * block_q, block_q), block_q)
        if masked:
            allowed = pair_allowed(
                start_ref[0:1, rows], key_first, block_k, query_first, block_q
            )
        for head in range(heads_in):
            queries = masked_q[head, rows, :]
            grads = masked_g[head, rows, :]
            scores = dot_last(keys, queries)
            probs = jnp.exp(scores - log_ref[0, head : head + 1, rows])
            if masked:
                probs = jnp.where(allowed, probs, 0.0)
            value_sum[...] += dot_plain(probs.astype(jnp.bfloat16), grads)
            prob_grad = dot_last(values, grads)
            score_grad = (probs * (prob_grad - delta[head : head + 1, rows])).astype(jnp.bfloat16)
            key_sum[...] += dot_plain(score_grad, queries)
            lanes = slice(head * HEAD, (head + 1) * HEAD)
            tall_q[lanes, rows] += dot_plain(turned[lanes, key_rows], score_grad)

    def step(i, carry):
        whole = (key_first >= last_ref[i]) & (key_first + block_k - 1 <= i * block_q)

        @pl.when(whole)
        def _():
            visit(i, False)

        @pl.when(jnp.logical_not(whole))
        def _():
            visit(i, True)

        return carry

    lax.fori_loop(key_first // block_q, (end_ref[index] - 1) // block_q + 1, step, 0)
    out_ref[key_rows, LANES : 2 * LANES] = turn_back(key_sum[...], key_rows).astype(jnp.bfloat16)
    out_ref[key_rows, 2 * LANES :] = value_sum[...].astype(jnp.bfloat16)

    @pl.when(index == pl.num_programs(1) - 1)
    def _():
        def finish(j, carry):
            rows = pl.ds(pl.multiple_of(j * block_k, block_k), block_k)
            field = tall_q[:, rows].T * HEAD ** (-0.5)
            out_ref[rows, :LANES] = turn_back(field, rows).astype(jnp.bfloat16)
            return carry

        lax.fori_loop(0, count // block_k, finish, 0)


def attend_back(
    packed, slots, last, end, starts, cosine, sine, tall, logs, grads, heads_in, block_q, block_k
):
    count, width = packed.shape
    pairs = width // 3 // LANES
    return pl.pallas_call(
        partial(attend_back_kernel, block_q, block_k, heads_in),
        out_shape=jax.ShapeDtypeStruct((count, width), jnp.bfloat16),
        grid_spec=pltpu.PrefetchScalarGridSpec(
            num_scalar_prefetch=3,
            grid=(pairs, count // block_k),
            in_specs=[
                pl.BlockSpec((1, count), lambda p, i, *_: (0, 0)),
                pl.BlockSpec((count, LANES), lambda p, i, *_: (0, 0)),
                pl.BlockSpec((count, LANES), lambda p, i, *_: (0, 0)),
                pl.BlockSpec((count, LANES), lambda p, i, *_: (0, 3 * p)),
                pl.BlockSpec((count, LANES), lambda p, i, *_: (0, 3 * p + 1)),
                pl.BlockSpec((count, LANES), lambda p, i, *_: (0, 3 * p + 2)),
                pl.BlockSpec((LANES, count), lambda p, i, *_: (p, 0)),
                pl.BlockSpec((1, 8, count), lambda p, i, *_: (p, 0, 0)),
                pl.BlockSpec((count, LANES), lambda p, i, *_: (0, p)),
            ],
            out_specs=pl.BlockSpec((count, 3 * LANES), lambda p, i, *_: (0, p)),
            scratch_shapes=[
                pltpu.VMEM((LANES, count), jnp.bfloat16),
                pltpu.VMEM((heads_in, count, LANES), jnp.bfloat16),
                pltpu.VMEM((heads_in, count, LANES), jnp.bfloat16),
                pltpu.VMEM((8, count), jnp.float32),
                pltpu.VMEM((LANES, count), jnp.float32),
                pltpu.VMEM((block_k, LANES), jnp.float32),
                pltpu.VMEM((block_k, LANES), jnp.float32),
            ],
        ),
        compiler_params=pltpu.CompilerParams(vmem_limit_bytes=60 << 20),
        cost_estimate=short,
        name="attend_back",
    )(
        slots, last, end, starts.reshape(1, count), cosine, sine,
        packed, packed, packed, tall, logs, grads,
    )


def finish_kernel(narrow_count, wide_count, own_units, per_shard, entries, *refs):
    exchange = own_units > 0
    if exchange:
        (
            parts_ref, piece_ref, feed_ref, sent_ref, total_ref, stats_ref, arrived_ref, block_ref,
            mine, near, far, near_sum, send_near, recv_near, send_far, recv_far, send_ring, recv_ring,
            send_piece, recv_piece,
        ) = refs
    else:
        (
            parts_ref, piece_ref, feed_ref, sent_ref, total_ref, stats_ref, arrived_ref,
            mine, near, far, near_sum, send_near, recv_near, send_far, recv_far, send_ring, recv_ring,
        ) = refs
    narrow_me = lax.axis_index("narrow")
    wide_me = lax.axis_index("wide")

    def place(narrow_at, wide_at):
        return {"narrow": narrow_at, "wide": wide_at}

    def square_sum(value):
        value = value.astype(jnp.float32)
        return jnp.sum(
            jnp.sum(value * value, axis=0, keepdims=True), axis=1, keepdims=True
        )

    norm_rows = 2 * D // LANES
    row_at = lax.broadcasted_iota(jnp.int32, mine.shape, 0)
    lane_at = lax.broadcasted_iota(jnp.int32, mine.shape, 1)
    mine[...] = parts_ref[...] + jnp.where(
        (row_at == norm_rows) & (lane_at == 0),
        square_sum(piece_ref[...]) + square_sum(feed_ref[...]),
        0.0,
    )
    mesh_ids = pl.DeviceIdType.MESH
    barrier = pltpu.get_barrier_semaphore()
    greeted = 0
    for ahead in range(narrow_count):
        for across in range(wide_count):
            if (ahead > 0) + (across > 0) == 0 or (not exchange and ahead > 0 and across > 0):
                continue
            greeted += 1
            pl.semaphore_signal(
                barrier,
                inc=1,
                device_id=place(
                    lax.rem(narrow_me + ahead, narrow_count), lax.rem(wide_me + across, wide_count)
                ),
                device_id_type=mesh_ids,
            )
    pl.semaphore_wait(barrier, greeted)
    near_copies = []
    for ahead in range(1, narrow_count):
        copy = pltpu.make_async_remote_copy(
            src_ref=mine,
            dst_ref=near.at[narrow_me],
            send_sem=send_near.at[ahead - 1],
            recv_sem=recv_near.at[ahead - 1],
            device_id=place(lax.rem(narrow_me + ahead, narrow_count), wide_me),
            device_id_type=mesh_ids,
        )
        copy.start()
        near_copies.append(copy)
    near[narrow_me] = mine[...]
    if exchange:
        rows = piece_ref.shape[0]
        halves = block_ref.shape[0] // rows
        half_me = lax.rem(wide_me, halves)
        narrow_to = lax.div(wide_me, halves)
        moves = []
        for unit in range(3 * own_units):
            whole_unit = (unit % 3) * (D // LANES) + narrow_me * own_units + unit // 3
            wide_to = lax.div(whole_unit, per_shard)
            column = lax.rem(whole_unit, per_shard)
            source = piece_ref.at[:, unit * LANES : (unit + 1) * LANES]
            target = block_ref.at[
                pl.ds(pl.multiple_of(half_me * rows, rows), rows),
                pl.ds(pl.multiple_of(column * LANES, LANES), LANES),
            ]
            arrived = recv_piece.at[half_me * per_shard + column]
            remote = pltpu.make_async_remote_copy(
                src_ref=source,
                dst_ref=target,
                send_sem=send_piece.at[unit],
                recv_sem=arrived,
                device_id=place(narrow_to, wide_to),
                device_id_type=mesh_ids,
            )
            here = pltpu.make_async_copy(source, target, arrived)
            stays = (narrow_to == narrow_me) & (wide_to == wide_me)
            pl.when(jnp.logical_not(stays))(remote.start)
            pl.when(stays)(here.start)
            moves.append((stays, remote))
    for copy in near_copies:
        copy.wait()
    ring = pltpu.make_async_remote_copy(
        src_ref=sent_ref,
        dst_ref=arrived_ref,
        send_sem=send_ring,
        recv_sem=recv_ring,
        device_id=place(lax.rem(narrow_me + 1, narrow_count), wide_me),
        device_id_type=mesh_ids,
    )
    ring.start()
    value = near[0]
    for k in range(1, narrow_count):
        value = value + near[k]
    near_sum[...] = value
    far_copies = []
    for across in range(1, wide_count):
        copy = pltpu.make_async_remote_copy(
            src_ref=near_sum,
            dst_ref=far.at[wide_me],
            send_sem=send_far.at[across - 1],
            recv_sem=recv_far.at[across - 1],
            device_id=place(narrow_me, lax.rem(wide_me + across, wide_count)),
            device_id_type=mesh_ids,
        )
        copy.start()
        far_copies.append(copy)
    far[wide_me] = value
    for copy in far_copies:
        copy.wait()
    value = far[0]
    for k in range(1, wide_count):
        value = value + far[k]
    total_ref[...] = value
    grad_norm = jnp.sqrt(square_sum(value[:norm_rows]) + value[norm_rows : norm_rows + 1, 0:1])
    stats = [jnp.minimum(1.0, math.sqrt(NPARAMS) / grad_norm), grad_norm] + [
        jnp.sqrt(value[norm_rows : norm_rows + 1, k : k + 1] / entries) for k in (1, 2, 3)
    ]
    stats_ref[...] = jnp.zeros_like(stats_ref)
    for row, stat in enumerate(stats):
        stats_ref[row : row + 1, :] = jnp.broadcast_to(stat, (1, LANES))
    if exchange:
        for stays, remote in moves:
            pl.when(jnp.logical_not(stays))(remote.wait_send)
        for half in range(halves):
            for column in range(per_shard):
                pltpu.make_async_copy(
                    piece_ref.at[:, 0:LANES],
                    block_ref.at[
                        half * rows : (half + 1) * rows, column * LANES : (column + 1) * LANES
                    ],
                    recv_piece.at[half * per_shard + column],
                ).wait()
    ring.wait()


def finish(
    parts, piece, feed_piece, sent, exchange, narrow_count, wide_count, own_width, proj_cols, entries
):
    shape = parts.shape
    own_units = own_width // LANES if exchange else 0
    per_shard = proj_cols // LANES
    vmem = pl.BlockSpec(memory_space=pltpu.VMEM)
    shapes = [
        jax.ShapeDtypeStruct(shape, jnp.float32),
        jax.ShapeDtypeStruct((8, LANES), jnp.float32),
        jax.ShapeDtypeStruct(sent.shape, sent.dtype),
    ]
    whole = pl.BlockSpec(memory_space=pl.ANY)
    scratch = [
        pltpu.VMEM(shape, jnp.float32),
        pltpu.VMEM((narrow_count,) + shape, jnp.float32),
        pltpu.VMEM((wide_count,) + shape, jnp.float32),
        pltpu.VMEM(shape, jnp.float32),
        pltpu.SemaphoreType.DMA((narrow_count - 1,)),
        pltpu.SemaphoreType.DMA((narrow_count - 1,)),
        pltpu.SemaphoreType.DMA((wide_count - 1,)),
        pltpu.SemaphoreType.DMA((wide_count - 1,)),
        pltpu.SemaphoreType.DMA,
        pltpu.SemaphoreType.DMA,
    ]
    if exchange:
        shapes.append(jax.ShapeDtypeStruct((D // narrow_count, proj_cols), jnp.bfloat16))
        scratch += [
            pltpu.SemaphoreType.DMA((3 * own_units,)),
            pltpu.SemaphoreType.DMA((3 * own_units,)),
        ]
    return pl.pallas_call(
        partial(finish_kernel, narrow_count, wide_count, own_units, per_shard, entries),
        out_shape=tuple(shapes),
        in_specs=[vmem] * 3 + [whole],
        out_specs=(vmem, vmem, whole) + (vmem,) * (len(shapes) - 3),
        scratch_shapes=scratch,
        compiler_params=pltpu.CompilerParams(collective_id=0, has_side_effects=True),
        name="finish",
    )(parts, piece, feed_piece, sent)


def adam_update(
    weight, first_moment, second_moment, grad_value, step_rate, decay_coef, first_fix, second_fix
):
    new_first = beta_first * first_moment + (1.0 - beta_first) * grad_value
    new_second = beta_second * second_moment + (1.0 - beta_second) * grad_value * grad_value
    step_ratio = new_first / first_fix / (jnp.sqrt(new_second / second_fix) + adam_eps)
    return (weight - step_rate * (step_ratio + decay_coef * weight), new_first, new_second)


def adam_step(weight, first_moment, second_moment, gradient, step_rate, decay_coef, scales):
    new_first = beta_first * first_moment + (1.0 - beta_first) * gradient
    new_second = beta_second * second_moment + (1.0 - beta_second) * gradient * gradient
    ratio = new_first * scales[0] / (jnp.sqrt(new_second * scales[1]) + adam_eps)
    return (weight - step_rate * (ratio + decay_coef * weight), new_first, new_second)


def adam_kernel(scale_ref, stats_ref, grads_ref, total_ref, proj_ref, merge_ref, *refs):
    states, outs = refs[:15], refs[15:-1]
    norm_grads = refs[-1]
    matrix_step, norm_step = scale_ref[0, 0], scale_ref[0, 1]
    scales = (scale_ref[0, 2], scale_ref[0, 3])
    clip_factor = stats_ref[0:1, 0:1]

    def update(matrix, rows, gradient, step_rate, decay_coef):
        state = [ref[rows, :] for ref in states[3 * matrix : 3 * matrix + 3]]
        new = adam_step(*state, gradient * clip_factor, step_rate, decay_coef, scales)
        for out_ref, value in zip(outs[4 * matrix : 4 * matrix + 3], new):
            out_ref[rows, :] = value
        if matrix < 4:
            outs[4 * matrix + 3][rows, :] = new[0].astype(jnp.bfloat16)

    def feed_rows(rows):
        for matrix in range(2):
            gradient = grads_ref[0, matrix, rows, :].astype(jnp.float32)
            update(matrix, rows, gradient, matrix_step, decay_rate)

    in_chunks(states[0].shape[0], 32, feed_rows)

    @pl.when(pl.program_id(0) == 0)
    def _():
        def proj_rows(rows):
            update(2, rows, proj_ref[rows, :].astype(jnp.float32), matrix_step, decay_rate)

        in_chunks(proj_ref.shape[0], 64, proj_rows)
        update(3, slice(None), merge_ref[...].astype(jnp.float32).T, matrix_step, decay_rate)
        per_row = D // LANES
        for k in range(2 * per_row):
            at = k % per_row
            norm_grads[k // per_row : k // per_row + 1, at * LANES : (at + 1) * LANES] = total_ref[
                k : k + 1, :
            ]
        update(4, slice(None), norm_grads[...], norm_step, 0.0)
        outs[19][...] = norm_grads[...] * clip_factor


def adam_all(scales, stats, grads_all, total, proj_block, heads_part, own_width, states):
    count, matrices, rows, cols = grads_all.shape
    block = pl.BlockSpec((rows, cols), lambda i: (i, 0))

    def same(array):
        return pl.BlockSpec(array.shape, lambda i: (0, 0))

    feed_out = jax.ShapeDtypeStruct((count * rows, cols), jnp.float32)
    feed_copy = jax.ShapeDtypeStruct((count * rows, cols), jnp.bfloat16)
    shapes = [feed_out, feed_out, feed_out, feed_copy] * 2
    specs = [block] * 8
    for state in states[6::3]:
        full = jax.ShapeDtypeStruct(state.shape, jnp.float32)
        copy = jax.ShapeDtypeStruct(
            state.shape, jnp.float32 if state is states[12] else jnp.bfloat16
        )
        shapes += [full, full, full, copy]
        specs += [same(state)] * 4
    return pl.pallas_call(
        adam_kernel,
        out_shape=tuple(shapes),
        grid=(count,),
        in_specs=[
            pl.BlockSpec(memory_space=pltpu.SMEM),
            same(stats),
            pl.BlockSpec((1, matrices, rows, cols), lambda i: (i, 0, 0, 0)),
            same(total),
            same(proj_block),
            pl.BlockSpec((heads_part.shape[0], own_width), lambda i: (0, 3)),
        ]
        + [block] * 6
        + [same(state) for state in states[6:]],
        out_specs=tuple(specs),
        scratch_shapes=[pltpu.VMEM((2, D), jnp.float32)],
        cost_estimate=short,
        name="adam_all",
    )(scales, stats, grads_all, total, proj_block, heads_part, *states)


def settle_kernel(arrived_ref, term_ref, tokens_ref, cotangent_ref, params_ref, out_ref):
    unit, inv_std = normalize(tokens_ref[...])
    unit_grad = (arrived_ref[...].astype(jnp.float32) + term_ref[...]) * params_ref[0:1, :]
    out_ref[...] = cotangent_ref[...].astype(jnp.float32) + inv_std * (
        unit_grad
        - jnp.mean(unit_grad, axis=1, keepdims=True)
        - unit * jnp.mean(unit_grad * unit, axis=1, keepdims=True)
    )


def settle(arrived, term, tokens, cotangent, params):
    rows, depth = tokens.shape
    block = pl.BlockSpec((rows // 8, depth), lambda i: (i, 0))
    return pl.pallas_call(
        settle_kernel,
        out_shape=jax.ShapeDtypeStruct((rows, depth), jnp.float32),
        grid=(8,),
        in_specs=[block] * 4 + [pl.BlockSpec((2, depth), lambda i: (0, 0))],
        out_specs=block,
        cost_estimate=short,
        name="settle",
    )(arrived, term, tokens, cotangent, params)


def shards(
    tokens,
    cotangent,
    seq_lengths,
    step_count,
    norm_params,
    norm_first,
    norm_second,
    proj_weight,
    proj_first,
    proj_second,
    merge_weight,
    merge_first,
    merge_second,
    up_weight,
    up_first,
    up_second,
    down_weight,
    down_first,
    down_second,
):
    tok_rows = tokens.shape[0]
    narrow_count = lax.axis_size("narrow")
    wide_count = lax.axis_size("wide")
    span_index = lax.axis_index("narrow")
    group_rows = tok_rows * narrow_count
    own_width = HEADS // narrow_count * HEAD
    held_width = max(own_width, LANES)
    heads_in = min(own_width, LANES) // HEAD
    shard_rows = D // narrow_count
    proj_cols = proj_weight.shape[1]
    lengths = seq_lengths[0]
    onward = [(i, (i + 1) % narrow_count) for i in range(narrow_count)]
    slots = lax.rem(
        span_index + narrow_count - jnp.arange(narrow_count, dtype=jnp.int32), narrow_count
    )

    def pad_lanes(array, axis):
        extra = [(0, 0)] * array.ndim
        extra[axis] = (0, held_width - own_width)
        return jnp.pad(array, extra) if held_width > own_width else array

    def meet(*values):
        return lax.optimization_barrier(values)

    def send_on(array):
        return lax.ppermute(array, "narrow", onward)

    def rows_of(array, slot):
        return array[slot * tok_rows : (slot + 1) * tok_rows]

    direct = own_width % LANES == 0 and proj_cols % LANES == 0 and merge_weight.shape[1] == LANES
    weight_part = jnp.concatenate(
        [proj_weight.astype(jnp.bfloat16), merge_weight.astype(jnp.bfloat16)], axis=1
    )
    weight_rows = lax.all_gather(weight_part, "narrow", axis=0, tiled=True)
    up_slice = up_weight.astype(jnp.bfloat16)
    down_slice = down_weight.astype(jnp.bfloat16)

    def wide_all(array):
        return lax.all_gather(array, "wide", axis=0).reshape(
            wide_count, narrow_count, shard_rows, -1
        )

    order = list(range(1, narrow_count)) + [0]
    pairs = held_width // LANES
    token_blocks = [tokens]
    held = ()
    for slot in range(narrow_count - 1):
        moving = send_on(token_blocks[slot])
        held = feed(slot, narrow_count, token_blocks[slot], norm_params, up_slice, held)
        if slot > 0:
            ready = [slot - 1, slot] if slot == narrow_count - 2 else [slot - 1]
            for block in ready:
                kept = jnp.bfloat16 if block == 1 else jnp.float32
                branch_terms.append(down_term(block, narrow_count, held[1], down_slice, kept))
            if slot == 2:
                if direct:
                    merge_turn = pick_merge(merge_all, slots, own_width)
                else:
                    merge_turn = jnp.take(
                        jnp.transpose(merge_all, (1, 2, 0, 3)).reshape(
                            narrow_count, own_width, D
                        ),
                        slots,
                        axis=0,
                    ).reshape(D, D)
                moving, merge_turn = meet(moving, merge_turn)
            moving, held, branch_terms, down_slice = meet(moving, held, branch_terms, down_slice)
        else:
            moving, held = meet(moving, held)
        if slot == 0:
            lengths, slots, moving, weight_rows, down_slice = meet(
                lengths, slots, moving, weight_rows, down_slice
            )
            proj_all = wide_all(weight_rows[:, :proj_cols])
            merge_all = wide_all(weight_rows[:, proj_cols:])
            branch_terms = []
        if slot == 1:
            places = (
                slots[:, None] * tok_rows + jnp.arange(tok_rows, dtype=jnp.int32)[None, :]
            ).reshape(group_rows)
            seq_start, unused = locate(lengths, places)
            cosine, sine = rotary_tables(places - seq_start)
            block_first = jnp.arange(narrow_count, dtype=jnp.int32) * tok_rows
            first_start, unused = locate(lengths, block_first)
            last_start, last_end = locate(lengths, block_first + (tok_rows - 1))
            moving, cosine, sine, first_start, last_start, last_end = meet(
                moving, cosine, sine, first_start, last_start, last_end
            )
        token_blocks.append(moving)
    grad_first, last_block = meet(cotangent, token_blocks[-1])
    token_blocks[-1] = last_block
    grad_blocks = [grad_first]

    moving = send_on(grad_first)
    gathered, activated, slope = feed(
        narrow_count - 1, narrow_count, last_block, norm_params, up_slice, held
    )
    if direct:
        packed, proj_own = project_all(
            gathered, proj_all, span_index, own_width, cosine, sine
        )
        merge_own = merge_all
    else:
        proj_copy = jnp.transpose(proj_all, (1, 2, 0, 3)).reshape(
            D, 3, narrow_count, own_width
        )
        proj_own = pad_lanes(
            lax.dynamic_index_in_dim(proj_copy, span_index, axis=2, keepdims=False), 2
        ).reshape(D, 3 * held_width)
        merge_copy = jnp.transpose(merge_all, (1, 2, 0, 3)).reshape(
            narrow_count, own_width, D
        )
        merge_own = pad_lanes(
            lax.dynamic_index_in_dim(merge_copy, span_index, axis=0, keepdims=False), 0
        )
        packed = project(gathered, proj_own, cosine, sine)

    def push_slot(slot, push_held):
        return push(
            slot, narrow_count, grad_blocks[slot], slope, down_slice, merge_own, span_index,
            push_held,
        )

    push_held = push_slot(0, ())
    branch_terms.append(
        down_term(narrow_count - 1, narrow_count, activated, down_slice, jnp.float32)
    )
    moving, packed, activated, slope, push_held, branch_terms = meet(
        moving, packed, activated, slope, push_held, branch_terms
    )
    grad_blocks.append(moving)

    def wide_sum(grad):
        return lax.psum_scatter(grad, "wide", scatter_dimension=0, tiled=True)

    def attend_pair(pair, attended_held):
        return attend(
            pair, packed, slots, first_start, last_start, seq_start,
            heads_in, tok_rows, tok_rows, attended_held,
        )

    attended_held = ()
    for hop in range(2, narrow_count):
        moving = send_on(grad_blocks[-1])
        if hop - 2 < pairs:
            attended_held = attend_pair(hop - 2, attended_held)
        push_held = push_slot(hop - 1, push_held)
        moving, attended_held, push_held = meet(moving, attended_held, push_held)
        grad_blocks.append(moving)
    for pair in range(narrow_count - 2, pairs):
        attended_held = attend_pair(pair, attended_held)
    attended, tall, logs = attended_held

    moving = send_on(branch_terms[1])
    push_held = push_slot(narrow_count - 1, push_held)
    grads_all, hidden_grad, attended_grad = push_held
    part_rows = D // wide_count
    if direct:
        feed_grad = outer(wide_count, gathered, hidden_grad, activated, grads_all)
    else:
        down_grad = dot_first(activated, grads_all).astype(jnp.bfloat16)
        up_grad = dot_first(gathered, hidden_grad).astype(jnp.bfloat16)
        feed_grad = jnp.stack(
            [
                up_grad.reshape(wide_count, part_rows, -1),
                down_grad.reshape(wide_count, part_rows, -1),
            ],
            axis=1,
        )
    feed_grad = feed_grad.reshape(2 * D, -1)
    pieces = [
        rows_of(attended, (narrow_count - ahead) % narrow_count)[:, :own_width]
        for ahead in range(narrow_count)
    ]
    moving, pieces, feed_grad, attended_grad = meet(moving, pieces, feed_grad, attended_grad)
    feed_part = wide_sum(feed_grad)

    for ahead in range(1, narrow_count):
        pieces[ahead] = lax.ppermute(
            pieces[ahead],
            "narrow",
            [(i, (i + ahead) % narrow_count) for i in range(narrow_count)],
        )
    terms = []
    norm_part = jnp.zeros((2, D), jnp.float32)

    def pull_more(count, mixed, norm_part):
        for slot in order[len(terms) : len(terms) + count]:
            kept = jnp.float32 if terms else jnp.bfloat16
            term, sums = pull(
                slot, mixed, hidden_grad, proj_own, up_slice, token_blocks[slot], kept
            )
            terms.append(term)
            norm_part = norm_part + sums
        return norm_part

    for place, slot in enumerate(order[1:-1]):
        moving = send_on((moving.astype(jnp.float32) + branch_terms[slot]).astype(jnp.bfloat16))
        if place == 0:
            mixed_grad = attend_back(
                packed, slots, last_start, last_end, seq_start, cosine, sine,
                tall, logs, attended_grad, heads_in, tok_rows, tok_rows,
            )
            if direct:
                heads_grad = outer(0, gathered, mixed_grad, grads_all, attended)
            else:
                proj_grad = dot_first(gathered, mixed_grad).astype(jnp.bfloat16)
                merge_grad = dot_first(grads_all, attended).astype(jnp.bfloat16)
                proj_grad = proj_grad.reshape(D, 3, held_width)[:, :, :own_width]
                heads_grad = jnp.concatenate(
                    [proj_grad.reshape(D, 3 * own_width), merge_grad[:, :own_width]], axis=1
                )
            moving, pieces, mixed_grad, heads_grad, feed_part = meet(
                moving, pieces, mixed_grad, heads_grad, feed_part
            )
            heads_part = wide_sum(heads_grad)
        else:
            norm_part = pull_more(3, mixed_grad, norm_part)
            moving, terms, norm_part, feed_part = meet(moving, terms, norm_part, feed_part)
        if place == narrow_count - 3:
            feed_all = lax.all_gather(feed_part, "wide", axis=0).reshape(
                wide_count, 2, part_rows, -1
            )
    branch_moving = moving
    moving = send_on(terms[0])
    norm_part = pull_more(narrow_count, mixed_grad, norm_part)
    branch = branch_moving.astype(jnp.float32) + branch_terms[0]
    merged = dot_plain(jnp.concatenate(pieces, axis=1), merge_turn)
    output_rows = tokens.astype(jnp.float32) + merged + branch
    layer_out = output_rows.astype(jnp.bfloat16)

    def squares(array):
        value = array.astype(jnp.float32)
        return jnp.sum(value * value)

    row_squares = [squares(output_rows), squares(merged), squares(branch)]
    scalars = jnp.stack([jnp.zeros((), jnp.float32)] + row_squares)
    parts = jnp.concatenate(
        [norm_part.reshape(2 * D // LANES, LANES), jnp.pad(scalars, (0, LANES - 4))[None, :]]
    )
    parts = jnp.pad(parts, ((0, 7), (0, 0)))
    step_value = step_count[0].astype(jnp.float32)
    first_fix = 1.0 - jnp.power(beta_first, step_value)
    second_fix = 1.0 - jnp.power(beta_second, step_value)
    ramp = jnp.minimum(1.0, step_value / warmup_steps)
    scales = jnp.stack(
        [matrix_rate * ramp, norm_rate * ramp, 1.0 / first_fix, 1.0 / second_fix]
    ).reshape(1, 4)
    entries = wide_count * group_rows * D
    for place in range(1, narrow_count - 1):
        if place == narrow_count - 3:
            moving, parts, heads_part, scales = meet(moving, parts, heads_part, scales)
        sent = (moving.astype(jnp.float32) + terms[place]).astype(jnp.bfloat16)
        if place == narrow_count - 3:
            total, stats, moving, *proj_block = finish(
                parts, heads_part, feed_part, sent, direct, narrow_count, wide_count, own_width,
                proj_cols, entries,
            )
            continue
        if place == narrow_count - 2:
            sent, total, stats, proj_block = meet(sent, total, stats, proj_block)
        moving = send_on(sent)

    if direct:
        updated = adam_all(
            scales, stats, feed_all, total, proj_block[0], heads_part, own_width,
            [
                up_weight, up_first, up_second, down_weight, down_first, down_second,
                proj_weight, proj_first, proj_second, merge_weight, merge_first, merge_second,
                norm_params, norm_first, norm_second,
            ],
        )
    else:
        clip_factor = stats[0, 0:1]
        cross = lax.all_gather(heads_part[:, : 3 * own_width], "narrow", axis=0).reshape(
            narrow_count, part_rows, 3, own_width
        )
        cross = jnp.transpose(cross, (1, 2, 0, 3)).reshape(part_rows, wide_count, proj_cols)
        cross = lax.all_to_all(jnp.transpose(cross, (1, 0, 2)), "wide", 0, 0)
        proj_block = lax.dynamic_slice_in_dim(
            cross.reshape(D, proj_cols), span_index * shard_rows, shard_rows, axis=0
        )
        merge_block = heads_part[:, 3 * own_width :].T
        norm_total = total[: 2 * D // LANES].reshape(2, D)
        feed_sums = feed_all.astype(jnp.float32)
        updated = []
        for state, gradient, step_rate, decay_coef in (
            ((up_weight, up_first, up_second), feed_sums[:, 0], matrix_rate, decay_rate),
            ((down_weight, down_first, down_second), feed_sums[:, 1], matrix_rate, decay_rate),
            ((proj_weight, proj_first, proj_second), proj_block, matrix_rate, decay_rate),
            ((merge_weight, merge_first, merge_second), merge_block, matrix_rate, decay_rate),
            ((norm_params, norm_first, norm_second), norm_total, norm_rate, 0.0),
        ):
            clipped = gradient.reshape(state[0].shape).astype(jnp.float32) * clip_factor
            new = adam_update(
                *state, clipped, step_rate * ramp, decay_coef, first_fix, second_fix
            )
            updated += [*new, clipped if state[0] is norm_params else new[0].astype(jnp.bfloat16)]
    new_up, new_down, new_proj, new_merge, new_norm = [
        updated[4 * k : 4 * k + 4] for k in range(5)
    ]
    moving, new_up = meet(moving, new_up)
    input_grad = settle(moving, terms[-1], tokens, cotangent, norm_params)
    return (
        layer_out,
        input_grad,
        stats[1, 0:1],
        stats[2, 0:1],
        new_norm[3],
        new_norm[0],
        new_norm[1],
        new_norm[2],
        new_proj[0],
        new_proj[1],
        new_proj[2],
        new_merge[0],
        new_merge[1],
        new_merge[2],
        new_up[0],
        new_up[1],
        new_up[2],
        new_down[0],
        new_down[1],
        new_down[2],
        stats[3:5, 0],
        new_proj[3],
        new_merge[3],
        new_up[3],
        new_down[3],
    )


def solution(mesh):
    placed = (
        P(("wide", "narrow"), None),
        P(("wide", "narrow"), None),
        P("wide", None),
        P(),
        P(),
        P(),
        P(),
        P("narrow", "wide"),
        P("narrow", "wide"),
        P("narrow", "wide"),
        P("narrow", "wide"),
        P("narrow", "wide"),
        P("narrow", "wide"),
        P(None, "narrow"),
        P(None, "narrow"),
        P(None, "narrow"),
        P("narrow", None),
        P("narrow", None),
        P("narrow", None),
    )
    return jax.shard_map(
        shards,
        mesh=mesh,
        in_specs=placed,
        out_specs=(
            P(("wide", "narrow"), None),
            P(("wide", "narrow"), None),
            P(),
            P(),
            P(),
            P(),
            P(),
            P(),
            P("narrow", "wide"),
            P("narrow", "wide"),
            P("narrow", "wide"),
            P("narrow", "wide"),
            P("narrow", "wide"),
            P("narrow", "wide"),
            P(None, "narrow"),
            P(None, "narrow"),
            P(None, "narrow"),
            P("narrow", None),
            P("narrow", None),
            P("narrow", None),
            P(),
            P("narrow", "wide"),
            P("narrow", "wide"),
            P(None, "narrow"),
            P("narrow", None),
        ),
        check_vma=False,
    )
```

```python
from functools import partial
import math

import jax
import jax.numpy as jnp
from jax import lax
from jax.experimental import pallas as pl
from jax.experimental.pallas import tpu as pltpu
from jax.sharding import PartitionSpec as P

HEADS = 16
HEAD = 64
D = 1024
ROT = 16
LANES = 128
ROW_BLOCK = 512
NPARAMS = 12584960


norm_eps = 1e-05
adam_eps = 1e-08
beta_first = 0.5
beta_second = 0.5
decay_rate = 0.01
matrix_rate = 0.1
norm_rate = 1.0
warmup_steps = 20.0
masked_score = -1e30
short = pl.CostEstimate(flops=0, bytes_accessed=0, transcendentals=0)


def dot_last(left_side, right_side):
    return lax.dot_general(
        left_side, right_side, (((1,), (1,)), ((), ())), preferred_element_type=jnp.float32
    )


def dot_plain(left_side, right_side):
    return lax.dot_general(
        left_side, right_side, (((1,), (0,)), ((), ())), preferred_element_type=jnp.float32
    )


def dot_first(left_side, right_side):
    return lax.dot_general(
        left_side, right_side, (((0,), (0,)), ((), ())), preferred_element_type=jnp.float32
    )


def in_chunks(total, chunk, body):
    def step(index, carry):
        body(pl.ds(pl.multiple_of(index * chunk, chunk), chunk))
        return carry

    lax.fori_loop(0, total // chunk, step, 0)


def locate(lengths, token_index):
    seq_ends = jnp.cumsum(lengths)
    starts = seq_ends - lengths
    segment = jnp.sum(
        (seq_ends[None, :] <= token_index[:, None]).astype(jnp.int32), axis=1, dtype=jnp.int32
    )
    choose = segment[:, None] == jnp.arange(lengths.shape[0], dtype=jnp.int32)[None, :]
    seq_start = jnp.sum(jnp.where(choose, starts[None, :], 0), axis=1, dtype=jnp.int32)
    seq_end = jnp.sum(jnp.where(choose, seq_ends[None, :], 0), axis=1, dtype=jnp.int32)
    return (seq_start, seq_end)


def rotary_tables(position):
    half_rot = ROT // 2
    frequency = jnp.power(10000.0, -2.0 * jnp.arange(half_rot, dtype=jnp.float32) / ROT)
    row = jnp.concatenate([frequency, frequency, jnp.zeros((HEAD - ROT,), jnp.float32)])
    row = jnp.tile(row, LANES // HEAD)
    sign = jnp.where(jnp.arange(LANES) % HEAD < half_rot, -1.0, 1.0)
    phases = position.astype(jnp.float32)[:, None] * row[None, :]
    return (jnp.cos(phases), jnp.sin(phases) * sign[None, :])


def partner(field):
    half_rot = ROT // 2
    lane = lax.broadcasted_iota(jnp.int32, field.shape, 1) % HEAD
    return jnp.where(
        lane < half_rot,
        pltpu.roll(field, LANES - half_rot, 1),
        pltpu.roll(field, half_rot, 1),
    )


def project_kernel(rows_ref, weight_ref, cos_ref, sin_ref, out_ref):
    def pair(index, carry):
        first = pl.multiple_of(index * 3 * LANES, LANES)
        projected = dot_plain(rows_ref[...], weight_ref[:, pl.ds(first, 3 * LANES)])
        for part in range(3):
            piece = projected[:, part * LANES : (part + 1) * LANES]
            if part < 2:
                piece = piece * cos_ref[...] + partner(piece) * sin_ref[...]
            if part == 0:
                piece = piece * HEAD ** (-0.5)
            out_ref[:, pl.ds(first + part * LANES, LANES)] = piece.astype(jnp.bfloat16)
        return carry

    lax.fori_loop(0, out_ref.shape[1] // (3 * LANES), pair, 0)


def project(rows, weight, cosine, sine):
    count, depth = rows.shape
    width = weight.shape[1]
    block = min(ROW_BLOCK, count)
    return pl.pallas_call(
        project_kernel,
        out_shape=jax.ShapeDtypeStruct((count, width), jnp.bfloat16),
        grid=(count // block,),
        in_specs=[
            pl.BlockSpec((block, depth), lambda i: (i, 0)),
            pl.BlockSpec((depth, width), lambda i: (0, 0)),
            pl.BlockSpec((block, LANES), lambda i: (i, 0)),
            pl.BlockSpec((block, LANES), lambda i: (i, 0)),
        ],
        out_specs=pl.BlockSpec((block, width), lambda i: (i, 0)),
        cost_estimate=short,
        name="project",
    )(rows, weight, cosine, sine)


def normalize(tokens):
    residual = tokens.astype(jnp.float32)
    center = residual - jnp.mean(residual, axis=1, keepdims=True)
    inv_std = lax.rsqrt(jnp.mean(center * center, axis=1, keepdims=True) + norm_eps)
    return (center * inv_std, inv_std)


def feed_kernel(tokens_ref, params_ref, weight_ref, *refs):
    normed_ref, act_ref, slope_ref = refs[-3:]
    unit, unused = normalize(tokens_ref[...])
    normed_ref[...] = (unit * params_ref[0:1, :] + params_ref[1:2, :]).astype(jnp.bfloat16)
    width = act_ref.shape[1]

    def column(cols):
        hidden = dot_plain(normed_ref[...], weight_ref[:, cols])
        share = 0.5 + 0.5 * lax.erf(hidden * math.sqrt(0.5))
        bell = jnp.exp(hidden * hidden * -0.5) * (1.0 / math.sqrt(2.0 * math.pi))
        act_ref[:, cols] = (hidden * share).astype(jnp.bfloat16)
        slope_ref[:, cols] = share + hidden * bell

    in_chunks(width, min(256, width), column)


def feed(slot, slots, tokens, params, weight, held):
    rows, depth = tokens.shape
    width = weight.shape[1]
    whole = pl.BlockSpec(memory_space=pl.ANY)
    return pl.pallas_call(
        feed_kernel,
        out_shape=(
            jax.ShapeDtypeStruct((slots * rows, depth), jnp.bfloat16),
            jax.ShapeDtypeStruct((slots * rows, width), jnp.bfloat16),
            jax.ShapeDtypeStruct((slots * rows, width), jnp.float32),
        ),
        grid=(2,),
        in_specs=[
            pl.BlockSpec((rows // 2, depth), lambda i: (i, 0)),
            pl.BlockSpec((2, depth), lambda i: (0, 0)),
            pl.BlockSpec((depth, width), lambda i: (0, 0)),
        ]
        + [whole] * len(held),
        out_specs=(
            pl.BlockSpec((rows // 2, depth), lambda i: (2 * slot + i, 0)),
            pl.BlockSpec((rows // 2, width), lambda i: (2 * slot + i, 0)),
            pl.BlockSpec((rows // 2, width), lambda i: (2 * slot + i, 0)),
        ),
        input_output_aliases={3 + k: k for k in range(len(held))},
        cost_estimate=short,
        name="feed",
    )(tokens, params, weight, *held)


def down_kernel(active_ref, down_ref, out_ref):
    def column(cols):
        out_ref[:, cols] = dot_plain(active_ref[...], down_ref[:, cols]).astype(out_ref.dtype)

    in_chunks(out_ref.shape[1], 512, column)


def down_term(slot, slots, activated, down, kept):
    rows = activated.shape[0] // slots
    width, depth = down.shape
    half = rows // 2
    return pl.pallas_call(
        down_kernel,
        out_shape=jax.ShapeDtypeStruct((rows, depth), kept),
        grid=(2,),
        in_specs=[
            pl.BlockSpec((half, width), lambda i: (2 * slot + i, 0)),
            pl.BlockSpec((width, depth), lambda i: (0, 0)),
        ],
        out_specs=pl.BlockSpec((half, depth), lambda i: (i, 0)),
        cost_estimate=short,
        name="down_term",
    )(activated, down)


def outer_kernel(split, first_left, first_right, second_left, second_right, out_ref, first, second):
    begun = pl.program_id(0) > 0
    for left_ref, right_ref, total in (
        (first_left, first_right, first),
        (second_left, second_right, second),
    ):

        def chunk(rows):
            term = dot_first(left_ref[:, rows], right_ref[...])
            total[rows, :] = jnp.where(begun, total[rows, :], 0.0) + term

        in_chunks(total.shape[0], 512, chunk)

    @pl.when(pl.program_id(0) == pl.num_programs(0) - 1)
    def _():
        if split:
            blocks, unused, rows, cols = out_ref.shape

            def write(block, carry):
                at = pl.ds(pl.multiple_of(block * rows, rows), rows)
                out_ref[block, 0] = first[at, :].astype(jnp.bfloat16)
                out_ref[block, 1] = second[at, :].astype(jnp.bfloat16)
                return carry

            lax.fori_loop(0, blocks, write, 0)
        else:
            width = first.shape[1]

            def write_rows(rows):
                out_ref[rows, :width] = first[rows, :].astype(jnp.bfloat16)
                out_ref[rows, width:] = second[rows, :].astype(jnp.bfloat16)

            in_chunks(first.shape[0], 128, write_rows)


def outer(blocks, first_left, first_right, second_left, second_right):
    count, depth = first_left.shape
    rows = min(ROW_BLOCK, count)
    widths = [first_right.shape[1], second_right.shape[1]]
    shape = (blocks, 2, depth // blocks, widths[0]) if blocks else (depth, sum(widths))
    operands = (first_left, first_right, second_left, second_right)
    return pl.pallas_call(
        partial(outer_kernel, bool(blocks)),
        out_shape=jax.ShapeDtypeStruct(shape, jnp.bfloat16),
        grid=(count // rows,),
        in_specs=[pl.BlockSpec((rows, array.shape[1]), lambda k: (k, 0)) for array in operands],
        out_specs=pl.BlockSpec(shape, lambda k: (0,) * len(shape)),
        scratch_shapes=[pltpu.VMEM((depth, width), jnp.float32) for width in widths],
        cost_estimate=short,
        name="outer",
    )(*operands)


def push_kernel(index_ref, grad_ref, slope_ref, down_ref, merge_ref, *refs):
    all_ref, hidden_ref, attended_ref, merge_own = refs[-4:]

    @pl.when(pl.program_id(0) == 0)
    def _():
        if len(merge_ref.shape) == 4:
            for w in range(merge_ref.shape[0]):
                merge_own[:, w * LANES : (w + 1) * LANES] = merge_ref[w, 0]
        else:
            merge_own[...] = merge_ref[...]

    grads = grad_ref[...]
    all_ref[...] = grads
    hidden_ref[...] = (dot_last(grads, down_ref[...]) * slope_ref[...]).astype(jnp.bfloat16)
    attended_ref[...] = dot_last(grads, merge_own[...]).astype(jnp.bfloat16)


def push(slot, slots, grads, slope, down, merge, span_index, held):
    rows, depth = grads.shape
    width = slope.shape[1]
    half = rows // 2
    whole = pl.BlockSpec(memory_space=pl.ANY)
    if merge.ndim == 4:
        own = merge.shape[2]
        merge_spec = pl.BlockSpec(
            (merge.shape[0], 1, own, LANES), lambda i, index_ref: (0, index_ref[0], 0, 0)
        )
    else:
        own = merge.shape[0]
        merge_spec = pl.BlockSpec(merge.shape, lambda i, index_ref: (0, 0))

    def place(i, index_ref):
        return (2 * slot + i, 0)

    return pl.pallas_call(
        push_kernel,
        out_shape=(
            jax.ShapeDtypeStruct((slots * rows, depth), jnp.bfloat16),
            jax.ShapeDtypeStruct((slots * rows, width), jnp.bfloat16),
            jax.ShapeDtypeStruct((slots * rows, own), jnp.bfloat16),
        ),
        grid_spec=pltpu.PrefetchScalarGridSpec(
            num_scalar_prefetch=1,
            grid=(2,),
            in_specs=[
                pl.BlockSpec((half, depth), lambda i, index_ref: (i, 0)),
                pl.BlockSpec((half, width), place),
                pl.BlockSpec(down.shape, lambda i, index_ref: (0, 0)),
                merge_spec,
            ]
            + [whole] * len(held),
            out_specs=(
                pl.BlockSpec((half, depth), place),
                pl.BlockSpec((half, width), place),
                pl.BlockSpec((half, own), place),
            ),
            scratch_shapes=[pltpu.VMEM((own, depth), jnp.bfloat16)],
        ),
        input_output_aliases={5 + k: k for k in range(len(held))},
        cost_estimate=short,
        name="push",
    )(span_index.reshape(1), grads, slope, down, merge, *held)


def pull_kernel(blocks, mixed_ref, hidden_ref, proj_ref, up_ref, *refs):
    tokens_refs, (lead_ref, out_ref, sums_ref, rows_ref) = refs[:blocks], refs[blocks:]
    index = pl.program_id(0)
    for block, tokens_ref in enumerate(tokens_refs):

        @pl.when(index // 2 == block)
        def _():
            rows_ref[...] = tokens_ref[...]

    partial_grad = dot_last(mixed_ref[...], proj_ref[...]) + dot_last(hidden_ref[...], up_ref[...])
    out_ref[...] = partial_grad

    @pl.when(index < 2)
    def _():
        lead_ref[...] = partial_grad.astype(jnp.bfloat16)

    unit, unused = normalize(rows_ref[...])
    gain = jnp.sum(partial_grad * unit, axis=0, keepdims=True)
    bias = jnp.sum(partial_grad, axis=0, keepdims=True)
    both = jnp.concatenate([gain, bias], axis=0)
    sums_ref[...] = jnp.where(index > 0, sums_ref[...], 0.0) + both


def pull(slot, mixed, hidden_grad, proj, up, token_blocks):
    rows, depth = token_blocks[0].shape
    blocks = len(token_blocks)
    half = rows // 2

    def part(block, i):
        return (jnp.clip(i - 2 * block, 0, 1), 0)

    return pl.pallas_call(
        partial(pull_kernel, blocks),
        out_shape=(
            jax.ShapeDtypeStruct((rows, depth), jnp.bfloat16),
            jax.ShapeDtypeStruct((blocks * rows, depth), jnp.float32),
            jax.ShapeDtypeStruct((2, depth), jnp.float32),
        ),
        grid=(2 * blocks,),
        in_specs=[
            pl.BlockSpec((half, mixed.shape[1]), lambda i: (2 * slot + i, 0)),
            pl.BlockSpec((half, hidden_grad.shape[1]), lambda i: (2 * slot + i, 0)),
            pl.BlockSpec(proj.shape, lambda i: (0, 0)),
            pl.BlockSpec(up.shape, lambda i: (0, 0)),
        ]
        + [pl.BlockSpec((half, depth), partial(part, block)) for block in range(blocks)],
        out_specs=(
            pl.BlockSpec((half, depth), partial(part, 0)),
            pl.BlockSpec((half, depth), lambda i: (i, 0)),
            pl.BlockSpec((2, depth), lambda i: (0, 0)),
        ),
        scratch_shapes=[pltpu.VMEM((half, depth), jnp.bfloat16)],
        cost_estimate=short,
        name="pull",
    )(mixed, hidden_grad, proj, up, *token_blocks)


def project_all_kernel(index_ref, rows_ref, cos_ref, sin_ref, *refs):
    unit_refs, (out_ref, weight_ref) = refs[:-2], refs[-2:]

    @pl.when(pl.program_id(0) == 0)
    def _():
        for c, unit_ref in enumerate(unit_refs):
            weight_ref[:, c * LANES : (c + 1) * LANES] = unit_ref[...].reshape(D, LANES)

    project_kernel(rows_ref, weight_ref, cos_ref, sin_ref, out_ref)


def project_all(rows, weight_all, span_index, own_width, cosine, sine):
    count, depth = rows.shape
    shards, narrow_count, shard_rows, cols = weight_all.shape
    units = own_width // LANES
    width = 3 * own_width
    per_shard = cols // LANES
    per_part = D // LANES
    block = min(ROW_BLOCK, count)

    def source(c, i, index_ref):
        unit = (c % 3) * per_part + index_ref[0] * units + c // 3
        return (unit // per_shard, 0, 0, unit % per_shard)

    return pl.pallas_call(
        project_all_kernel,
        out_shape=(
            jax.ShapeDtypeStruct((count, width), jnp.bfloat16),
            jax.ShapeDtypeStruct((D, width), jnp.bfloat16),
        ),
        grid_spec=pltpu.PrefetchScalarGridSpec(
            num_scalar_prefetch=1,
            grid=(count // block,),
            in_specs=[
                pl.BlockSpec((block, depth), lambda i, index_ref: (i, 0)),
                pl.BlockSpec((block, LANES), lambda i, index_ref: (i, 0)),
                pl.BlockSpec((block, LANES), lambda i, index_ref: (i, 0)),
            ]
            + [
                pl.BlockSpec((1, narrow_count, shard_rows, LANES), partial(source, c))
                for c in range(3 * units)
            ],
            out_specs=(
                pl.BlockSpec((block, width), lambda i, index_ref: (i, 0)),
                pl.BlockSpec((D, width), lambda i, index_ref: (0, 0)),
            ),
        ),
        cost_estimate=short,
        name="project_all",
    )(span_index.reshape(1), rows, cosine, sine, *[weight_all] * (3 * units))


def turn_kernel(slots_ref, all_ref, out_ref):
    unused, narrow_count, rows, cols = all_ref.shape
    for t in range(narrow_count):
        out_ref[t * rows : (t + 1) * rows, :] = all_ref[0, slots_ref[t]]


def pick_merge(weight_all, slots, own_width):
    shards, narrow_count, rows, cols = weight_all.shape
    return pl.pallas_call(
        turn_kernel,
        out_shape=jax.ShapeDtypeStruct((D, D), jnp.bfloat16),
        grid_spec=pltpu.PrefetchScalarGridSpec(
            num_scalar_prefetch=1,
            grid=(shards,),
            in_specs=[
                pl.BlockSpec(
                    (1, narrow_count, rows, LANES),
                    lambda j, slots_ref: (j, 0, 0, 0),
                )
            ],
            out_specs=pl.BlockSpec((D, LANES), lambda j, slots_ref: (0, j)),
        ),
        cost_estimate=short,
        name="pick_merge",
    )(slots, weight_all)


def head_lanes(field, head):
    lane = lax.broadcasted_iota(jnp.int32, field.shape, 1)
    keep = (lane >= head * HEAD) & (lane < (head + 1) * HEAD)
    return jnp.where(keep, field, jnp.zeros_like(field))


def pair_allowed(start_row, key_first, key_count, query_first, query_count):
    key_index = key_first + lax.broadcasted_iota(jnp.int32, (key_count, query_count), 0)
    query_index = query_first + lax.broadcasted_iota(jnp.int32, (key_count, query_count), 1)
    return (key_index >= start_row) & (key_index <= query_index)


def attend_kernel(
    block_q,
    block_k,
    heads_in,
    slots_ref,
    first_ref,
    last_ref,
    start_ref,
    query_ref,
    key_ref,
    value_ref,
    *refs,
):
    out_ref, tall_ref, log_ref, turned, best, total, summed = refs[-7:]
    index = pl.program_id(0)
    key_blocks = key_ref.shape[0] // block_k

    @pl.when(index == 0)
    def _():
        for j in range(key_blocks):
            piece = value_ref[j * block_k : (j + 1) * block_k, :].astype(jnp.float32)
            turned[:, j * block_k : (j + 1) * block_k] = piece.T.astype(jnp.bfloat16)

    query_first = index * block_q
    low = first_ref[index] // block_k
    high = (query_first + block_q - 1) // block_k + 1
    start_row = start_ref[...]
    queries = [head_lanes(query_ref[...], head) for head in range(heads_in)]
    best[...] = jnp.full_like(best, masked_score)
    total[...] = jnp.zeros_like(total)
    summed[...] = jnp.zeros_like(summed)

    def visit(j, masked):
        key_rows = pl.ds(pl.multiple_of(slots_ref[j] * block_k, block_k), block_k)
        keys = key_ref[key_rows, :]
        if masked:
            allowed = pair_allowed(start_row, j * block_k, block_k, query_first, block_q)
        for head in range(heads_in):
            scores = dot_last(keys, queries[head])
            if masked:
                scores = jnp.where(allowed, scores, masked_score)
            old = best[head : head + 1, :]
            new = jnp.maximum(old, jnp.max(scores, axis=0, keepdims=True))
            weights = jnp.exp(scores - new)
            if masked:
                weights = jnp.where(allowed, weights, 0.0)
            factor = jnp.exp(old - new)
            best[head : head + 1, :] = new
            total[head : head + 1, :] = total[head : head + 1, :] * factor + jnp.sum(
                weights, axis=0, keepdims=True
            )
            rows = slice(head * HEAD, (head + 1) * HEAD)
            summed[rows, :] = summed[rows, :] * factor + dot_plain(
                turned[rows, key_rows], weights.astype(jnp.bfloat16)
            )

    def step(j, carry):
        whole = (j * block_k >= last_ref[index]) & ((j + 1) * block_k - 1 <= query_first)

        @pl.when(whole)
        def _():
            visit(j, False)

        @pl.when(jnp.logical_not(whole))
        def _():
            visit(j, True)

        return carry

    lax.fori_loop(low, high, step, 0)
    for head in range(heads_in):
        rows = slice(head * HEAD, (head + 1) * HEAD)
        weight = total[head : head + 1, :]
        tall_ref[rows, :] = summed[rows, :] / weight
        log_ref[0, head : head + 1, :] = best[head : head + 1, :] + jnp.log(weight)
    if heads_in * HEAD < LANES:
        tall_ref[heads_in * HEAD :, :] = jnp.zeros_like(tall_ref[heads_in * HEAD :, :])
    log_ref[0, heads_in:, :] = jnp.zeros_like(log_ref[0, heads_in:, :])
    out_ref[...] = tall_ref[...].T.astype(jnp.bfloat16)


def attend(pair, packed, slots, first, last, starts, heads_in, block_q, block_k, held):
    count, width = packed.shape
    pairs = width // 3 // LANES
    whole = pl.BlockSpec(memory_space=pl.ANY)
    return pl.pallas_call(
        partial(attend_kernel, block_q, block_k, heads_in),
        out_shape=(
            jax.ShapeDtypeStruct((count, pairs * LANES), jnp.bfloat16),
            jax.ShapeDtypeStruct((pairs * LANES, count), jnp.float32),
            jax.ShapeDtypeStruct((pairs, 8, count), jnp.float32),
        ),
        grid_spec=pltpu.PrefetchScalarGridSpec(
            num_scalar_prefetch=3,
            grid=(count // block_q,),
            in_specs=[
                pl.BlockSpec((1, block_q), lambda i, slots_ref, *_: (0, slots_ref[i])),
                pl.BlockSpec((block_q, LANES), lambda i, slots_ref, *_: (slots_ref[i], 3 * pair)),
                pl.BlockSpec((count, LANES), lambda i, *_: (0, 3 * pair + 1)),
                pl.BlockSpec((count, LANES), lambda i, *_: (0, 3 * pair + 2)),
            ]
            + [whole] * len(held),
            out_specs=(
                pl.BlockSpec((block_q, LANES), lambda i, slots_ref, *_: (slots_ref[i], pair)),
                pl.BlockSpec((LANES, block_q), lambda i, slots_ref, *_: (pair, slots_ref[i])),
                pl.BlockSpec((1, 8, block_q), lambda i, slots_ref, *_: (pair, 0, slots_ref[i])),
            ),
            scratch_shapes=[
                pltpu.VMEM((LANES, count), jnp.bfloat16),
                pltpu.VMEM((8, block_q), jnp.float32),
                pltpu.VMEM((8, block_q), jnp.float32),
                pltpu.VMEM((LANES, block_q), jnp.float32),
            ],
        ),
        input_output_aliases={7 + k: k for k in range(len(held))},
        cost_estimate=short,
        name="attend",
    )(slots, first, last, starts.reshape(1, count), packed, packed, packed, *held)


def attend_back_kernel(
    block_q,
    block_k,
    heads_in,
    slots_ref,
    last_ref,
    end_ref,
    start_ref,
    cos_ref,
    sin_ref,
    query_ref,
    key_ref,
    value_ref,
    tall_ref,
    log_ref,
    grad_ref,
    out_ref,
    turned,
    masked_q,
    masked_g,
    delta,
    tall_q,
    key_sum,
    value_sum,
):
    index = pl.program_id(1)
    count = query_ref.shape[0]

    def turn_back(field, rows):
        return field * cos_ref[rows, :] - partner(field) * sin_ref[rows, :]

    @pl.when(index == 0)
    def _():
        def prepare(j, carry):
            rows = pl.ds(pl.multiple_of(j * block_k, block_k), block_k)
            turned[:, rows] = key_ref[rows, :].astype(jnp.float32).T.astype(jnp.bfloat16)
            grads = grad_ref[rows, :]
            product = grads.astype(jnp.float32).T * tall_ref[:, rows]
            for head in range(heads_in):
                masked_q[head, rows, :] = head_lanes(query_ref[rows, :], head)
                masked_g[head, rows, :] = head_lanes(grads, head)
                delta[head : head + 1, rows] = jnp.sum(
                    product[head * HEAD : (head + 1) * HEAD, :], axis=0, keepdims=True
                )
            tall_q[:, rows] = jnp.zeros((LANES, block_k), jnp.float32)
            return carry

        lax.fori_loop(0, count // block_k, prepare, 0)

    key_first = index * block_k
    key_rows = pl.ds(pl.multiple_of(slots_ref[index] * block_k, block_k), block_k)
    keys = key_ref[key_rows, :]
    values = value_ref[key_rows, :]
    key_sum[...] = jnp.zeros_like(key_sum)
    value_sum[...] = jnp.zeros_like(value_sum)

    def visit(i, masked):
        query_first = i * block_q
        rows = pl.ds(pl.multiple_of(slots_ref[i] * block_q, block_q), block_q)
        if masked:
            allowed = pair_allowed(
                start_ref[0:1, rows], key_first, block_k, query_first, block_q
            )
        for head in range(heads_in):
            queries = masked_q[head, rows, :]
            grads = masked_g[head, rows, :]
            scores = dot_last(keys, queries)
            probs = jnp.exp(scores - log_ref[0, head : head + 1, rows])
            if masked:
                probs = jnp.where(allowed, probs, 0.0)
            value_sum[...] += dot_plain(probs.astype(jnp.bfloat16), grads)
            prob_grad = dot_last(values, grads)
            score_grad = (probs * (prob_grad - delta[head : head + 1, rows])).astype(jnp.bfloat16)
            key_sum[...] += dot_plain(score_grad, queries)
            lanes = slice(head * HEAD, (head + 1) * HEAD)
            tall_q[lanes, rows] += dot_plain(turned[lanes, key_rows], score_grad)

    def step(i, carry):
        whole = (key_first >= last_ref[i]) & (key_first + block_k - 1 <= i * block_q)

        @pl.when(whole)
        def _():
            visit(i, False)

        @pl.when(jnp.logical_not(whole))
        def _():
            visit(i, True)

        return carry

    lax.fori_loop(key_first // block_q, (end_ref[index] - 1) // block_q + 1, step, 0)
    out_ref[key_rows, LANES : 2 * LANES] = turn_back(key_sum[...], key_rows).astype(jnp.bfloat16)
    out_ref[key_rows, 2 * LANES :] = value_sum[...].astype(jnp.bfloat16)

    @pl.when(index == pl.num_programs(1) - 1)
    def _():
        def finish(j, carry):
            rows = pl.ds(pl.multiple_of(j * block_k, block_k), block_k)
            field = tall_q[:, rows].T * HEAD ** (-0.5)
            out_ref[rows, :LANES] = turn_back(field, rows).astype(jnp.bfloat16)
            return carry

        lax.fori_loop(0, count // block_k, finish, 0)


def attend_back(
    packed, slots, last, end, starts, cosine, sine, tall, logs, grads, heads_in, block_q, block_k
):
    count, width = packed.shape
    pairs = width // 3 // LANES
    return pl.pallas_call(
        partial(attend_back_kernel, block_q, block_k, heads_in),
        out_shape=jax.ShapeDtypeStruct((count, width), jnp.bfloat16),
        grid_spec=pltpu.PrefetchScalarGridSpec(
            num_scalar_prefetch=3,
            grid=(pairs, count // block_k),
            in_specs=[
                pl.BlockSpec((1, count), lambda p, i, *_: (0, 0)),
                pl.BlockSpec((count, LANES), lambda p, i, *_: (0, 0)),
                pl.BlockSpec((count, LANES), lambda p, i, *_: (0, 0)),
                pl.BlockSpec((count, LANES), lambda p, i, *_: (0, 3 * p)),
                pl.BlockSpec((count, LANES), lambda p, i, *_: (0, 3 * p + 1)),
                pl.BlockSpec((count, LANES), lambda p, i, *_: (0, 3 * p + 2)),
                pl.BlockSpec((LANES, count), lambda p, i, *_: (p, 0)),
                pl.BlockSpec((1, 8, count), lambda p, i, *_: (p, 0, 0)),
                pl.BlockSpec((count, LANES), lambda p, i, *_: (0, p)),
            ],
            out_specs=pl.BlockSpec((count, 3 * LANES), lambda p, i, *_: (0, p)),
            scratch_shapes=[
                pltpu.VMEM((LANES, count), jnp.bfloat16),
                pltpu.VMEM((heads_in, count, LANES), jnp.bfloat16),
                pltpu.VMEM((heads_in, count, LANES), jnp.bfloat16),
                pltpu.VMEM((8, count), jnp.float32),
                pltpu.VMEM((LANES, count), jnp.float32),
                pltpu.VMEM((block_k, LANES), jnp.float32),
                pltpu.VMEM((block_k, LANES), jnp.float32),
            ],
        ),
        compiler_params=pltpu.CompilerParams(vmem_limit_bytes=60 << 20),
        cost_estimate=short,
        name="attend_back",
    )(
        slots, last, end, starts.reshape(1, count), cosine, sine,
        packed, packed, packed, tall, logs, grads,
    )


def finish_kernel(narrow_count, wide_count, own_units, per_shard, entries, *refs):
    exchange = own_units > 0
    if exchange:
        (
            parts_ref, piece_ref, feed_ref, sent_ref, total_ref, stats_ref, arrived_ref, block_ref,
            mine, near, far, near_sum, send_near, recv_near, send_far, recv_far, send_ring, recv_ring,
            send_piece, recv_piece,
        ) = refs
    else:
        (
            parts_ref, piece_ref, feed_ref, sent_ref, total_ref, stats_ref, arrived_ref,
            mine, near, far, near_sum, send_near, recv_near, send_far, recv_far, send_ring, recv_ring,
        ) = refs
    narrow_me = lax.axis_index("narrow")
    wide_me = lax.axis_index("wide")

    def place(narrow_at, wide_at):
        return {"narrow": narrow_at, "wide": wide_at}

    def square_sum(value):
        value = value.astype(jnp.float32)
        return jnp.sum(
            jnp.sum(value * value, axis=0, keepdims=True), axis=1, keepdims=True
        )

    norm_rows = 2 * D // LANES
    row_at = lax.broadcasted_iota(jnp.int32, mine.shape, 0)
    lane_at = lax.broadcasted_iota(jnp.int32, mine.shape, 1)
    mine[...] = parts_ref[...] + jnp.where(
        (row_at == norm_rows) & (lane_at == 0),
        square_sum(piece_ref[...]) + square_sum(feed_ref[...]),
        0.0,
    )
    mesh_ids = pl.DeviceIdType.MESH
    barrier = pltpu.get_barrier_semaphore()
    greeted = 0
    for ahead in range(narrow_count):
        for across in range(wide_count):
            if (ahead > 0) + (across > 0) == 0 or (not exchange and ahead > 0 and across > 0):
                continue
            greeted += 1
            pl.semaphore_signal(
                barrier,
                inc=1,
                device_id=place(
                    lax.rem(narrow_me + ahead, narrow_count), lax.rem(wide_me + across, wide_count)
                ),
                device_id_type=mesh_ids,
            )
    pl.semaphore_wait(barrier, greeted)
    near_copies = []
    for ahead in range(1, narrow_count):
        copy = pltpu.make_async_remote_copy(
            src_ref=mine,
            dst_ref=near.at[narrow_me],
            send_sem=send_near.at[ahead - 1],
            recv_sem=recv_near.at[ahead - 1],
            device_id=place(lax.rem(narrow_me + ahead, narrow_count), wide_me),
            device_id_type=mesh_ids,
        )
        copy.start()
        near_copies.append(copy)
    near[narrow_me] = mine[...]
    if exchange:
        rows = piece_ref.shape[0]
        halves = block_ref.shape[0] // rows
        half_me = lax.rem(wide_me, halves)
        narrow_to = lax.div(wide_me, halves)
        moves = []
        for unit in range(3 * own_units):
            whole_unit = (unit % 3) * (D // LANES) + narrow_me * own_units + unit // 3
            wide_to = lax.div(whole_unit, per_shard)
            column = lax.rem(whole_unit, per_shard)
            source = piece_ref.at[:, unit * LANES : (unit + 1) * LANES]
            target = block_ref.at[
                pl.ds(pl.multiple_of(half_me * rows, rows), rows),
                pl.ds(pl.multiple_of(column * LANES, LANES), LANES),
            ]
            arrived = recv_piece.at[half_me * per_shard + column]
            remote = pltpu.make_async_remote_copy(
                src_ref=source,
                dst_ref=target,
                send_sem=send_piece.at[unit],
                recv_sem=arrived,
                device_id=place(narrow_to, wide_to),
                device_id_type=mesh_ids,
            )
            here = pltpu.make_async_copy(source, target, arrived)
            stays = (narrow_to == narrow_me) & (wide_to == wide_me)
            pl.when(jnp.logical_not(stays))(remote.start)
            pl.when(stays)(here.start)
            moves.append((stays, remote))
    for copy in near_copies:
        copy.wait()
    ring = pltpu.make_async_remote_copy(
        src_ref=sent_ref,
        dst_ref=arrived_ref,
        send_sem=send_ring,
        recv_sem=recv_ring,
        device_id=place(lax.rem(narrow_me + 1, narrow_count), wide_me),
        device_id_type=mesh_ids,
    )
    ring.start()
    value = near[0]
    for k in range(1, narrow_count):
        value = value + near[k]
    near_sum[...] = value
    far_copies = []
    for across in range(1, wide_count):
        copy = pltpu.make_async_remote_copy(
            src_ref=near_sum,
            dst_ref=far.at[wide_me],
            send_sem=send_far.at[across - 1],
            recv_sem=recv_far.at[across - 1],
            device_id=place(narrow_me, lax.rem(wide_me + across, wide_count)),
            device_id_type=mesh_ids,
        )
        copy.start()
        far_copies.append(copy)
    far[wide_me] = value
    for copy in far_copies:
        copy.wait()
    value = far[0]
    for k in range(1, wide_count):
        value = value + far[k]
    total_ref[...] = value
    grad_norm = jnp.sqrt(square_sum(value[:norm_rows]) + value[norm_rows : norm_rows + 1, 0:1])
    stats = [jnp.minimum(1.0, math.sqrt(NPARAMS) / grad_norm), grad_norm] + [
        jnp.sqrt(value[norm_rows : norm_rows + 1, k : k + 1] / entries) for k in (1, 2, 3)
    ]
    stats_ref[...] = jnp.zeros_like(stats_ref)
    for row, stat in enumerate(stats):
        stats_ref[row : row + 1, :] = jnp.broadcast_to(stat, (1, LANES))
    if exchange:
        for stays, remote in moves:
            pl.when(jnp.logical_not(stays))(remote.wait_send)
        for half in range(halves):
            for column in range(per_shard):
                pltpu.make_async_copy(
                    piece_ref.at[:, 0:LANES],
                    block_ref.at[
                        half * rows : (half + 1) * rows, column * LANES : (column + 1) * LANES
                    ],
                    recv_piece.at[half * per_shard + column],
                ).wait()
    ring.wait()


def finish(
    parts, piece, feed_piece, sent, exchange, narrow_count, wide_count, own_width, proj_cols, entries
):
    shape = parts.shape
    own_units = own_width // LANES if exchange else 0
    per_shard = proj_cols // LANES
    vmem = pl.BlockSpec(memory_space=pltpu.VMEM)
    shapes = [
        jax.ShapeDtypeStruct(shape, jnp.float32),
        jax.ShapeDtypeStruct((8, LANES), jnp.float32),
        jax.ShapeDtypeStruct(sent.shape, sent.dtype),
    ]
    whole = pl.BlockSpec(memory_space=pl.ANY)
    scratch = [
        pltpu.VMEM(shape, jnp.float32),
        pltpu.VMEM((narrow_count,) + shape, jnp.float32),
        pltpu.VMEM((wide_count,) + shape, jnp.float32),
        pltpu.VMEM(shape, jnp.float32),
        pltpu.SemaphoreType.DMA((narrow_count - 1,)),
        pltpu.SemaphoreType.DMA((narrow_count - 1,)),
        pltpu.SemaphoreType.DMA((wide_count - 1,)),
        pltpu.SemaphoreType.DMA((wide_count - 1,)),
        pltpu.SemaphoreType.DMA,
        pltpu.SemaphoreType.DMA,
    ]
    if exchange:
        shapes.append(jax.ShapeDtypeStruct((D // narrow_count, proj_cols), jnp.bfloat16))
        scratch += [
            pltpu.SemaphoreType.DMA((3 * own_units,)),
            pltpu.SemaphoreType.DMA((3 * own_units,)),
        ]
    return pl.pallas_call(
        partial(finish_kernel, narrow_count, wide_count, own_units, per_shard, entries),
        out_shape=tuple(shapes),
        in_specs=[vmem] * 3 + [whole],
        out_specs=(vmem, vmem, whole) + (vmem,) * (len(shapes) - 3),
        scratch_shapes=scratch,
        compiler_params=pltpu.CompilerParams(collective_id=0, has_side_effects=True),
        name="finish",
    )(parts, piece, feed_piece, sent)


def adam_update(
    weight, first_moment, second_moment, grad_value, step_rate, decay_coef, first_fix, second_fix
):
    new_first = beta_first * first_moment + (1.0 - beta_first) * grad_value
    new_second = beta_second * second_moment + (1.0 - beta_second) * grad_value * grad_value
    step_ratio = new_first / first_fix / (jnp.sqrt(new_second / second_fix) + adam_eps)
    return (weight - step_rate * (step_ratio + decay_coef * weight), new_first, new_second)


def adam_step(weight, first_moment, second_moment, gradient, step_rate, decay_coef, scales):
    new_first = beta_first * first_moment + (1.0 - beta_first) * gradient
    new_second = beta_second * second_moment + (1.0 - beta_second) * gradient * gradient
    ratio = new_first * scales[0] / (jnp.sqrt(new_second * scales[1]) + adam_eps)
    return (weight - step_rate * (ratio + decay_coef * weight), new_first, new_second)


def adam_kernel(scale_ref, stats_ref, grads_ref, total_ref, proj_ref, merge_ref, *refs):
    states, outs = refs[:15], refs[15:-1]
    norm_grads = refs[-1]
    matrix_step, norm_step = scale_ref[0, 0], scale_ref[0, 1]
    scales = (scale_ref[0, 2], scale_ref[0, 3])
    clip_factor = stats_ref[0:1, 0:1]

    def update(matrix, rows, gradient, step_rate, decay_coef):
        state = [ref[rows, :] for ref in states[3 * matrix : 3 * matrix + 3]]
        new = adam_step(*state, gradient * clip_factor, step_rate, decay_coef, scales)
        for out_ref, value in zip(outs[4 * matrix : 4 * matrix + 3], new):
            out_ref[rows, :] = value
        if matrix < 4:
            outs[4 * matrix + 3][rows, :] = new[0].astype(jnp.bfloat16)

    def feed_rows(rows):
        for matrix in range(2):
            gradient = grads_ref[0, matrix, rows, :].astype(jnp.float32)
            update(matrix, rows, gradient, matrix_step, decay_rate)

    in_chunks(states[0].shape[0], 16, feed_rows)

    @pl.when(pl.program_id(0) == 0)
    def _():
        def proj_rows(rows):
            update(2, rows, proj_ref[rows, :].astype(jnp.float32), matrix_step, decay_rate)

        in_chunks(proj_ref.shape[0], 32, proj_rows)
        update(3, slice(None), merge_ref[...].astype(jnp.float32).T, matrix_step, decay_rate)
        per_row = D // LANES
        for k in range(2 * per_row):
            at = k % per_row
            norm_grads[k // per_row : k // per_row + 1, at * LANES : (at + 1) * LANES] = total_ref[
                k : k + 1, :
            ]
        update(4, slice(None), norm_grads[...], norm_step, 0.0)
        outs[19][...] = norm_grads[...] * clip_factor


def adam_all(scales, stats, grads_all, total, proj_block, heads_part, own_width, states):
    count, matrices, rows, cols = grads_all.shape
    block = pl.BlockSpec((rows, cols), lambda i: (i, 0))

    def same(array):
        return pl.BlockSpec(array.shape, lambda i: (0, 0))

    feed_out = jax.ShapeDtypeStruct((count * rows, cols), jnp.float32)
    feed_copy = jax.ShapeDtypeStruct((count * rows, cols), jnp.bfloat16)
    shapes = [feed_out, feed_out, feed_out, feed_copy] * 2
    specs = [block] * 8
    for state in states[6::3]:
        full = jax.ShapeDtypeStruct(state.shape, jnp.float32)
        copy = jax.ShapeDtypeStruct(
            state.shape, jnp.float32 if state is states[12] else jnp.bfloat16
        )
        shapes += [full, full, full, copy]
        specs += [same(state)] * 4
    return pl.pallas_call(
        adam_kernel,
        out_shape=tuple(shapes),
        grid=(count,),
        in_specs=[
            pl.BlockSpec(memory_space=pltpu.SMEM),
            same(stats),
            pl.BlockSpec((1, matrices, rows, cols), lambda i: (i, 0, 0, 0)),
            same(total),
            same(proj_block),
            pl.BlockSpec((heads_part.shape[0], own_width), lambda i: (0, 3)),
        ]
        + [block] * 6
        + [same(state) for state in states[6:]],
        out_specs=tuple(specs),
        scratch_shapes=[pltpu.VMEM((2, D), jnp.float32)],
        cost_estimate=short,
        name="adam_all",
    )(scales, stats, grads_all, total, proj_block, heads_part, *states)


def settle_kernel(arrived_ref, term_ref, tokens_ref, cotangent_ref, params_ref, out_ref):
    unit, inv_std = normalize(tokens_ref[...])
    unit_grad = (arrived_ref[...].astype(jnp.float32) + term_ref[...]) * params_ref[0:1, :]
    out_ref[...] = cotangent_ref[...].astype(jnp.float32) + inv_std * (
        unit_grad
        - jnp.mean(unit_grad, axis=1, keepdims=True)
        - unit * jnp.mean(unit_grad * unit, axis=1, keepdims=True)
    )


def settle(arrived, term, tokens, cotangent, params):
    rows, depth = tokens.shape
    block = pl.BlockSpec((rows // 4, depth), lambda i: (i, 0))
    return pl.pallas_call(
        settle_kernel,
        out_shape=jax.ShapeDtypeStruct((rows, depth), jnp.float32),
        grid=(4,),
        in_specs=[block] * 4 + [pl.BlockSpec((2, depth), lambda i: (0, 0))],
        out_specs=block,
        cost_estimate=short,
        name="settle",
    )(arrived, term, tokens, cotangent, params)


def shards(
    tokens,
    cotangent,
    seq_lengths,
    step_count,
    norm_params,
    norm_first,
    norm_second,
    proj_weight,
    proj_first,
    proj_second,
    merge_weight,
    merge_first,
    merge_second,
    up_weight,
    up_first,
    up_second,
    down_weight,
    down_first,
    down_second,
):
    tok_rows = tokens.shape[0]
    narrow_count = lax.axis_size("narrow")
    wide_count = lax.axis_size("wide")
    span_index = lax.axis_index("narrow")
    group_rows = tok_rows * narrow_count
    own_width = HEADS // narrow_count * HEAD
    held_width = max(own_width, LANES)
    heads_in = min(own_width, LANES) // HEAD
    shard_rows = D // narrow_count
    proj_cols = proj_weight.shape[1]
    lengths = seq_lengths[0]
    onward = [(i, (i + 1) % narrow_count) for i in range(narrow_count)]
    slots = lax.rem(
        span_index + narrow_count - jnp.arange(narrow_count, dtype=jnp.int32), narrow_count
    )

    def pad_lanes(array, axis):
        extra = [(0, 0)] * array.ndim
        extra[axis] = (0, held_width - own_width)
        return jnp.pad(array, extra) if held_width > own_width else array

    def meet(*values):
        return lax.optimization_barrier(values)

    def send_on(array):
        return lax.ppermute(array, "narrow", onward)

    def rows_of(array, slot):
        return array[slot * tok_rows : (slot + 1) * tok_rows]

    direct = own_width % LANES == 0 and proj_cols % LANES == 0 and merge_weight.shape[1] == LANES
    weight_part = jnp.concatenate(
        [proj_weight.astype(jnp.bfloat16), merge_weight.astype(jnp.bfloat16)], axis=1
    )
    weight_rows = lax.all_gather(weight_part, "narrow", axis=0, tiled=True)
    up_slice = up_weight.astype(jnp.bfloat16)
    down_slice = down_weight.astype(jnp.bfloat16)

    def wide_all(array):
        return lax.all_gather(array, "wide", axis=0).reshape(
            wide_count, narrow_count, shard_rows, -1
        )

    order = list(range(1, narrow_count)) + [0]
    pairs = held_width // LANES
    token_blocks = [tokens]
    held = ()
    for slot in range(narrow_count - 1):
        moving = send_on(token_blocks[slot])
        held = feed(slot, narrow_count, token_blocks[slot], norm_params, up_slice, held)
        if slot > 0:
            ready = [slot - 1, slot] if slot == narrow_count - 2 else [slot - 1]
            for block in ready:
                kept = jnp.bfloat16 if block == 1 else jnp.float32
                branch_terms.append(down_term(block, narrow_count, held[1], down_slice, kept))
            if slot == 2:
                if direct:
                    merge_turn = pick_merge(merge_all, slots, own_width)
                else:
                    merge_turn = jnp.take(
                        jnp.transpose(merge_all, (1, 2, 0, 3)).reshape(
                            narrow_count, own_width, D
                        ),
                        slots,
                        axis=0,
                    ).reshape(D, D)
                moving, merge_turn = meet(moving, merge_turn)
            moving, held, branch_terms, down_slice = meet(moving, held, branch_terms, down_slice)
        else:
            moving, held = meet(moving, held)
        if slot == 0:
            lengths, slots, moving, weight_rows, down_slice = meet(
                lengths, slots, moving, weight_rows, down_slice
            )
            proj_all = wide_all(weight_rows[:, :proj_cols])
            merge_all = wide_all(weight_rows[:, proj_cols:])
            branch_terms = []
        if slot == 1:
            places = (
                slots[:, None] * tok_rows + jnp.arange(tok_rows, dtype=jnp.int32)[None, :]
            ).reshape(group_rows)
            seq_start, unused = locate(lengths, places)
            cosine, sine = rotary_tables(places - seq_start)
            block_first = jnp.arange(narrow_count, dtype=jnp.int32) * tok_rows
            first_start, unused = locate(lengths, block_first)
            last_start, last_end = locate(lengths, block_first + (tok_rows - 1))
            moving, cosine, sine, first_start, last_start, last_end = meet(
                moving, cosine, sine, first_start, last_start, last_end
            )
        token_blocks.append(moving)
    grad_first, last_block = meet(cotangent, token_blocks[-1])
    token_blocks[-1] = last_block
    grad_blocks = [grad_first]

    moving = send_on(grad_first)
    gathered, activated, slope = feed(
        narrow_count - 1, narrow_count, last_block, norm_params, up_slice, held
    )
    if direct:
        packed, proj_own = project_all(
            gathered, proj_all, span_index, own_width, cosine, sine
        )
        merge_own = merge_all
    else:
        proj_copy = jnp.transpose(proj_all, (1, 2, 0, 3)).reshape(
            D, 3, narrow_count, own_width
        )
        proj_own = pad_lanes(
            lax.dynamic_index_in_dim(proj_copy, span_index, axis=2, keepdims=False), 2
        ).reshape(D, 3 * held_width)
        merge_copy = jnp.transpose(merge_all, (1, 2, 0, 3)).reshape(
            narrow_count, own_width, D
        )
        merge_own = pad_lanes(
            lax.dynamic_index_in_dim(merge_copy, span_index, axis=0, keepdims=False), 0
        )
        packed = project(gathered, proj_own, cosine, sine)

    def push_slot(slot, push_held):
        return push(
            slot, narrow_count, grad_blocks[slot], slope, down_slice, merge_own, span_index,
            push_held,
        )

    push_held = push_slot(0, ())
    branch_terms.append(
        down_term(narrow_count - 1, narrow_count, activated, down_slice, jnp.float32)
    )
    moving, packed, activated, slope, push_held, branch_terms = meet(
        moving, packed, activated, slope, push_held, branch_terms
    )
    grad_blocks.append(moving)

    def wide_sum(grad):
        return lax.psum_scatter(grad, "wide", scatter_dimension=0, tiled=True)

    def attend_pair(pair, attended_held):
        return attend(
            pair, packed, slots, first_start, last_start, seq_start,
            heads_in, tok_rows, tok_rows, attended_held,
        )

    attended_held = ()
    for hop in range(2, narrow_count):
        moving = send_on(grad_blocks[-1])
        if hop - 2 < pairs:
            attended_held = attend_pair(hop - 2, attended_held)
        push_held = push_slot(hop - 1, push_held)
        moving, attended_held, push_held = meet(moving, attended_held, push_held)
        grad_blocks.append(moving)
    for pair in range(narrow_count - 2, pairs):
        attended_held = attend_pair(pair, attended_held)
    attended, tall, logs = attended_held

    moving = send_on(branch_terms[1])
    push_held = push_slot(narrow_count - 1, push_held)
    grads_all, hidden_grad, attended_grad = push_held
    part_rows = D // wide_count
    if direct:
        feed_grad = outer(wide_count, gathered, hidden_grad, activated, grads_all)
    else:
        down_grad = dot_first(activated, grads_all).astype(jnp.bfloat16)
        up_grad = dot_first(gathered, hidden_grad).astype(jnp.bfloat16)
        feed_grad = jnp.stack(
            [
                up_grad.reshape(wide_count, part_rows, -1),
                down_grad.reshape(wide_count, part_rows, -1),
            ],
            axis=1,
        )
    feed_grad = feed_grad.reshape(2 * D, -1)
    pieces = [
        rows_of(attended, (narrow_count - ahead) % narrow_count)[:, :own_width]
        for ahead in range(narrow_count)
    ]
    moving, pieces, feed_grad, attended_grad = meet(moving, pieces, feed_grad, attended_grad)
    feed_part = wide_sum(feed_grad)

    for ahead in range(1, narrow_count):
        pieces[ahead] = lax.ppermute(
            pieces[ahead],
            "narrow",
            [(i, (i + ahead) % narrow_count) for i in range(narrow_count)],
        )
    terms = []
    term_blocks = []

    def term_at(place):
        block, at = terms[place]
        return rows_of(term_blocks[block], at)

    norm_part = jnp.zeros((2, D), jnp.float32)

    def pull_more(slots_now, norm_part):
        if slots_now:
            lead, block, sums = pull(
                slots_now[0], mixed_grad, hidden_grad, proj_own, up_slice,
                [token_blocks[slot] for slot in slots_now],
            )
            if not term_blocks:
                term_blocks.append(lead)
            term_blocks.append(block)
            for place in range(len(slots_now)):
                terms.append((len(term_blocks) - 1, place))
            norm_part = norm_part + sums
        return norm_part

    for place, slot in enumerate(order[1:-1]):
        moving = send_on((moving.astype(jnp.float32) + branch_terms[slot]).astype(jnp.bfloat16))
        if place == 0:
            mixed_grad = attend_back(
                packed, slots, last_start, last_end, seq_start, cosine, sine,
                tall, logs, attended_grad, heads_in, tok_rows, tok_rows,
            )
            if direct:
                heads_grad = outer(0, gathered, mixed_grad, grads_all, attended)
            else:
                proj_grad = dot_first(gathered, mixed_grad).astype(jnp.bfloat16)
                merge_grad = dot_first(grads_all, attended).astype(jnp.bfloat16)
                proj_grad = proj_grad.reshape(D, 3, held_width)[:, :, :own_width]
                heads_grad = jnp.concatenate(
                    [proj_grad.reshape(D, 3 * own_width), merge_grad[:, :own_width]], axis=1
                )
            moving, pieces, mixed_grad, heads_grad, feed_part = meet(
                moving, pieces, mixed_grad, heads_grad, feed_part
            )
            heads_part = wide_sum(heads_grad)
        else:
            norm_part = pull_more(order[:-1][len(terms) : len(terms) + 3], norm_part)
            moving, term_blocks[:], norm_part, feed_part = meet(
                moving, term_blocks, norm_part, feed_part
            )
        if place == narrow_count - 3:
            feed_all = lax.all_gather(feed_part, "wide", axis=0).reshape(
                wide_count, 2, part_rows, -1
            )
    branch_moving = moving
    moving = send_on(term_blocks[0])
    norm_part = pull_more(order[len(terms) : -1], norm_part)
    norm_part = pull_more([0], norm_part)
    branch = branch_moving.astype(jnp.float32) + branch_terms[0]
    merged = dot_plain(jnp.concatenate(pieces, axis=1), merge_turn)
    output_rows = tokens.astype(jnp.float32) + merged + branch
    layer_out = output_rows.astype(jnp.bfloat16)

    def squares(array):
        value = array.astype(jnp.float32)
        return jnp.sum(value * value)

    row_squares = [squares(output_rows), squares(merged), squares(branch)]
    scalars = jnp.stack([jnp.zeros((), jnp.float32)] + row_squares)
    parts = jnp.concatenate(
        [norm_part.reshape(2 * D // LANES, LANES), jnp.pad(scalars, (0, LANES - 4))[None, :]]
    )
    parts = jnp.pad(parts, ((0, 7), (0, 0)))
    step_value = step_count[0].astype(jnp.float32)
    first_fix = 1.0 - jnp.power(beta_first, step_value)
    second_fix = 1.0 - jnp.power(beta_second, step_value)
    ramp = jnp.minimum(1.0, step_value / warmup_steps)
    scales = jnp.stack(
        [matrix_rate * ramp, norm_rate * ramp, 1.0 / first_fix, 1.0 / second_fix]
    ).reshape(1, 4)
    entries = wide_count * group_rows * D
    for place in range(1, narrow_count - 1):
        if place == narrow_count - 3:
            moving, parts, heads_part, scales = meet(moving, parts, heads_part, scales)
        sent = (moving.astype(jnp.float32) + term_at(place)).astype(jnp.bfloat16)
        if place == narrow_count - 3:
            total, stats, moving, *proj_block = finish(
                parts, heads_part, feed_part, sent, direct, narrow_count, wide_count, own_width,
                proj_cols, entries,
            )
            continue
        if place == narrow_count - 2:
            sent, total, stats, proj_block = meet(sent, total, stats, proj_block)
        moving = send_on(sent)

    if direct:
        updated = adam_all(
            scales, stats, feed_all, total, proj_block[0], heads_part, own_width,
            [
                up_weight, up_first, up_second, down_weight, down_first, down_second,
                proj_weight, proj_first, proj_second, merge_weight, merge_first, merge_second,
                norm_params, norm_first, norm_second,
            ],
        )
    else:
        clip_factor = stats[0, 0:1]
        cross = lax.all_gather(heads_part[:, : 3 * own_width], "narrow", axis=0).reshape(
            narrow_count, part_rows, 3, own_width
        )
        cross = jnp.transpose(cross, (1, 2, 0, 3)).reshape(part_rows, wide_count, proj_cols)
        cross = lax.all_to_all(jnp.transpose(cross, (1, 0, 2)), "wide", 0, 0)
        proj_block = lax.dynamic_slice_in_dim(
            cross.reshape(D, proj_cols), span_index * shard_rows, shard_rows, axis=0
        )
        merge_block = heads_part[:, 3 * own_width :].T
        norm_total = total[: 2 * D // LANES].reshape(2, D)
        feed_sums = feed_all.astype(jnp.float32)
        updated = []
        for state, gradient, step_rate, decay_coef in (
            ((up_weight, up_first, up_second), feed_sums[:, 0], matrix_rate, decay_rate),
            ((down_weight, down_first, down_second), feed_sums[:, 1], matrix_rate, decay_rate),
            ((proj_weight, proj_first, proj_second), proj_block, matrix_rate, decay_rate),
            ((merge_weight, merge_first, merge_second), merge_block, matrix_rate, decay_rate),
            ((norm_params, norm_first, norm_second), norm_total, norm_rate, 0.0),
        ):
            clipped = gradient.reshape(state[0].shape).astype(jnp.float32) * clip_factor
            new = adam_update(
                *state, clipped, step_rate * ramp, decay_coef, first_fix, second_fix
            )
            updated += [*new, clipped if state[0] is norm_params else new[0].astype(jnp.bfloat16)]
    new_up, new_down, new_proj, new_merge, new_norm = [
        updated[4 * k : 4 * k + 4] for k in range(5)
    ]
    moving, new_up = meet(moving, new_up)
    input_grad = settle(moving, term_at(-1), tokens, cotangent, norm_params)
    return (
        layer_out,
        input_grad,
        stats[1, 0:1],
        stats[2, 0:1],
        new_norm[3],
        new_norm[0],
        new_norm[1],
        new_norm[2],
        new_proj[0],
        new_proj[1],
        new_proj[2],
        new_merge[0],
        new_merge[1],
        new_merge[2],
        new_up[0],
        new_up[1],
        new_up[2],
        new_down[0],
        new_down[1],
        new_down[2],
        stats[3:5, 0],
        new_proj[3],
        new_merge[3],
        new_up[3],
        new_down[3],
    )


def solution(mesh):
    placed = (
        P(("wide", "narrow"), None),
        P(("wide", "narrow"), None),
        P("wide", None),
        P(),
        P(),
        P(),
        P(),
        P("narrow", "wide"),
        P("narrow", "wide"),
        P("narrow", "wide"),
        P("narrow", "wide"),
        P("narrow", "wide"),
        P("narrow", "wide"),
        P(None, "narrow"),
        P(None, "narrow"),
        P(None, "narrow"),
        P("narrow", None),
        P("narrow", None),
        P("narrow", None),
    )
    return jax.shard_map(
        shards,
        mesh=mesh,
        in_specs=placed,
        out_specs=(
            P(("wide", "narrow"), None),
            P(("wide", "narrow"), None),
            P(),
            P(),
            P(),
            P(),
            P(),
            P(),
            P("narrow", "wide"),
            P("narrow", "wide"),
            P("narrow", "wide"),
            P("narrow", "wide"),
            P("narrow", "wide"),
            P("narrow", "wide"),
            P(None, "narrow"),
            P(None, "narrow"),
            P(None, "narrow"),
            P("narrow", None),
            P("narrow", None),
            P("narrow", None),
            P(),
            P("narrow", "wide"),
            P("narrow", "wide"),
            P(None, "narrow"),
            P("narrow", None),
        ),
        check_vma=False,
    )
```

```python
from functools import partial
import math

import jax
import jax.numpy as jnp
from jax import lax
from jax.experimental import pallas as pl
from jax.experimental.pallas import tpu as pltpu
from jax.sharding import PartitionSpec as P

HEADS = 16
HEAD = 64
D = 1024
ROT = 16
LANES = 128
ROW_BLOCK = 512
NPARAMS = 12584960


norm_eps = 1e-05
adam_eps = 1e-08
beta_first = 0.5
beta_second = 0.5
decay_rate = 0.01
matrix_rate = 0.1
norm_rate = 1.0
warmup_steps = 20.0
masked_score = -1e30
short = pl.CostEstimate(flops=0, bytes_accessed=0, transcendentals=0)


def dot_last(left_side, right_side):
    return lax.dot_general(
        left_side, right_side, (((1,), (1,)), ((), ())), preferred_element_type=jnp.float32
    )


def dot_plain(left_side, right_side):
    return lax.dot_general(
        left_side, right_side, (((1,), (0,)), ((), ())), preferred_element_type=jnp.float32
    )


def dot_first(left_side, right_side):
    return lax.dot_general(
        left_side, right_side, (((0,), (0,)), ((), ())), preferred_element_type=jnp.float32
    )


def in_chunks(total, chunk, body):
    def step(index, carry):
        body(pl.ds(pl.multiple_of(index * chunk, chunk), chunk))
        return carry

    lax.fori_loop(0, total // chunk, step, 0)


def locate(lengths, token_index):
    seq_ends = jnp.cumsum(lengths)
    starts = seq_ends - lengths
    segment = jnp.sum(
        (seq_ends[None, :] <= token_index[:, None]).astype(jnp.int32), axis=1, dtype=jnp.int32
    )
    choose = segment[:, None] == jnp.arange(lengths.shape[0], dtype=jnp.int32)[None, :]
    seq_start = jnp.sum(jnp.where(choose, starts[None, :], 0), axis=1, dtype=jnp.int32)
    seq_end = jnp.sum(jnp.where(choose, seq_ends[None, :], 0), axis=1, dtype=jnp.int32)
    return (seq_start, seq_end)


def rotary_tables(position):
    half_rot = ROT // 2
    frequency = jnp.power(10000.0, -2.0 * jnp.arange(half_rot, dtype=jnp.float32) / ROT)
    row = jnp.concatenate([frequency, frequency, jnp.zeros((HEAD - ROT,), jnp.float32)])
    row = jnp.tile(row, LANES // HEAD)
    sign = jnp.where(jnp.arange(LANES) % HEAD < half_rot, -1.0, 1.0)
    phases = position.astype(jnp.float32)[:, None] * row[None, :]
    return (jnp.cos(phases), jnp.sin(phases) * sign[None, :])


def partner(field):
    half_rot = ROT // 2
    lane = lax.broadcasted_iota(jnp.int32, field.shape, 1) % HEAD
    return jnp.where(
        lane < half_rot,
        pltpu.roll(field, LANES - half_rot, 1),
        pltpu.roll(field, half_rot, 1),
    )


def project_kernel(rows_ref, weight_ref, cos_ref, sin_ref, out_ref):
    width = out_ref.shape[1]
    projected = dot_plain(rows_ref[...], weight_ref[...])
    for first in range(0, width, LANES):
        piece = projected[:, first : first + LANES]
        part = first // LANES % 3
        if part < 2:
            piece = piece * cos_ref[...] + partner(piece) * sin_ref[...]
        if part == 0:
            piece = piece * HEAD ** (-0.5)
        out_ref[:, first : first + LANES] = piece.astype(jnp.bfloat16)


def project(rows, weight, cosine, sine):
    count, depth = rows.shape
    width = weight.shape[1]
    block = min(ROW_BLOCK, count)
    return pl.pallas_call(
        project_kernel,
        out_shape=jax.ShapeDtypeStruct((count, width), jnp.bfloat16),
        grid=(count // block,),
        in_specs=[
            pl.BlockSpec((block, depth), lambda i: (i, 0)),
            pl.BlockSpec((depth, width), lambda i: (0, 0)),
            pl.BlockSpec((block, LANES), lambda i: (i, 0)),
            pl.BlockSpec((block, LANES), lambda i: (i, 0)),
        ],
        out_specs=pl.BlockSpec((block, width), lambda i: (i, 0)),
        cost_estimate=short,
        name="project",
    )(rows, weight, cosine, sine)


def normalize(tokens):
    residual = tokens.astype(jnp.float32)
    center = residual - jnp.mean(residual, axis=1, keepdims=True)
    inv_std = lax.rsqrt(jnp.mean(center * center, axis=1, keepdims=True) + norm_eps)
    return (center * inv_std, inv_std)


def feed_kernel(tokens_ref, params_ref, weight_ref, *refs):
    normed_ref, act_ref, slope_ref = refs[-3:]
    unit, unused = normalize(tokens_ref[...])
    normed_ref[...] = (unit * params_ref[0:1, :] + params_ref[1:2, :]).astype(jnp.bfloat16)
    width = act_ref.shape[1]

    def column(cols):
        hidden = dot_plain(normed_ref[...], weight_ref[:, cols])
        share = 0.5 + 0.5 * lax.erf(hidden * math.sqrt(0.5))
        bell = jnp.exp(hidden * hidden * -0.5) * (1.0 / math.sqrt(2.0 * math.pi))
        act_ref[:, cols] = (hidden * share).astype(jnp.bfloat16)
        slope_ref[:, cols] = share + hidden * bell

    in_chunks(width, min(256, width), column)


def feed(slot, slots, tokens, params, weight, held):
    rows, depth = tokens.shape
    width = weight.shape[1]
    whole = pl.BlockSpec(memory_space=pl.ANY)
    return pl.pallas_call(
        feed_kernel,
        out_shape=(
            jax.ShapeDtypeStruct((slots * rows, depth), jnp.bfloat16),
            jax.ShapeDtypeStruct((slots * rows, width), jnp.bfloat16),
            jax.ShapeDtypeStruct((slots * rows, width), jnp.float32),
        ),
        grid=(2,),
        in_specs=[
            pl.BlockSpec((rows // 2, depth), lambda i: (i, 0)),
            pl.BlockSpec((2, depth), lambda i: (0, 0)),
            pl.BlockSpec((depth, width), lambda i: (0, 0)),
        ]
        + [whole] * len(held),
        out_specs=(
            pl.BlockSpec((rows // 2, depth), lambda i: (2 * slot + i, 0)),
            pl.BlockSpec((rows // 2, width), lambda i: (2 * slot + i, 0)),
            pl.BlockSpec((rows // 2, width), lambda i: (2 * slot + i, 0)),
        ),
        input_output_aliases={3 + k: k for k in range(len(held))},
        cost_estimate=short,
        name="feed",
    )(tokens, params, weight, *held)


def down_kernel(active_ref, down_ref, out_ref):
    def column(cols):
        out_ref[:, cols] = dot_plain(active_ref[...], down_ref[:, cols]).astype(out_ref.dtype)

    in_chunks(out_ref.shape[1], 256, column)


def down_term(slot, slots, activated, down, kept):
    rows = activated.shape[0] // slots
    width, depth = down.shape
    half = rows // 2
    return pl.pallas_call(
        down_kernel,
        out_shape=jax.ShapeDtypeStruct((rows, depth), kept),
        grid=(2,),
        in_specs=[
            pl.BlockSpec((half, width), lambda i: (2 * slot + i, 0)),
            pl.BlockSpec((width, depth), lambda i: (0, 0)),
        ],
        out_specs=pl.BlockSpec((half, depth), lambda i: (i, 0)),
        cost_estimate=short,
        name="down_term",
    )(activated, down)


def outer_kernel(split, first_left, first_right, second_left, second_right, out_ref, first, second):
    begun = pl.program_id(0) > 0
    for left_ref, right_ref, total in (
        (first_left, first_right, first),
        (second_left, second_right, second),
    ):

        def chunk(rows):
            term = dot_first(left_ref[:, rows], right_ref[...])
            total[rows, :] = jnp.where(begun, total[rows, :], 0.0) + term

        in_chunks(total.shape[0], 512, chunk)

    @pl.when(pl.program_id(0) == pl.num_programs(0) - 1)
    def _():
        if split:
            blocks, unused, rows, cols = out_ref.shape

            def write(block, carry):
                at = pl.ds(pl.multiple_of(block * rows, rows), rows)
                out_ref[block, 0] = first[at, :].astype(jnp.bfloat16)
                out_ref[block, 1] = second[at, :].astype(jnp.bfloat16)
                return carry

            lax.fori_loop(0, blocks, write, 0)
        else:
            width = first.shape[1]

            def write_rows(rows):
                out_ref[rows, :width] = first[rows, :].astype(jnp.bfloat16)
                out_ref[rows, width:] = second[rows, :].astype(jnp.bfloat16)

            in_chunks(first.shape[0], 128, write_rows)


def outer(blocks, first_left, first_right, second_left, second_right):
    count, depth = first_left.shape
    rows = min(ROW_BLOCK, count)
    widths = [first_right.shape[1], second_right.shape[1]]
    shape = (blocks, 2, depth // blocks, widths[0]) if blocks else (depth, sum(widths))
    operands = (first_left, first_right, second_left, second_right)
    return pl.pallas_call(
        partial(outer_kernel, bool(blocks)),
        out_shape=jax.ShapeDtypeStruct(shape, jnp.bfloat16),
        grid=(count // rows,),
        in_specs=[pl.BlockSpec((rows, array.shape[1]), lambda k: (k, 0)) for array in operands],
        out_specs=pl.BlockSpec(shape, lambda k: (0,) * len(shape)),
        scratch_shapes=[pltpu.VMEM((depth, width), jnp.float32) for width in widths],
        cost_estimate=short,
        name="outer",
    )(*operands)


def push_kernel(index_ref, grad_ref, slope_ref, down_ref, merge_ref, *refs):
    all_ref, hidden_ref, attended_ref, merge_own = refs[-4:]

    @pl.when(pl.program_id(0) == 0)
    def _():
        if len(merge_ref.shape) == 4:
            for w in range(merge_ref.shape[0]):
                merge_own[:, w * LANES : (w + 1) * LANES] = merge_ref[w, 0]
        else:
            merge_own[...] = merge_ref[...]

    grads = grad_ref[...]
    all_ref[...] = grads
    hidden_ref[...] = (dot_last(grads, down_ref[...]) * slope_ref[...]).astype(jnp.bfloat16)
    attended_ref[...] = dot_last(grads, merge_own[...]).astype(jnp.bfloat16)


def push(slot, slots, grads, slope, down, merge, span_index, held):
    rows, depth = grads.shape
    width = slope.shape[1]
    half = rows // 2
    whole = pl.BlockSpec(memory_space=pl.ANY)
    if merge.ndim == 4:
        own = merge.shape[2]
        merge_spec = pl.BlockSpec(
            (merge.shape[0], 1, own, LANES), lambda i, index_ref: (0, index_ref[0], 0, 0)
        )
    else:
        own = merge.shape[0]
        merge_spec = pl.BlockSpec(merge.shape, lambda i, index_ref: (0, 0))

    def place(i, index_ref):
        return (2 * slot + i, 0)

    return pl.pallas_call(
        push_kernel,
        out_shape=(
            jax.ShapeDtypeStruct((slots * rows, depth), jnp.bfloat16),
            jax.ShapeDtypeStruct((slots * rows, width), jnp.bfloat16),
            jax.ShapeDtypeStruct((slots * rows, own), jnp.bfloat16),
        ),
        grid_spec=pltpu.PrefetchScalarGridSpec(
            num_scalar_prefetch=1,
            grid=(2,),
            in_specs=[
                pl.BlockSpec((half, depth), lambda i, index_ref: (i, 0)),
                pl.BlockSpec((half, width), place),
                pl.BlockSpec(down.shape, lambda i, index_ref: (0, 0)),
                merge_spec,
            ]
            + [whole] * len(held),
            out_specs=(
                pl.BlockSpec((half, depth), place),
                pl.BlockSpec((half, width), place),
                pl.BlockSpec((half, own), place),
            ),
            scratch_shapes=[pltpu.VMEM((own, depth), jnp.bfloat16)],
        ),
        input_output_aliases={5 + k: k for k in range(len(held))},
        cost_estimate=short,
        name="push",
    )(span_index.reshape(1), grads, slope, down, merge, *held)


def pull_kernel(blocks, mixed_ref, hidden_ref, proj_ref, up_ref, *refs):
    tokens_refs, (lead_ref, out_ref, sums_ref, rows_ref) = refs[:blocks], refs[blocks:]
    index = pl.program_id(0)
    for block, tokens_ref in enumerate(tokens_refs):

        @pl.when(index // 2 == block)
        def _():
            rows_ref[...] = tokens_ref[...]

    partial_grad = dot_last(mixed_ref[...], proj_ref[...]) + dot_last(hidden_ref[...], up_ref[...])
    out_ref[...] = partial_grad

    @pl.when(index < 2)
    def _():
        lead_ref[...] = partial_grad.astype(jnp.bfloat16)

    unit, unused = normalize(rows_ref[...])
    gain = jnp.sum(partial_grad * unit, axis=0, keepdims=True)
    bias = jnp.sum(partial_grad, axis=0, keepdims=True)
    both = jnp.concatenate([gain, bias], axis=0)
    sums_ref[...] = jnp.where(index > 0, sums_ref[...], 0.0) + both


def pull(slot, mixed, hidden_grad, proj, up, token_blocks):
    rows, depth = token_blocks[0].shape
    blocks = len(token_blocks)
    half = rows // 2

    def part(block, i):
        return (jnp.clip(i - 2 * block, 0, 1), 0)

    return pl.pallas_call(
        partial(pull_kernel, blocks),
        out_shape=(
            jax.ShapeDtypeStruct((rows, depth), jnp.bfloat16),
            jax.ShapeDtypeStruct((blocks * rows, depth), jnp.float32),
            jax.ShapeDtypeStruct((2, depth), jnp.float32),
        ),
        grid=(2 * blocks,),
        in_specs=[
            pl.BlockSpec((half, mixed.shape[1]), lambda i: (2 * slot + i, 0)),
            pl.BlockSpec((half, hidden_grad.shape[1]), lambda i: (2 * slot + i, 0)),
            pl.BlockSpec(proj.shape, lambda i: (0, 0)),
            pl.BlockSpec(up.shape, lambda i: (0, 0)),
        ]
        + [pl.BlockSpec((half, depth), partial(part, block)) for block in range(blocks)],
        out_specs=(
            pl.BlockSpec((half, depth), partial(part, 0)),
            pl.BlockSpec((half, depth), lambda i: (i, 0)),
            pl.BlockSpec((2, depth), lambda i: (0, 0)),
        ),
        scratch_shapes=[pltpu.VMEM((half, depth), jnp.bfloat16)],
        cost_estimate=short,
        name="pull",
    )(mixed, hidden_grad, proj, up, *token_blocks)


def project_all_kernel(index_ref, rows_ref, cos_ref, sin_ref, *refs):
    unit_refs, (out_ref, weight_ref) = refs[:-2], refs[-2:]

    @pl.when(pl.program_id(0) == 0)
    def _():
        for c, unit_ref in enumerate(unit_refs):
            weight_ref[:, c * LANES : (c + 1) * LANES] = unit_ref[...].reshape(D, LANES)

    project_kernel(rows_ref, weight_ref, cos_ref, sin_ref, out_ref)


def project_all(rows, weight_all, span_index, own_width, cosine, sine):
    count, depth = rows.shape
    shards, narrow_count, shard_rows, cols = weight_all.shape
    units = own_width // LANES
    width = 3 * own_width
    per_shard = cols // LANES
    per_part = D // LANES
    block = min(ROW_BLOCK, count)

    def source(c, i, index_ref):
        unit = (c % 3) * per_part + index_ref[0] * units + c // 3
        return (unit // per_shard, 0, 0, unit % per_shard)

    return pl.pallas_call(
        project_all_kernel,
        out_shape=(
            jax.ShapeDtypeStruct((count, width), jnp.bfloat16),
            jax.ShapeDtypeStruct((D, width), jnp.bfloat16),
        ),
        grid_spec=pltpu.PrefetchScalarGridSpec(
            num_scalar_prefetch=1,
            grid=(count // block,),
            in_specs=[
                pl.BlockSpec((block, depth), lambda i, index_ref: (i, 0)),
                pl.BlockSpec((block, LANES), lambda i, index_ref: (i, 0)),
                pl.BlockSpec((block, LANES), lambda i, index_ref: (i, 0)),
            ]
            + [
                pl.BlockSpec((1, narrow_count, shard_rows, LANES), partial(source, c))
                for c in range(3 * units)
            ],
            out_specs=(
                pl.BlockSpec((block, width), lambda i, index_ref: (i, 0)),
                pl.BlockSpec((D, width), lambda i, index_ref: (0, 0)),
            ),
        ),
        cost_estimate=short,
        name="project_all",
    )(span_index.reshape(1), rows, cosine, sine, *[weight_all] * (3 * units))


def turn_kernel(slots_ref, all_ref, out_ref):
    unused, narrow_count, rows, cols = all_ref.shape
    for t in range(narrow_count):
        out_ref[t * rows : (t + 1) * rows, :] = all_ref[0, slots_ref[t]]


def pick_merge(weight_all, slots, own_width):
    shards, narrow_count, rows, cols = weight_all.shape
    return pl.pallas_call(
        turn_kernel,
        out_shape=jax.ShapeDtypeStruct((D, D), jnp.bfloat16),
        grid_spec=pltpu.PrefetchScalarGridSpec(
            num_scalar_prefetch=1,
            grid=(shards,),
            in_specs=[
                pl.BlockSpec(
                    (1, narrow_count, rows, LANES),
                    lambda j, slots_ref: (j, 0, 0, 0),
                )
            ],
            out_specs=pl.BlockSpec((D, LANES), lambda j, slots_ref: (0, j)),
        ),
        cost_estimate=short,
        name="pick_merge",
    )(slots, weight_all)


def head_lanes(field, head):
    lane = lax.broadcasted_iota(jnp.int32, field.shape, 1)
    keep = (lane >= head * HEAD) & (lane < (head + 1) * HEAD)
    return jnp.where(keep, field, jnp.zeros_like(field))


def pair_allowed(start_row, key_first, key_count, query_first, query_count):
    key_index = key_first + lax.broadcasted_iota(jnp.int32, (key_count, query_count), 0)
    query_index = query_first + lax.broadcasted_iota(jnp.int32, (key_count, query_count), 1)
    return (key_index >= start_row) & (key_index <= query_index)


def attend_kernel(
    block_q,
    block_k,
    heads_in,
    slots_ref,
    first_ref,
    last_ref,
    start_ref,
    query_ref,
    key_ref,
    value_ref,
    *refs,
):
    out_ref, tall_ref, log_ref, turned, best, total, summed = refs[-7:]
    index = pl.program_id(0)
    key_blocks = key_ref.shape[0] // block_k

    @pl.when(index == 0)
    def _():
        for j in range(key_blocks):
            piece = value_ref[j * block_k : (j + 1) * block_k, :].astype(jnp.float32)
            turned[:, j * block_k : (j + 1) * block_k] = piece.T.astype(jnp.bfloat16)

    query_first = index * block_q
    low = first_ref[index] // block_k
    high = (query_first + block_q - 1) // block_k + 1
    start_row = start_ref[...]
    queries = [head_lanes(query_ref[...], head) for head in range(heads_in)]
    best[...] = jnp.full_like(best, masked_score)
    total[...] = jnp.zeros_like(total)
    summed[...] = jnp.zeros_like(summed)

    def visit(j, masked):
        key_rows = pl.ds(pl.multiple_of(slots_ref[j] * block_k, block_k), block_k)
        keys = key_ref[key_rows, :]
        if masked:
            allowed = pair_allowed(start_row, j * block_k, block_k, query_first, block_q)
        for head in range(heads_in):
            scores = dot_last(keys, queries[head])
            if masked:
                scores = jnp.where(allowed, scores, masked_score)
            old = best[head : head + 1, :]
            new = jnp.maximum(old, jnp.max(scores, axis=0, keepdims=True))
            weights = jnp.exp(scores - new)
            if masked:
                weights = jnp.where(allowed, weights, 0.0)
            factor = jnp.exp(old - new)
            best[head : head + 1, :] = new
            total[head : head + 1, :] = total[head : head + 1, :] * factor + jnp.sum(
                weights, axis=0, keepdims=True
            )
            rows = slice(head * HEAD, (head + 1) * HEAD)
            summed[rows, :] = summed[rows, :] * factor + dot_plain(
                turned[rows, key_rows], weights.astype(jnp.bfloat16)
            )

    def step(j, carry):
        whole = (j * block_k >= last_ref[index]) & ((j + 1) * block_k - 1 <= query_first)

        @pl.when(whole)
        def _():
            visit(j, False)

        @pl.when(jnp.logical_not(whole))
        def _():
            visit(j, True)

        return carry

    lax.fori_loop(low, high, step, 0)
    for head in range(heads_in):
        rows = slice(head * HEAD, (head + 1) * HEAD)
        weight = total[head : head + 1, :]
        tall_ref[rows, :] = summed[rows, :] / weight
        log_ref[0, head : head + 1, :] = best[head : head + 1, :] + jnp.log(weight)
    if heads_in * HEAD < LANES:
        tall_ref[heads_in * HEAD :, :] = jnp.zeros_like(tall_ref[heads_in * HEAD :, :])
    log_ref[0, heads_in:, :] = jnp.zeros_like(log_ref[0, heads_in:, :])
    out_ref[...] = tall_ref[...].T.astype(jnp.bfloat16)


def attend(pair, packed, slots, first, last, starts, heads_in, block_q, block_k, held):
    count, width = packed.shape
    pairs = width // 3 // LANES
    whole = pl.BlockSpec(memory_space=pl.ANY)
    return pl.pallas_call(
        partial(attend_kernel, block_q, block_k, heads_in),
        out_shape=(
            jax.ShapeDtypeStruct((count, pairs * LANES), jnp.bfloat16),
            jax.ShapeDtypeStruct((pairs * LANES, count), jnp.float32),
            jax.ShapeDtypeStruct((pairs, 8, count), jnp.float32),
        ),
        grid_spec=pltpu.PrefetchScalarGridSpec(
            num_scalar_prefetch=3,
            grid=(count // block_q,),
            in_specs=[
                pl.BlockSpec((1, block_q), lambda i, slots_ref, *_: (0, slots_ref[i])),
                pl.BlockSpec((block_q, LANES), lambda i, slots_ref, *_: (slots_ref[i], 3 * pair)),
                pl.BlockSpec((count, LANES), lambda i, *_: (0, 3 * pair + 1)),
                pl.BlockSpec((count, LANES), lambda i, *_: (0, 3 * pair + 2)),
            ]
            + [whole] * len(held),
            out_specs=(
                pl.BlockSpec((block_q, LANES), lambda i, slots_ref, *_: (slots_ref[i], pair)),
                pl.BlockSpec((LANES, block_q), lambda i, slots_ref, *_: (pair, slots_ref[i])),
                pl.BlockSpec((1, 8, block_q), lambda i, slots_ref, *_: (pair, 0, slots_ref[i])),
            ),
            scratch_shapes=[
                pltpu.VMEM((LANES, count), jnp.bfloat16),
                pltpu.VMEM((8, block_q), jnp.float32),
                pltpu.VMEM((8, block_q), jnp.float32),
                pltpu.VMEM((LANES, block_q), jnp.float32),
            ],
        ),
        input_output_aliases={7 + k: k for k in range(len(held))},
        cost_estimate=short,
        name="attend",
    )(slots, first, last, starts.reshape(1, count), packed, packed, packed, *held)


def attend_back_kernel(
    block_q,
    block_k,
    heads_in,
    slots_ref,
    last_ref,
    end_ref,
    start_ref,
    cos_ref,
    sin_ref,
    query_ref,
    key_ref,
    value_ref,
    tall_ref,
    log_ref,
    grad_ref,
    out_ref,
    turned,
    masked_q,
    masked_g,
    delta,
    tall_q,
    key_sum,
    value_sum,
):
    index = pl.program_id(1)
    count = query_ref.shape[0]

    def turn_back(field, rows):
        return field * cos_ref[rows, :] - partner(field) * sin_ref[rows, :]

    @pl.when(index == 0)
    def _():
        def prepare(j, carry):
            rows = pl.ds(pl.multiple_of(j * block_k, block_k), block_k)
            turned[:, rows] = key_ref[rows, :].astype(jnp.float32).T.astype(jnp.bfloat16)
            grads = grad_ref[rows, :]
            product = grads.astype(jnp.float32).T * tall_ref[:, rows]
            for head in range(heads_in):
                masked_q[head, rows, :] = head_lanes(query_ref[rows, :], head)
                masked_g[head, rows, :] = head_lanes(grads, head)
                delta[head : head + 1, rows] = jnp.sum(
                    product[head * HEAD : (head + 1) * HEAD, :], axis=0, keepdims=True
                )
            tall_q[:, rows] = jnp.zeros((LANES, block_k), jnp.float32)
            return carry

        lax.fori_loop(0, count // block_k, prepare, 0)

    key_first = index * block_k
    key_rows = pl.ds(pl.multiple_of(slots_ref[index] * block_k, block_k), block_k)
    keys = key_ref[key_rows, :]
    values = value_ref[key_rows, :]
    key_sum[...] = jnp.zeros_like(key_sum)
    value_sum[...] = jnp.zeros_like(value_sum)

    def visit(i, masked):
        query_first = i * block_q
        rows = pl.ds(pl.multiple_of(slots_ref[i] * block_q, block_q), block_q)
        if masked:
            allowed = pair_allowed(
                start_ref[0:1, rows], key_first, block_k, query_first, block_q
            )
        for head in range(heads_in):
            queries = masked_q[head, rows, :]
            grads = masked_g[head, rows, :]
            scores = dot_last(keys, queries)
            probs = jnp.exp(scores - log_ref[0, head : head + 1, rows])
            if masked:
                probs = jnp.where(allowed, probs, 0.0)
            value_sum[...] += dot_plain(probs.astype(jnp.bfloat16), grads)
            prob_grad = dot_last(values, grads)
            score_grad = (probs * (prob_grad - delta[head : head + 1, rows])).astype(jnp.bfloat16)
            key_sum[...] += dot_plain(score_grad, queries)
            lanes = slice(head * HEAD, (head + 1) * HEAD)
            tall_q[lanes, rows] += dot_plain(turned[lanes, key_rows], score_grad)

    def step(i, carry):
        whole = (key_first >= last_ref[i]) & (key_first + block_k - 1 <= i * block_q)

        @pl.when(whole)
        def _():
            visit(i, False)

        @pl.when(jnp.logical_not(whole))
        def _():
            visit(i, True)

        return carry

    lax.fori_loop(key_first // block_q, (end_ref[index] - 1) // block_q + 1, step, 0)
    out_ref[key_rows, LANES : 2 * LANES] = turn_back(key_sum[...], key_rows).astype(jnp.bfloat16)
    out_ref[key_rows, 2 * LANES :] = value_sum[...].astype(jnp.bfloat16)

    @pl.when(index == pl.num_programs(1) - 1)
    def _():
        def finish(j, carry):
            rows = pl.ds(pl.multiple_of(j * block_k, block_k), block_k)
            field = tall_q[:, rows].T * HEAD ** (-0.5)
            out_ref[rows, :LANES] = turn_back(field, rows).astype(jnp.bfloat16)
            return carry

        lax.fori_loop(0, count // block_k, finish, 0)


def attend_back(
    packed, slots, last, end, starts, cosine, sine, tall, logs, grads, heads_in, block_q, block_k
):
    count, width = packed.shape
    pairs = width // 3 // LANES
    return pl.pallas_call(
        partial(attend_back_kernel, block_q, block_k, heads_in),
        out_shape=jax.ShapeDtypeStruct((count, width), jnp.bfloat16),
        grid_spec=pltpu.PrefetchScalarGridSpec(
            num_scalar_prefetch=3,
            grid=(pairs, count // block_k),
            in_specs=[
                pl.BlockSpec((1, count), lambda p, i, *_: (0, 0)),
                pl.BlockSpec((count, LANES), lambda p, i, *_: (0, 0)),
                pl.BlockSpec((count, LANES), lambda p, i, *_: (0, 0)),
                pl.BlockSpec((count, LANES), lambda p, i, *_: (0, 3 * p)),
                pl.BlockSpec((count, LANES), lambda p, i, *_: (0, 3 * p + 1)),
                pl.BlockSpec((count, LANES), lambda p, i, *_: (0, 3 * p + 2)),
                pl.BlockSpec((LANES, count), lambda p, i, *_: (p, 0)),
                pl.BlockSpec((1, 8, count), lambda p, i, *_: (p, 0, 0)),
                pl.BlockSpec((count, LANES), lambda p, i, *_: (0, p)),
            ],
            out_specs=pl.BlockSpec((count, 3 * LANES), lambda p, i, *_: (0, p)),
            scratch_shapes=[
                pltpu.VMEM((LANES, count), jnp.bfloat16),
                pltpu.VMEM((heads_in, count, LANES), jnp.bfloat16),
                pltpu.VMEM((heads_in, count, LANES), jnp.bfloat16),
                pltpu.VMEM((8, count), jnp.float32),
                pltpu.VMEM((LANES, count), jnp.float32),
                pltpu.VMEM((block_k, LANES), jnp.float32),
                pltpu.VMEM((block_k, LANES), jnp.float32),
            ],
        ),
        compiler_params=pltpu.CompilerParams(vmem_limit_bytes=60 << 20),
        cost_estimate=short,
        name="attend_back",
    )(
        slots, last, end, starts.reshape(1, count), cosine, sine,
        packed, packed, packed, tall, logs, grads,
    )


def finish_kernel(narrow_count, wide_count, own_units, per_shard, entries, *refs):
    exchange = own_units > 0
    if exchange:
        (
            parts_ref, piece_ref, feed_ref, sent_ref, total_ref, stats_ref, arrived_ref, block_ref,
            mine, near, far, near_sum, send_near, recv_near, send_far, recv_far, send_ring, recv_ring,
            send_piece, recv_piece,
        ) = refs
    else:
        (
            parts_ref, piece_ref, feed_ref, sent_ref, total_ref, stats_ref, arrived_ref,
            mine, near, far, near_sum, send_near, recv_near, send_far, recv_far, send_ring, recv_ring,
        ) = refs
    narrow_me = lax.axis_index("narrow")
    wide_me = lax.axis_index("wide")

    def place(narrow_at, wide_at):
        return {"narrow": narrow_at, "wide": wide_at}

    def square_sum(value):
        value = value.astype(jnp.float32)
        return jnp.sum(
            jnp.sum(value * value, axis=0, keepdims=True), axis=1, keepdims=True
        )

    norm_rows = 2 * D // LANES
    row_at = lax.broadcasted_iota(jnp.int32, mine.shape, 0)
    lane_at = lax.broadcasted_iota(jnp.int32, mine.shape, 1)
    mine[...] = parts_ref[...] + jnp.where(
        (row_at == norm_rows) & (lane_at == 0),
        square_sum(piece_ref[...]) + square_sum(feed_ref[...]),
        0.0,
    )
    mesh_ids = pl.DeviceIdType.MESH
    barrier = pltpu.get_barrier_semaphore()
    greeted = 0
    for ahead in range(narrow_count):
        for across in range(wide_count):
            if (ahead > 0) + (across > 0) == 0 or (not exchange and ahead > 0 and across > 0):
                continue
            greeted += 1
            pl.semaphore_signal(
                barrier,
                inc=1,
                device_id=place(
                    lax.rem(narrow_me + ahead, narrow_count), lax.rem(wide_me + across, wide_count)
                ),
                device_id_type=mesh_ids,
            )
    pl.semaphore_wait(barrier, greeted)
    near_copies = []
    for ahead in range(1, narrow_count):
        copy = pltpu.make_async_remote_copy(
            src_ref=mine,
            dst_ref=near.at[narrow_me],
            send_sem=send_near.at[ahead - 1],
            recv_sem=recv_near.at[ahead - 1],
            device_id=place(lax.rem(narrow_me + ahead, narrow_count), wide_me),
            device_id_type=mesh_ids,
        )
        copy.start()
        near_copies.append(copy)
    near[narrow_me] = mine[...]
    if exchange:
        rows = piece_ref.shape[0]
        halves = block_ref.shape[0] // rows
        half_me = lax.rem(wide_me, halves)
        narrow_to = lax.div(wide_me, halves)
        moves = []
        for unit in range(3 * own_units):
            whole_unit = (unit % 3) * (D // LANES) + narrow_me * own_units + unit // 3
            wide_to = lax.div(whole_unit, per_shard)
            column = lax.rem(whole_unit, per_shard)
            source = piece_ref.at[:, unit * LANES : (unit + 1) * LANES]
            target = block_ref.at[
                pl.ds(pl.multiple_of(half_me * rows, rows), rows),
                pl.ds(pl.multiple_of(column * LANES, LANES), LANES),
            ]
            arrived = recv_piece.at[half_me * per_shard + column]
            remote = pltpu.make_async_remote_copy(
                src_ref=source,
                dst_ref=target,
                send_sem=send_piece.at[unit],
                recv_sem=arrived,
                device_id=place(narrow_to, wide_to),
                device_id_type=mesh_ids,
            )
            here = pltpu.make_async_copy(source, target, arrived)
            stays = (narrow_to == narrow_me) & (wide_to == wide_me)
            pl.when(jnp.logical_not(stays))(remote.start)
            pl.when(stays)(here.start)
            moves.append((stays, remote))
    for copy in near_copies:
        copy.wait()
    ring = pltpu.make_async_remote_copy(
        src_ref=sent_ref,
        dst_ref=arrived_ref,
        send_sem=send_ring,
        recv_sem=recv_ring,
        device_id=place(lax.rem(narrow_me + 1, narrow_count), wide_me),
        device_id_type=mesh_ids,
    )
    ring.start()
    value = near[0]
    for k in range(1, narrow_count):
        value = value + near[k]
    near_sum[...] = value
    far_copies = []
    for across in range(1, wide_count):
        copy = pltpu.make_async_remote_copy(
            src_ref=near_sum,
            dst_ref=far.at[wide_me],
            send_sem=send_far.at[across - 1],
            recv_sem=recv_far.at[across - 1],
            device_id=place(narrow_me, lax.rem(wide_me + across, wide_count)),
            device_id_type=mesh_ids,
        )
        copy.start()
        far_copies.append(copy)
    far[wide_me] = value
    for copy in far_copies:
        copy.wait()
    value = far[0]
    for k in range(1, wide_count):
        value = value + far[k]
    total_ref[...] = value
    grad_norm = jnp.sqrt(square_sum(value[:norm_rows]) + value[norm_rows : norm_rows + 1, 0:1])
    stats = [jnp.minimum(1.0, math.sqrt(NPARAMS) / grad_norm), grad_norm] + [
        jnp.sqrt(value[norm_rows : norm_rows + 1, k : k + 1] / entries) for k in (1, 2, 3)
    ]
    stats_ref[...] = jnp.zeros_like(stats_ref)
    for row, stat in enumerate(stats):
        stats_ref[row : row + 1, :] = jnp.broadcast_to(stat, (1, LANES))
    if exchange:
        for stays, remote in moves:
            pl.when(jnp.logical_not(stays))(remote.wait_send)
        for half in range(halves):
            for column in range(per_shard):
                pltpu.make_async_copy(
                    piece_ref.at[:, 0:LANES],
                    block_ref.at[
                        half * rows : (half + 1) * rows, column * LANES : (column + 1) * LANES
                    ],
                    recv_piece.at[half * per_shard + column],
                ).wait()
    ring.wait()


def finish(
    parts, piece, feed_piece, sent, exchange, narrow_count, wide_count, own_width, proj_cols, entries
):
    shape = parts.shape
    own_units = own_width // LANES if exchange else 0
    per_shard = proj_cols // LANES
    vmem = pl.BlockSpec(memory_space=pltpu.VMEM)
    shapes = [
        jax.ShapeDtypeStruct(shape, jnp.float32),
        jax.ShapeDtypeStruct((8, LANES), jnp.float32),
        jax.ShapeDtypeStruct(sent.shape, sent.dtype),
    ]
    whole = pl.BlockSpec(memory_space=pl.ANY)
    scratch = [
        pltpu.VMEM(shape, jnp.float32),
        pltpu.VMEM((narrow_count,) + shape, jnp.float32),
        pltpu.VMEM((wide_count,) + shape, jnp.float32),
        pltpu.VMEM(shape, jnp.float32),
        pltpu.SemaphoreType.DMA((narrow_count - 1,)),
        pltpu.SemaphoreType.DMA((narrow_count - 1,)),
        pltpu.SemaphoreType.DMA((wide_count - 1,)),
        pltpu.SemaphoreType.DMA((wide_count - 1,)),
        pltpu.SemaphoreType.DMA,
        pltpu.SemaphoreType.DMA,
    ]
    if exchange:
        shapes.append(jax.ShapeDtypeStruct((D // narrow_count, proj_cols), jnp.bfloat16))
        scratch += [
            pltpu.SemaphoreType.DMA((3 * own_units,)),
            pltpu.SemaphoreType.DMA((3 * own_units,)),
        ]
    return pl.pallas_call(
        partial(finish_kernel, narrow_count, wide_count, own_units, per_shard, entries),
        out_shape=tuple(shapes),
        in_specs=[vmem] * 3 + [whole],
        out_specs=(vmem, vmem, whole) + (vmem,) * (len(shapes) - 3),
        scratch_shapes=scratch,
        compiler_params=pltpu.CompilerParams(collective_id=0, has_side_effects=True),
        name="finish",
    )(parts, piece, feed_piece, sent)


def adam_update(
    weight, first_moment, second_moment, grad_value, step_rate, decay_coef, first_fix, second_fix
):
    new_first = beta_first * first_moment + (1.0 - beta_first) * grad_value
    new_second = beta_second * second_moment + (1.0 - beta_second) * grad_value * grad_value
    step_ratio = new_first / first_fix / (jnp.sqrt(new_second / second_fix) + adam_eps)
    return (weight - step_rate * (step_ratio + decay_coef * weight), new_first, new_second)


def adam_step(weight, first_moment, second_moment, gradient, step_rate, decay_coef, scales):
    new_first = beta_first * first_moment + (1.0 - beta_first) * gradient
    new_second = beta_second * second_moment + (1.0 - beta_second) * gradient * gradient
    ratio = new_first * scales[0] / (jnp.sqrt(new_second * scales[1]) + adam_eps)
    return (weight - step_rate * (ratio + decay_coef * weight), new_first, new_second)


def adam_kernel(scale_ref, stats_ref, grads_ref, total_ref, proj_ref, merge_ref, *refs):
    states, outs = refs[:15], refs[15:-1]
    norm_grads = refs[-1]
    matrix_step, norm_step = scale_ref[0, 0], scale_ref[0, 1]
    scales = (scale_ref[0, 2], scale_ref[0, 3])
    clip_factor = stats_ref[0:1, 0:1]

    def update(matrix, rows, gradient, step_rate, decay_coef):
        state = [ref[rows, :] for ref in states[3 * matrix : 3 * matrix + 3]]
        new = adam_step(*state, gradient * clip_factor, step_rate, decay_coef, scales)
        for out_ref, value in zip(outs[4 * matrix : 4 * matrix + 3], new):
            out_ref[rows, :] = value
        if matrix < 4:
            outs[4 * matrix + 3][rows, :] = new[0].astype(jnp.bfloat16)

    def feed_rows(rows):
        for matrix in range(2):
            gradient = grads_ref[0, matrix, rows, :].astype(jnp.float32)
            update(matrix, rows, gradient, matrix_step, decay_rate)

    in_chunks(states[0].shape[0], 16, feed_rows)

    @pl.when(pl.program_id(0) == 0)
    def _():
        def proj_rows(rows):
            update(2, rows, proj_ref[rows, :].astype(jnp.float32), matrix_step, decay_rate)

        in_chunks(proj_ref.shape[0], 32, proj_rows)
        update(3, slice(None), merge_ref[...].astype(jnp.float32).T, matrix_step, decay_rate)
        per_row = D // LANES
        for k in range(2 * per_row):
            at = k % per_row
            norm_grads[k // per_row : k // per_row + 1, at * LANES : (at + 1) * LANES] = total_ref[
                k : k + 1, :
            ]
        update(4, slice(None), norm_grads[...], norm_step, 0.0)
        outs[19][...] = norm_grads[...] * clip_factor


def adam_all(scales, stats, grads_all, total, proj_block, heads_part, own_width, states):
    count, matrices, rows, cols = grads_all.shape
    block = pl.BlockSpec((rows, cols), lambda i: (i, 0))

    def same(array):
        return pl.BlockSpec(array.shape, lambda i: (0, 0))

    feed_out = jax.ShapeDtypeStruct((count * rows, cols), jnp.float32)
    feed_copy = jax.ShapeDtypeStruct((count * rows, cols), jnp.bfloat16)
    shapes = [feed_out, feed_out, feed_out, feed_copy] * 2
    specs = [block] * 8
    for state in states[6::3]:
        full = jax.ShapeDtypeStruct(state.shape, jnp.float32)
        copy = jax.ShapeDtypeStruct(
            state.shape, jnp.float32 if state is states[12] else jnp.bfloat16
        )
        shapes += [full, full, full, copy]
        specs += [same(state)] * 4
    return pl.pallas_call(
        adam_kernel,
        out_shape=tuple(shapes),
        grid=(count,),
        in_specs=[
            pl.BlockSpec(memory_space=pltpu.SMEM),
            same(stats),
            pl.BlockSpec((1, matrices, rows, cols), lambda i: (i, 0, 0, 0)),
            same(total),
            same(proj_block),
            pl.BlockSpec((heads_part.shape[0], own_width), lambda i: (0, 3)),
        ]
        + [block] * 6
        + [same(state) for state in states[6:]],
        out_specs=tuple(specs),
        scratch_shapes=[pltpu.VMEM((2, D), jnp.float32)],
        cost_estimate=short,
        name="adam_all",
    )(scales, stats, grads_all, total, proj_block, heads_part, *states)


def settle_kernel(arrived_ref, term_ref, tokens_ref, cotangent_ref, params_ref, out_ref):
    unit, inv_std = normalize(tokens_ref[...])
    unit_grad = (arrived_ref[...].astype(jnp.float32) + term_ref[...]) * params_ref[0:1, :]
    out_ref[...] = cotangent_ref[...].astype(jnp.float32) + inv_std * (
        unit_grad
        - jnp.mean(unit_grad, axis=1, keepdims=True)
        - unit * jnp.mean(unit_grad * unit, axis=1, keepdims=True)
    )


def settle(arrived, term, tokens, cotangent, params):
    rows, depth = tokens.shape
    block = pl.BlockSpec((rows // 4, depth), lambda i: (i, 0))
    return pl.pallas_call(
        settle_kernel,
        out_shape=jax.ShapeDtypeStruct((rows, depth), jnp.float32),
        grid=(4,),
        in_specs=[block] * 4 + [pl.BlockSpec((2, depth), lambda i: (0, 0))],
        out_specs=block,
        cost_estimate=short,
        name="settle",
    )(arrived, term, tokens, cotangent, params)


def shards(
    tokens,
    cotangent,
    seq_lengths,
    step_count,
    norm_params,
    norm_first,
    norm_second,
    proj_weight,
    proj_first,
    proj_second,
    merge_weight,
    merge_first,
    merge_second,
    up_weight,
    up_first,
    up_second,
    down_weight,
    down_first,
    down_second,
):
    tok_rows = tokens.shape[0]
    narrow_count = lax.axis_size("narrow")
    wide_count = lax.axis_size("wide")
    span_index = lax.axis_index("narrow")
    group_rows = tok_rows * narrow_count
    own_width = HEADS // narrow_count * HEAD
    held_width = max(own_width, LANES)
    heads_in = min(own_width, LANES) // HEAD
    shard_rows = D // narrow_count
    proj_cols = proj_weight.shape[1]
    lengths = seq_lengths[0]
    onward = [(i, (i + 1) % narrow_count) for i in range(narrow_count)]
    slots = lax.rem(
        span_index + narrow_count - jnp.arange(narrow_count, dtype=jnp.int32), narrow_count
    )

    def pad_lanes(array, axis):
        extra = [(0, 0)] * array.ndim
        extra[axis] = (0, held_width - own_width)
        return jnp.pad(array, extra) if held_width > own_width else array

    def meet(*values):
        return lax.optimization_barrier(values)

    def send_on(array):
        return lax.ppermute(array, "narrow", onward)

    def rows_of(array, slot):
        return array[slot * tok_rows : (slot + 1) * tok_rows]

    direct = own_width % LANES == 0 and proj_cols % LANES == 0 and merge_weight.shape[1] == LANES
    weight_part = jnp.concatenate(
        [proj_weight.astype(jnp.bfloat16), merge_weight.astype(jnp.bfloat16)], axis=1
    )
    weight_rows = lax.all_gather(weight_part, "narrow", axis=0, tiled=True)
    up_slice = up_weight.astype(jnp.bfloat16)
    down_slice = down_weight.astype(jnp.bfloat16)

    def wide_all(array):
        return lax.all_gather(array, "wide", axis=0).reshape(
            wide_count, narrow_count, shard_rows, -1
        )

    order = list(range(1, narrow_count)) + [0]
    pairs = held_width // LANES
    token_blocks = [tokens]
    held = ()
    for slot in range(narrow_count - 1):
        moving = send_on(token_blocks[slot])
        held = feed(slot, narrow_count, token_blocks[slot], norm_params, up_slice, held)
        if slot == 1:
            held, weight_rows = meet(held, weight_rows)
            merge_all = wide_all(weight_rows[:, proj_cols:])
        if slot > 0:
            ready = [slot - 1, slot] if slot == narrow_count - 2 else [slot - 1]
            for block in ready:
                kept = jnp.bfloat16 if block == 1 else jnp.float32
                branch_terms.append(down_term(block, narrow_count, held[1], down_slice, kept))
            moving, held, branch_terms, down_slice = meet(moving, held, branch_terms, down_slice)
        else:
            moving, held = meet(moving, held)
        if slot == 0:
            lengths, slots, moving, weight_rows, down_slice = meet(
                lengths, slots, moving, weight_rows, down_slice
            )
            proj_rows, weight_rows = meet(weight_rows[:, :proj_cols], weight_rows)
            proj_all = wide_all(proj_rows)
            branch_terms = []
        if slot == 1:
            places = (
                slots[:, None] * tok_rows + jnp.arange(tok_rows, dtype=jnp.int32)[None, :]
            ).reshape(group_rows)
            seq_start, unused = locate(lengths, places)
            cosine, sine = rotary_tables(places - seq_start)
            block_first = jnp.arange(narrow_count, dtype=jnp.int32) * tok_rows
            first_start, unused = locate(lengths, block_first)
            last_start, last_end = locate(lengths, block_first + (tok_rows - 1))
            moving, cosine, sine, first_start, last_start, last_end = meet(
                moving, cosine, sine, first_start, last_start, last_end
            )
        token_blocks.append(moving)
    grad_first, last_block = meet(cotangent, token_blocks[-1])
    token_blocks[-1] = last_block
    grad_blocks = [grad_first]

    moving = send_on(grad_first)
    gathered, activated, slope = feed(
        narrow_count - 1, narrow_count, last_block, norm_params, up_slice, held
    )
    if direct:
        packed, proj_own = project_all(
            gathered, proj_all, span_index, own_width, cosine, sine
        )
        merge_own = merge_all
    else:
        proj_copy = jnp.transpose(proj_all, (1, 2, 0, 3)).reshape(
            D, 3, narrow_count, own_width
        )
        proj_own = pad_lanes(
            lax.dynamic_index_in_dim(proj_copy, span_index, axis=2, keepdims=False), 2
        ).reshape(D, 3 * held_width)
        merge_copy = jnp.transpose(merge_all, (1, 2, 0, 3)).reshape(
            narrow_count, own_width, D
        )
        merge_own = pad_lanes(
            lax.dynamic_index_in_dim(merge_copy, span_index, axis=0, keepdims=False), 0
        )
        packed = project(gathered, proj_own, cosine, sine)

    def push_slot(slot, push_held):
        return push(
            slot, narrow_count, grad_blocks[slot], slope, down_slice, merge_own, span_index,
            push_held,
        )

    packed, grad_blocks[0] = meet(packed, grad_blocks[0])
    push_held = push_slot(0, ())
    branch_terms.append(
        down_term(narrow_count - 1, narrow_count, activated, down_slice, jnp.float32)
    )
    moving, packed, activated, slope, push_held, branch_terms = meet(
        moving, packed, activated, slope, push_held, branch_terms
    )
    grad_blocks.append(moving)

    def wide_sum(grad):
        return lax.psum_scatter(grad, "wide", scatter_dimension=0, tiled=True)

    def attend_pair(pair, attended_held):
        return attend(
            pair, packed, slots, first_start, last_start, seq_start,
            heads_in, tok_rows, tok_rows, attended_held,
        )

    attended_held = ()
    for hop in range(2, narrow_count):
        moving = send_on(grad_blocks[-1])
        if hop - 2 < pairs:
            attended_held = attend_pair(hop - 2, attended_held)
        push_held = push_slot(hop - 1, push_held)
        moving, attended_held, push_held = meet(moving, attended_held, push_held)
        grad_blocks.append(moving)
    for pair in range(narrow_count - 2, pairs):
        attended_held = attend_pair(pair, attended_held)
    attended, tall, logs = attended_held

    moving = send_on(branch_terms[1])
    push_held = push_slot(narrow_count - 1, push_held)
    grads_all, hidden_grad, attended_grad = push_held
    part_rows = D // wide_count
    if direct:
        feed_grad = outer(wide_count, gathered, hidden_grad, activated, grads_all)
    else:
        down_grad = dot_first(activated, grads_all).astype(jnp.bfloat16)
        up_grad = dot_first(gathered, hidden_grad).astype(jnp.bfloat16)
        feed_grad = jnp.stack(
            [
                up_grad.reshape(wide_count, part_rows, -1),
                down_grad.reshape(wide_count, part_rows, -1),
            ],
            axis=1,
        )
    feed_grad = feed_grad.reshape(2 * D, -1)
    pieces = [
        rows_of(attended, (narrow_count - ahead) % narrow_count)[:, :own_width]
        for ahead in range(narrow_count)
    ]
    moving, pieces, feed_grad, attended_grad = meet(moving, pieces, feed_grad, attended_grad)
    feed_part = wide_sum(feed_grad)

    for ahead in range(1, narrow_count):
        pieces[ahead] = lax.ppermute(
            pieces[ahead],
            "narrow",
            [(i, (i + ahead) % narrow_count) for i in range(narrow_count)],
        )
    terms = []
    term_blocks = []

    def term_at(place):
        block, at = terms[place]
        return rows_of(term_blocks[block], at)

    norm_part = jnp.zeros((2, D), jnp.float32)

    def pull_more(slots_now, norm_part):
        if slots_now:
            lead, block, sums = pull(
                slots_now[0], mixed_grad, hidden_grad, proj_own, up_slice,
                [token_blocks[slot] for slot in slots_now],
            )
            if not term_blocks:
                term_blocks.append(lead)
            term_blocks.append(block)
            for place in range(len(slots_now)):
                terms.append((len(term_blocks) - 1, place))
            norm_part = norm_part + sums
        return norm_part

    for place, slot in enumerate(order[1:-1]):
        moving = send_on((moving.astype(jnp.float32) + branch_terms[slot]).astype(jnp.bfloat16))
        if place == 0:
            mixed_grad = attend_back(
                packed, slots, last_start, last_end, seq_start, cosine, sine,
                tall, logs, attended_grad, heads_in, tok_rows, tok_rows,
            )
            if direct:
                heads_grad = outer(0, gathered, mixed_grad, grads_all, attended)
            else:
                proj_grad = dot_first(gathered, mixed_grad).astype(jnp.bfloat16)
                merge_grad = dot_first(grads_all, attended).astype(jnp.bfloat16)
                proj_grad = proj_grad.reshape(D, 3, held_width)[:, :, :own_width]
                heads_grad = jnp.concatenate(
                    [proj_grad.reshape(D, 3 * own_width), merge_grad[:, :own_width]], axis=1
                )
            moving, pieces, mixed_grad, heads_grad, feed_part = meet(
                moving, pieces, mixed_grad, heads_grad, feed_part
            )
            heads_part = wide_sum(heads_grad)
        else:
            norm_part = pull_more(order[:-1][len(terms) : len(terms) + 3], norm_part)
            moving, term_blocks[:], norm_part, feed_part, merge_all, slots = meet(
                moving, term_blocks, norm_part, feed_part, merge_all, slots
            )
        if place == narrow_count - 3:
            feed_all = lax.all_gather(feed_part, "wide", axis=0).reshape(
                wide_count, 2, part_rows, -1
            )
    branch_moving = moving
    moving = send_on(term_blocks[0])
    norm_part = pull_more(order[len(terms) : -1], norm_part)
    norm_part = pull_more([0], norm_part)
    branch = branch_moving.astype(jnp.float32) + branch_terms[0]
    if direct:
        merge_turn = pick_merge(merge_all, slots, own_width)
    else:
        merge_turn = jnp.take(
            jnp.transpose(merge_all, (1, 2, 0, 3)).reshape(narrow_count, own_width, D),
            slots,
            axis=0,
        ).reshape(D, D)
    merged = dot_plain(jnp.concatenate(pieces, axis=1), merge_turn)
    output_rows = tokens.astype(jnp.float32) + merged + branch
    layer_out = output_rows.astype(jnp.bfloat16)

    def squares(array):
        value = array.astype(jnp.float32)
        return jnp.sum(value * value)

    row_squares = [squares(output_rows), squares(merged), squares(branch)]
    scalars = jnp.stack([jnp.zeros((), jnp.float32)] + row_squares)
    parts = jnp.concatenate(
        [norm_part.reshape(2 * D // LANES, LANES), jnp.pad(scalars, (0, LANES - 4))[None, :]]
    )
    parts = jnp.pad(parts, ((0, 7), (0, 0)))
    step_value = step_count[0].astype(jnp.float32)
    first_fix = 1.0 - jnp.power(beta_first, step_value)
    second_fix = 1.0 - jnp.power(beta_second, step_value)
    ramp = jnp.minimum(1.0, step_value / warmup_steps)
    scales = jnp.stack(
        [matrix_rate * ramp, norm_rate * ramp, 1.0 / first_fix, 1.0 / second_fix]
    ).reshape(1, 4)
    entries = wide_count * group_rows * D
    for place in range(1, narrow_count - 1):
        if place == narrow_count - 3:
            moving, parts, heads_part, scales = meet(moving, parts, heads_part, scales)
        sent = (moving.astype(jnp.float32) + term_at(place)).astype(jnp.bfloat16)
        if place == narrow_count - 3:
            total, stats, moving, *proj_block = finish(
                parts, heads_part, feed_part, sent, direct, narrow_count, wide_count, own_width,
                proj_cols, entries,
            )
            continue
        if place == narrow_count - 2:
            sent, total, stats, proj_block = meet(sent, total, stats, proj_block)
        moving = send_on(sent)

    if direct:
        updated = adam_all(
            scales, stats, feed_all, total, proj_block[0], heads_part, own_width,
            [
                up_weight, up_first, up_second, down_weight, down_first, down_second,
                proj_weight, proj_first, proj_second, merge_weight, merge_first, merge_second,
                norm_params, norm_first, norm_second,
            ],
        )
    else:
        clip_factor = stats[0, 0:1]
        cross = lax.all_gather(heads_part[:, : 3 * own_width], "narrow", axis=0).reshape(
            narrow_count, part_rows, 3, own_width
        )
        cross = jnp.transpose(cross, (1, 2, 0, 3)).reshape(part_rows, wide_count, proj_cols)
        cross = lax.all_to_all(jnp.transpose(cross, (1, 0, 2)), "wide", 0, 0)
        proj_block = lax.dynamic_slice_in_dim(
            cross.reshape(D, proj_cols), span_index * shard_rows, shard_rows, axis=0
        )
        merge_block = heads_part[:, 3 * own_width :].T
        norm_total = total[: 2 * D // LANES].reshape(2, D)
        feed_sums = feed_all.astype(jnp.float32)
        updated = []
        for state, gradient, step_rate, decay_coef in (
            ((up_weight, up_first, up_second), feed_sums[:, 0], matrix_rate, decay_rate),
            ((down_weight, down_first, down_second), feed_sums[:, 1], matrix_rate, decay_rate),
            ((proj_weight, proj_first, proj_second), proj_block, matrix_rate, decay_rate),
            ((merge_weight, merge_first, merge_second), merge_block, matrix_rate, decay_rate),
            ((norm_params, norm_first, norm_second), norm_total, norm_rate, 0.0),
        ):
            clipped = gradient.reshape(state[0].shape).astype(jnp.float32) * clip_factor
            new = adam_update(
                *state, clipped, step_rate * ramp, decay_coef, first_fix, second_fix
            )
            updated += [*new, clipped if state[0] is norm_params else new[0].astype(jnp.bfloat16)]
    new_up, new_down, new_proj, new_merge, new_norm = [
        updated[4 * k : 4 * k + 4] for k in range(5)
    ]
    moving, new_up = meet(moving, new_up)
    input_grad = settle(moving, term_at(-1), tokens, cotangent, norm_params)
    return (
        layer_out,
        input_grad,
        stats[1, 0:1],
        stats[2, 0:1],
        new_norm[3],
        new_norm[0],
        new_norm[1],
        new_norm[2],
        new_proj[0],
        new_proj[1],
        new_proj[2],
        new_merge[0],
        new_merge[1],
        new_merge[2],
        new_up[0],
        new_up[1],
        new_up[2],
        new_down[0],
        new_down[1],
        new_down[2],
        stats[3:5, 0],
        new_proj[3],
        new_merge[3],
        new_up[3],
        new_down[3],
    )


def solution(mesh):
    placed = (
        P(("wide", "narrow"), None),
        P(("wide", "narrow"), None),
        P("wide", None),
        P(),
        P(),
        P(),
        P(),
        P("narrow", "wide"),
        P("narrow", "wide"),
        P("narrow", "wide"),
        P("narrow", "wide"),
        P("narrow", "wide"),
        P("narrow", "wide"),
        P(None, "narrow"),
        P(None, "narrow"),
        P(None, "narrow"),
        P("narrow", None),
        P("narrow", None),
        P("narrow", None),
    )
    return jax.shard_map(
        shards,
        mesh=mesh,
        in_specs=placed,
        out_specs=(
            P(("wide", "narrow"), None),
            P(("wide", "narrow"), None),
            P(),
            P(),
            P(),
            P(),
            P(),
            P(),
            P("narrow", "wide"),
            P("narrow", "wide"),
            P("narrow", "wide"),
            P("narrow", "wide"),
            P("narrow", "wide"),
            P("narrow", "wide"),
            P(None, "narrow"),
            P(None, "narrow"),
            P(None, "narrow"),
            P("narrow", None),
            P("narrow", None),
            P("narrow", None),
            P(),
            P("narrow", "wide"),
            P("narrow", "wide"),
            P(None, "narrow"),
            P("narrow", None),
        ),
        check_vma=False,
    )
```
